32 devices in a mesh: bx: 8 (over z, y), by: 4 (over x, core).
Axes of the slice: x: 2, y: 2, z: 4, core: 2. Of those that a mesh axis runs over, the one named last changes fastest.
Arguments:
- polarization: float32 [3, 8, 256, 512], P(None, None, 'bx', 'by'), may hold values from -1.6 to 1.6
- alpha_field: float32 [8, 256, 512], P(None, 'bx', 'by'), may hold values from -1 to 1
- landau: float32 [3, 8], replicated, may hold values from 0.05 to 0.25
- stiffness: float32 [8], replicated, may hold values from 0.5 to 1.5
- permittivity: float32 [8], replicated, may hold values from 0.5 to 2
- interfaces: float32 [9], replicated, may hold values from 0.0002 to 0.0008
Outputs:
- polar_next: float32 [3, 8, 256, 512], P(None, None, 'bx', 'by')
- depol_field: float32 [3, 8, 256, 512], P(None, None, 'bx', 'by')
The draws below stay inside these ranges and needn't reach their ends.
All inputs are finite; a program needn't handle non-finite values.
Results may differ from the reference program's by a relative error of at most 0.0003.
Values sent between devices are 32-bit elements; how exact they have to be, the bound alone decides.
A program may use at most 64 MiB of HBM per device.

```python
import math
import jax
import jax.numpy as jnp
from jax import lax

LAYERS = 8
STEPS = 2
NX = 256
NY = 512


def draw_polarization(key, part):
    return 0.5 * jax.random.truncated_normal(key, -3.2, 3.2, (3, LAYERS, NX, NY), jnp.float32)


def shard_levels(stream_key, shape, pieces, least, top_value):
    factor_of, own = 1.0, jax.random.fold_in(stream_key, 6)
    for axis_at, blocks in pieces:
        draws = jnp.exp(jax.random.uniform(jax.random.fold_in(own, axis_at), (blocks,), jnp.float32, least / len(pieces), top_value / len(pieces)))
        factor_of = factor_of * jnp.repeat(draws, shape[axis_at] // blocks).reshape([-1 if axis == axis_at else 1 for axis in range(len(shape))])
    return factor_of


def setup_inputs(seed: int = 0) -> dict:
    key_of = jax.random.split(jax.random.key(seed), 7)
    return {
        "polarization": draw_polarization(jax.random.fold_in(key_of[6], 71), 0),
        "alpha_field": jnp.clip(jax.random.uniform(key_of[1], (LAYERS, NX, NY), jnp.float32, -1.0, 1.0) * shard_levels(key_of[1], (LAYERS, NX, NY), ((1, 8), (2, 4)), -0.4, 0.0), -1.0, 1.0),
        "landau": jnp.clip(jax.random.uniform(key_of[2], (3, LAYERS), jnp.float32, 0.05, 0.25), 0.05, 0.25),
        "stiffness": jnp.clip(jax.random.uniform(key_of[3], (LAYERS,), jnp.float32, 0.5, 1.5), 0.5, 1.5),
        "permittivity": jnp.clip(jnp.exp(jax.random.uniform(key_of[4], (LAYERS,), jnp.float32, math.log(0.5), math.log(2.0))), 0.5, 2.0),
        "interfaces": jnp.clip(jnp.exp(jax.random.uniform(key_of[5], (LAYERS + 1,), jnp.float32, math.log(0.0002), math.log(0.0008))), 0.0002, 0.0008),
    }


step_size = 0.05


def shift_up(source, axis_no):
    upper_part = lax.slice_in_dim(source, 1, source.shape[axis_no], axis=axis_no)
    return jnp.concatenate([upper_part, jnp.zeros_like(lax.slice_in_dim(source, 0, 1, axis=axis_no))], axis=axis_no)


def shift_down(source, axis_no):
    lower_part = lax.slice_in_dim(source, 0, source.shape[axis_no] - 1, axis=axis_no)
    return jnp.concatenate([jnp.zeros_like(lax.slice_in_dim(source, 0, 1, axis=axis_no)), lower_part], axis=axis_no)


def central(source, axis_no):
    return 0.5 * (jnp.roll(source, -1, axis_no) - jnp.roll(source, 1, axis_no))


def depolarize(polar_now, permittivity, interfaces):
    charge = -(central(polar_now[0], 1) + central(polar_now[1], 2)
               + 0.5 * (shift_up(polar_now[2], 0) - shift_down(polar_now[2], 0)))
    spectrum = jnp.fft.fft2(charge)
    layers = charge.shape[0]
    grid_x = charge.shape[1]
    grid_y = charge.shape[2]
    wave_x = jnp.sin(jnp.pi * jnp.arange(grid_x).astype(jnp.float32) / grid_x)
    wave_y = jnp.sin(jnp.pi * jnp.arange(grid_y).astype(jnp.float32) / grid_y)
    lateral = 4.0 * wave_x[:, None] ** 2 + 4.0 * wave_y[None, :] ** 2
    ratios = []
    primes = []
    for layer_no in range(layers):
        diagonal = permittivity[layer_no] * lateral + interfaces[layer_no] + interfaces[layer_no + 1]
        source = spectrum[layer_no]
        if layer_no == 0:
            pivot_now = diagonal
            primed = source / pivot_now
        else:
            pivot_now = diagonal - interfaces[layer_no] * ratios[-1]
            primed = (source + interfaces[layer_no] * primes[-1]) / pivot_now
        primes.append(primed)
        ratios.append(interfaces[layer_no + 1] / pivot_now)
    values = [primes[-1]]
    for layer_no in range(layers - 2, -1, -1):
        values.insert(0, primes[layer_no] + ratios[layer_no] * values[0])
    potential = jnp.real(jnp.fft.ifft2(jnp.stack(values)))
    along_x = -0.5 * (jnp.roll(potential, -1, 1) - jnp.roll(potential, 1, 1))
    along_y = -0.5 * (jnp.roll(potential, -1, 2) - jnp.roll(potential, 1, 2))
    along_z = -0.5 * (shift_up(potential, 0) - shift_down(potential, 0))
    return jnp.stack([along_x, along_y, along_z])


def evolve(centre, alpha_field, landau, stiffness, field_now):
    squares = centre * centre
    total = squares[0] + squares[1] + squares[2]
    quartic = landau[0][None, :, None, None]
    mixed = landau[1][None, :, None, None]
    sextic = landau[2][None, :, None, None]
    kappa = stiffness[None, :, None, None]
    lateral = (jnp.roll(centre, -1, 2) + jnp.roll(centre, 1, 2) + jnp.roll(centre, -1, 3)
               + jnp.roll(centre, 1, 3) - 4.0 * centre)
    vertical = shift_up(centre, 1) + shift_down(centre, 1) - 2.0 * centre
    drive = (2.0 * alpha_field[None] * centre + 4.0 * quartic * centre * squares
             + 2.0 * mixed * centre * (total[None] - squares) + 6.0 * sextic * centre * squares * squares)
    smooth = kappa * (lateral + vertical)
    return centre - step_size * (drive - smooth - field_now)


def reference(polarization, alpha_field, landau, stiffness, permittivity, interfaces):
    polar_now = polarization
    field_now = jnp.zeros_like(polarization)
    for step_no in range(STEPS):
        field_now = depolarize(polar_now, permittivity, interfaces)
        polar_now = evolve(polar_now, alpha_field, landau, stiffness, field_now)
    return polar_now, field_now
```

```python
import functools

import jax
import jax.numpy as jnp
import numpy as np
from jax import lax
from jax.experimental import pallas as pl
from jax.experimental.pallas import tpu as pltpu
from jax.sharding import PartitionSpec as P

STEPS = 2
step_size = 0.05
MESH = pl.DeviceIdType.MESH
PAD = 8


def cas_table(left, right, length):
    turns = left * right % length
    angle = 2.0 * jnp.pi / length * turns.astype(jnp.float32)
    table = jnp.cos(angle) + jnp.sin(angle)
    high = lax.reduce_precision(table, 8, 7)
    return jnp.stack([high.astype(jnp.bfloat16), (table - high).astype(jnp.bfloat16)])


def fixed_table(left, right, length):
    angle = 2.0 * np.pi / length * (left * right % length)
    table = (np.cos(angle) + np.sin(angle)).astype(np.float32)
    high = table.astype(jnp.bfloat16)
    low = (table - high.astype(np.float32)).astype(jnp.bfloat16)
    return jnp.asarray(np.stack([high, low]))


def is_wide(rows, nbx, nby, layers):
    return layers % nbx == 0 and rows % (8 * nby) == 0


def halves(value):
    high = value.astype(jnp.bfloat16)
    low = (value - high.astype(jnp.float32)).astype(jnp.bfloat16)
    return high, low


def product(left, right):
    dot = functools.partial(jnp.dot, preferred_element_type=jnp.float32)
    return dot(left[0], right[0]) + (dot(left[0], right[1]) + dot(left[1], right[0]))


def kernel(sizes, p_in, alpha_h, landau, stiff, perm, inter, lam, hx_h, hy_h, p_out, f_out, *scratch):
    L, R, C, nbx, nby, rep, lp, own = sizes
    (p_mid, base, coef, ratio, q, inb, outs, rec_i,
     row_s, row_r, col_s, col_r, pc_s, pc_r, ssem, rsem,
     alpha, hx, hy, local_sem) = scratch[:20]
    wide = is_wide(R, nbx, nby, L)
    if wide:
        z_in, w_out = scratch[20:]
    else:
        rec_f, ybuf, phat, u = scratch[20:]
    thin = R // nby
    R2 = R + PAD
    bx = lax.axis_index("bx")
    by = lax.axis_index("by")
    group = bx // rep
    part = bx % rep
    scale = 1.0 / (R * nbx * C * nby)
    loads = [pltpu.make_async_copy(src, dst, local_sem.at[at]) for at, (src, dst) in
             enumerate(((alpha_h, alpha), (hx_h, hx), (hy_h, hy)))]
    for load in loads:
        load.start()
    slots = [0]
    sends = []

    barrier = pltpu.get_barrier_semaphore()
    others = [(a, b) for b in range(nby) for a in range(nbx) if a or b]
    greeted = [(a, b) for a, b in others if wide or not a or not b]
    for a, b in greeted:
        pl.semaphore_signal(
            barrier, inc=1, device_id={"bx": (bx + a) % nbx, "by": (by + b) % nby},
            device_id_type=MESH)

    def remote(src, dst, device, slot):
        return pltpu.make_async_remote_copy(
            src_ref=src, dst_ref=dst, send_sem=ssem.at[slot], recv_sem=rsem.at[slot],
            device_id=device, device_id_type=MESH)

    def fresh():
        slots[0] += 1
        return slots[0] - 1

    def push(src, dst, device):
        copy = remote(src, dst, device, fresh())
        copy.start()
        sends.append(copy.wait_send)
        return copy

    rows = lax.broadcasted_iota(jnp.int32, (R, C), 0)
    lanes = lax.broadcasted_iota(jnp.int32, (R, C), 1)

    def x_next(f, high):
        return jnp.where(rows == R - 1, high, pltpu.roll(f, R - 1, 0))

    def x_prev(f, low):
        return jnp.where(rows == 0, low, pltpu.roll(f, 1, 0))

    def y_next(f, high):
        return jnp.where(lanes == C - 1, high, pltpu.roll(f, C - 1, 1))

    def y_prev(f, low):
        return jnp.where(lanes == 0, low, pltpu.roll(f, 1, 1))

    def column_tile(blocks):
        tile = jnp.zeros((R, C), jnp.float32)
        for at, block in enumerate(blocks):
            tile = jnp.where(lanes == at, block[:, 0:1], tile)
            tile = jnp.where(lanes == C // 2 + at, block[:, C - 1:C], tile)
        return tile

    def x_start(src, n):
        mine = inb.at[n, :, pl.ds(pl.multiple_of(bx * R, R), R)]
        copies = []
        for k in range(1, nbx):
            to = (bx + k) % nbx
            copies.append(push(src.at[pl.ds(to // rep * lp, lp)], mine, {"bx": to}))
        for layer in range(lp):
            inb[n, layer, pl.ds(pl.multiple_of(bx * R, R), R)] = src[group * lp + layer]
        return copies

    def x_mix(copies, n):
        for copy in copies:
            copy.wait_recv()
        table = (hx[0], hx[1])
        for layer in range(lp):
            outs[n, :, layer] = product(table, halves(inb[n, layer])).reshape(own, R2, C)

    def spread(n, step):
        copies = []
        for a, b in others:
            to_x, to_y = (bx + a) % nbx, (by + b) % nby
            copies.append(push(
                outs.at[n, to_x, :, pl.ds(pl.multiple_of(to_y * thin, thin), thin)],
                z_in.at[step, by, pl.ds(bx * lp, lp)], {"bx": to_x, "by": to_y}))
        for layer in range(lp):
            z_in[step, by, bx * lp + layer] = outs[
                n, bx, layer, pl.ds(pl.multiple_of(by * thin, thin), thin)]
        for copy in copies:
            copy.wait_recv()

    def collect(n, step):
        at = pl.ds(pl.multiple_of(bx * R + by * thin, thin), thin)
        copies = []
        for a, b in others:
            to_x, to_y = (bx + a) % nbx, (by + b) % nby
            copies.append(push(
                w_out.at[step, to_y, pl.ds(to_x * lp, lp)], inb.at[n, :, at],
                {"bx": to_x, "by": to_y}))
        for layer in range(lp):
            inb[n, layer, at] = w_out[step, by, bx * lp + layer]
        return copies

    def solve(spectrum, height):
        primes = []
        for l in range(L):
            source = spectrum[l * height:(l + 1) * height] * scale
            if l:
                source = source + inter[l] * primes[-1]
            primes.append(source * coef[l])
        values = [primes[-1]]
        for l in range(L - 2, -1, -1):
            values.insert(0, primes[l] + ratio[l] * values[0])
        return values

    def x_finish(n, dst, height):
        waits = []
        landing = dst.at[pl.ds(group * lp, lp)]
        for t in range(own):
            local = (group + t) % own
            to = part * own + local
            src = outs.at[n, local, :, pl.ds(0, height)]
            if rep == 1:
                if t == 0:
                    continue
                waits.append(push(src, landing, {"bx": to}).wait_recv)
                continue
            slot = fresh()

            def go(src=src, to=to, slot=slot):
                remote(src, landing, {"bx": to}, slot).start()

            def gone(src=src, to=to, slot=slot):
                @pl.when(to != bx)
                def _():
                    remote(src, landing, {"bx": to}, slot).wait_send()

            def came(src=src, to=to, slot=slot, t=t):
                origin = (bx % own + own - t) % own * rep + bx // own

                @pl.when(origin != bx)
                def _():
                    remote(src, landing, {"bx": to}, slot).wait_recv()

            pl.when(to != bx)(go)
            sends.append(gone)
            waits.append(came)

        def keep():
            for layer in range(lp):
                dst[group * lp + layer] = outs[n, bx % own, layer, 0:height]

        if rep == 1:
            keep()
        else:
            pl.when(bx // own == part)(keep)
        for wait in waits:
            wait()

    def y_pass(src, n):
        copies = [push(src, ybuf.at[n, k - 1], {"by": (by + k) % nby}) for k in range(1, nby)]
        total = product(halves(src[...].reshape(L * R, C)), (hy[0, by], hy[1, by]))
        for k in range(1, nby):
            copies[k - 1].wait_recv()
            origin = (by + nby - k) % nby
            total += product(halves(ybuf[n, k - 1].reshape(L * R, C)), (hy[0, origin], hy[1, origin]))
        return total

    def flank_start(rows_too, step, src):
        copies = []
        if rows_too:
            for c in range(3):
                for l in range(L):
                    at = c * L + l
                    row_s[step, 0, at:at + 1] = src[c, l, 0:1]
                    row_s[step, 1, at:at + 1] = src[c, l, R - 1:R]
            col_s[step] = column_tile([src[c, l] for c in range(3) for l in range(L)])
            if step == 0:
                pl.semaphore_wait(barrier, len(greeted))
            copies.append(push(row_s.at[step, 1], row_r.at[step, 0], {"bx": (bx + 1) % nbx}))
            copies.append(push(row_s.at[step, 0], row_r.at[step, 1], {"bx": (bx + nbx - 1) % nbx}))
            tile, land = col_s.at[step], col_r
        else:
            pc_s[step] = column_tile([src[l, 0:R] for l in range(L)])
            tile, land = pc_s.at[step], pc_r
        copies.append(push(tile, land.at[step, 0], {"by": (by + 1) % nby}))
        copies.append(push(tile, land.at[step, 1], {"by": (by + nby - 1) % nby}))
        return copies

    for step in range(STEPS):
        src = p_in if step == 0 else p_mid
        flanks = flank_start(True, step, src)
        if step == 0:
            lateral = lam[...]
            previous = None
            for l in range(L):
                pivot = perm[l] * lateral + inter[l] + inter[l + 1]
                if l:
                    pivot = pivot - inter[l] * previous
                inverse = 1.0 / pivot
                coef[l] = inverse
                previous = inter[l + 1] * inverse
                ratio[l] = previous
        for copy in flanks:
            copy.wait_recv()
        low_col = col_r[step, 0]
        high_col = col_r[step, 1]

        def edges(c, l):
            at = c * L + l
            return (row_r[step, 0, at:at + 1], row_r[step, 1, at:at + 1],
                    low_col[:, C // 2 + at:C // 2 + at + 1], high_col[:, at:at + 1])

        zero = jnp.zeros((R, C), jnp.float32)
        for l in range(L):
            low, high, _, _ = edges(0, l)
            _, _, left, right = edges(1, l)
            along_x, along_y = src[0, l], src[1, l]
            above = src[2, l + 1] if l + 1 < L else zero
            below = src[2, l - 1] if l else zero
            q[step, l] = -0.5 * (
                (x_next(along_x, high) - x_prev(along_x, low))
                + (y_next(along_y, right) - y_prev(along_y, left)) + (above - below))
        copies = x_start(q.at[step], 2 * step)
        if step == 0:
            for load in loads:
                load.wait()
        for l in range(L):
            cells = [src[c, l] for c in range(3)]
            squares = [cell * cell for cell in cells]
            whole = squares[0] + squares[1] + squares[2]
            for c in range(3):
                cell, square = cells[c], squares[c]
                low, high, left, right = edges(c, l)
                above = src[c, l + 1] if l + 1 < L else zero
                below = src[c, l - 1] if l else zero
                smooth = stiff[l] * (
                    (x_next(cell, high) + x_prev(cell, low) + y_next(cell, right)
                     + y_prev(cell, left) - 4.0 * cell) + (above + below - 2.0 * cell))
                drive = cell * (
                    2.0 * alpha[l] + 4.0 * landau[0, l] * square
                    + 2.0 * landau[1, l] * (whole - square)
                    + 6.0 * landau[2, l] * (square * square))
                base[c, l] = cell - step_size * (drive - smooth)
        n = 2 * step
        x_mix(copies, n)
        if wide:
            spread(n, step)
            table = (hy[0], hy[1])
            full = jnp.concatenate(
                [z_in[step, j].reshape(L * thin, C) for j in range(nby)], axis=1)
            values = solve(product(halves(full), table), thin)
            full = product(halves(jnp.concatenate(values, axis=0)), table)
            for j in range(nby):
                w_out[step, j] = full[:, j * C:(j + 1) * C].reshape(L, thin, C)
            copies = collect(n + 1, step)
        else:
            x_finish(n, rec_f.at[step], R)
            for l, value in enumerate(solve(y_pass(rec_f.at[step], n), R)):
                phat[step, l] = value
            u[step] = y_pass(phat.at[step], n + 1).reshape(L, R, C)
            copies = x_start(u.at[step], n + 1)
        x_mix(copies, n + 1)
        x_finish(n + 1, rec_i.at[step], R2)
        flanks = flank_start(False, step, rec_i.at[step])
        last = step == STEPS - 1
        target = p_out if last else p_mid
        for l in range(L):
            phi = rec_i[step, l, 0:R]
            low = rec_i[step, l, R:R + 1]
            high = rec_i[step, l, R + 1:R + 2]
            along_x = -0.5 * (x_next(phi, high) - x_prev(phi, low))
            above = rec_i[step, l + 1, 0:R] if l + 1 < L else zero
            below = rec_i[step, l - 1, 0:R] if l else zero
            along_z = -0.5 * (above - below)
            target[0, l] = base[0, l] + step_size * along_x
            target[2, l] = base[2, l] + step_size * along_z
            if last:
                f_out[0, l] = along_x
                f_out[2, l] = along_z
        for copy in flanks:
            copy.wait_recv()
        low_phi = pc_r[step, 0]
        high_phi = pc_r[step, 1]
        for l in range(L):
            phi = rec_i[step, l, 0:R]
            along_y = -0.5 * (y_next(phi, high_phi[:, l:l + 1])
                              - y_prev(phi, low_phi[:, C // 2 + l:C // 2 + l + 1]))
            target[1, l] = base[1, l] + step_size * along_y
            if last:
                f_out[1, l] = along_y
    for wait in sends:
        wait()


def shards(polarization, alpha_field, landau, stiffness, permittivity, interfaces):
    _, L, R, C = polarization.shape
    nbx = lax.axis_size("bx")
    nby = lax.axis_size("by")
    bx = lax.axis_index("bx")
    by = lax.axis_index("by")
    rep = max(1, nbx // L)
    lp = max(1, L // nbx)
    own = nbx // rep
    grid_x, grid_y = nbx * R, nby * C
    R2 = R + PAD
    wide = is_wide(R, nbx, nby, L)
    pool = np if wide else jnp
    make = fixed_table if wide else cas_table
    line = pool.arange(R2, dtype=jnp.int32)
    line = pool.where(line < R, line, pool.where(line == R, -1, R))
    owners = pool.arange(own, dtype=jnp.int32)
    if not wide:
        owners = owners + bx % rep * own
    wanted = ((owners[:, None] * R + line[None, :] + grid_x) % grid_x).reshape(own * R2, 1)
    hx = make(wanted, pool.arange(grid_x, dtype=jnp.int32)[None, :], grid_x)
    every_col = pool.arange(grid_y, dtype=jnp.int32)
    my_rows = bx * R + jnp.arange(R, dtype=jnp.int32)
    my_cols = by * C + jnp.arange(C, dtype=jnp.int32)
    if wide:
        hy = make(every_col[:, None], every_col[None, :], grid_y)
        my_rows = bx * R + by * (R // nby) + jnp.arange(R // nby, dtype=jnp.int32)
        my_cols = jnp.arange(grid_y, dtype=jnp.int32)
    else:
        hy = make(every_col[:, None], my_cols[None, :], grid_y).reshape(2, nby, C, C)
    wave_x = jnp.sin(jnp.pi * my_rows.astype(jnp.float32) / grid_x)
    wave_y = jnp.sin(jnp.pi * my_cols.astype(jnp.float32) / grid_y)
    lam = 4.0 * wave_x[:, None] ** 2 + 4.0 * wave_y[None, :] ** 2
    sizes = (L, R, C, nbx, nby, rep, lp, own)
    n_copies = STEPS * (6 + 2 * (nbx * nby + own if wide else nbx + own + nby))
    f32 = jnp.float32
    vmem = pl.BlockSpec(memory_space=pltpu.VMEM)
    hbm = pl.BlockSpec(memory_space=pltpu.HBM)
    smem = pl.BlockSpec(memory_space=pltpu.SMEM)
    S = STEPS
    scratch = [
        pltpu.VMEM((3, L, R, C), f32), pltpu.VMEM((3, L, R, C), f32),
        pltpu.VMEM((L,) + lam.shape, f32), pltpu.VMEM((L,) + lam.shape, f32),
        pltpu.VMEM((S, L, R, C), f32), pltpu.VMEM((2 * S, lp, grid_x, C), f32),
        pltpu.VMEM((2 * S, own, lp, R2, C), f32), pltpu.VMEM((S, L, R2, C), f32),
        pltpu.VMEM((S, 2, 3 * L, C), f32), pltpu.VMEM((S, 2, 3 * L, C), f32),
        pltpu.VMEM((S, R, C), f32), pltpu.VMEM((S, 2, R, C), f32),
        pltpu.VMEM((S, R, C), f32), pltpu.VMEM((S, 2, R, C), f32),
        pltpu.SemaphoreType.DMA((n_copies,)), pltpu.SemaphoreType.DMA((n_copies,)),
        pltpu.VMEM((L, R, C), f32), pltpu.VMEM(hx.shape, hx.dtype),
        pltpu.VMEM(hy.shape, hy.dtype), pltpu.SemaphoreType.DMA((3,)),
    ]
    if wide:
        thin = (S, nby, L, R // nby, C)
        scratch += [pltpu.VMEM(thin, f32), pltpu.VMEM(thin, f32)]
    else:
        scratch += [
            pltpu.VMEM((S, L, R, C), f32), pltpu.VMEM((2 * S, nby - 1, L, R, C), f32),
            pltpu.VMEM((S, L, R, C), f32), pltpu.VMEM((S, L, R, C), f32),
        ]
    out = jax.ShapeDtypeStruct(polarization.shape, f32)
    return pl.pallas_call(
        functools.partial(kernel, sizes),
        out_shape=(out, out),
        in_specs=[vmem, hbm, smem, smem, smem, smem, vmem, hbm, hbm],
        out_specs=(vmem, vmem),
        scratch_shapes=scratch,
        compiler_params=pltpu.CompilerParams(
            collective_id=0, has_side_effects=True, vmem_limit_bytes=65 * 1000 * 1000),
    )(polarization, alpha_field, landau, stiffness, permittivity, interfaces, lam, hx, hy)


def fits(L, R, C, nbx, nby):
    slab = R // nby
    return (L == nbx and slab == 8 and slab * nby == R and nby > 1 and C % L == 0
            and L & (L - 1) == 0)


def join(parts, axis):
    return jnp.concatenate(parts, axis=axis)


def fused(sizes, p_in, alpha_h, landau, stiff, perm, inter, wx_h, wy_h, hx_h, hy_h,
          p_out, f_out, *scratch):
    L, R, C, nbx, nby = sizes
    (p_mid, base, coef, ratio, a_s, a_r, b_s, b_r, c_s, c_r, d_s, d_r,
     row_s, row_r, col_s, col_r, ssem, rsem, alpha, wx, wy, hx, hy, local_sem) = scratch
    slab = R // nby
    per = C // L
    NX, NY = nbx * R, nby * C
    thick = slab + 1
    bx = lax.axis_index("bx")
    by = lax.axis_index("by")
    scale = 1.0 / (NX * NY)
    f32 = jnp.float32
    dot = functools.partial(jnp.dot, preferred_element_type=f32)
    mine = pl.multiple_of((bx * nby + by) * per, per)
    loads = [pltpu.make_async_copy(src, dst, local_sem.at[at]) for at, (src, dst) in enumerate((
        (alpha_h, alpha), (wx_h, wx), (wy_h.at[pl.ds(mine, per)], wy), (hx_h, hx), (hy_h, hy)))]
    for load in loads:
        load.start()
    slots = [0]
    sends = []

    barrier = pltpu.get_barrier_semaphore()
    others = [(a, b) for b in range(nby) for a in range(nbx) if a or b]
    for a, b in others:
        pl.semaphore_signal(
            barrier, inc=1, device_id={"bx": (bx + a) % nbx, "by": (by + b) % nby},
            device_id_type=MESH)

    def push(src, dst, device):
        slot = slots[0]
        slots[0] += 1
        copy = pltpu.make_async_remote_copy(
            src_ref=src, dst_ref=dst, send_sem=ssem.at[slot], recv_sem=rsem.at[slot],
            device_id=device, device_id_type=MESH)
        copy.start()
        sends.append(copy.wait_send)
        return copy

    rows = lax.broadcasted_iota(jnp.int32, (R, C), 0)
    lanes = lax.broadcasted_iota(jnp.int32, (R, C), 1)
    rows8 = lax.broadcasted_iota(jnp.int32, (slab, C), 0)
    lanes8 = lax.broadcasted_iota(jnp.int32, (slab, C), 1)
    zero = jnp.zeros((R, C), f32)
    zero8 = jnp.zeros((slab, C), f32)

    def x_next(f, high):
        return jnp.where(rows == R - 1, high, pltpu.roll(f, R - 1, 0))

    def x_prev(f, low):
        return jnp.where(rows == 0, low, pltpu.roll(f, 1, 0))

    def y_next(f, high):
        return jnp.where(lanes == C - 1, high, pltpu.roll(f, C - 1, 1))

    def y_prev(f, low):
        return jnp.where(lanes == 0, low, pltpu.roll(f, 1, 1))

    def charge(n, src):
        edge = zero
        for l in range(L):
            along_x, along_y = src[0, l], src[1, l]
            above = src[2, l + 1] if l + 1 < L else zero
            below = src[2, l - 1] if l else zero
            value = -0.5 * ((x_next(along_x, 0.0) - x_prev(along_x, 0.0))
                            + (y_next(along_y, 0.0) - y_prev(along_y, 0.0)) + (above - below))
            for j in range(nby):
                a_s[n, j, l] = value[j * slab:(j + 1) * slab]
            a_s[n, 0, L + 1, l:l + 1] = -0.5 * along_x[0:1]
            a_s[n, nby - 1, L + 1, l:l + 1] = 0.5 * along_x[R - 1:R]
            edge = jnp.where(lanes == l, -0.5 * along_y[:, 0:1], edge)
            edge = jnp.where(lanes == L + l, 0.5 * along_y[:, C - 1:C], edge)
        for j in range(nby):
            a_s[n, j, L] = edge[j * slab:(j + 1) * slab]
            if 0 < j < nby - 1:
                a_s[n, j, L + 1] = jnp.zeros((L, C), f32)

    def among_y(source, landing, n):
        copies = []
        for b in range(1, nby):
            to = (by + b) % nby
            copies.append(push(source.at[n, to], landing.at[n, by], {"by": to}))
        landing[n, by] = source[n, by]
        return copies

    def wait(copies):
        for copy in copies:
            copy.wait_recv()

    def spread(source, landing, n, flip):
        part = pl.ds(0, thick)
        copies = []
        for a, b in others:
            to_x, to_y = (bx + a) % nbx, (by + b) % nby
            if flip:
                src, dst = source.at[n, to_x, to_y, part], landing.at[n, by, bx, part]
            else:
                src, dst = source.at[n, to_y, to_x, part], landing.at[n, bx, by, part]
            copies.append(push(src, dst, {"bx": to_x, "by": to_y}))
        if flip:
            landing[n, by, bx, 0:thick] = source[n, bx, by, 0:thick]
        else:
            landing[n, bx, by, 0:thick] = source[n, by, bx, 0:thick]
        return copies

    def swap_groups(tiles):
        height = tiles[0].shape[0]
        group = lax.broadcasted_iota(jnp.int32, (height, C), 1) // per
        tiles = list(tiles)
        s = 1
        while s < L:
            upper = group % (2 * s) >= s
            for at in range(L):
                if at % (2 * s) < s:
                    low, high = tiles[at], tiles[at + s]
                    tiles[at] = jnp.where(upper, pltpu.roll(high, s * per, 1), low)
                    tiles[at + s] = jnp.where(upper, high, pltpu.roll(low, C - s * per, 1))
            s *= 2
        return tiles

    def swap_rows(tile):
        group = lanes8 // per
        s = 1
        while s < L:
            upper = group % (2 * s) >= s
            later = rows8 % (2 * s) >= s
            ahead = pltpu.roll(pltpu.roll(tile, L - s, 0), s * per, 1)
            behind = pltpu.roll(pltpu.roll(tile, s, 0), C - s * per, 1)
            tile = jnp.where(later, jnp.where(upper, tile, behind), jnp.where(upper, ahead, tile))
            s *= 2
        return tile

    def y_table(full):
        height = full.shape[0]
        high = full.astype(jnp.bfloat16)
        wide = high.astype(f32)
        both = join([wide, full - wide], 0).astype(jnp.bfloat16)
        first = dot(both, hy[0])
        return first[:height] + first[height:] + dot(high, hy[1])

    def y_forward(n):
        columns = []
        for j in range(nby):
            from_left = a_r[n, (j + nby - 1) % nby, L]
            from_right = a_r[n, (j + 1) % nby, L]
            tiles = []
            for l in range(L):
                extra = jnp.where(
                    lanes8 == 0, from_left[:, L + l:L + l + 1],
                    jnp.where(lanes8 == C - 1, from_right[:, l:l + 1], 0.0))
                tiles.append(a_r[n, j, l] + extra)
            columns.append(join(tiles + [a_r[n, j, L + 1], zero8], 0))
        out = y_table(join(columns, 1))
        tiles = [join([out[l * slab:(l + 1) * slab, t * C:(t + 1) * C] for t in range(nby)], 0)
                 for l in range(L)]
        tiles = swap_groups(tiles)
        for t in range(nby):
            halo = swap_rows(out[L * slab:L * slab + L, t * C:(t + 1) * C])
            for e in range(L):
                b_s[n, t, e, 0:slab] = tiles[e][t * slab:(t + 1) * slab]
                b_s[n, t, e, slab:thick] = halo[e:e + 1]

    def y_backward(n):
        tiles = swap_groups([join([c_r[n, t, e, 0:slab] for t in range(nby)], 0)
                             for e in range(L)])
        halos = [swap_rows(join([c_r[n, t, e, slab:thick] for e in range(L)], 0))
                 for t in range(nby)]
        lines = [join([tiles[l][t * slab:(t + 1) * slab] for t in range(nby)], 1)
                 for l in range(L)]
        lines += [join(halos, 1), jnp.zeros((slab, NY), f32)]
        out = y_table(join(lines, 0))
        for j in range(nby):
            edge = zero8
            left, right = (j + nby - 1) % nby, (j + 1) % nby
            for l in range(L):
                line = out[l * slab:(l + 1) * slab]
                d_s[n, j, l] = line[:, j * C:(j + 1) * C]
                edge = jnp.where(lanes8 == l, line[:, left * C + C - 1:left * C + C], edge)
                edge = jnp.where(lanes8 == L + l, line[:, right * C:right * C + 1], edge)
            d_s[n, j, L] = edge
            d_s[n, j, L + 1] = out[L * slab:L * slab + L, j * C:(j + 1) * C]

    def spectrum(n):
        tiles = []
        for i in range(nbx):
            for j in range(nby):
                tile = b_r[n, i, j, 0:slab]
                if j == 0:
                    tile = tile + jnp.where(
                        rows8 == 0, b_r[n, (i + nbx - 1) % nbx, nby - 1, slab:thick], 0.0)
                if j == nby - 1:
                    tile = tile + jnp.where(
                        rows8 == slab - 1, b_r[n, (i + 1) % nbx, 0, slab:thick], 0.0)
                tiles.append(tile)
        full = join(tiles, 0).T
        high = full.astype(jnp.bfloat16)
        wide = high.astype(f32)
        both = join([wide, full - wide], 0).astype(jnp.bfloat16)
        first = dot(both, hx[0])
        out = (first[:C] + first[C:] + dot(high, hx[1])) * scale
        return [out[l * per:(l + 1) * per] for l in range(L)]

    def solve(sources):
        primes = []
        for l in range(L):
            source = sources[l]
            if l:
                source = source + inter[l] * primes[-1]
            primes.append(source * coef[l])
        values = [primes[-1]]
        for l in range(L - 2, -1, -1):
            values.insert(0, primes[l] + ratio[l] * values[0])
        return values

    def x_backward(n, values):
        high, low = halves(join(values, 0))
        turn = functools.partial(
            lax.dot_general, dimension_numbers=(((1,), (1,)), ((), ())),
            preferred_element_type=f32)
        first = turn(hx[...].reshape(2 * NX, NX), high)
        out = first[:NX] + first[NX:] + turn(hx[0], low)
        for i in range(nbx):
            for j in range(nby):
                at = i * R + j * slab
                c_s[n, i, j, 0:slab] = out[at:at + slab]
                if j == 0:
                    line = (at + NX - 1) % NX
                else:
                    line = (at + slab) % NX
                c_s[n, i, j, slab:thick] = out[line:line + 1]

    def flank_start(n, src):
        tile = zero
        for c in range(3):
            for l in range(L):
                at = c * L + l
                cell = src[c, l]
                row_s[n, 0, at:at + 1] = cell[0:1]
                row_s[n, 1, at:at + 1] = cell[R - 1:R]
                tile = jnp.where(lanes == at, cell[:, 0:1], tile)
                tile = jnp.where(lanes == C // 2 + at, cell[:, C - 1:C], tile)
        col_s[n] = tile

    def flank_send(n):
        return [
            push(row_s.at[n, 1], row_r.at[n, 0], {"bx": (bx + 1) % nbx}),
            push(row_s.at[n, 0], row_r.at[n, 1], {"bx": (bx + nbx - 1) % nbx}),
            push(col_s.at[n], col_r.at[n, 0], {"by": (by + 1) % nby}),
            push(col_s.at[n], col_r.at[n, 1], {"by": (by + nby - 1) % nby})]

    def relax_inside(src):
        for l in range(L):
            cells = [src[c, l] for c in range(3)]
            squares = [cell * cell for cell in cells]
            whole = squares[0] + squares[1] + squares[2]
            for c in range(3):
                cell, square = cells[c], squares[c]
                above = src[c, l + 1] if l + 1 < L else zero
                below = src[c, l - 1] if l else zero
                smooth = stiff[l] * (
                    (x_next(cell, 0.0) + x_prev(cell, 0.0) + y_next(cell, 0.0)
                     + y_prev(cell, 0.0) - 4.0 * cell) + (above + below - 2.0 * cell))
                drive = cell * (
                    2.0 * alpha[l] + 4.0 * landau[0, l] * square
                    + 2.0 * landau[1, l] * (whole - square)
                    + 6.0 * landau[2, l] * (square * square))
                base[c, l] = cell - step_size * (drive - smooth)

    def relax_edges(n):
        low_col = col_r[n, 0]
        high_col = col_r[n, 1]
        for l in range(L):
            weight = step_size * stiff[l]
            for c in range(3):
                at = c * L + l
                add = jnp.where(lanes == 0, low_col[:, C // 2 + at:C // 2 + at + 1], 0.0)
                add = add + jnp.where(lanes == C - 1, high_col[:, at:at + 1], 0.0)
                add = add + jnp.where(rows == 0, row_r[n, 0, at:at + 1], 0.0)
                add = add + jnp.where(rows == R - 1, row_r[n, 1, at:at + 1], 0.0)
                base[c, l] += weight * add

    def field(n):
        edge = join([d_r[n, j, L] for j in range(nby)], 0)
        phis = [join([d_r[n, j, l] for j in range(nby)], 0) for l in range(L)]
        for l in range(L):
            phi = phis[l]
            low = d_r[n, 0, L + 1, l:l + 1]
            high = d_r[n, nby - 1, L + 1, l:l + 1]
            along_x = -0.5 * (x_next(phi, high) - x_prev(phi, low))
            along_y = -0.5 * (y_next(phi, edge[:, L + l:L + l + 1])
                              - y_prev(phi, edge[:, l:l + 1]))
            above = phis[l + 1] if l + 1 < L else zero
            below = phis[l - 1] if l else zero
            yield l, (along_x, along_y, -0.5 * (above - below))

    charge(0, p_in)
    flank_start(0, p_in)
    pl.semaphore_wait(barrier, len(others))
    first_a = among_y(a_s, a_r, 0)
    flanks = flank_send(0)
    loads[0].wait()
    relax_inside(p_in)
    loads[1].wait()
    loads[2].wait()
    wave_x = wx[0:1]
    wave_y = join([wy[...]] * (NX // C), 1)
    lateral = wave_x + wave_y
    previous = None
    for l in range(L):
        pivot = perm[l] * lateral + inter[l] + inter[l + 1]
        if l:
            pivot = pivot - inter[l] * previous
        inverse = 1.0 / pivot
        coef[l] = inverse
        previous = inter[l + 1] * inverse
        ratio[l] = previous
    loads[3].wait()
    loads[4].wait()
    wait(first_a)
    y_forward(0)
    first_b = spread(b_s, b_r, 0, False)
    wait(flanks)
    relax_edges(0)
    charge(1, base)
    second_a = among_y(a_s, a_r, 1)
    wait(second_a)
    y_forward(1)
    second_b = spread(b_s, b_r, 1, False)
    wait(first_b)
    values = solve(spectrum(0))
    x_backward(0, values)
    first_c = spread(c_s, c_r, 0, True)
    bend = -(wave_x * (1.0 - 0.25 * wave_x) + wave_y * (1.0 - 0.25 * wave_y))
    slopes = []
    none = jnp.zeros_like(values[0])
    for l in range(L):
        above = values[l + 1] if l + 1 < L else none
        below = values[l - 1] if l else none
        slopes.append(0.5 * (above - below))
    moved = []
    for l in range(L):
        above = slopes[l + 1] if l + 1 < L else none
        below = slopes[l - 1] if l else none
        moved.append(step_size * (bend * values[l] + 0.5 * (above - below)))
    wait(second_b)
    x_backward(1, solve([here + more for here, more in zip(spectrum(1), moved)]))
    second_c = spread(c_s, c_r, 1, True)
    wait(first_c)
    y_backward(0)
    first_d = among_y(d_s, d_r, 0)
    wait(first_d)
    for l, parts in field(0):
        for c in range(3):
            p_mid[c, l] = base[c, l] + step_size * parts[c]
    flank_start(1, p_mid)
    flanks = flank_send(1)
    wait(second_c)
    y_backward(1)
    second_d = among_y(d_s, d_r, 1)
    relax_inside(p_mid)
    wait(flanks)
    relax_edges(1)
    wait(second_d)
    for l, parts in field(1):
        for c in range(3):
            f_out[c, l] = parts[c]
            p_out[c, l] = base[c, l] + step_size * parts[c]
    for send in sends:
        send()


def fused_shards(polarization, alpha_field, landau, stiffness, permittivity, interfaces):
    _, L, R, C = polarization.shape
    nbx = lax.axis_size("bx")
    nby = lax.axis_size("by")
    grid_x, grid_y = nbx * R, nby * C
    per = C // L
    line = np.arange(grid_x)
    hx = fixed_table(line[:, None], line[None, :], grid_x)
    line = np.arange(grid_y)
    hy = fixed_table(line[:, None], line[None, :], grid_y)
    wave_x = 4.0 * np.sin(np.pi * np.arange(grid_x) / grid_x) ** 2
    wave_x = jnp.asarray(np.tile(wave_x[None, :], (8, 1)).astype(np.float32))
    at = np.arange(nbx * nby)
    first = (at % nby) * C + (at // nby) * per
    mode = (first[:, None] + np.arange(per)[None, :]).reshape(-1)
    wave_y = 4.0 * np.sin(np.pi * mode / grid_y) ** 2
    wave_y = jnp.asarray(np.tile(wave_y[:, None], (1, C)).astype(np.float32))
    f32 = jnp.float32
    vmem = pl.BlockSpec(memory_space=pltpu.VMEM)
    hbm = pl.BlockSpec(memory_space=pltpu.HBM)
    smem = pl.BlockSpec(memory_space=pltpu.SMEM)
    S = 2
    n_copies = S * (4 + 2 * (nby - 1) + 2 * (nbx * nby - 1))
    by_y = pltpu.VMEM((S, nby, L + 2, 8, C), f32)
    by_mode = pltpu.VMEM((S, nby, nbx, 16, C), f32)
    by_place = pltpu.VMEM((S, nbx, nby, 16, C), f32)
    scratch = [
        pltpu.VMEM((3, L, R, C), f32), pltpu.VMEM((3, L, R, C), f32),
        pltpu.VMEM((L, per, grid_x), f32), pltpu.VMEM((L, per, grid_x), f32),
        by_y, by_y, by_mode, by_place, by_place, by_mode, by_y, by_y,
        pltpu.VMEM((S, 2, 3 * L, C), f32), pltpu.VMEM((S, 2, 3 * L, C), f32),
        pltpu.VMEM((S, R, C), f32), pltpu.VMEM((S, 2, R, C), f32),
        pltpu.SemaphoreType.DMA((n_copies,)), pltpu.SemaphoreType.DMA((n_copies,)),
        pltpu.VMEM((L, R, C), f32), pltpu.VMEM(wave_x.shape, f32), pltpu.VMEM((per, C), f32),
        pltpu.VMEM(hx.shape, hx.dtype), pltpu.VMEM(hy.shape, hy.dtype),
        pltpu.SemaphoreType.DMA((5,)),
    ]
    out = jax.ShapeDtypeStruct(polarization.shape, f32)
    return pl.pallas_call(
        functools.partial(fused, (L, R, C, nbx, nby)),
        out_shape=(out, out),
        in_specs=[vmem, hbm, smem, smem, smem, smem, hbm, hbm, hbm, hbm],
        out_specs=(vmem, vmem),
        scratch_shapes=scratch,
        compiler_params=pltpu.CompilerParams(
            collective_id=0, has_side_effects=True, vmem_limit_bytes=60 * 1000 * 1000),
    )(polarization, alpha_field, landau, stiffness, permittivity, interfaces,
      wave_x, wave_y, hx, hy)


def solution(mesh):
    def run(polarization, *rest):
        _, L, R, C = polarization.shape
        body = fused_shards if fits(L, R, C, lax.axis_size("bx"), lax.axis_size("by")) else shards
        return body(polarization, *rest)

    return jax.shard_map(
        run,
        mesh=mesh,
        in_specs=(P(None, None, "bx", "by"), P(None, "bx", "by"), P(), P(), P(), P()),
        out_specs=(P(None, None, "bx", "by"), P(None, None, "bx", "by")),
        check_vma=False,
    )
```

```python
import functools

import jax
import jax.numpy as jnp
import numpy as np
from jax import lax
from jax.experimental import pallas as pl
from jax.experimental.pallas import tpu as pltpu
from jax.sharding import PartitionSpec as P

STEPS = 2
step_size = 0.05
MESH = pl.DeviceIdType.MESH
PAD = 8


def cas_table(left, right, length):
    turns = left * right % length
    angle = 2.0 * jnp.pi / length * turns.astype(jnp.float32)
    table = jnp.cos(angle) + jnp.sin(angle)
    high = lax.reduce_precision(table, 8, 7)
    return jnp.stack([high.astype(jnp.bfloat16), (table - high).astype(jnp.bfloat16)])


def fixed_table(left, right, length):
    angle = 2.0 * np.pi / length * (left * right % length)
    table = (np.cos(angle) + np.sin(angle)).astype(np.float32)
    high = table.astype(jnp.bfloat16)
    low = (table - high.astype(np.float32)).astype(jnp.bfloat16)
    return jnp.asarray(np.stack([high, low]))


def is_wide(rows, nbx, nby, layers):
    return layers % nbx == 0 and rows % (8 * nby) == 0


def halves(value):
    high = value.astype(jnp.bfloat16)
    low = (value - high.astype(jnp.float32)).astype(jnp.bfloat16)
    return high, low


def product(left, right):
    dot = functools.partial(jnp.dot, preferred_element_type=jnp.float32)
    return dot(left[0], right[0]) + (dot(left[0], right[1]) + dot(left[1], right[0]))


def kernel(sizes, p_in, alpha_h, landau, stiff, perm, inter, lam, hx_h, hy_h, p_out, f_out, *scratch):
    L, R, C, nbx, nby, rep, lp, own = sizes
    (p_mid, base, coef, ratio, q, inb, outs, rec_i,
     row_s, row_r, col_s, col_r, pc_s, pc_r, ssem, rsem,
     alpha, hx, hy, local_sem) = scratch[:20]
    wide = is_wide(R, nbx, nby, L)
    if wide:
        z_in, w_out = scratch[20:]
    else:
        rec_f, ybuf, phat, u = scratch[20:]
    thin = R // nby
    R2 = R + PAD
    bx = lax.axis_index("bx")
    by = lax.axis_index("by")
    group = bx // rep
    part = bx % rep
    scale = 1.0 / (R * nbx * C * nby)
    loads = [pltpu.make_async_copy(src, dst, local_sem.at[at]) for at, (src, dst) in
             enumerate(((alpha_h, alpha), (hx_h, hx), (hy_h, hy)))]
    for load in loads:
        load.start()
    slots = [0]
    sends = []

    barrier = pltpu.get_barrier_semaphore()
    others = [(a, b) for b in range(nby) for a in range(nbx) if a or b]
    greeted = [(a, b) for a, b in others if wide or not a or not b]
    for a, b in greeted:
        pl.semaphore_signal(
            barrier, inc=1, device_id={"bx": (bx + a) % nbx, "by": (by + b) % nby},
            device_id_type=MESH)

    def remote(src, dst, device, slot):
        return pltpu.make_async_remote_copy(
            src_ref=src, dst_ref=dst, send_sem=ssem.at[slot], recv_sem=rsem.at[slot],
            device_id=device, device_id_type=MESH)

    def fresh():
        slots[0] += 1
        return slots[0] - 1

    def push(src, dst, device):
        copy = remote(src, dst, device, fresh())
        copy.start()
        sends.append(copy.wait_send)
        return copy

    rows = lax.broadcasted_iota(jnp.int32, (R, C), 0)
    lanes = lax.broadcasted_iota(jnp.int32, (R, C), 1)

    def x_next(f, high):
        return jnp.where(rows == R - 1, high, pltpu.roll(f, R - 1, 0))

    def x_prev(f, low):
        return jnp.where(rows == 0, low, pltpu.roll(f, 1, 0))

    def y_next(f, high):
        return jnp.where(lanes == C - 1, high, pltpu.roll(f, C - 1, 1))

    def y_prev(f, low):
        return jnp.where(lanes == 0, low, pltpu.roll(f, 1, 1))

    def column_tile(blocks):
        tile = jnp.zeros((R, C), jnp.float32)
        for at, block in enumerate(blocks):
            tile = jnp.where(lanes == at, block[:, 0:1], tile)
            tile = jnp.where(lanes == C // 2 + at, block[:, C - 1:C], tile)
        return tile

    def x_start(src, n):
        mine = inb.at[n, :, pl.ds(pl.multiple_of(bx * R, R), R)]
        copies = []
        for k in range(1, nbx):
            to = (bx + k) % nbx
            copies.append(push(src.at[pl.ds(to // rep * lp, lp)], mine, {"bx": to}))
        for layer in range(lp):
            inb[n, layer, pl.ds(pl.multiple_of(bx * R, R), R)] = src[group * lp + layer]
        return copies

    def x_mix(copies, n):
        for copy in copies:
            copy.wait_recv()
        table = (hx[0], hx[1])
        for layer in range(lp):
            outs[n, :, layer] = product(table, halves(inb[n, layer])).reshape(own, R2, C)

    def spread(n, step):
        copies = []
        for a, b in others:
            to_x, to_y = (bx + a) % nbx, (by + b) % nby
            copies.append(push(
                outs.at[n, to_x, :, pl.ds(pl.multiple_of(to_y * thin, thin), thin)],
                z_in.at[step, by, pl.ds(bx * lp, lp)], {"bx": to_x, "by": to_y}))
        for layer in range(lp):
            z_in[step, by, bx * lp + layer] = outs[
                n, bx, layer, pl.ds(pl.multiple_of(by * thin, thin), thin)]
        for copy in copies:
            copy.wait_recv()

    def collect(n, step):
        at = pl.ds(pl.multiple_of(bx * R + by * thin, thin), thin)
        copies = []
        for a, b in others:
            to_x, to_y = (bx + a) % nbx, (by + b) % nby
            copies.append(push(
                w_out.at[step, to_y, pl.ds(to_x * lp, lp)], inb.at[n, :, at],
                {"bx": to_x, "by": to_y}))
        for layer in range(lp):
            inb[n, layer, at] = w_out[step, by, bx * lp + layer]
        return copies

    def solve(spectrum, height):
        primes = []
        for l in range(L):
            source = spectrum[l * height:(l + 1) * height] * scale
            if l:
                source = source + inter[l] * primes[-1]
            primes.append(source * coef[l])
        values = [primes[-1]]
        for l in range(L - 2, -1, -1):
            values.insert(0, primes[l] + ratio[l] * values[0])
        return values

    def x_finish(n, dst, height):
        waits = []
        landing = dst.at[pl.ds(group * lp, lp)]
        for t in range(own):
            local = (group + t) % own
            to = part * own + local
            src = outs.at[n, local, :, pl.ds(0, height)]
            if rep == 1:
                if t == 0:
                    continue
                waits.append(push(src, landing, {"bx": to}).wait_recv)
                continue
            slot = fresh()

            def go(src=src, to=to, slot=slot):
                remote(src, landing, {"bx": to}, slot).start()

            def gone(src=src, to=to, slot=slot):
                @pl.when(to != bx)
                def _():
                    remote(src, landing, {"bx": to}, slot).wait_send()

            def came(src=src, to=to, slot=slot, t=t):
                origin = (bx % own + own - t) % own * rep + bx // own

                @pl.when(origin != bx)
                def _():
                    remote(src, landing, {"bx": to}, slot).wait_recv()

            pl.when(to != bx)(go)
            sends.append(gone)
            waits.append(came)

        def keep():
            for layer in range(lp):
                dst[group * lp + layer] = outs[n, bx % own, layer, 0:height]

        if rep == 1:
            keep()
        else:
            pl.when(bx // own == part)(keep)
        for wait in waits:
            wait()

    def y_pass(src, n):
        copies = [push(src, ybuf.at[n, k - 1], {"by": (by + k) % nby}) for k in range(1, nby)]
        total = product(halves(src[...].reshape(L * R, C)), (hy[0, by], hy[1, by]))
        for k in range(1, nby):
            copies[k - 1].wait_recv()
            origin = (by + nby - k) % nby
            total += product(halves(ybuf[n, k - 1].reshape(L * R, C)), (hy[0, origin], hy[1, origin]))
        return total

    def flank_start(rows_too, step, src):
        copies = []
        if rows_too:
            for c in range(3):
                for l in range(L):
                    at = c * L + l
                    row_s[step, 0, at:at + 1] = src[c, l, 0:1]
                    row_s[step, 1, at:at + 1] = src[c, l, R - 1:R]
            col_s[step] = column_tile([src[c, l] for c in range(3) for l in range(L)])
            if step == 0:
                pl.semaphore_wait(barrier, len(greeted))
            copies.append(push(row_s.at[step, 1], row_r.at[step, 0], {"bx": (bx + 1) % nbx}))
            copies.append(push(row_s.at[step, 0], row_r.at[step, 1], {"bx": (bx + nbx - 1) % nbx}))
            tile, land = col_s.at[step], col_r
        else:
            pc_s[step] = column_tile([src[l, 0:R] for l in range(L)])
            tile, land = pc_s.at[step], pc_r
        copies.append(push(tile, land.at[step, 0], {"by": (by + 1) % nby}))
        copies.append(push(tile, land.at[step, 1], {"by": (by + nby - 1) % nby}))
        return copies

    for step in range(STEPS):
        src = p_in if step == 0 else p_mid
        flanks = flank_start(True, step, src)
        if step == 0:
            lateral = lam[...]
            previous = None
            for l in range(L):
                pivot = perm[l] * lateral + inter[l] + inter[l + 1]
                if l:
                    pivot = pivot - inter[l] * previous
                inverse = 1.0 / pivot
                coef[l] = inverse
                previous = inter[l + 1] * inverse
                ratio[l] = previous
        for copy in flanks:
            copy.wait_recv()
        low_col = col_r[step, 0]
        high_col = col_r[step, 1]

        def edges(c, l):
            at = c * L + l
            return (row_r[step, 0, at:at + 1], row_r[step, 1, at:at + 1],
                    low_col[:, C // 2 + at:C // 2 + at + 1], high_col[:, at:at + 1])

        zero = jnp.zeros((R, C), jnp.float32)
        for l in range(L):
            low, high, _, _ = edges(0, l)
            _, _, left, right = edges(1, l)
            along_x, along_y = src[0, l], src[1, l]
            above = src[2, l + 1] if l + 1 < L else zero
            below = src[2, l - 1] if l else zero
            q[step, l] = -0.5 * (
                (x_next(along_x, high) - x_prev(along_x, low))
                + (y_next(along_y, right) - y_prev(along_y, left)) + (above - below))
        copies = x_start(q.at[step], 2 * step)
        if step == 0:
            for load in loads:
                load.wait()
        for l in range(L):
            cells = [src[c, l] for c in range(3)]
            squares = [cell * cell for cell in cells]
            whole = squares[0] + squares[1] + squares[2]
            for c in range(3):
                cell, square = cells[c], squares[c]
                low, high, left, right = edges(c, l)
                above = src[c, l + 1] if l + 1 < L else zero
                below = src[c, l - 1] if l else zero
                smooth = stiff[l] * (
                    (x_next(cell, high) + x_prev(cell, low) + y_next(cell, right)
                     + y_prev(cell, left) - 4.0 * cell) + (above + below - 2.0 * cell))
                drive = cell * (
                    2.0 * alpha[l] + 4.0 * landau[0, l] * square
                    + 2.0 * landau[1, l] * (whole - square)
                    + 6.0 * landau[2, l] * (square * square))
                base[c, l] = cell - step_size * (drive - smooth)
        n = 2 * step
        x_mix(copies, n)
        if wide:
            spread(n, step)
            table = (hy[0], hy[1])
            full = jnp.concatenate(
                [z_in[step, j].reshape(L * thin, C) for j in range(nby)], axis=1)
            values = solve(product(halves(full), table), thin)
            full = product(halves(jnp.concatenate(values, axis=0)), table)
            for j in range(nby):
                w_out[step, j] = full[:, j * C:(j + 1) * C].reshape(L, thin, C)
            copies = collect(n + 1, step)
        else:
            x_finish(n, rec_f.at[step], R)
            for l, value in enumerate(solve(y_pass(rec_f.at[step], n), R)):
                phat[step, l] = value
            u[step] = y_pass(phat.at[step], n + 1).reshape(L, R, C)
            copies = x_start(u.at[step], n + 1)
        x_mix(copies, n + 1)
        x_finish(n + 1, rec_i.at[step], R2)
        flanks = flank_start(False, step, rec_i.at[step])
        last = step == STEPS - 1
        target = p_out if last else p_mid
        for l in range(L):
            phi = rec_i[step, l, 0:R]
            low = rec_i[step, l, R:R + 1]
            high = rec_i[step, l, R + 1:R + 2]
            along_x = -0.5 * (x_next(phi, high) - x_prev(phi, low))
            above = rec_i[step, l + 1, 0:R] if l + 1 < L else zero
            below = rec_i[step, l - 1, 0:R] if l else zero
            along_z = -0.5 * (above - below)
            target[0, l] = base[0, l] + step_size * along_x
            target[2, l] = base[2, l] + step_size * along_z
            if last:
                f_out[0, l] = along_x
                f_out[2, l] = along_z
        for copy in flanks:
            copy.wait_recv()
        low_phi = pc_r[step, 0]
        high_phi = pc_r[step, 1]
        for l in range(L):
            phi = rec_i[step, l, 0:R]
            along_y = -0.5 * (y_next(phi, high_phi[:, l:l + 1])
                              - y_prev(phi, low_phi[:, C // 2 + l:C // 2 + l + 1]))
            target[1, l] = base[1, l] + step_size * along_y
            if last:
                f_out[1, l] = along_y
    for wait in sends:
        wait()


def shards(polarization, alpha_field, landau, stiffness, permittivity, interfaces):
    _, L, R, C = polarization.shape
    nbx = lax.axis_size("bx")
    nby = lax.axis_size("by")
    bx = lax.axis_index("bx")
    by = lax.axis_index("by")
    rep = max(1, nbx // L)
    lp = max(1, L // nbx)
    own = nbx // rep
    grid_x, grid_y = nbx * R, nby * C
    R2 = R + PAD
    wide = is_wide(R, nbx, nby, L)
    pool = np if wide else jnp
    make = fixed_table if wide else cas_table
    line = pool.arange(R2, dtype=jnp.int32)
    line = pool.where(line < R, line, pool.where(line == R, -1, R))
    owners = pool.arange(own, dtype=jnp.int32)
    if not wide:
        owners = owners + bx % rep * own
    wanted = ((owners[:, None] * R + line[None, :] + grid_x) % grid_x).reshape(own * R2, 1)
    hx = make(wanted, pool.arange(grid_x, dtype=jnp.int32)[None, :], grid_x)
    every_col = pool.arange(grid_y, dtype=jnp.int32)
    my_rows = bx * R + jnp.arange(R, dtype=jnp.int32)
    my_cols = by * C + jnp.arange(C, dtype=jnp.int32)
    if wide:
        hy = make(every_col[:, None], every_col[None, :], grid_y)
        my_rows = bx * R + by * (R // nby) + jnp.arange(R // nby, dtype=jnp.int32)
        my_cols = jnp.arange(grid_y, dtype=jnp.int32)
    else:
        hy = make(every_col[:, None], my_cols[None, :], grid_y).reshape(2, nby, C, C)
    wave_x = jnp.sin(jnp.pi * my_rows.astype(jnp.float32) / grid_x)
    wave_y = jnp.sin(jnp.pi * my_cols.astype(jnp.float32) / grid_y)
    lam = 4.0 * wave_x[:, None] ** 2 + 4.0 * wave_y[None, :] ** 2
    sizes = (L, R, C, nbx, nby, rep, lp, own)
    n_copies = STEPS * (6 + 2 * (nbx * nby + own if wide else nbx + own + nby))
    f32 = jnp.float32
    vmem = pl.BlockSpec(memory_space=pltpu.VMEM)
    hbm = pl.BlockSpec(memory_space=pltpu.HBM)
    smem = pl.BlockSpec(memory_space=pltpu.SMEM)
    S = STEPS
    scratch = [
        pltpu.VMEM((3, L, R, C), f32), pltpu.VMEM((3, L, R, C), f32),
        pltpu.VMEM((L,) + lam.shape, f32), pltpu.VMEM((L,) + lam.shape, f32),
        pltpu.VMEM((S, L, R, C), f32), pltpu.VMEM((2 * S, lp, grid_x, C), f32),
        pltpu.VMEM((2 * S, own, lp, R2, C), f32), pltpu.VMEM((S, L, R2, C), f32),
        pltpu.VMEM((S, 2, 3 * L, C), f32), pltpu.VMEM((S, 2, 3 * L, C), f32),
        pltpu.VMEM((S, R, C), f32), pltpu.VMEM((S, 2, R, C), f32),
        pltpu.VMEM((S, R, C), f32), pltpu.VMEM((S, 2, R, C), f32),
        pltpu.SemaphoreType.DMA((n_copies,)), pltpu.SemaphoreType.DMA((n_copies,)),
        pltpu.VMEM((L, R, C), f32), pltpu.VMEM(hx.shape, hx.dtype),
        pltpu.VMEM(hy.shape, hy.dtype), pltpu.SemaphoreType.DMA((3,)),
    ]
    if wide:
        thin = (S, nby, L, R // nby, C)
        scratch += [pltpu.VMEM(thin, f32), pltpu.VMEM(thin, f32)]
    else:
        scratch += [
            pltpu.VMEM((S, L, R, C), f32), pltpu.VMEM((2 * S, nby - 1, L, R, C), f32),
            pltpu.VMEM((S, L, R, C), f32), pltpu.VMEM((S, L, R, C), f32),
        ]
    out = jax.ShapeDtypeStruct(polarization.shape, f32)
    return pl.pallas_call(
        functools.partial(kernel, sizes),
        out_shape=(out, out),
        in_specs=[vmem, hbm, smem, smem, smem, smem, vmem, hbm, hbm],
        out_specs=(vmem, vmem),
        scratch_shapes=scratch,
        compiler_params=pltpu.CompilerParams(
            collective_id=0, has_side_effects=True, vmem_limit_bytes=65 * 1000 * 1000),
    )(polarization, alpha_field, landau, stiffness, permittivity, interfaces, lam, hx, hy)


def fits(L, R, C, nbx, nby):
    slab = R // nby
    return (L == nbx and slab == 8 and slab * nby == R and nby > 1 and C % L == 0
            and nbx & (nbx - 1) == 0 and nby & (nby - 1) == 0)


def partner(index, mask, size):
    other = 0
    bit = 1
    while bit < size:
        here = index // bit % 2
        other = other + bit * (1 - here if mask // bit % 2 else here)
        bit *= 2
    return other


def join(parts, axis):
    return jnp.concatenate(parts, axis=axis)


def fused(sizes, p_h, alpha_h, landau, stiff, perm, inter, wx_h, wy_h, hx_h, hy_h,
          base_o, down_o, *scratch):
    L, R, C, nbx, nby = sizes
    (p_mid, base, coef, ratio, a_s, a_r, b_s, b_r, c_s, c_r, d_s, d_r,
     row_s, row_r, col_s, col_r, ssem, rsem, p_in, alpha, wx, wy, hx, hy, local_sem) = scratch
    slab = R // nby
    per = C // L
    NX, NY = nbx * R, nby * C
    thick = slab + 1
    bx = lax.axis_index("bx")
    by = lax.axis_index("by")
    scale = 1.0 / (NX * NY)
    f32 = jnp.float32
    dot = functools.partial(jnp.dot, preferred_element_type=f32)
    slots = [0]
    sends = []

    barrier = pltpu.get_barrier_semaphore()
    at_x = [partner(bx, a, nbx) for a in range(nbx)]
    at_y = [partner(by, b, nby) for b in range(nby)]
    others = [(a, b) for b in range(nby) for a in range(nbx) if a or b]
    others.sort(key=lambda ab: -(ab[0] // 2 + ab[0] % 2 + ab[1] // 2))
    for a, b in others:
        pl.semaphore_signal(
            barrier, inc=1, device_id={"bx": at_x[a], "by": at_y[b]}, device_id_type=MESH)
    mine = pl.multiple_of((bx * nby + by) * per, per)
    loads = [pltpu.make_async_copy(src, dst, local_sem.at[at]) for at, (src, dst) in enumerate((
        (p_h, p_in), (alpha_h, alpha), (wx_h, wx), (wy_h.at[pl.ds(mine, per)], wy), (hx_h, hx),
        (hy_h, hy)))]
    for load in loads:
        load.start()

    def push(src, dst, device):
        slot = slots[0]
        slots[0] += 1
        copy = pltpu.make_async_remote_copy(
            src_ref=src, dst_ref=dst, send_sem=ssem.at[slot], recv_sem=rsem.at[slot],
            device_id=device, device_id_type=MESH)
        copy.start()
        sends.append(copy.wait_send)
        return copy

    rows = lax.broadcasted_iota(jnp.int32, (R, C), 0)
    lanes = lax.broadcasted_iota(jnp.int32, (R, C), 1)
    rows8 = lax.broadcasted_iota(jnp.int32, (slab, C), 0)
    lanes8 = lax.broadcasted_iota(jnp.int32, (slab, C), 1)
    zero = jnp.zeros((R, C), f32)
    zero8 = jnp.zeros((slab, C), f32)

    def x_next(f, high):
        return jnp.where(rows == R - 1, high, pltpu.roll(f, R - 1, 0))

    def x_prev(f, low):
        return jnp.where(rows == 0, low, pltpu.roll(f, 1, 0))

    def y_next(f, high):
        return jnp.where(lanes == C - 1, high, pltpu.roll(f, C - 1, 1))

    def y_prev(f, low):
        return jnp.where(lanes == 0, low, pltpu.roll(f, 1, 1))

    def charge(n, src):
        edge = zero
        for l in range(L):
            along_x, along_y = src[0, l], src[1, l]
            above = src[2, l + 1] if l + 1 < L else zero
            below = src[2, l - 1] if l else zero
            value = -0.5 * ((x_next(along_x, 0.0) - x_prev(along_x, 0.0))
                            + (y_next(along_y, 0.0) - y_prev(along_y, 0.0)) + (above - below))
            for j in range(nby):
                a_s[n, j, l] = value[j * slab:(j + 1) * slab]
            a_s[n, 0, L + 1, l:l + 1] = -0.5 * along_x[0:1]
            a_s[n, nby - 1, L + 1, l:l + 1] = 0.5 * along_x[R - 1:R]
            edge = jnp.where(lanes == l, -0.5 * along_y[:, 0:1], edge)
            edge = jnp.where(lanes == L + l, 0.5 * along_y[:, C - 1:C], edge)
        for j in range(nby):
            a_s[n, j, L] = edge[j * slab:(j + 1) * slab]
            if 0 < j < nby - 1:
                a_s[n, j, L + 1] = jnp.zeros((L, C), f32)

    def among_y(source, landing, n):
        copies = []
        for b in range(nby - 1, 0, -1):
            to = at_y[b]
            copies.append(push(source.at[n, to], landing.at[n, by], {"by": to}))
        landing[n, by] = source[n, by]
        return copies

    def wait(copies):
        for copy in copies:
            copy.wait_recv()

    def spread(source, landing, n, flip):
        part = pl.ds(0, thick)
        copies = []
        for a, b in others:
            to_x, to_y = at_x[a], at_y[b]
            if flip:
                src, dst = source.at[n, to_x, to_y, part], landing.at[n, by, bx, part]
            else:
                src, dst = source.at[n, to_y, to_x, part], landing.at[n, bx, by, part]
            copies.append(push(src, dst, {"bx": to_x, "by": to_y}))
        if flip:
            landing[n, by, bx, 0:thick] = source[n, bx, by, 0:thick]
        else:
            landing[n, bx, by, 0:thick] = source[n, by, bx, 0:thick]
        return copies

    def swap_groups(tiles):
        height = tiles[0].shape[0]
        group = lax.broadcasted_iota(jnp.int32, (height, C), 1) // per
        tiles = list(tiles)
        s = 1
        while s < L:
            upper = group % (2 * s) >= s
            for at in range(L):
                if at % (2 * s) < s:
                    low, high = tiles[at], tiles[at + s]
                    tiles[at] = jnp.where(upper, pltpu.roll(high, s * per, 1), low)
                    tiles[at + s] = jnp.where(upper, high, pltpu.roll(low, C - s * per, 1))
            s *= 2
        return tiles

    def swap_rows(tile):
        group = lanes8 // per
        s = 1
        while s < L:
            upper = group % (2 * s) >= s
            later = rows8 % (2 * s) >= s
            ahead = pltpu.roll(pltpu.roll(tile, L - s, 0), s * per, 1)
            behind = pltpu.roll(pltpu.roll(tile, s, 0), C - s * per, 1)
            tile = jnp.where(later, jnp.where(upper, tile, behind), jnp.where(upper, ahead, tile))
            s *= 2
        return tile

    def y_table(full):
        height = full.shape[0]
        high = full.astype(jnp.bfloat16)
        wide = high.astype(f32)
        both = join([wide, full - wide], 0).astype(jnp.bfloat16)
        first = dot(both, hy[0])
        return first[:height] + first[height:] + dot(high, hy[1])

    def y_forward(n):
        columns = []
        for j in range(nby):
            from_left = a_r[n, (j + nby - 1) % nby, L]
            from_right = a_r[n, (j + 1) % nby, L]
            tiles = []
            for l in range(L):
                extra = jnp.where(
                    lanes8 == 0, from_left[:, L + l:L + l + 1],
                    jnp.where(lanes8 == C - 1, from_right[:, l:l + 1], 0.0))
                tiles.append(a_r[n, j, l] + extra)
            columns.append(join(tiles + [a_r[n, j, L + 1], zero8], 0))
        out = y_table(join(columns, 1))
        tiles = [join([out[l * slab:(l + 1) * slab, t * C:(t + 1) * C] for t in range(nby)], 0)
                 for l in range(L)]
        tiles = swap_groups(tiles)
        for t in range(nby):
            halo = swap_rows(out[L * slab:L * slab + L, t * C:(t + 1) * C])
            for e in range(L):
                b_s[n, t, e, 0:slab] = tiles[e][t * slab:(t + 1) * slab]
                b_s[n, t, e, slab:thick] = halo[e:e + 1]

    def y_backward(n):
        tiles = swap_groups([join([c_r[n, t, e, 0:slab] for t in range(nby)], 0)
                             for e in range(L)])
        halos = [swap_rows(join([c_r[n, t, e, slab:thick] for e in range(L)], 0))
                 for t in range(nby)]
        lines = [join([tiles[l][t * slab:(t + 1) * slab] for t in range(nby)], 1)
                 for l in range(L)]
        lines += [join(halos, 1), jnp.zeros((slab, NY), f32)]
        out = y_table(join(lines, 0))
        for j in range(nby):
            edge = zero8
            left, right = (j + nby - 1) % nby, (j + 1) % nby
            for l in range(L):
                line = out[l * slab:(l + 1) * slab]
                d_s[n, j, l] = line[:, j * C:(j + 1) * C]
                edge = jnp.where(lanes8 == l, line[:, left * C + C - 1:left * C + C], edge)
                edge = jnp.where(lanes8 == L + l, line[:, right * C:right * C + 1], edge)
            d_s[n, j, L] = edge
            d_s[n, j, L + 1] = out[L * slab:L * slab + L, j * C:(j + 1) * C]

    def spectrum(n):
        tiles = []
        for i in range(nbx):
            for j in range(nby):
                tile = b_r[n, i, j, 0:slab]
                if j == 0:
                    tile = tile + jnp.where(
                        rows8 == 0, b_r[n, (i + nbx - 1) % nbx, nby - 1, slab:thick], 0.0)
                if j == nby - 1:
                    tile = tile + jnp.where(
                        rows8 == slab - 1, b_r[n, (i + 1) % nbx, 0, slab:thick], 0.0)
                tiles.append(tile)
        full = join(tiles, 0).T
        high = full.astype(jnp.bfloat16)
        wide = high.astype(f32)
        both = join([wide, full - wide], 0).astype(jnp.bfloat16)
        first = dot(both, hx[0])
        out = (first[:C] + first[C:] + dot(high, hx[1])) * scale
        return [out[l * per:(l + 1) * per] for l in range(L)]

    def solve(sources):
        primes = []
        for l in range(L):
            source = sources[l]
            if l:
                source = source + inter[l] * primes[-1]
            primes.append(source * coef[l])
        values = [primes[-1]]
        for l in range(L - 2, -1, -1):
            values.insert(0, primes[l] + ratio[l] * values[0])
        return values

    def x_backward(n, values):
        high, low = halves(join(values, 0))
        turn = functools.partial(
            lax.dot_general, dimension_numbers=(((1,), (1,)), ((), ())),
            preferred_element_type=f32)
        first = turn(hx[...].reshape(2 * NX, NX), high)
        out = first[:NX] + first[NX:] + turn(hx[0], low)
        for i in range(nbx):
            for j in range(nby):
                at = i * R + j * slab
                c_s[n, i, j, 0:slab] = out[at:at + slab]
                if j == 0:
                    line = (at + NX - 1) % NX
                else:
                    line = (at + slab) % NX
                c_s[n, i, j, slab:thick] = out[line:line + 1]

    def flank_start(n, src):
        tile = zero
        for c in range(3):
            for l in range(L):
                at = c * L + l
                cell = src[c, l]
                row_s[n, 0, at:at + 1] = cell[0:1]
                row_s[n, 1, at:at + 1] = cell[R - 1:R]
                tile = jnp.where(lanes == at, cell[:, 0:1], tile)
                tile = jnp.where(lanes == C // 2 + at, cell[:, C - 1:C], tile)
        col_s[n] = tile

    def flank_send(n):
        return [
            push(row_s.at[n, 1], row_r.at[n, 0], {"bx": (bx + 1) % nbx}),
            push(row_s.at[n, 0], row_r.at[n, 1], {"bx": (bx + nbx - 1) % nbx}),
            push(col_s.at[n], col_r.at[n, 0], {"by": (by + 1) % nby}),
            push(col_s.at[n], col_r.at[n, 1], {"by": (by + nby - 1) % nby})]

    def relax_inside(src):
        for l in range(L):
            cells = [src[c, l] for c in range(3)]
            squares = [cell * cell for cell in cells]
            whole = squares[0] + squares[1] + squares[2]
            for c in range(3):
                cell, square = cells[c], squares[c]
                above = src[c, l + 1] if l + 1 < L else zero
                below = src[c, l - 1] if l else zero
                smooth = stiff[l] * (
                    (x_next(cell, 0.0) + x_prev(cell, 0.0) + y_next(cell, 0.0)
                     + y_prev(cell, 0.0) - 4.0 * cell) + (above + below - 2.0 * cell))
                drive = cell * (
                    2.0 * alpha[l] + 4.0 * landau[0, l] * square
                    + 2.0 * landau[1, l] * (whole - square)
                    + 6.0 * landau[2, l] * (square * square))
                base[c, l] = cell - step_size * (drive - smooth)

    def relax_edges(n, target):
        low_col = col_r[n, 0]
        high_col = col_r[n, 1]
        for l in range(L):
            weight = step_size * stiff[l]
            for c in range(3):
                at = c * L + l
                add = jnp.where(lanes == 0, low_col[:, C // 2 + at:C // 2 + at + 1], 0.0)
                add = add + jnp.where(lanes == C - 1, high_col[:, at:at + 1], 0.0)
                add = add + jnp.where(rows == 0, row_r[n, 0, at:at + 1], 0.0)
                add = add + jnp.where(rows == R - 1, row_r[n, 1, at:at + 1], 0.0)
                target[c, l] = base[c, l] + weight * add

    def field(n):
        edge = join([d_r[n, j, L] for j in range(nby)], 0)
        phis = [join([d_r[n, j, l] for j in range(nby)], 0) for l in range(L)]
        for l in range(L):
            phi = phis[l]
            low = d_r[n, 0, L + 1, l:l + 1]
            high = d_r[n, nby - 1, L + 1, l:l + 1]
            along_x = 0.5 * (x_next(phi, high) - x_prev(phi, low))
            along_y = 0.5 * (y_next(phi, edge[:, L + l:L + l + 1])
                             - y_prev(phi, edge[:, l:l + 1]))
            above = phis[l + 1] if l + 1 < L else zero
            below = phis[l - 1] if l else zero
            yield l, (along_x, along_y, 0.5 * (above - below))

    loads[0].wait()
    charge(0, p_in)
    flank_start(0, p_in)
    pl.semaphore_wait(barrier, len(others))
    first_a = among_y(a_s, a_r, 0)
    flanks = flank_send(0)
    loads[1].wait()
    relax_inside(p_in)
    loads[2].wait()
    loads[3].wait()
    wave_x = wx[0:1]
    wave_y = join([wy[...]] * (NX // C), 1)
    lateral = wave_x + wave_y
    previous = None
    for l in range(L):
        pivot = perm[l] * lateral + inter[l] + inter[l + 1]
        if l:
            pivot = pivot - inter[l] * previous
        inverse = 1.0 / pivot
        coef[l] = inverse
        previous = inter[l + 1] * inverse
        ratio[l] = previous
    loads[4].wait()
    loads[5].wait()
    wait(first_a)
    y_forward(0)
    first_b = spread(b_s, b_r, 0, False)
    wait(flanks)
    relax_edges(0, base)
    charge(1, base)
    second_a = among_y(a_s, a_r, 1)
    wait(second_a)
    y_forward(1)
    second_b = spread(b_s, b_r, 1, False)
    wait(first_b)
    values = solve(spectrum(0))
    x_backward(0, values)
    first_c = spread(c_s, c_r, 0, True)
    bend = -(wave_x * (1.0 - 0.25 * wave_x) + wave_y * (1.0 - 0.25 * wave_y))
    slopes = []
    none = jnp.zeros_like(values[0])
    for l in range(L):
        above = values[l + 1] if l + 1 < L else none
        below = values[l - 1] if l else none
        slopes.append(0.5 * (above - below))
    moved = []
    for l in range(L):
        above = slopes[l + 1] if l + 1 < L else none
        below = slopes[l - 1] if l else none
        moved.append(step_size * (bend * values[l] + 0.5 * (above - below)))
    wait(second_b)
    x_backward(1, solve([here + more for here, more in zip(spectrum(1), moved)]))
    second_c = spread(c_s, c_r, 1, True)
    wait(first_c)
    y_backward(0)
    first_d = among_y(d_s, d_r, 0)
    wait(second_c)
    y_backward(1)
    second_d = among_y(d_s, d_r, 1)
    wait(first_d)
    for l, parts in field(0):
        for c in range(3):
            p_mid[c, l] = base[c, l] - step_size * parts[c]
    flank_start(1, p_mid)
    flanks = flank_send(1)
    relax_inside(p_mid)
    wait(flanks)
    relax_edges(1, base_o)
    wait(second_d)
    for l, parts in field(1):
        for c in range(3):
            down_o[c, l] = parts[c]
    for send in sends:
        send()


def fused_shards(polarization, alpha_field, landau, stiffness, permittivity, interfaces):
    _, L, R, C = polarization.shape
    nbx = lax.axis_size("bx")
    nby = lax.axis_size("by")
    grid_x, grid_y = nbx * R, nby * C
    per = C // L
    line = np.arange(grid_x)
    hx = fixed_table(line[:, None], line[None, :], grid_x)
    line = np.arange(grid_y)
    hy = fixed_table(line[:, None], line[None, :], grid_y)
    wave_x = 4.0 * np.sin(np.pi * np.arange(grid_x) / grid_x) ** 2
    wave_x = jnp.asarray(np.tile(wave_x[None, :], (8, 1)).astype(np.float32))
    at = np.arange(nbx * nby)
    first = (at % nby) * C + (at // nby) * per
    mode = (first[:, None] + np.arange(per)[None, :]).reshape(-1)
    wave_y = 4.0 * np.sin(np.pi * mode / grid_y) ** 2
    wave_y = jnp.asarray(np.tile(wave_y[:, None], (1, C)).astype(np.float32))
    f32 = jnp.float32
    hbm = pl.BlockSpec(memory_space=pltpu.HBM)
    smem = pl.BlockSpec(memory_space=pltpu.SMEM)
    S = 2
    n_copies = S * (4 + 2 * (nby - 1) + 2 * (nbx * nby - 1))
    by_y = pltpu.VMEM((S, nby, L + 2, 8, C), f32)
    by_mode = pltpu.VMEM((S, nby, nbx, 16, C), f32)
    by_place = pltpu.VMEM((S, nbx, nby, 16, C), f32)
    scratch = [
        pltpu.VMEM((3, L, R, C), f32), pltpu.VMEM((3, L, R, C), f32),
        pltpu.VMEM((L, per, grid_x), f32), pltpu.VMEM((L, per, grid_x), f32),
        by_y, by_y, by_mode, by_place, by_place, by_mode, by_y, by_y,
        pltpu.VMEM((S, 2, 3 * L, C), f32), pltpu.VMEM((S, 2, 3 * L, C), f32),
        pltpu.VMEM((S, R, C), f32), pltpu.VMEM((S, 2, R, C), f32),
        pltpu.SemaphoreType.DMA((n_copies,)), pltpu.SemaphoreType.DMA((n_copies,)),
        pltpu.VMEM((3, L, R, C), f32),
        pltpu.VMEM((L, R, C), f32), pltpu.VMEM(wave_x.shape, f32), pltpu.VMEM((per, C), f32),
        pltpu.VMEM(hx.shape, hx.dtype), pltpu.VMEM(hy.shape, hy.dtype),
        pltpu.SemaphoreType.DMA((6,)),
    ]
    out = pltpu.VMEM(polarization.shape, f32)
    base, down = pl.pallas_call(
        functools.partial(fused, (L, R, C, nbx, nby)),
        out_shape=(out, out),
        in_specs=[hbm, hbm, smem, smem, smem, smem, hbm, hbm, hbm, hbm],
        out_specs=(pl.BlockSpec(memory_space=pltpu.VMEM), pl.BlockSpec(memory_space=pltpu.VMEM)),
        scratch_shapes=scratch,
        compiler_params=pltpu.CompilerParams(
            collective_id=0, has_side_effects=True, vmem_limit_bytes=66 * 1000 * 1000),
    )(polarization, alpha_field, landau, stiffness, permittivity, interfaces,
      wave_x, wave_y, hx, hy)
    return base - step_size * down, -down


def solution(mesh):
    def run(polarization, *rest):
        _, L, R, C = polarization.shape
        body = fused_shards if fits(L, R, C, lax.axis_size("bx"), lax.axis_size("by")) else shards
        return body(polarization, *rest)

    return jax.shard_map(
        run,
        mesh=mesh,
        in_specs=(P(None, None, "bx", "by"), P(None, "bx", "by"), P(), P(), P(), P()),
        out_specs=(P(None, None, "bx", "by"), P(None, None, "bx", "by")),
        check_vma=False,
    )
```

```python
import functools

import jax
import jax.numpy as jnp
import numpy as np
from jax import lax
from jax.experimental import pallas as pl
from jax.experimental.pallas import tpu as pltpu
from jax.sharding import PartitionSpec as P

STEPS = 2
step_size = 0.05
MESH = pl.DeviceIdType.MESH
PAD = 8


def cas_table(left, right, length):
    turns = left * right % length
    angle = 2.0 * jnp.pi / length * turns.astype(jnp.float32)
    table = jnp.cos(angle) + jnp.sin(angle)
    high = lax.reduce_precision(table, 8, 7)
    return jnp.stack([high.astype(jnp.bfloat16), (table - high).astype(jnp.bfloat16)])


def fixed_table(left, right, length):
    angle = 2.0 * np.pi / length * (left * right % length)
    table = (np.cos(angle) + np.sin(angle)).astype(np.float32)
    high = table.astype(jnp.bfloat16)
    low = (table - high.astype(np.float32)).astype(jnp.bfloat16)
    return jnp.asarray(np.stack([high, low]))


def is_wide(rows, nbx, nby, layers):
    return layers % nbx == 0 and rows % (8 * nby) == 0


def halves(value):
    high = value.astype(jnp.bfloat16)
    low = (value - high.astype(jnp.float32)).astype(jnp.bfloat16)
    return high, low


def product(left, right):
    dot = functools.partial(jnp.dot, preferred_element_type=jnp.float32)
    return dot(left[0], right[0]) + (dot(left[0], right[1]) + dot(left[1], right[0]))


def kernel(sizes, p_in, alpha_h, landau, stiff, perm, inter, lam, hx_h, hy_h, p_out, f_out, *scratch):
    L, R, C, nbx, nby, rep, lp, own = sizes
    (p_mid, base, coef, ratio, q, inb, outs, rec_i,
     row_s, row_r, col_s, col_r, pc_s, pc_r, ssem, rsem,
     alpha, hx, hy, local_sem) = scratch[:20]
    wide = is_wide(R, nbx, nby, L)
    if wide:
        z_in, w_out = scratch[20:]
    else:
        rec_f, ybuf, phat, u = scratch[20:]
    thin = R // nby
    R2 = R + PAD
    bx = lax.axis_index("bx")
    by = lax.axis_index("by")
    group = bx // rep
    part = bx % rep
    scale = 1.0 / (R * nbx * C * nby)
    loads = [pltpu.make_async_copy(src, dst, local_sem.at[at]) for at, (src, dst) in
             enumerate(((alpha_h, alpha), (hx_h, hx), (hy_h, hy)))]
    for load in loads:
        load.start()
    slots = [0]
    sends = []

    barrier = pltpu.get_barrier_semaphore()
    others = [(a, b) for b in range(nby) for a in range(nbx) if a or b]
    greeted = [(a, b) for a, b in others if wide or not a or not b]
    for a, b in greeted:
        pl.semaphore_signal(
            barrier, inc=1, device_id={"bx": (bx + a) % nbx, "by": (by + b) % nby},
            device_id_type=MESH)

    def remote(src, dst, device, slot):
        return pltpu.make_async_remote_copy(
            src_ref=src, dst_ref=dst, send_sem=ssem.at[slot], recv_sem=rsem.at[slot],
            device_id=device, device_id_type=MESH)

    def fresh():
        slots[0] += 1
        return slots[0] - 1

    def push(src, dst, device):
        copy = remote(src, dst, device, fresh())
        copy.start()
        sends.append(copy.wait_send)
        return copy

    rows = lax.broadcasted_iota(jnp.int32, (R, C), 0)
    lanes = lax.broadcasted_iota(jnp.int32, (R, C), 1)

    def x_next(f, high):
        return jnp.where(rows == R - 1, high, pltpu.roll(f, R - 1, 0))

    def x_prev(f, low):
        return jnp.where(rows == 0, low, pltpu.roll(f, 1, 0))

    def y_next(f, high):
        return jnp.where(lanes == C - 1, high, pltpu.roll(f, C - 1, 1))

    def y_prev(f, low):
        return jnp.where(lanes == 0, low, pltpu.roll(f, 1, 1))

    def column_tile(blocks):
        tile = jnp.zeros((R, C), jnp.float32)
        for at, block in enumerate(blocks):
            tile = jnp.where(lanes == at, block[:, 0:1], tile)
            tile = jnp.where(lanes == C // 2 + at, block[:, C - 1:C], tile)
        return tile

    def x_start(src, n):
        mine = inb.at[n, :, pl.ds(pl.multiple_of(bx * R, R), R)]
        copies = []
        for k in range(1, nbx):
            to = (bx + k) % nbx
            copies.append(push(src.at[pl.ds(to // rep * lp, lp)], mine, {"bx": to}))
        for layer in range(lp):
            inb[n, layer, pl.ds(pl.multiple_of(bx * R, R), R)] = src[group * lp + layer]
        return copies

    def x_mix(copies, n):
        for copy in copies:
            copy.wait_recv()
        table = (hx[0], hx[1])
        for layer in range(lp):
            outs[n, :, layer] = product(table, halves(inb[n, layer])).reshape(own, R2, C)

    def spread(n, step):
        copies = []
        for a, b in others:
            to_x, to_y = (bx + a) % nbx, (by + b) % nby
            copies.append(push(
                outs.at[n, to_x, :, pl.ds(pl.multiple_of(to_y * thin, thin), thin)],
                z_in.at[step, by, pl.ds(bx * lp, lp)], {"bx": to_x, "by": to_y}))
        for layer in range(lp):
            z_in[step, by, bx * lp + layer] = outs[
                n, bx, layer, pl.ds(pl.multiple_of(by * thin, thin), thin)]
        for copy in copies:
            copy.wait_recv()

    def collect(n, step):
        at = pl.ds(pl.multiple_of(bx * R + by * thin, thin), thin)
        copies = []
        for a, b in others:
            to_x, to_y = (bx + a) % nbx, (by + b) % nby
            copies.append(push(
                w_out.at[step, to_y, pl.ds(to_x * lp, lp)], inb.at[n, :, at],
                {"bx": to_x, "by": to_y}))
        for layer in range(lp):
            inb[n, layer, at] = w_out[step, by, bx * lp + layer]
        return copies

    def solve(spectrum, height):
        primes = []
        for l in range(L):
            source = spectrum[l * height:(l + 1) * height] * scale
            if l:
                source = source + inter[l] * primes[-1]
            primes.append(source * coef[l])
        values = [primes[-1]]
        for l in range(L - 2, -1, -1):
            values.insert(0, primes[l] + ratio[l] * values[0])
        return values

    def x_finish(n, dst, height):
        waits = []
        landing = dst.at[pl.ds(group * lp, lp)]
        for t in range(own):
            local = (group + t) % own
            to = part * own + local
            src = outs.at[n, local, :, pl.ds(0, height)]
            if rep == 1:
                if t == 0:
                    continue
                waits.append(push(src, landing, {"bx": to}).wait_recv)
                continue
            slot = fresh()

            def go(src=src, to=to, slot=slot):
                remote(src, landing, {"bx": to}, slot).start()

            def gone(src=src, to=to, slot=slot):
                @pl.when(to != bx)
                def _():
                    remote(src, landing, {"bx": to}, slot).wait_send()

            def came(src=src, to=to, slot=slot, t=t):
                origin = (bx % own + own - t) % own * rep + bx // own

                @pl.when(origin != bx)
                def _():
                    remote(src, landing, {"bx": to}, slot).wait_recv()

            pl.when(to != bx)(go)
            sends.append(gone)
            waits.append(came)

        def keep():
            for layer in range(lp):
                dst[group * lp + layer] = outs[n, bx % own, layer, 0:height]

        if rep == 1:
            keep()
        else:
            pl.when(bx // own == part)(keep)
        for wait in waits:
            wait()

    def y_pass(src, n):
        copies = [push(src, ybuf.at[n, k - 1], {"by": (by + k) % nby}) for k in range(1, nby)]
        total = product(halves(src[...].reshape(L * R, C)), (hy[0, by], hy[1, by]))
        for k in range(1, nby):
            copies[k - 1].wait_recv()
            origin = (by + nby - k) % nby
            total += product(halves(ybuf[n, k - 1].reshape(L * R, C)), (hy[0, origin], hy[1, origin]))
        return total

    def flank_start(rows_too, step, src):
        copies = []
        if rows_too:
            for c in range(3):
                for l in range(L):
                    at = c * L + l
                    row_s[step, 0, at:at + 1] = src[c, l, 0:1]
                    row_s[step, 1, at:at + 1] = src[c, l, R - 1:R]
            col_s[step] = column_tile([src[c, l] for c in range(3) for l in range(L)])
            if step == 0:
                pl.semaphore_wait(barrier, len(greeted))
            copies.append(push(row_s.at[step, 1], row_r.at[step, 0], {"bx": (bx + 1) % nbx}))
            copies.append(push(row_s.at[step, 0], row_r.at[step, 1], {"bx": (bx + nbx - 1) % nbx}))
            tile, land = col_s.at[step], col_r
        else:
            pc_s[step] = column_tile([src[l, 0:R] for l in range(L)])
            tile, land = pc_s.at[step], pc_r
        copies.append(push(tile, land.at[step, 0], {"by": (by + 1) % nby}))
        copies.append(push(tile, land.at[step, 1], {"by": (by + nby - 1) % nby}))
        return copies

    for step in range(STEPS):
        src = p_in if step == 0 else p_mid
        flanks = flank_start(True, step, src)
        if step == 0:
            lateral = lam[...]
            previous = None
            for l in range(L):
                pivot = perm[l] * lateral + inter[l] + inter[l + 1]
                if l:
                    pivot = pivot - inter[l] * previous
                inverse = 1.0 / pivot
                coef[l] = inverse
                previous = inter[l + 1] * inverse
                ratio[l] = previous
        for copy in flanks:
            copy.wait_recv()
        low_col = col_r[step, 0]
        high_col = col_r[step, 1]

        def edges(c, l):
            at = c * L + l
            return (row_r[step, 0, at:at + 1], row_r[step, 1, at:at + 1],
                    low_col[:, C // 2 + at:C // 2 + at + 1], high_col[:, at:at + 1])

        zero = jnp.zeros((R, C), jnp.float32)
        for l in range(L):
            low, high, _, _ = edges(0, l)
            _, _, left, right = edges(1, l)
            along_x, along_y = src[0, l], src[1, l]
            above = src[2, l + 1] if l + 1 < L else zero
            below = src[2, l - 1] if l else zero
            q[step, l] = -0.5 * (
                (x_next(along_x, high) - x_prev(along_x, low))
                + (y_next(along_y, right) - y_prev(along_y, left)) + (above - below))
        copies = x_start(q.at[step], 2 * step)
        if step == 0:
            for load in loads:
                load.wait()
        for l in range(L):
            cells = [src[c, l] for c in range(3)]
            squares = [cell * cell for cell in cells]
            whole = squares[0] + squares[1] + squares[2]
            for c in range(3):
                cell, square = cells[c], squares[c]
                low, high, left, right = edges(c, l)
                above = src[c, l + 1] if l + 1 < L else zero
                below = src[c, l - 1] if l else zero
                smooth = stiff[l] * (
                    (x_next(cell, high) + x_prev(cell, low) + y_next(cell, right)
                     + y_prev(cell, left) - 4.0 * cell) + (above + below - 2.0 * cell))
                drive = cell * (
                    2.0 * alpha[l] + 4.0 * landau[0, l] * square
                    + 2.0 * landau[1, l] * (whole - square)
                    + 6.0 * landau[2, l] * (square * square))
                base[c, l] = cell - step_size * (drive - smooth)
        n = 2 * step
        x_mix(copies, n)
        if wide:
            spread(n, step)
            table = (hy[0], hy[1])
            full = jnp.concatenate(
                [z_in[step, j].reshape(L * thin, C) for j in range(nby)], axis=1)
            values = solve(product(halves(full), table), thin)
            full = product(halves(jnp.concatenate(values, axis=0)), table)
            for j in range(nby):
                w_out[step, j] = full[:, j * C:(j + 1) * C].reshape(L, thin, C)
            copies = collect(n + 1, step)
        else:
            x_finish(n, rec_f.at[step], R)
            for l, value in enumerate(solve(y_pass(rec_f.at[step], n), R)):
                phat[step, l] = value
            u[step] = y_pass(phat.at[step], n + 1).reshape(L, R, C)
            copies = x_start(u.at[step], n + 1)
        x_mix(copies, n + 1)
        x_finish(n + 1, rec_i.at[step], R2)
        flanks = flank_start(False, step, rec_i.at[step])
        last = step == STEPS - 1
        target = p_out if last else p_mid
        for l in range(L):
            phi = rec_i[step, l, 0:R]
            low = rec_i[step, l, R:R + 1]
            high = rec_i[step, l, R + 1:R + 2]
            along_x = -0.5 * (x_next(phi, high) - x_prev(phi, low))
            above = rec_i[step, l + 1, 0:R] if l + 1 < L else zero
            below = rec_i[step, l - 1, 0:R] if l else zero
            along_z = -0.5 * (above - below)
            target[0, l] = base[0, l] + step_size * along_x
            target[2, l] = base[2, l] + step_size * along_z
            if last:
                f_out[0, l] = along_x
                f_out[2, l] = along_z
        for copy in flanks:
            copy.wait_recv()
        low_phi = pc_r[step, 0]
        high_phi = pc_r[step, 1]
        for l in range(L):
            phi = rec_i[step, l, 0:R]
            along_y = -0.5 * (y_next(phi, high_phi[:, l:l + 1])
                              - y_prev(phi, low_phi[:, C // 2 + l:C // 2 + l + 1]))
            target[1, l] = base[1, l] + step_size * along_y
            if last:
                f_out[1, l] = along_y
    for wait in sends:
        wait()


def shards(polarization, alpha_field, landau, stiffness, permittivity, interfaces):
    _, L, R, C = polarization.shape
    nbx = lax.axis_size("bx")
    nby = lax.axis_size("by")
    bx = lax.axis_index("bx")
    by = lax.axis_index("by")
    rep = max(1, nbx // L)
    lp = max(1, L // nbx)
    own = nbx // rep
    grid_x, grid_y = nbx * R, nby * C
    R2 = R + PAD
    wide = is_wide(R, nbx, nby, L)
    pool = np if wide else jnp
    make = fixed_table if wide else cas_table
    line = pool.arange(R2, dtype=jnp.int32)
    line = pool.where(line < R, line, pool.where(line == R, -1, R))
    owners = pool.arange(own, dtype=jnp.int32)
    if not wide:
        owners = owners + bx % rep * own
    wanted = ((owners[:, None] * R + line[None, :] + grid_x) % grid_x).reshape(own * R2, 1)
    hx = make(wanted, pool.arange(grid_x, dtype=jnp.int32)[None, :], grid_x)
    every_col = pool.arange(grid_y, dtype=jnp.int32)
    my_rows = bx * R + jnp.arange(R, dtype=jnp.int32)
    my_cols = by * C + jnp.arange(C, dtype=jnp.int32)
    if wide:
        hy = make(every_col[:, None], every_col[None, :], grid_y)
        my_rows = bx * R + by * (R // nby) + jnp.arange(R // nby, dtype=jnp.int32)
        my_cols = jnp.arange(grid_y, dtype=jnp.int32)
    else:
        hy = make(every_col[:, None], my_cols[None, :], grid_y).reshape(2, nby, C, C)
    wave_x = jnp.sin(jnp.pi * my_rows.astype(jnp.float32) / grid_x)
    wave_y = jnp.sin(jnp.pi * my_cols.astype(jnp.float32) / grid_y)
    lam = 4.0 * wave_x[:, None] ** 2 + 4.0 * wave_y[None, :] ** 2
    sizes = (L, R, C, nbx, nby, rep, lp, own)
    n_copies = STEPS * (6 + 2 * (nbx * nby + own if wide else nbx + own + nby))
    f32 = jnp.float32
    vmem = pl.BlockSpec(memory_space=pltpu.VMEM)
    hbm = pl.BlockSpec(memory_space=pltpu.HBM)
    smem = pl.BlockSpec(memory_space=pltpu.SMEM)
    S = STEPS
    scratch = [
        pltpu.VMEM((3, L, R, C), f32), pltpu.VMEM((3, L, R, C), f32),
        pltpu.VMEM((L,) + lam.shape, f32), pltpu.VMEM((L,) + lam.shape, f32),
        pltpu.VMEM((S, L, R, C), f32), pltpu.VMEM((2 * S, lp, grid_x, C), f32),
        pltpu.VMEM((2 * S, own, lp, R2, C), f32), pltpu.VMEM((S, L, R2, C), f32),
        pltpu.VMEM((S, 2, 3 * L, C), f32), pltpu.VMEM((S, 2, 3 * L, C), f32),
        pltpu.VMEM((S, R, C), f32), pltpu.VMEM((S, 2, R, C), f32),
        pltpu.VMEM((S, R, C), f32), pltpu.VMEM((S, 2, R, C), f32),
        pltpu.SemaphoreType.DMA((n_copies,)), pltpu.SemaphoreType.DMA((n_copies,)),
        pltpu.VMEM((L, R, C), f32), pltpu.VMEM(hx.shape, hx.dtype),
        pltpu.VMEM(hy.shape, hy.dtype), pltpu.SemaphoreType.DMA((3,)),
    ]
    if wide:
        thin = (S, nby, L, R // nby, C)
        scratch += [pltpu.VMEM(thin, f32), pltpu.VMEM(thin, f32)]
    else:
        scratch += [
            pltpu.VMEM((S, L, R, C), f32), pltpu.VMEM((2 * S, nby - 1, L, R, C), f32),
            pltpu.VMEM((S, L, R, C), f32), pltpu.VMEM((S, L, R, C), f32),
        ]
    out = jax.ShapeDtypeStruct(polarization.shape, f32)
    return pl.pallas_call(
        functools.partial(kernel, sizes),
        out_shape=(out, out),
        in_specs=[vmem, hbm, smem, smem, smem, smem, vmem, hbm, hbm],
        out_specs=(vmem, vmem),
        scratch_shapes=scratch,
        compiler_params=pltpu.CompilerParams(
            collective_id=0, has_side_effects=True, vmem_limit_bytes=65 * 1000 * 1000),
    )(polarization, alpha_field, landau, stiffness, permittivity, interfaces, lam, hx, hy)


def fits(L, R, C, nbx, nby):
    slab = R // nby
    return (L == nbx and slab == 8 and slab * nby == R and nby > 1 and C % L == 0
            and nbx > 2 and nbx & (nbx - 1) == 0 and nby & (nby - 1) == 0)


def partner(index, mask, size):
    other = 0
    bit = 1
    while bit < size:
        here = index // bit % 2
        other = other + bit * (1 - here if mask // bit % 2 else here)
        bit *= 2
    return other


def join(parts, axis):
    return jnp.concatenate(parts, axis=axis)


def fused(sizes, p_h, alpha_h, landau, stiff, perm, inter, wx_h, wy_h, hx_h, hy_h,
          base_o, down_o, *scratch):
    L, R, C, nbx, nby = sizes
    (p_mid, base, coef, ratio, a_s, a_r, b_s, b_r, c_s, c_r, d_s, d_r,
     row_s, row_r, col_s, col_r, ssem, rsem, known, p_in, alpha, wx, wy, hx, hy, local_sem) = scratch
    slab = R // nby
    per = C // L
    NX, NY = nbx * R, nby * C
    bx = lax.axis_index("bx")
    by = lax.axis_index("by")
    scale = 1.0 / (NX * NY)
    f32 = jnp.float32
    dot = functools.partial(jnp.dot, preferred_element_type=f32)
    slots = [0]
    sends = []

    barrier = pltpu.get_barrier_semaphore()
    at_x = [partner(bx, a, nbx) for a in range(nbx)]
    at_y = [partner(by, b, nby) for b in range(nby)]
    others = [(a, b) for b in range(nby) for a in range(nbx) if a or b]
    others.sort(key=lambda ab: -(ab[0] // 2 + ab[0] % 2 + ab[1] // 2))
    reach = [1 << i for i in range(1, nbx.bit_length() - 1)]
    greeted = [(a, b) for a, b in others if a < 2] + [(a, 0) for a in reach]
    for a, b in greeted:
        pl.semaphore_signal(
            barrier, inc=1, device_id={"bx": at_x[a], "by": at_y[b]}, device_id_type=MESH)
    mine = pl.multiple_of((bx * nby + by) * per, per)
    loads = [pltpu.make_async_copy(src, dst, local_sem.at[at]) for at, (src, dst) in enumerate((
        (p_h, p_in), (alpha_h, alpha), (wx_h, wx), (wy_h.at[pl.ds(mine, per)], wy), (hx_h, hx),
        (hy_h, hy)))]
    for load in loads:
        load.start()

    def push(src, dst, device):
        slot = slots[0]
        slots[0] += 1
        copy = pltpu.make_async_remote_copy(
            src_ref=src, dst_ref=dst, send_sem=ssem.at[slot], recv_sem=rsem.at[slot],
            device_id=device, device_id_type=MESH)
        copy.start()
        sends.append(copy.wait_send)
        return copy

    rows = lax.broadcasted_iota(jnp.int32, (R, C), 0)
    lanes = lax.broadcasted_iota(jnp.int32, (R, C), 1)
    rows8 = lax.broadcasted_iota(jnp.int32, (slab, C), 0)
    lanes8 = lax.broadcasted_iota(jnp.int32, (slab, C), 1)
    zero = jnp.zeros((R, C), f32)
    zero8 = jnp.zeros((slab, C), f32)

    def x_next(f, high):
        return jnp.where(rows == R - 1, high, pltpu.roll(f, R - 1, 0))

    def x_prev(f, low):
        return jnp.where(rows == 0, low, pltpu.roll(f, 1, 0))

    def y_next(f, high):
        return jnp.where(lanes == C - 1, high, pltpu.roll(f, C - 1, 1))

    def y_prev(f, low):
        return jnp.where(lanes == 0, low, pltpu.roll(f, 1, 1))

    def charge(n, src, ring):
        sides = (0, nby - 1)
        edge = zero
        for l in range(L):
            along_x, along_y = src[0, l], src[1, l]
            above = src[2, l + 1] if l + 1 < L else zero
            below = src[2, l - 1] if l else zero
            low = high = left = right = 0.0
            if ring:
                lines, column = ring
                low, high = lines[0][0][l:l + 1], lines[1][0][l:l + 1]
                left = column[:, L + l:L + l + 1]
                right = column[:, C // 2 + L + l:C // 2 + L + l + 1]
            value = -0.5 * ((x_next(along_x, high) - x_prev(along_x, low))
                            + (y_next(along_y, right) - y_prev(along_y, left)) + (above - below))
            for j in range(nby):
                a_s[n, j, l] = value[j * slab:(j + 1) * slab]
            edge = jnp.where(lanes == l, -0.5 * along_y[:, 0:1], edge)
            edge = jnp.where(lanes == L + l, 0.5 * along_y[:, C - 1:C], edge)
        near = [-0.5 * join([src[0, l, 0:1] for l in range(L)], 0),
                0.5 * join([src[0, l, R - 1:R] for l in range(L)], 0)]
        corner = [None, None]
        if ring:
            for side, sign in enumerate((-0.5, 0.5)):
                first, second, third = lines[side]
                turned = (jnp.where(lanes8 == C - 1, 0.0, pltpu.roll(second, C - 1, 1))
                          - jnp.where(lanes8 == 0, 0.0, pltpu.roll(second, 1, 1)))
                risen = (jnp.where(rows8 == L - 1, 0.0, pltpu.roll(third, L - 1, 0))
                         - jnp.where(rows8 == 0, 0.0, pltpu.roll(third, 1, 0)))
                near[side] = near[side] - 0.5 * (turned + risen)
                a_s[n, sides[side], L + 2] = sign * first
                corner[side] = jnp.where(
                    lanes8 == 4 * L, sign * first[:, 0:1] - 0.5 * second[:, 0:1],
                    jnp.where(lanes8 == 4 * L + 1,
                              sign * first[:, C - 1:C] + 0.5 * second[:, C - 1:C], 0.0))
            layer = lanes % L
            turned = -0.5 * (x_next(column, 0.0) - x_prev(column, 0.0))
            risen = -0.5 * (jnp.where(layer == L - 1, 0.0, pltpu.roll(column, C - 1, 1))
                            - jnp.where(layer == 0, 0.0, pltpu.roll(column, 1, 1)))
            both = turned + pltpu.roll(risen, C - 2 * L, 1)
            low = edge + both
            high = edge + pltpu.roll(both, C // 2 + L, 1)
            far_low = -0.5 * pltpu.roll(column, L, 1)
            far_high = 0.5 * pltpu.roll(column, C // 2 + 2 * L, 1)
            group = lanes // L
            edge = jnp.where(group == 0, low, jnp.where(group == 1, high, jnp.where(
                group == 2, far_low, jnp.where(group == 3, far_high, 0.0))))
        for side in range(2):
            a_s[n, sides[side], L + 1] = near[side]
        for j in range(nby):
            piece = edge[j * slab:(j + 1) * slab]
            if ring and j in sides:
                piece = piece + corner[sides.index(j)]
            a_s[n, j, L] = piece
            if j not in sides:
                a_s[n, j, L + 1] = jnp.zeros((L, C), f32)
                if ring:
                    a_s[n, j, L + 2] = jnp.zeros((L, C), f32)

    def ring_of(n):
        weight8 = zero8
        weight = zero
        layer = lanes % L
        for l in range(L):
            weight8 = jnp.where(rows8 == l, step_size * stiff[l], weight8)
            weight = jnp.where(layer == l, step_size * stiff[l], weight)
        lines = [[weight8 * row_s[n, side, c * L:(c + 1) * L] for c in range(3)]
                 for side in range(2)]
        return lines, weight * col_s[n]

    def among_y(source, landing, n, count):
        part = pl.ds(0, count)
        copies = []
        for b in range(nby - 1, 0, -1):
            to = at_y[b]
            copies.append(push(source.at[n, to, part], landing.at[n, by, part], {"by": to}))
        landing[n, by, 0:count] = source[n, by, 0:count]
        return copies

    def wait(copies):
        for copy in copies:
            copy.wait_recv()

    def spread(source, landing, n, flip, thick):
        part = pl.ds(0, thick)
        copies = []
        for a, b in others:
            to_x, to_y = at_x[a], at_y[b]
            if flip:
                src, dst = source.at[n, to_x, to_y, part], landing.at[n, by, bx, part]
            else:
                src, dst = source.at[n, to_y, to_x, part], landing.at[n, bx, by, part]
            copies.append(push(src, dst, {"bx": to_x, "by": to_y}))
        if flip:
            landing[n, by, bx, 0:thick] = source[n, bx, by, 0:thick]
        else:
            landing[n, bx, by, 0:thick] = source[n, by, bx, 0:thick]
        return copies

    def swap_groups(tiles):
        height = tiles[0].shape[0]
        group = lax.broadcasted_iota(jnp.int32, (height, C), 1) // per
        tiles = list(tiles)
        s = 1
        while s < L:
            upper = group % (2 * s) >= s
            for at in range(L):
                if at % (2 * s) < s:
                    low, high = tiles[at], tiles[at + s]
                    tiles[at] = jnp.where(upper, pltpu.roll(high, s * per, 1), low)
                    tiles[at + s] = jnp.where(upper, high, pltpu.roll(low, C - s * per, 1))
            s *= 2
        return tiles

    def swap_rows(tile):
        group = lanes8 // per
        s = 1
        while s < L:
            upper = group % (2 * s) >= s
            later = rows8 % (2 * s) >= s
            ahead = pltpu.roll(pltpu.roll(tile, L - s, 0), s * per, 1)
            behind = pltpu.roll(pltpu.roll(tile, s, 0), C - s * per, 1)
            tile = jnp.where(later, jnp.where(upper, tile, behind), jnp.where(upper, ahead, tile))
            s *= 2
        return tile

    def y_table(full):
        height = full.shape[0]
        high = full.astype(jnp.bfloat16)
        wide = high.astype(f32)
        both = join([wide, full - wide], 0).astype(jnp.bfloat16)
        first = dot(both, hy[0])
        return first[:height] + first[height:] + dot(high, hy[1])

    def y_forward(n):
        columns = []
        for j in range(nby):
            from_left = a_r[n, (j + nby - 1) % nby, L]
            from_right = a_r[n, (j + 1) % nby, L]
            tiles = []
            for l in range(L):
                extra = jnp.where(
                    lanes8 == 0, from_left[:, L + l:L + l + 1],
                    jnp.where(lanes8 == C - 1, from_right[:, l:l + 1], 0.0))
                if n:
                    extra = jnp.where(
                        lanes8 == 1, from_left[:, 3 * L + l:3 * L + l + 1],
                        jnp.where(lanes8 == C - 2, from_right[:, 2 * L + l:2 * L + l + 1], extra))
                tiles.append(a_r[n, j, l] + extra)
            near, far = a_r[n, j, L + 1], zero8
            if n:
                near = near + jnp.where(
                    lanes8 == 0, from_left[:, 4 * L + 1:4 * L + 2],
                    jnp.where(lanes8 == C - 1, from_right[:, 4 * L:4 * L + 1], 0.0))
                far = a_r[n, j, L + 2]
            columns.append(join(tiles + [near, far], 0))
        out = y_table(join(columns, 1))
        tiles = [join([out[l * slab:(l + 1) * slab, t * C:(t + 1) * C] for t in range(nby)], 0)
                 for l in range(L)]
        tiles = swap_groups(tiles)
        for t in range(nby):
            halos = [swap_rows(out[(L + k) * slab:(L + k) * slab + L, t * C:(t + 1) * C])
                     for k in range(1 + n)]
            for e in range(L):
                b_s[n, t, e, 0:slab] = tiles[e][t * slab:(t + 1) * slab]
                for k, halo in enumerate(halos):
                    b_s[n, t, e, slab + k:slab + k + 1] = halo[e:e + 1]

    def y_backward(n):
        tiles = swap_groups([join([c_r[n, t, e, 0:slab] for t in range(nby)], 0)
                             for e in range(L)])
        halos = [swap_rows(join([c_r[n, t, e, slab:slab + 1] for e in range(L)], 0))
                 for t in range(nby)]
        lines = [join([tiles[l][t * slab:(t + 1) * slab] for t in range(nby)], 1)
                 for l in range(L)]
        lines += [join(halos, 1), jnp.zeros((slab, NY), f32)]
        out = y_table(join(lines, 0))
        for j in range(nby):
            edge = zero8
            left, right = (j + nby - 1) % nby, (j + 1) % nby
            for l in range(L):
                line = out[l * slab:(l + 1) * slab]
                d_s[n, j, l] = line[:, j * C:(j + 1) * C]
                edge = jnp.where(lanes8 == l, line[:, left * C + C - 1:left * C + C], edge)
                edge = jnp.where(lanes8 == L + l, line[:, right * C:right * C + 1], edge)
            d_s[n, j, L] = edge
            d_s[n, j, L + 1] = out[L * slab:L * slab + L, j * C:(j + 1) * C]

    def spectrum(n):
        tiles = []
        for i in range(nbx):
            for j in range(nby):
                tile = b_r[n, i, j, 0:slab]
                for k in range(1 + n):
                    line = slice(slab + k, slab + k + 1)
                    if j == 0:
                        tile = tile + jnp.where(
                            rows8 == k, b_r[n, (i + nbx - 1) % nbx, nby - 1, line], 0.0)
                    if j == nby - 1:
                        tile = tile + jnp.where(
                            rows8 == slab - 1 - k, b_r[n, (i + 1) % nbx, 0, line], 0.0)
                tiles.append(tile)
        full = join(tiles, 0).T
        high = full.astype(jnp.bfloat16)
        wide = high.astype(f32)
        both = join([wide, full - wide], 0).astype(jnp.bfloat16)
        first = dot(both, hx[0])
        out = (first[:C] + first[C:] + dot(high, hx[1])) * scale
        return [out[l * per:(l + 1) * per] for l in range(L)]

    def solve(sources):
        primes = []
        for l in range(L):
            source = sources[l]
            if l:
                source = source + inter[l] * primes[-1]
            primes.append(source * coef[l])
        values = [primes[-1]]
        for l in range(L - 2, -1, -1):
            values.insert(0, primes[l] + ratio[l] * values[0])
        return values

    def x_backward(n, values):
        high, low = halves(join(values, 0))
        turn = functools.partial(
            lax.dot_general, dimension_numbers=(((1,), (1,)), ((), ())),
            preferred_element_type=f32)
        first = turn(hx[...].reshape(2 * NX, NX), high)
        out = first[:NX] + first[NX:] + turn(hx[0], low)
        for i in range(nbx):
            for j in range(nby):
                at = i * R + j * slab
                c_s[n, i, j, 0:slab] = out[at:at + slab]
                if j == 0:
                    line = (at + NX - 1) % NX
                else:
                    line = (at + slab) % NX
                c_s[n, i, j, slab:slab + 1] = out[line:line + 1]

    def flank_start(n, src):
        tile = zero
        for c in range(3):
            for l in range(L):
                at = c * L + l
                cell = src[c, l]
                row_s[n, 0, at:at + 1] = cell[0:1]
                row_s[n, 1, at:at + 1] = cell[R - 1:R]
                tile = jnp.where(lanes == at, cell[:, 0:1], tile)
                tile = jnp.where(lanes == C // 2 + at, cell[:, C - 1:C], tile)
        col_s[n] = tile

    def flank_send(n):
        return [
            push(row_s.at[n, 1], row_r.at[n, 0], {"bx": (bx + 1) % nbx}),
            push(row_s.at[n, 0], row_r.at[n, 1], {"bx": (bx + nbx - 1) % nbx}),
            push(col_s.at[n], col_r.at[n, 0], {"by": (by + 1) % nby}),
            push(col_s.at[n], col_r.at[n, 1], {"by": (by + nby - 1) % nby})]

    def relax_inside(src):
        for l in range(L):
            cells = [src[c, l] for c in range(3)]
            squares = [cell * cell for cell in cells]
            whole = squares[0] + squares[1] + squares[2]
            for c in range(3):
                cell, square = cells[c], squares[c]
                above = src[c, l + 1] if l + 1 < L else zero
                below = src[c, l - 1] if l else zero
                smooth = stiff[l] * (
                    (x_next(cell, 0.0) + x_prev(cell, 0.0) + y_next(cell, 0.0)
                     + y_prev(cell, 0.0) - 4.0 * cell) + (above + below - 2.0 * cell))
                drive = cell * (
                    2.0 * alpha[l] + 4.0 * landau[0, l] * square
                    + 2.0 * landau[1, l] * (whole - square)
                    + 6.0 * landau[2, l] * (square * square))
                base[c, l] = cell - step_size * (drive - smooth)

    def relax_edges(n, target):
        low_col = col_r[n, 0]
        high_col = col_r[n, 1]
        for l in range(L):
            weight = step_size * stiff[l]
            for c in range(3):
                at = c * L + l
                add = jnp.where(lanes == 0, low_col[:, C // 2 + at:C // 2 + at + 1], 0.0)
                add = add + jnp.where(lanes == C - 1, high_col[:, at:at + 1], 0.0)
                add = add + jnp.where(rows == 0, row_r[n, 0, at:at + 1], 0.0)
                add = add + jnp.where(rows == R - 1, row_r[n, 1, at:at + 1], 0.0)
                target[c, l] = base[c, l] + weight * add

    def field(n):
        edge = join([d_r[n, j, L] for j in range(nby)], 0)
        phis = [join([d_r[n, j, l] for j in range(nby)], 0) for l in range(L)]
        for l in range(L):
            phi = phis[l]
            low = d_r[n, 0, L + 1, l:l + 1]
            high = d_r[n, nby - 1, L + 1, l:l + 1]
            along_x = 0.5 * (x_next(phi, high) - x_prev(phi, low))
            along_y = 0.5 * (y_next(phi, edge[:, L + l:L + l + 1])
                             - y_prev(phi, edge[:, l:l + 1]))
            above = phis[l + 1] if l + 1 < L else zero
            below = phis[l - 1] if l else zero
            yield l, (along_x, along_y, 0.5 * (above - below))

    loads[0].wait()
    charge(0, p_in, None)
    flank_start(0, p_in)
    loads[1].wait()
    relax_inside(p_in)
    charge(1, base, ring_of(0))
    pl.semaphore_wait(barrier, len(greeted))

    def tell(at):
        pl.semaphore_signal(
            known.at[at], inc=1, device_id={"bx": at_x[reach[at]]}, device_id_type=MESH)

    tell(0)
    first_a = among_y(a_s, a_r, 0, L + 2)
    second_a = among_y(a_s, a_r, 1, L + 3)
    for at in range(1, len(reach)):
        pl.semaphore_wait(known.at[at - 1], 1)
        tell(at)
    loads[2].wait()
    loads[3].wait()
    wave_x = wx[0:1]
    wave_y = join([wy[...]] * (NX // C), 1)
    lateral = wave_x + wave_y
    previous = None
    for l in range(L):
        pivot = perm[l] * lateral + inter[l] + inter[l + 1]
        if l:
            pivot = pivot - inter[l] * previous
        inverse = 1.0 / pivot
        coef[l] = inverse
        previous = inter[l + 1] * inverse
        ratio[l] = previous
    loads[4].wait()
    loads[5].wait()
    wait(first_a)
    y_forward(0)
    pl.semaphore_wait(known.at[len(reach) - 1], 1)
    first_b = spread(b_s, b_r, 0, False, slab + 1)
    wait(second_a)
    y_forward(1)
    second_b = spread(b_s, b_r, 1, False, slab + 2)
    flanks = flank_send(0)
    wait(first_b)
    values = solve(spectrum(0))
    x_backward(0, values)
    first_c = spread(c_s, c_r, 0, True, slab + 1)
    wait(flanks)
    relax_edges(0, base)
    bend = -(wave_x * (1.0 - 0.25 * wave_x) + wave_y * (1.0 - 0.25 * wave_y))
    slopes = []
    none = jnp.zeros_like(values[0])
    for l in range(L):
        above = values[l + 1] if l + 1 < L else none
        below = values[l - 1] if l else none
        slopes.append(0.5 * (above - below))
    moved = []
    for l in range(L):
        above = slopes[l + 1] if l + 1 < L else none
        below = slopes[l - 1] if l else none
        moved.append(step_size * (bend * values[l] + 0.5 * (above - below)))
    wait(second_b)
    x_backward(1, solve([here + more for here, more in zip(spectrum(1), moved)]))
    second_c = spread(c_s, c_r, 1, True, slab + 1)
    wait(first_c)
    y_backward(0)
    first_d = among_y(d_s, d_r, 0, L + 2)
    wait(second_c)
    y_backward(1)
    second_d = among_y(d_s, d_r, 1, L + 2)
    wait(first_d)
    for l, parts in field(0):
        for c in range(3):
            p_mid[c, l] = base[c, l] - step_size * parts[c]
    flank_start(1, p_mid)
    flanks = flank_send(1)
    relax_inside(p_mid)
    wait(flanks)
    relax_edges(1, base_o)
    wait(second_d)
    for l, parts in field(1):
        for c in range(3):
            down_o[c, l] = parts[c]
    for send in sends:
        send()


def fused_shards(polarization, alpha_field, landau, stiffness, permittivity, interfaces):
    _, L, R, C = polarization.shape
    nbx = lax.axis_size("bx")
    nby = lax.axis_size("by")
    grid_x, grid_y = nbx * R, nby * C
    per = C // L
    line = np.arange(grid_x)
    hx = fixed_table(line[:, None], line[None, :], grid_x)
    line = np.arange(grid_y)
    hy = fixed_table(line[:, None], line[None, :], grid_y)
    wave_x = 4.0 * np.sin(np.pi * np.arange(grid_x) / grid_x) ** 2
    wave_x = jnp.asarray(np.tile(wave_x[None, :], (8, 1)).astype(np.float32))
    at = np.arange(nbx * nby)
    first = (at % nby) * C + (at // nby) * per
    mode = (first[:, None] + np.arange(per)[None, :]).reshape(-1)
    wave_y = 4.0 * np.sin(np.pi * mode / grid_y) ** 2
    wave_y = jnp.asarray(np.tile(wave_y[:, None], (1, C)).astype(np.float32))
    f32 = jnp.float32
    hbm = pl.BlockSpec(memory_space=pltpu.HBM)
    smem = pl.BlockSpec(memory_space=pltpu.SMEM)
    S = 2
    n_copies = S * (4 + 2 * (nby - 1) + 2 * (nbx * nby - 1))
    by_y = pltpu.VMEM((S, nby, L + 3, 8, C), f32)
    by_mode = pltpu.VMEM((S, nby, nbx, 16, C), f32)
    by_place = pltpu.VMEM((S, nbx, nby, 16, C), f32)
    scratch = [
        pltpu.VMEM((3, L, R, C), f32), pltpu.VMEM((3, L, R, C), f32),
        pltpu.VMEM((L, per, grid_x), f32), pltpu.VMEM((L, per, grid_x), f32),
        by_y, by_y, by_mode, by_place, by_place, by_mode, by_y, by_y,
        pltpu.VMEM((S, 2, 3 * L, C), f32), pltpu.VMEM((S, 2, 3 * L, C), f32),
        pltpu.VMEM((S, R, C), f32), pltpu.VMEM((S, 2, R, C), f32),
        pltpu.SemaphoreType.DMA((n_copies,)), pltpu.SemaphoreType.DMA((n_copies,)),
        pltpu.SemaphoreType.REGULAR((nbx.bit_length(),)), pltpu.VMEM((3, L, R, C), f32),
        pltpu.VMEM((L, R, C), f32), pltpu.VMEM(wave_x.shape, f32), pltpu.VMEM((per, C), f32),
        pltpu.VMEM(hx.shape, hx.dtype), pltpu.VMEM(hy.shape, hy.dtype),
        pltpu.SemaphoreType.DMA((6,)),
    ]
    out = pltpu.VMEM(polarization.shape, f32)
    base, down = pl.pallas_call(
        functools.partial(fused, (L, R, C, nbx, nby)),
        out_shape=(out, out),
        in_specs=[hbm, hbm, smem, smem, smem, smem, hbm, hbm, hbm, hbm],
        out_specs=(pl.BlockSpec(memory_space=pltpu.VMEM), pl.BlockSpec(memory_space=pltpu.VMEM)),
        scratch_shapes=scratch,
        compiler_params=pltpu.CompilerParams(
            collective_id=0, has_side_effects=True, vmem_limit_bytes=66 * 1000 * 1000),
    )(polarization, alpha_field, landau, stiffness, permittivity, interfaces,
      wave_x, wave_y, hx, hy)
    return base - step_size * down, -down


def solution(mesh):
    def run(polarization, *rest):
        _, L, R, C = polarization.shape
        body = fused_shards if fits(L, R, C, lax.axis_size("bx"), lax.axis_size("by")) else shards
        return body(polarization, *rest)

    return jax.shard_map(
        run,
        mesh=mesh,
        in_specs=(P(None, None, "bx", "by"), P(None, "bx", "by"), P(), P(), P(), P()),
        out_specs=(P(None, None, "bx", "by"), P(None, None, "bx", "by")),
        check_vma=False,
    )
```

```python
import functools

import jax
import jax.numpy as jnp
import numpy as np
from jax import lax
from jax.experimental import pallas as pl
from jax.experimental.pallas import tpu as pltpu
from jax.sharding import PartitionSpec as P

STEPS = 2
step_size = 0.05
MESH = pl.DeviceIdType.MESH
PAD = 8


def cas_table(left, right, length):
    turns = left * right % length
    angle = 2.0 * jnp.pi / length * turns.astype(jnp.float32)
    table = jnp.cos(angle) + jnp.sin(angle)
    high = lax.reduce_precision(table, 8, 7)
    return jnp.stack([high.astype(jnp.bfloat16), (table - high).astype(jnp.bfloat16)])


def fixed_table(left, right, length):
    angle = 2.0 * np.pi / length * (left * right % length)
    table = (np.cos(angle) + np.sin(angle)).astype(np.float32)
    high = table.astype(jnp.bfloat16)
    low = (table - high.astype(np.float32)).astype(jnp.bfloat16)
    return jnp.asarray(np.stack([high, low]))


def is_wide(rows, nbx, nby, layers):
    return layers % nbx == 0 and rows % (8 * nby) == 0


def halves(value):
    high = value.astype(jnp.bfloat16)
    low = (value - high.astype(jnp.float32)).astype(jnp.bfloat16)
    return high, low


def product(left, right):
    dot = functools.partial(jnp.dot, preferred_element_type=jnp.float32)
    return dot(left[0], right[0]) + (dot(left[0], right[1]) + dot(left[1], right[0]))


def kernel(sizes, p_in, alpha_h, landau, stiff, perm, inter, lam, hx_h, hy_h, p_out, f_out, *scratch):
    L, R, C, nbx, nby, rep, lp, own = sizes
    (p_mid, base, coef, ratio, q, inb, outs, rec_i,
     row_s, row_r, col_s, col_r, pc_s, pc_r, ssem, rsem,
     alpha, hx, hy, local_sem) = scratch[:20]
    wide = is_wide(R, nbx, nby, L)
    if wide:
        z_in, w_out = scratch[20:]
    else:
        rec_f, ybuf, phat, u = scratch[20:]
    thin = R // nby
    R2 = R + PAD
    bx = lax.axis_index("bx")
    by = lax.axis_index("by")
    group = bx // rep
    part = bx % rep
    scale = 1.0 / (R * nbx * C * nby)
    loads = [pltpu.make_async_copy(src, dst, local_sem.at[at]) for at, (src, dst) in
             enumerate(((alpha_h, alpha), (hx_h, hx), (hy_h, hy)))]
    for load in loads:
        load.start()
    slots = [0]
    sends = []

    barrier = pltpu.get_barrier_semaphore()
    others = [(a, b) for b in range(nby) for a in range(nbx) if a or b]
    greeted = [(a, b) for a, b in others if wide or not a or not b]
    for a, b in greeted:
        pl.semaphore_signal(
            barrier, inc=1, device_id={"bx": (bx + a) % nbx, "by": (by + b) % nby},
            device_id_type=MESH)

    def remote(src, dst, device, slot):
        return pltpu.make_async_remote_copy(
            src_ref=src, dst_ref=dst, send_sem=ssem.at[slot], recv_sem=rsem.at[slot],
            device_id=device, device_id_type=MESH)

    def fresh():
        slots[0] += 1
        return slots[0] - 1

    def push(src, dst, device):
        copy = remote(src, dst, device, fresh())
        copy.start()
        sends.append(copy.wait_send)
        return copy

    rows = lax.broadcasted_iota(jnp.int32, (R, C), 0)
    lanes = lax.broadcasted_iota(jnp.int32, (R, C), 1)

    def x_next(f, high):
        return jnp.where(rows == R - 1, high, pltpu.roll(f, R - 1, 0))

    def x_prev(f, low):
        return jnp.where(rows == 0, low, pltpu.roll(f, 1, 0))

    def y_next(f, high):
        return jnp.where(lanes == C - 1, high, pltpu.roll(f, C - 1, 1))

    def y_prev(f, low):
        return jnp.where(lanes == 0, low, pltpu.roll(f, 1, 1))

    def column_tile(blocks):
        tile = jnp.zeros((R, C), jnp.float32)
        for at, block in enumerate(blocks):
            tile = jnp.where(lanes == at, block[:, 0:1], tile)
            tile = jnp.where(lanes == C // 2 + at, block[:, C - 1:C], tile)
        return tile

    def x_start(src, n):
        mine = inb.at[n, :, pl.ds(pl.multiple_of(bx * R, R), R)]
        copies = []
        for k in range(1, nbx):
            to = (bx + k) % nbx
            copies.append(push(src.at[pl.ds(to // rep * lp, lp)], mine, {"bx": to}))
        for layer in range(lp):
            inb[n, layer, pl.ds(pl.multiple_of(bx * R, R), R)] = src[group * lp + layer]
        return copies

    def x_mix(copies, n):
        for copy in copies:
            copy.wait_recv()
        table = (hx[0], hx[1])
        for layer in range(lp):
            outs[n, :, layer] = product(table, halves(inb[n, layer])).reshape(own, R2, C)

    def spread(n, step):
        copies = []
        for a, b in others:
            to_x, to_y = (bx + a) % nbx, (by + b) % nby
            copies.append(push(
                outs.at[n, to_x, :, pl.ds(pl.multiple_of(to_y * thin, thin), thin)],
                z_in.at[step, by, pl.ds(bx * lp, lp)], {"bx": to_x, "by": to_y}))
        for layer in range(lp):
            z_in[step, by, bx * lp + layer] = outs[
                n, bx, layer, pl.ds(pl.multiple_of(by * thin, thin), thin)]
        for copy in copies:
            copy.wait_recv()

    def collect(n, step):
        at = pl.ds(pl.multiple_of(bx * R + by * thin, thin), thin)
        copies = []
        for a, b in others:
            to_x, to_y = (bx + a) % nbx, (by + b) % nby
            copies.append(push(
                w_out.at[step, to_y, pl.ds(to_x * lp, lp)], inb.at[n, :, at],
                {"bx": to_x, "by": to_y}))
        for layer in range(lp):
            inb[n, layer, at] = w_out[step, by, bx * lp + layer]
        return copies

    def solve(spectrum, height):
        primes = []
        for l in range(L):
            source = spectrum[l * height:(l + 1) * height] * scale
            if l:
                source = source + inter[l] * primes[-1]
            primes.append(source * coef[l])
        values = [primes[-1]]
        for l in range(L - 2, -1, -1):
            values.insert(0, primes[l] + ratio[l] * values[0])
        return values

    def x_finish(n, dst, height):
        waits = []
        landing = dst.at[pl.ds(group * lp, lp)]
        for t in range(own):
            local = (group + t) % own
            to = part * own + local
            src = outs.at[n, local, :, pl.ds(0, height)]
            if rep == 1:
                if t == 0:
                    continue
                waits.append(push(src, landing, {"bx": to}).wait_recv)
                continue
            slot = fresh()

            def go(src=src, to=to, slot=slot):
                remote(src, landing, {"bx": to}, slot).start()

            def gone(src=src, to=to, slot=slot):
                @pl.when(to != bx)
                def _():
                    remote(src, landing, {"bx": to}, slot).wait_send()

            def came(src=src, to=to, slot=slot, t=t):
                origin = (bx % own + own - t) % own * rep + bx // own

                @pl.when(origin != bx)
                def _():
                    remote(src, landing, {"bx": to}, slot).wait_recv()

            pl.when(to != bx)(go)
            sends.append(gone)
            waits.append(came)

        def keep():
            for layer in range(lp):
                dst[group * lp + layer] = outs[n, bx % own, layer, 0:height]

        if rep == 1:
            keep()
        else:
            pl.when(bx // own == part)(keep)
        for wait in waits:
            wait()

    def y_pass(src, n):
        copies = [push(src, ybuf.at[n, k - 1], {"by": (by + k) % nby}) for k in range(1, nby)]
        total = product(halves(src[...].reshape(L * R, C)), (hy[0, by], hy[1, by]))
        for k in range(1, nby):
            copies[k - 1].wait_recv()
            origin = (by + nby - k) % nby
            total += product(halves(ybuf[n, k - 1].reshape(L * R, C)), (hy[0, origin], hy[1, origin]))
        return total

    def flank_start(rows_too, step, src):
        copies = []
        if rows_too:
            for c in range(3):
                for l in range(L):
                    at = c * L + l
                    row_s[step, 0, at:at + 1] = src[c, l, 0:1]
                    row_s[step, 1, at:at + 1] = src[c, l, R - 1:R]
            col_s[step] = column_tile([src[c, l] for c in range(3) for l in range(L)])
            if step == 0:
                pl.semaphore_wait(barrier, len(greeted))
            copies.append(push(row_s.at[step, 1], row_r.at[step, 0], {"bx": (bx + 1) % nbx}))
            copies.append(push(row_s.at[step, 0], row_r.at[step, 1], {"bx": (bx + nbx - 1) % nbx}))
            tile, land = col_s.at[step], col_r
        else:
            pc_s[step] = column_tile([src[l, 0:R] for l in range(L)])
            tile, land = pc_s.at[step], pc_r
        copies.append(push(tile, land.at[step, 0], {"by": (by + 1) % nby}))
        copies.append(push(tile, land.at[step, 1], {"by": (by + nby - 1) % nby}))
        return copies

    for step in range(STEPS):
        src = p_in if step == 0 else p_mid
        flanks = flank_start(True, step, src)
        if step == 0:
            lateral = lam[...]
            previous = None
            for l in range(L):
                pivot = perm[l] * lateral + inter[l] + inter[l + 1]
                if l:
                    pivot = pivot - inter[l] * previous
                inverse = 1.0 / pivot
                coef[l] = inverse
                previous = inter[l + 1] * inverse
                ratio[l] = previous
        for copy in flanks:
            copy.wait_recv()
        low_col = col_r[step, 0]
        high_col = col_r[step, 1]

        def edges(c, l):
            at = c * L + l
            return (row_r[step, 0, at:at + 1], row_r[step, 1, at:at + 1],
                    low_col[:, C // 2 + at:C // 2 + at + 1], high_col[:, at:at + 1])

        zero = jnp.zeros((R, C), jnp.float32)
        for l in range(L):
            low, high, _, _ = edges(0, l)
            _, _, left, right = edges(1, l)
            along_x, along_y = src[0, l], src[1, l]
            above = src[2, l + 1] if l + 1 < L else zero
            below = src[2, l - 1] if l else zero
            q[step, l] = -0.5 * (
                (x_next(along_x, high) - x_prev(along_x, low))
                + (y_next(along_y, right) - y_prev(along_y, left)) + (above - below))
        copies = x_start(q.at[step], 2 * step)
        if step == 0:
            for load in loads:
                load.wait()
        for l in range(L):
            cells = [src[c, l] for c in range(3)]
            squares = [cell * cell for cell in cells]
            whole = squares[0] + squares[1] + squares[2]
            for c in range(3):
                cell, square = cells[c], squares[c]
                low, high, left, right = edges(c, l)
                above = src[c, l + 1] if l + 1 < L else zero
                below = src[c, l - 1] if l else zero
                smooth = stiff[l] * (
                    (x_next(cell, high) + x_prev(cell, low) + y_next(cell, right)
                     + y_prev(cell, left) - 4.0 * cell) + (above + below - 2.0 * cell))
                drive = cell * (
                    2.0 * alpha[l] + 4.0 * landau[0, l] * square
                    + 2.0 * landau[1, l] * (whole - square)
                    + 6.0 * landau[2, l] * (square * square))
                base[c, l] = cell - step_size * (drive - smooth)
        n = 2 * step
        x_mix(copies, n)
        if wide:
            spread(n, step)
            table = (hy[0], hy[1])
            full = jnp.concatenate(
                [z_in[step, j].reshape(L * thin, C) for j in range(nby)], axis=1)
            values = solve(product(halves(full), table), thin)
            full = product(halves(jnp.concatenate(values, axis=0)), table)
            for j in range(nby):
                w_out[step, j] = full[:, j * C:(j + 1) * C].reshape(L, thin, C)
            copies = collect(n + 1, step)
        else:
            x_finish(n, rec_f.at[step], R)
            for l, value in enumerate(solve(y_pass(rec_f.at[step], n), R)):
                phat[step, l] = value
            u[step] = y_pass(phat.at[step], n + 1).reshape(L, R, C)
            copies = x_start(u.at[step], n + 1)
        x_mix(copies, n + 1)
        x_finish(n + 1, rec_i.at[step], R2)
        flanks = flank_start(False, step, rec_i.at[step])
        last = step == STEPS - 1
        target = p_out if last else p_mid
        for l in range(L):
            phi = rec_i[step, l, 0:R]
            low = rec_i[step, l, R:R + 1]
            high = rec_i[step, l, R + 1:R + 2]
            along_x = -0.5 * (x_next(phi, high) - x_prev(phi, low))
            above = rec_i[step, l + 1, 0:R] if l + 1 < L else zero
            below = rec_i[step, l - 1, 0:R] if l else zero
            along_z = -0.5 * (above - below)
            target[0, l] = base[0, l] + step_size * along_x
            target[2, l] = base[2, l] + step_size * along_z
            if last:
                f_out[0, l] = along_x
                f_out[2, l] = along_z
        for copy in flanks:
            copy.wait_recv()
        low_phi = pc_r[step, 0]
        high_phi = pc_r[step, 1]
        for l in range(L):
            phi = rec_i[step, l, 0:R]
            along_y = -0.5 * (y_next(phi, high_phi[:, l:l + 1])
                              - y_prev(phi, low_phi[:, C // 2 + l:C // 2 + l + 1]))
            target[1, l] = base[1, l] + step_size * along_y
            if last:
                f_out[1, l] = along_y
    for wait in sends:
        wait()


def shards(polarization, alpha_field, landau, stiffness, permittivity, interfaces):
    _, L, R, C = polarization.shape
    nbx = lax.axis_size("bx")
    nby = lax.axis_size("by")
    bx = lax.axis_index("bx")
    by = lax.axis_index("by")
    rep = max(1, nbx // L)
    lp = max(1, L // nbx)
    own = nbx // rep
    grid_x, grid_y = nbx * R, nby * C
    R2 = R + PAD
    wide = is_wide(R, nbx, nby, L)
    pool = np if wide else jnp
    make = fixed_table if wide else cas_table
    line = pool.arange(R2, dtype=jnp.int32)
    line = pool.where(line < R, line, pool.where(line == R, -1, R))
    owners = pool.arange(own, dtype=jnp.int32)
    if not wide:
        owners = owners + bx % rep * own
    wanted = ((owners[:, None] * R + line[None, :] + grid_x) % grid_x).reshape(own * R2, 1)
    hx = make(wanted, pool.arange(grid_x, dtype=jnp.int32)[None, :], grid_x)
    every_col = pool.arange(grid_y, dtype=jnp.int32)
    my_rows = bx * R + jnp.arange(R, dtype=jnp.int32)
    my_cols = by * C + jnp.arange(C, dtype=jnp.int32)
    if wide:
        hy = make(every_col[:, None], every_col[None, :], grid_y)
        my_rows = bx * R + by * (R // nby) + jnp.arange(R // nby, dtype=jnp.int32)
        my_cols = jnp.arange(grid_y, dtype=jnp.int32)
    else:
        hy = make(every_col[:, None], my_cols[None, :], grid_y).reshape(2, nby, C, C)
    wave_x = jnp.sin(jnp.pi * my_rows.astype(jnp.float32) / grid_x)
    wave_y = jnp.sin(jnp.pi * my_cols.astype(jnp.float32) / grid_y)
    lam = 4.0 * wave_x[:, None] ** 2 + 4.0 * wave_y[None, :] ** 2
    sizes = (L, R, C, nbx, nby, rep, lp, own)
    n_copies = STEPS * (6 + 2 * (nbx * nby + own if wide else nbx + own + nby))
    f32 = jnp.float32
    vmem = pl.BlockSpec(memory_space=pltpu.VMEM)
    hbm = pl.BlockSpec(memory_space=pltpu.HBM)
    smem = pl.BlockSpec(memory_space=pltpu.SMEM)
    S = STEPS
    scratch = [
        pltpu.VMEM((3, L, R, C), f32), pltpu.VMEM((3, L, R, C), f32),
        pltpu.VMEM((L,) + lam.shape, f32), pltpu.VMEM((L,) + lam.shape, f32),
        pltpu.VMEM((S, L, R, C), f32), pltpu.VMEM((2 * S, lp, grid_x, C), f32),
        pltpu.VMEM((2 * S, own, lp, R2, C), f32), pltpu.VMEM((S, L, R2, C), f32),
        pltpu.VMEM((S, 2, 3 * L, C), f32), pltpu.VMEM((S, 2, 3 * L, C), f32),
        pltpu.VMEM((S, R, C), f32), pltpu.VMEM((S, 2, R, C), f32),
        pltpu.VMEM((S, R, C), f32), pltpu.VMEM((S, 2, R, C), f32),
        pltpu.SemaphoreType.DMA((n_copies,)), pltpu.SemaphoreType.DMA((n_copies,)),
        pltpu.VMEM((L, R, C), f32), pltpu.VMEM(hx.shape, hx.dtype),
        pltpu.VMEM(hy.shape, hy.dtype), pltpu.SemaphoreType.DMA((3,)),
    ]
    if wide:
        thin = (S, nby, L, R // nby, C)
        scratch += [pltpu.VMEM(thin, f32), pltpu.VMEM(thin, f32)]
    else:
        scratch += [
            pltpu.VMEM((S, L, R, C), f32), pltpu.VMEM((2 * S, nby - 1, L, R, C), f32),
            pltpu.VMEM((S, L, R, C), f32), pltpu.VMEM((S, L, R, C), f32),
        ]
    out = jax.ShapeDtypeStruct(polarization.shape, f32)
    return pl.pallas_call(
        functools.partial(kernel, sizes),
        out_shape=(out, out),
        in_specs=[vmem, hbm, smem, smem, smem, smem, vmem, hbm, hbm],
        out_specs=(vmem, vmem),
        scratch_shapes=scratch,
        compiler_params=pltpu.CompilerParams(
            collective_id=0, has_side_effects=True, vmem_limit_bytes=65 * 1000 * 1000),
    )(polarization, alpha_field, landau, stiffness, permittivity, interfaces, lam, hx, hy)


def fits(L, R, C, nbx, nby):
    slab = R // nby
    return (L == nbx and slab == 8 and slab * nby == R and nby > 1 and C % (8 * L) == 0
            and nbx > 2 and nbx & (nbx - 1) == 0 and nby & (nby - 1) == 0)


def partner(index, mask, size):
    other = 0
    bit = 1
    while bit < size:
        here = index // bit % 2
        other = other + bit * (1 - here if mask // bit % 2 else here)
        bit *= 2
    return other


def join(parts, axis):
    return jnp.concatenate(parts, axis=axis)


def fused(sizes, p_h, alpha_h, landau, stiff, perm, inter, wx_h, wy_h, hx_h, hy_h,
          base_o, down_o, *scratch):
    L, R, C, nbx, nby = sizes
    (p_mid, base, coef, ratio, a_s, a_r, b_s, b_r, c_s, c_r, d_s, d_r,
     row_s, row_r, col_s, col_r, ssem, rsem, known, p_in, alpha, wx, wy, hx, hy, local_sem) = scratch
    slab = R // nby
    per = C // L
    NX, NY = nbx * R, nby * C
    bx = lax.axis_index("bx")
    by = lax.axis_index("by")
    scale = 1.0 / (NX * NY)
    f32 = jnp.float32
    dot = functools.partial(jnp.dot, preferred_element_type=f32)
    slots = [0]
    sends = []

    barrier = pltpu.get_barrier_semaphore()
    at_x = [partner(bx, a, nbx) for a in range(nbx)]
    at_y = [partner(by, b, nby) for b in range(nby)]
    others = [(a, b) for b in range(nby) for a in range(nbx) if a or b]
    others.sort(key=lambda ab: -(ab[0] // 2 + ab[0] % 2 + ab[1] // 2))
    reach = [1 << i for i in range(1, nbx.bit_length() - 1)]
    greeted = [(a, b) for a, b in others if a < 2] + [(a, 0) for a in reach]
    for a, b in greeted:
        pl.semaphore_signal(
            barrier, inc=1, device_id={"bx": at_x[a], "by": at_y[b]}, device_id_type=MESH)
    mine = pl.multiple_of((bx * nby + by) * per, per)
    loads = [pltpu.make_async_copy(src, dst, local_sem.at[at]) for at, (src, dst) in enumerate((
        (p_h, p_in), (alpha_h, alpha), (wx_h, wx), (wy_h.at[pl.ds(mine, per)], wy), (hx_h, hx),
        (hy_h, hy)))]
    for load in loads:
        load.start()

    def push(src, dst, device):
        slot = slots[0]
        slots[0] += 1
        copy = pltpu.make_async_remote_copy(
            src_ref=src, dst_ref=dst, send_sem=ssem.at[slot], recv_sem=rsem.at[slot],
            device_id=device, device_id_type=MESH)
        copy.start()
        sends.append(copy.wait_send)
        return copy

    rows = lax.broadcasted_iota(jnp.int32, (R, C), 0)
    lanes = lax.broadcasted_iota(jnp.int32, (R, C), 1)
    rows8 = lax.broadcasted_iota(jnp.int32, (slab, C), 0)
    lanes8 = lax.broadcasted_iota(jnp.int32, (slab, C), 1)
    zero = jnp.zeros((R, C), f32)
    zero8 = jnp.zeros((slab, C), f32)

    def x_next(f, high):
        return jnp.where(rows == R - 1, high, pltpu.roll(f, R - 1, 0))

    def x_prev(f, low):
        return jnp.where(rows == 0, low, pltpu.roll(f, 1, 0))

    def y_next(f, high):
        return jnp.where(lanes == C - 1, high, pltpu.roll(f, C - 1, 1))

    def y_prev(f, low):
        return jnp.where(lanes == 0, low, pltpu.roll(f, 1, 1))

    def charge(n, src, ring):
        sides = (0, nby - 1)
        edge = zero
        for l in range(L):
            along_x, along_y = src[0, l], src[1, l]
            above = src[2, l + 1] if l + 1 < L else zero
            below = src[2, l - 1] if l else zero
            low = high = left = right = 0.0
            if ring:
                lines, column = ring
                low, high = lines[0][0][l:l + 1], lines[1][0][l:l + 1]
                left = column[:, L + l:L + l + 1]
                right = column[:, C // 2 + L + l:C // 2 + L + l + 1]
            value = -0.5 * ((x_next(along_x, high) - x_prev(along_x, low))
                            + (y_next(along_y, right) - y_prev(along_y, left)) + (above - below))
            for j in range(nby):
                a_s[n, j, l] = value[j * slab:(j + 1) * slab]
            edge = jnp.where(lanes == l, -0.5 * along_y[:, 0:1], edge)
            edge = jnp.where(lanes == L + l, 0.5 * along_y[:, C - 1:C], edge)
        near = [-0.5 * join([src[0, l, 0:1] for l in range(L)], 0),
                0.5 * join([src[0, l, R - 1:R] for l in range(L)], 0)]
        corner = [None, None]
        if ring:
            for side, sign in enumerate((-0.5, 0.5)):
                first, second, third = lines[side]
                turned = (jnp.where(lanes8 == C - 1, 0.0, pltpu.roll(second, C - 1, 1))
                          - jnp.where(lanes8 == 0, 0.0, pltpu.roll(second, 1, 1)))
                risen = (jnp.where(rows8 == L - 1, 0.0, pltpu.roll(third, L - 1, 0))
                         - jnp.where(rows8 == 0, 0.0, pltpu.roll(third, 1, 0)))
                near[side] = near[side] - 0.5 * (turned + risen)
                a_s[n, sides[side], L + 2] = sign * first
                corner[side] = jnp.where(
                    lanes8 == 4 * L, sign * first[:, 0:1] - 0.5 * second[:, 0:1],
                    jnp.where(lanes8 == 4 * L + 1,
                              sign * first[:, C - 1:C] + 0.5 * second[:, C - 1:C], 0.0))
            layer = lanes % L
            turned = -0.5 * (x_next(column, 0.0) - x_prev(column, 0.0))
            risen = -0.5 * (jnp.where(layer == L - 1, 0.0, pltpu.roll(column, C - 1, 1))
                            - jnp.where(layer == 0, 0.0, pltpu.roll(column, 1, 1)))
            both = turned + pltpu.roll(risen, C - 2 * L, 1)
            low = edge + both
            high = edge + pltpu.roll(both, C // 2 + L, 1)
            far_low = -0.5 * pltpu.roll(column, L, 1)
            far_high = 0.5 * pltpu.roll(column, C // 2 + 2 * L, 1)
            group = lanes // L
            edge = jnp.where(group == 0, low, jnp.where(group == 1, high, jnp.where(
                group == 2, far_low, jnp.where(group == 3, far_high, 0.0))))
        for side in range(2):
            a_s[n, sides[side], L + 1] = near[side]
        for j in range(nby):
            piece = edge[j * slab:(j + 1) * slab]
            if ring and j in sides:
                piece = piece + corner[sides.index(j)]
            a_s[n, j, L] = piece
            if j not in sides:
                a_s[n, j, L + 1] = jnp.zeros((L, C), f32)
                if ring:
                    a_s[n, j, L + 2] = jnp.zeros((L, C), f32)

    def ring_of(n):
        weight8 = zero8
        weight = zero
        layer = lanes % L
        for l in range(L):
            weight8 = jnp.where(rows8 == l, step_size * stiff[l], weight8)
            weight = jnp.where(layer == l, step_size * stiff[l], weight)
        lines = [[weight8 * row_s[n, side, c * L:(c + 1) * L] for c in range(3)]
                 for side in range(2)]
        return lines, weight * col_s[n]

    def among_y(source, landing, n, count):
        part = pl.ds(0, count)
        copies = []
        for b in range(nby - 1, 0, -1):
            to = at_y[b]
            copies.append(push(source.at[n, to, part], landing.at[n, by, part], {"by": to}))
        landing[n, by, 0:count] = source[n, by, 0:count]
        return copies

    def wait(copies):
        for copy in copies:
            copy.wait_recv()

    def spread(source, landing, n, flip, thick):
        part = pl.ds(0, thick)
        copies = []
        for a, b in others:
            to_x, to_y = at_x[a], at_y[b]
            if flip:
                src, dst = source.at[n, to_x, to_y, part], landing.at[n, by, bx, part]
            else:
                src, dst = source.at[n, to_y, to_x, part], landing.at[n, bx, by, part]
            copies.append(push(src, dst, {"bx": to_x, "by": to_y}))
        if flip:
            landing[n, by, bx, 0:thick] = source[n, bx, by, 0:thick]
        else:
            landing[n, bx, by, 0:thick] = source[n, by, bx, 0:thick]
        return copies

    def swap_groups(tiles):
        height = tiles[0].shape[0]
        group = lax.broadcasted_iota(jnp.int32, (height, C), 1) // per
        tiles = list(tiles)
        s = 1
        while s < L:
            upper = group % (2 * s) >= s
            for at in range(L):
                if at % (2 * s) < s:
                    low, high = tiles[at], tiles[at + s]
                    tiles[at] = jnp.where(upper, pltpu.roll(high, s * per, 1), low)
                    tiles[at + s] = jnp.where(upper, high, pltpu.roll(low, C - s * per, 1))
            s *= 2
        return tiles

    def swap_rows(tile):
        group = lanes8 // per
        s = 1
        while s < L:
            upper = group % (2 * s) >= s
            later = rows8 % (2 * s) >= s
            ahead = pltpu.roll(pltpu.roll(tile, L - s, 0), s * per, 1)
            behind = pltpu.roll(pltpu.roll(tile, s, 0), C - s * per, 1)
            tile = jnp.where(later, jnp.where(upper, tile, behind), jnp.where(upper, ahead, tile))
            s *= 2
        return tile

    def y_table(full):
        height = full.shape[0]
        high = full.astype(jnp.bfloat16)
        wide = high.astype(f32)
        both = join([wide, full - wide], 0).astype(jnp.bfloat16)
        first = dot(both, hy[0])
        return first[:height] + first[height:] + dot(high, hy[1])

    def y_forward(n):
        columns = []
        for j in range(nby):
            from_left = a_r[n, (j + nby - 1) % nby, L]
            from_right = a_r[n, (j + 1) % nby, L]
            tiles = []
            for l in range(L):
                extra = jnp.where(
                    lanes8 == 0, from_left[:, L + l:L + l + 1],
                    jnp.where(lanes8 == C - 1, from_right[:, l:l + 1], 0.0))
                if n:
                    extra = jnp.where(
                        lanes8 == 1, from_left[:, 3 * L + l:3 * L + l + 1],
                        jnp.where(lanes8 == C - 2, from_right[:, 2 * L + l:2 * L + l + 1], extra))
                tiles.append(a_r[n, j, l] + extra)
            near, far = a_r[n, j, L + 1], zero8
            if n:
                near = near + jnp.where(
                    lanes8 == 0, from_left[:, 4 * L + 1:4 * L + 2],
                    jnp.where(lanes8 == C - 1, from_right[:, 4 * L:4 * L + 1], 0.0))
                far = a_r[n, j, L + 2]
            columns.append(join(tiles + [near, far], 0))
        out = y_table(join(columns, 1))
        tiles = [join([out[l * slab:(l + 1) * slab, t * C:(t + 1) * C] for t in range(nby)], 0)
                 for l in range(L)]
        tiles = swap_groups(tiles)
        for t in range(nby):
            halos = [swap_rows(out[(L + k) * slab:(L + k) * slab + L, t * C:(t + 1) * C])
                     for k in range(1 + n)]
            for e in range(L):
                b_s[n, t, e, 0:slab] = tiles[e][t * slab:(t + 1) * slab]
                for k, halo in enumerate(halos):
                    b_s[n, t, e, slab + k:slab + k + 1] = halo[e:e + 1]

    def y_backward(n):
        tiles = swap_groups([join([c_r[n, t, e, 0:slab] for t in range(nby)], 0)
                             for e in range(L)])
        rims = [join([swap_rows(join([c_r[n, t, e, slab + k:slab + k + 1] for e in range(L)], 0))
                      for t in range(nby)], 1) for k in range(2 - n)]
        if n:
            rims.append(jnp.zeros((slab, NY), f32))
        lines = [join([tiles[l][t * slab:(t + 1) * slab] for t in range(nby)], 1)
                 for l in range(L)]
        out = y_table(join(lines + rims, 0))
        near = out[L * slab:L * slab + L]
        for j in range(nby):
            edge = zero8
            left, right = (j + nby - 1) % nby * C, (j + 1) % nby * C
            wanted = [left + C - 1, right]
            if n == 0:
                wanted += [left + C - 2, right + 1, None, j * C, j * C + C - 1]
                edge = jnp.where(lanes8 == 4 * L, near[:, left + C - 1:left + C],
                                 jnp.where(lanes8 == 4 * L + 1, near[:, right:right + 1], edge))
            for l in range(L):
                line = out[l * slab:(l + 1) * slab]
                d_s[n, j, l] = line[:, j * C:(j + 1) * C]
                for at, column in enumerate(wanted):
                    if column is not None:
                        edge = jnp.where(
                            lanes8 == at * L + l, line[:, column:column + 1], edge)
            d_s[n, j, L] = edge
            for k in range(2 - n):
                d_s[n, j, L + 1 + k] = out[(L + k) * slab:(L + k) * slab + L,
                                           j * C:(j + 1) * C]

    def spectrum(n):
        tiles = []
        for i in range(nbx):
            for j in range(nby):
                tile = b_r[n, i, j, 0:slab]
                for k in range(1 + n):
                    line = slice(slab + k, slab + k + 1)
                    if j == 0:
                        tile = tile + jnp.where(
                            rows8 == k, b_r[n, (i + nbx - 1) % nbx, nby - 1, line], 0.0)
                    if j == nby - 1:
                        tile = tile + jnp.where(
                            rows8 == slab - 1 - k, b_r[n, (i + 1) % nbx, 0, line], 0.0)
                tiles.append(tile)
        full = join(tiles, 0).T
        high = full.astype(jnp.bfloat16)
        wide = high.astype(f32)
        both = join([wide, full - wide], 0).astype(jnp.bfloat16)
        first = dot(both, hx[0])
        out = (first[:C] + first[C:] + dot(high, hx[1])) * scale
        return [out[l * per:(l + 1) * per] for l in range(L)]

    def solve(sources):
        primes = []
        for l in range(L):
            source = sources[l]
            if l:
                source = source + inter[l] * primes[-1]
            primes.append(source * coef[l])
        values = [primes[-1]]
        for l in range(L - 2, -1, -1):
            values.insert(0, primes[l] + ratio[l] * values[0])
        return values

    def x_backward(n, values):
        high, low = halves(join(values, 0))
        turn = functools.partial(
            lax.dot_general, dimension_numbers=(((1,), (1,)), ((), ())),
            preferred_element_type=f32)
        first = turn(hx[...].reshape(2 * NX, NX), high)
        out = first[:NX] + first[NX:] + turn(hx[0], low)
        for i in range(nbx):
            for j in range(nby):
                at = i * R + j * slab
                c_s[n, i, j, 0:slab] = out[at:at + slab]
                for k in range(2 - n):
                    line = (at - 1 - k if j == 0 else at + slab + k) % NX
                    c_s[n, i, j, slab + k:slab + k + 1] = out[line:line + 1]

    def flank_start(n, src):
        tile = zero
        for c in range(3):
            for l in range(L):
                at = c * L + l
                cell = src[c, l]
                row_s[n, 0, at:at + 1] = cell[0:1]
                row_s[n, 1, at:at + 1] = cell[R - 1:R]
                tile = jnp.where(lanes == at, cell[:, 0:1], tile)
                tile = jnp.where(lanes == C // 2 + at, cell[:, C - 1:C], tile)
        col_s[n] = tile

    def flank_send(n):
        return [
            push(row_s.at[n, 1], row_r.at[n, 0], {"bx": (bx + 1) % nbx}),
            push(row_s.at[n, 0], row_r.at[n, 1], {"bx": (bx + nbx - 1) % nbx}),
            push(col_s.at[n], col_r.at[n, 0], {"by": (by + 1) % nby}),
            push(col_s.at[n], col_r.at[n, 1], {"by": (by + nby - 1) % nby})]

    def relax_inside(src):
        for l in range(L):
            cells = [src[c, l] for c in range(3)]
            squares = [cell * cell for cell in cells]
            whole = squares[0] + squares[1] + squares[2]
            for c in range(3):
                cell, square = cells[c], squares[c]
                above = src[c, l + 1] if l + 1 < L else zero
                below = src[c, l - 1] if l else zero
                smooth = stiff[l] * (
                    (x_next(cell, 0.0) + x_prev(cell, 0.0) + y_next(cell, 0.0)
                     + y_prev(cell, 0.0) - 4.0 * cell) + (above + below - 2.0 * cell))
                drive = cell * (
                    2.0 * alpha[l] + 4.0 * landau[0, l] * square
                    + 2.0 * landau[1, l] * (whole - square)
                    + 6.0 * landau[2, l] * (square * square))
                base[c, l] = cell - step_size * (drive - smooth)

    def flank_lines(n):
        return [[row_r[n, side, c * L:(c + 1) * L] for c in range(3)] for side in range(2)]

    def relax_edges(lines, low_col, high_col, target):
        for l in range(L):
            weight = step_size * stiff[l]
            for c in range(3):
                at = c * L + l
                add = jnp.where(lanes == 0, low_col[:, C // 2 + at:C // 2 + at + 1], 0.0)
                add = add + jnp.where(lanes == C - 1, high_col[:, at:at + 1], 0.0)
                add = add + jnp.where(rows == 0, lines[0][c][l:l + 1], 0.0)
                add = add + jnp.where(rows == R - 1, lines[1][c][l:l + 1], 0.0)
                target[c, l] = base[c, l] + weight * add

    def moved_rim():
        lines = flank_lines(1)
        corners = []
        for side, owner in enumerate((0, nby - 1)):
            inner = join([d_r[0, owner, l, side * (slab - 1):side * (slab - 1) + 1]
                          for l in range(L)], 0)
            near, far = d_r[0, owner, L + 1], d_r[0, owner, L + 2]
            edge = d_r[0, owner, L]
            low, high = edge[:, 4 * L:4 * L + 1], edge[:, 4 * L + 1:4 * L + 2]
            down = [inner - far if side == 0 else far - inner,
                    jnp.where(lanes8 == C - 1, high, pltpu.roll(near, C - 1, 1))
                    - jnp.where(lanes8 == 0, low, pltpu.roll(near, 1, 1)),
                    jnp.where(rows8 == L - 1, 0.0, pltpu.roll(near, L - 1, 0))
                    - jnp.where(rows8 == 0, 0.0, pltpu.roll(near, 1, 0))]
            lines[side] = [line - (0.5 * step_size) * part
                           for line, part in zip(lines[side], down)]
            spot = jnp.where(lanes8 == rows8, low, jnp.where(lanes8 == rows8 + L, high, 0.0))
            corners.append(jnp.sum(spot, axis=0, keepdims=True))
        edge = join([d_r[0, j, L] for j in range(nby)], 0)
        layer = lanes % L
        group = lanes // L
        across = pltpu.roll(edge, C - 5 * L, 1) - pltpu.roll(edge, C - 2 * L, 1)
        down = [x_next(edge, corners[1]) - x_prev(edge, corners[0]),
                jnp.where(group == 0, across, -across),
                jnp.where(layer == L - 1, 0.0, pltpu.roll(edge, C - 1, 1))
                - jnp.where(layer == 0, 0.0, pltpu.roll(edge, 1, 1))]
        low_col, high_col = col_r[1, 0], col_r[1, 1]
        for c in range(3):
            part = (0.5 * step_size) * down[c]
            low_col = low_col - jnp.where(
                group == C // (2 * L) + c, pltpu.roll(part, C // 2 + c * L, 1), 0.0)
            high_col = high_col - jnp.where(
                group == c, pltpu.roll(part, (C + c * L - L) % C, 1), 0.0)
        return lines, low_col, high_col

    def field(n):
        edge = join([d_r[n, j, L] for j in range(nby)], 0)
        phis = [join([d_r[n, j, l] for j in range(nby)], 0) for l in range(L)]
        for l in range(L):
            phi = phis[l]
            low = d_r[n, 0, L + 1, l:l + 1]
            high = d_r[n, nby - 1, L + 1, l:l + 1]
            along_x = 0.5 * (x_next(phi, high) - x_prev(phi, low))
            along_y = 0.5 * (y_next(phi, edge[:, L + l:L + l + 1])
                             - y_prev(phi, edge[:, l:l + 1]))
            above = phis[l + 1] if l + 1 < L else zero
            below = phis[l - 1] if l else zero
            yield l, (along_x, along_y, 0.5 * (above - below))

    loads[0].wait()
    charge(0, p_in, None)
    flank_start(0, p_in)
    loads[1].wait()
    relax_inside(p_in)
    charge(1, base, ring_of(0))
    pl.semaphore_wait(barrier, len(greeted))

    def tell(at):
        pl.semaphore_signal(
            known.at[at], inc=1, device_id={"bx": at_x[reach[at]]}, device_id_type=MESH)

    tell(0)
    first_a = among_y(a_s, a_r, 0, L + 2)
    second_a = among_y(a_s, a_r, 1, L + 3)
    for at in range(1, len(reach)):
        pl.semaphore_wait(known.at[at - 1], 1)
        tell(at)
    loads[2].wait()
    loads[3].wait()
    wave_x = wx[0:1]
    wave_y = join([wy[...]] * (NX // C), 1)
    lateral = wave_x + wave_y
    previous = None
    for l in range(L):
        pivot = perm[l] * lateral + inter[l] + inter[l + 1]
        if l:
            pivot = pivot - inter[l] * previous
        inverse = 1.0 / pivot
        coef[l] = inverse
        previous = inter[l + 1] * inverse
        ratio[l] = previous
    loads[4].wait()
    loads[5].wait()
    wait(first_a)
    y_forward(0)
    pl.semaphore_wait(known.at[len(reach) - 1], 1)
    first_b = spread(b_s, b_r, 0, False, slab + 1)
    wait(second_a)
    y_forward(1)
    second_b = spread(b_s, b_r, 1, False, slab + 2)
    flanks = flank_send(0)
    wait(first_b)
    values = solve(spectrum(0))
    x_backward(0, values)
    first_c = spread(c_s, c_r, 0, True, slab + 2)
    bend = -(wave_x * (1.0 - 0.25 * wave_x) + wave_y * (1.0 - 0.25 * wave_y))
    slopes = []
    none = jnp.zeros_like(values[0])
    for l in range(L):
        above = values[l + 1] if l + 1 < L else none
        below = values[l - 1] if l else none
        slopes.append(0.5 * (above - below))
    moved = []
    for l in range(L):
        above = slopes[l + 1] if l + 1 < L else none
        below = slopes[l - 1] if l else none
        moved.append(step_size * (bend * values[l] + 0.5 * (above - below)))
    wait(second_b)
    x_backward(1, solve([here + more for here, more in zip(spectrum(1), moved)]))
    second_c = spread(c_s, c_r, 1, True, slab + 1)
    wait(flanks)
    relax_edges(flank_lines(0), col_r[0, 0], col_r[0, 1], base)
    flank_start(1, base)
    flanks = flank_send(1)
    wait(first_c)
    y_backward(0)
    first_d = among_y(d_s, d_r, 0, L + 3)
    wait(second_c)
    y_backward(1)
    second_d = among_y(d_s, d_r, 1, L + 2)
    wait(first_d)
    for l, parts in field(0):
        for c in range(3):
            p_mid[c, l] = base[c, l] - step_size * parts[c]
    wait(flanks)
    rim = moved_rim()
    relax_inside(p_mid)
    relax_edges(*rim, base_o)
    wait(second_d)
    for l, parts in field(1):
        for c in range(3):
            down_o[c, l] = parts[c]
    for send in sends:
        send()


def fused_shards(polarization, alpha_field, landau, stiffness, permittivity, interfaces):
    _, L, R, C = polarization.shape
    nbx = lax.axis_size("bx")
    nby = lax.axis_size("by")
    grid_x, grid_y = nbx * R, nby * C
    per = C // L
    line = np.arange(grid_x)
    hx = fixed_table(line[:, None], line[None, :], grid_x)
    line = np.arange(grid_y)
    hy = fixed_table(line[:, None], line[None, :], grid_y)
    wave_x = 4.0 * np.sin(np.pi * np.arange(grid_x) / grid_x) ** 2
    wave_x = jnp.asarray(np.tile(wave_x[None, :], (8, 1)).astype(np.float32))
    at = np.arange(nbx * nby)
    first = (at % nby) * C + (at // nby) * per
    mode = (first[:, None] + np.arange(per)[None, :]).reshape(-1)
    wave_y = 4.0 * np.sin(np.pi * mode / grid_y) ** 2
    wave_y = jnp.asarray(np.tile(wave_y[:, None], (1, C)).astype(np.float32))
    f32 = jnp.float32
    hbm = pl.BlockSpec(memory_space=pltpu.HBM)
    smem = pl.BlockSpec(memory_space=pltpu.SMEM)
    S = 2
    n_copies = S * (4 + 2 * (nby - 1) + 2 * (nbx * nby - 1))
    by_y = pltpu.VMEM((S, nby, L + 3, 8, C), f32)
    by_mode = pltpu.VMEM((S, nby, nbx, 16, C), f32)
    by_place = pltpu.VMEM((S, nbx, nby, 16, C), f32)
    scratch = [
        pltpu.VMEM((3, L, R, C), f32), pltpu.VMEM((3, L, R, C), f32),
        pltpu.VMEM((L, per, grid_x), f32), pltpu.VMEM((L, per, grid_x), f32),
        by_y, by_y, by_mode, by_place, by_place, by_mode, by_y, by_y,
        pltpu.VMEM((S, 2, 3 * L, C), f32), pltpu.VMEM((S, 2, 3 * L, C), f32),
        pltpu.VMEM((S, R, C), f32), pltpu.VMEM((S, 2, R, C), f32),
        pltpu.SemaphoreType.DMA((n_copies,)), pltpu.SemaphoreType.DMA((n_copies,)),
        pltpu.SemaphoreType.REGULAR((nbx.bit_length(),)), pltpu.VMEM((3, L, R, C), f32),
        pltpu.VMEM((L, R, C), f32), pltpu.VMEM(wave_x.shape, f32), pltpu.VMEM((per, C), f32),
        pltpu.VMEM(hx.shape, hx.dtype), pltpu.VMEM(hy.shape, hy.dtype),
        pltpu.SemaphoreType.DMA((6,)),
    ]
    out = pltpu.VMEM(polarization.shape, f32)
    base, down = pl.pallas_call(
        functools.partial(fused, (L, R, C, nbx, nby)),
        out_shape=(out, out),
        in_specs=[hbm, hbm, smem, smem, smem, smem, hbm, hbm, hbm, hbm],
        out_specs=(pl.BlockSpec(memory_space=pltpu.VMEM), pl.BlockSpec(memory_space=pltpu.VMEM)),
        scratch_shapes=scratch,
        compiler_params=pltpu.CompilerParams(
            collective_id=0, has_side_effects=True, vmem_limit_bytes=66 * 1000 * 1000),
    )(polarization, alpha_field, landau, stiffness, permittivity, interfaces,
      wave_x, wave_y, hx, hy)
    return base - step_size * down, -down


def solution(mesh):
    def run(polarization, *rest):
        _, L, R, C = polarization.shape
        body = fused_shards if fits(L, R, C, lax.axis_size("bx"), lax.axis_size("by")) else shards
        return body(polarization, *rest)

    return jax.shard_map(
        run,
        mesh=mesh,
        in_specs=(P(None, None, "bx", "by"), P(None, "bx", "by"), P(), P(), P(), P()),
        out_specs=(P(None, None, "bx", "by"), P(None, None, "bx", "by")),
        check_vma=False,
    )
```

```python
import functools

import jax
import jax.numpy as jnp
import numpy as np
from jax import lax
from jax.experimental import pallas as pl
from jax.experimental.pallas import tpu as pltpu
from jax.sharding import PartitionSpec as P

STEPS = 2
step_size = 0.05
MESH = pl.DeviceIdType.MESH
PAD = 8


def cas_table(left, right, length):
    turns = left * right % length
    angle = 2.0 * jnp.pi / length * turns.astype(jnp.float32)
    table = jnp.cos(angle) + jnp.sin(angle)
    high = lax.reduce_precision(table, 8, 7)
    return jnp.stack([high.astype(jnp.bfloat16), (table - high).astype(jnp.bfloat16)])


def fixed_table(left, right, length):
    angle = 2.0 * np.pi / length * (left * right % length)
    table = (np.cos(angle) + np.sin(angle)).astype(np.float32)
    high = table.astype(jnp.bfloat16)
    low = (table - high.astype(np.float32)).astype(jnp.bfloat16)
    return jnp.asarray(np.stack([high, low]))


def is_wide(rows, nbx, nby, layers):
    return layers % nbx == 0 and rows % (8 * nby) == 0


def halves(value):
    high = value.astype(jnp.bfloat16)
    low = (value - high.astype(jnp.float32)).astype(jnp.bfloat16)
    return high, low


def product(left, right):
    dot = functools.partial(jnp.dot, preferred_element_type=jnp.float32)
    return dot(left[0], right[0]) + (dot(left[0], right[1]) + dot(left[1], right[0]))


def kernel(sizes, p_in, alpha_h, landau, stiff, perm, inter, lam, hx_h, hy_h, p_out, f_out, *scratch):
    L, R, C, nbx, nby, rep, lp, own = sizes
    (p_mid, base, coef, ratio, q, inb, outs, rec_i,
     row_s, row_r, col_s, col_r, pc_s, pc_r, ssem, rsem,
     alpha, hx, hy, local_sem) = scratch[:20]
    wide = is_wide(R, nbx, nby, L)
    if wide:
        z_in, w_out = scratch[20:]
    else:
        rec_f, ybuf, phat, u = scratch[20:]
    thin = R // nby
    R2 = R + PAD
    bx = lax.axis_index("bx")
    by = lax.axis_index("by")
    group = bx // rep
    part = bx % rep
    scale = 1.0 / (R * nbx * C * nby)
    loads = [pltpu.make_async_copy(src, dst, local_sem.at[at]) for at, (src, dst) in
             enumerate(((alpha_h, alpha), (hx_h, hx), (hy_h, hy)))]
    for load in loads:
        load.start()
    slots = [0]
    sends = []

    barrier = pltpu.get_barrier_semaphore()
    others = [(a, b) for b in range(nby) for a in range(nbx) if a or b]
    greeted = [(a, b) for a, b in others if wide or not a or not b]
    for a, b in greeted:
        pl.semaphore_signal(
            barrier, inc=1, device_id={"bx": (bx + a) % nbx, "by": (by + b) % nby},
            device_id_type=MESH)

    def remote(src, dst, device, slot):
        return pltpu.make_async_remote_copy(
            src_ref=src, dst_ref=dst, send_sem=ssem.at[slot], recv_sem=rsem.at[slot],
            device_id=device, device_id_type=MESH)

    def fresh():
        slots[0] += 1
        return slots[0] - 1

    def push(src, dst, device):
        copy = remote(src, dst, device, fresh())
        copy.start()
        sends.append(copy.wait_send)
        return copy

    rows = lax.broadcasted_iota(jnp.int32, (R, C), 0)
    lanes = lax.broadcasted_iota(jnp.int32, (R, C), 1)

    def x_next(f, high):
        return jnp.where(rows == R - 1, high, pltpu.roll(f, R - 1, 0))

    def x_prev(f, low):
        return jnp.where(rows == 0, low, pltpu.roll(f, 1, 0))

    def y_next(f, high):
        return jnp.where(lanes == C - 1, high, pltpu.roll(f, C - 1, 1))

    def y_prev(f, low):
        return jnp.where(lanes == 0, low, pltpu.roll(f, 1, 1))

    def column_tile(blocks):
        tile = jnp.zeros((R, C), jnp.float32)
        for at, block in enumerate(blocks):
            tile = jnp.where(lanes == at, block[:, 0:1], tile)
            tile = jnp.where(lanes == C // 2 + at, block[:, C - 1:C], tile)
        return tile

    def x_start(src, n):
        mine = inb.at[n, :, pl.ds(pl.multiple_of(bx * R, R), R)]
        copies = []
        for k in range(1, nbx):
            to = (bx + k) % nbx
            copies.append(push(src.at[pl.ds(to // rep * lp, lp)], mine, {"bx": to}))
        for layer in range(lp):
            inb[n, layer, pl.ds(pl.multiple_of(bx * R, R), R)] = src[group * lp + layer]
        return copies

    def x_mix(copies, n):
        for copy in copies:
            copy.wait_recv()
        table = (hx[0], hx[1])
        for layer in range(lp):
            outs[n, :, layer] = product(table, halves(inb[n, layer])).reshape(own, R2, C)

    def spread(n, step):
        copies = []
        for a, b in others:
            to_x, to_y = (bx + a) % nbx, (by + b) % nby
            copies.append(push(
                outs.at[n, to_x, :, pl.ds(pl.multiple_of(to_y * thin, thin), thin)],
                z_in.at[step, by, pl.ds(bx * lp, lp)], {"bx": to_x, "by": to_y}))
        for layer in range(lp):
            z_in[step, by, bx * lp + layer] = outs[
                n, bx, layer, pl.ds(pl.multiple_of(by * thin, thin), thin)]
        for copy in copies:
            copy.wait_recv()

    def collect(n, step):
        at = pl.ds(pl.multiple_of(bx * R + by * thin, thin), thin)
        copies = []
        for a, b in others:
            to_x, to_y = (bx + a) % nbx, (by + b) % nby
            copies.append(push(
                w_out.at[step, to_y, pl.ds(to_x * lp, lp)], inb.at[n, :, at],
                {"bx": to_x, "by": to_y}))
        for layer in range(lp):
            inb[n, layer, at] = w_out[step, by, bx * lp + layer]
        return copies

    def solve(spectrum, height):
        primes = []
        for l in range(L):
            source = spectrum[l * height:(l + 1) * height] * scale
            if l:
                source = source + inter[l] * primes[-1]
            primes.append(source * coef[l])
        values = [primes[-1]]
        for l in range(L - 2, -1, -1):
            values.insert(0, primes[l] + ratio[l] * values[0])
        return values

    def x_finish(n, dst, height):
        waits = []
        landing = dst.at[pl.ds(group * lp, lp)]
        for t in range(own):
            local = (group + t) % own
            to = part * own + local
            src = outs.at[n, local, :, pl.ds(0, height)]
            if rep == 1:
                if t == 0:
                    continue
                waits.append(push(src, landing, {"bx": to}).wait_recv)
                continue
            slot = fresh()

            def go(src=src, to=to, slot=slot):
                remote(src, landing, {"bx": to}, slot).start()

            def gone(src=src, to=to, slot=slot):
                @pl.when(to != bx)
                def _():
                    remote(src, landing, {"bx": to}, slot).wait_send()

            def came(src=src, to=to, slot=slot, t=t):
                origin = (bx % own + own - t) % own * rep + bx // own

                @pl.when(origin != bx)
                def _():
                    remote(src, landing, {"bx": to}, slot).wait_recv()

            pl.when(to != bx)(go)
            sends.append(gone)
            waits.append(came)

        def keep():
            for layer in range(lp):
                dst[group * lp + layer] = outs[n, bx % own, layer, 0:height]

        if rep == 1:
            keep()
        else:
            pl.when(bx // own == part)(keep)
        for wait in waits:
            wait()

    def y_pass(src, n):
        copies = [push(src, ybuf.at[n, k - 1], {"by": (by + k) % nby}) for k in range(1, nby)]
        total = product(halves(src[...].reshape(L * R, C)), (hy[0, by], hy[1, by]))
        for k in range(1, nby):
            copies[k - 1].wait_recv()
            origin = (by + nby - k) % nby
            total += product(halves(ybuf[n, k - 1].reshape(L * R, C)), (hy[0, origin], hy[1, origin]))
        return total

    def flank_start(rows_too, step, src):
        copies = []
        if rows_too:
            for c in range(3):
                for l in range(L):
                    at = c * L + l
                    row_s[step, 0, at:at + 1] = src[c, l, 0:1]
                    row_s[step, 1, at:at + 1] = src[c, l, R - 1:R]
            col_s[step] = column_tile([src[c, l] for c in range(3) for l in range(L)])
            if step == 0:
                pl.semaphore_wait(barrier, len(greeted))
            copies.append(push(row_s.at[step, 1], row_r.at[step, 0], {"bx": (bx + 1) % nbx}))
            copies.append(push(row_s.at[step, 0], row_r.at[step, 1], {"bx": (bx + nbx - 1) % nbx}))
            tile, land = col_s.at[step], col_r
        else:
            pc_s[step] = column_tile([src[l, 0:R] for l in range(L)])
            tile, land = pc_s.at[step], pc_r
        copies.append(push(tile, land.at[step, 0], {"by": (by + 1) % nby}))
        copies.append(push(tile, land.at[step, 1], {"by": (by + nby - 1) % nby}))
        return copies

    for step in range(STEPS):
        src = p_in if step == 0 else p_mid
        flanks = flank_start(True, step, src)
        if step == 0:
            lateral = lam[...]
            previous = None
            for l in range(L):
                pivot = perm[l] * lateral + inter[l] + inter[l + 1]
                if l:
                    pivot = pivot - inter[l] * previous
                inverse = 1.0 / pivot
                coef[l] = inverse
                previous = inter[l + 1] * inverse
                ratio[l] = previous
        for copy in flanks:
            copy.wait_recv()
        low_col = col_r[step, 0]
        high_col = col_r[step, 1]

        def edges(c, l):
            at = c * L + l
            return (row_r[step, 0, at:at + 1], row_r[step, 1, at:at + 1],
                    low_col[:, C // 2 + at:C // 2 + at + 1], high_col[:, at:at + 1])

        zero = jnp.zeros((R, C), jnp.float32)
        for l in range(L):
            low, high, _, _ = edges(0, l)
            _, _, left, right = edges(1, l)
            along_x, along_y = src[0, l], src[1, l]
            above = src[2, l + 1] if l + 1 < L else zero
            below = src[2, l - 1] if l else zero
            q[step, l] = -0.5 * (
                (x_next(along_x, high) - x_prev(along_x, low))
                + (y_next(along_y, right) - y_prev(along_y, left)) + (above - below))
        copies = x_start(q.at[step], 2 * step)
        if step == 0:
            for load in loads:
                load.wait()
        for l in range(L):
            cells = [src[c, l] for c in range(3)]
            squares = [cell * cell for cell in cells]
            whole = squares[0] + squares[1] + squares[2]
            for c in range(3):
                cell, square = cells[c], squares[c]
                low, high, left, right = edges(c, l)
                above = src[c, l + 1] if l + 1 < L else zero
                below = src[c, l - 1] if l else zero
                smooth = stiff[l] * (
                    (x_next(cell, high) + x_prev(cell, low) + y_next(cell, right)
                     + y_prev(cell, left) - 4.0 * cell) + (above + below - 2.0 * cell))
                drive = cell * (
                    2.0 * alpha[l] + 4.0 * landau[0, l] * square
                    + 2.0 * landau[1, l] * (whole - square)
                    + 6.0 * landau[2, l] * (square * square))
                base[c, l] = cell - step_size * (drive - smooth)
        n = 2 * step
        x_mix(copies, n)
        if wide:
            spread(n, step)
            table = (hy[0], hy[1])
            full = jnp.concatenate(
                [z_in[step, j].reshape(L * thin, C) for j in range(nby)], axis=1)
            values = solve(product(halves(full), table), thin)
            full = product(halves(jnp.concatenate(values, axis=0)), table)
            for j in range(nby):
                w_out[step, j] = full[:, j * C:(j + 1) * C].reshape(L, thin, C)
            copies = collect(n + 1, step)
        else:
            x_finish(n, rec_f.at[step], R)
            for l, value in enumerate(solve(y_pass(rec_f.at[step], n), R)):
                phat[step, l] = value
            u[step] = y_pass(phat.at[step], n + 1).reshape(L, R, C)
            copies = x_start(u.at[step], n + 1)
        x_mix(copies, n + 1)
        x_finish(n + 1, rec_i.at[step], R2)
        flanks = flank_start(False, step, rec_i.at[step])
        last = step == STEPS - 1
        target = p_out if last else p_mid
        for l in range(L):
            phi = rec_i[step, l, 0:R]
            low = rec_i[step, l, R:R + 1]
            high = rec_i[step, l, R + 1:R + 2]
            along_x = -0.5 * (x_next(phi, high) - x_prev(phi, low))
            above = rec_i[step, l + 1, 0:R] if l + 1 < L else zero
            below = rec_i[step, l - 1, 0:R] if l else zero
            along_z = -0.5 * (above - below)
            target[0, l] = base[0, l] + step_size * along_x
            target[2, l] = base[2, l] + step_size * along_z
            if last:
                f_out[0, l] = along_x
                f_out[2, l] = along_z
        for copy in flanks:
            copy.wait_recv()
        low_phi = pc_r[step, 0]
        high_phi = pc_r[step, 1]
        for l in range(L):
            phi = rec_i[step, l, 0:R]
            along_y = -0.5 * (y_next(phi, high_phi[:, l:l + 1])
                              - y_prev(phi, low_phi[:, C // 2 + l:C // 2 + l + 1]))
            target[1, l] = base[1, l] + step_size * along_y
            if last:
                f_out[1, l] = along_y
    for wait in sends:
        wait()


def shards(polarization, alpha_field, landau, stiffness, permittivity, interfaces):
    _, L, R, C = polarization.shape
    nbx = lax.axis_size("bx")
    nby = lax.axis_size("by")
    bx = lax.axis_index("bx")
    by = lax.axis_index("by")
    rep = max(1, nbx // L)
    lp = max(1, L // nbx)
    own = nbx // rep
    grid_x, grid_y = nbx * R, nby * C
    R2 = R + PAD
    wide = is_wide(R, nbx, nby, L)
    pool = np if wide else jnp
    make = fixed_table if wide else cas_table
    line = pool.arange(R2, dtype=jnp.int32)
    line = pool.where(line < R, line, pool.where(line == R, -1, R))
    owners = pool.arange(own, dtype=jnp.int32)
    if not wide:
        owners = owners + bx % rep * own
    wanted = ((owners[:, None] * R + line[None, :] + grid_x) % grid_x).reshape(own * R2, 1)
    hx = make(wanted, pool.arange(grid_x, dtype=jnp.int32)[None, :], grid_x)
    every_col = pool.arange(grid_y, dtype=jnp.int32)
    my_rows = bx * R + jnp.arange(R, dtype=jnp.int32)
    my_cols = by * C + jnp.arange(C, dtype=jnp.int32)
    if wide:
        hy = make(every_col[:, None], every_col[None, :], grid_y)
        my_rows = bx * R + by * (R // nby) + jnp.arange(R // nby, dtype=jnp.int32)
        my_cols = jnp.arange(grid_y, dtype=jnp.int32)
    else:
        hy = make(every_col[:, None], my_cols[None, :], grid_y).reshape(2, nby, C, C)
    wave_x = jnp.sin(jnp.pi * my_rows.astype(jnp.float32) / grid_x)
    wave_y = jnp.sin(jnp.pi * my_cols.astype(jnp.float32) / grid_y)
    lam = 4.0 * wave_x[:, None] ** 2 + 4.0 * wave_y[None, :] ** 2
    sizes = (L, R, C, nbx, nby, rep, lp, own)
    n_copies = STEPS * (6 + 2 * (nbx * nby + own if wide else nbx + own + nby))
    f32 = jnp.float32
    vmem = pl.BlockSpec(memory_space=pltpu.VMEM)
    hbm = pl.BlockSpec(memory_space=pltpu.HBM)
    smem = pl.BlockSpec(memory_space=pltpu.SMEM)
    S = STEPS
    scratch = [
        pltpu.VMEM((3, L, R, C), f32), pltpu.VMEM((3, L, R, C), f32),
        pltpu.VMEM((L,) + lam.shape, f32), pltpu.VMEM((L,) + lam.shape, f32),
        pltpu.VMEM((S, L, R, C), f32), pltpu.VMEM((2 * S, lp, grid_x, C), f32),
        pltpu.VMEM((2 * S, own, lp, R2, C), f32), pltpu.VMEM((S, L, R2, C), f32),
        pltpu.VMEM((S, 2, 3 * L, C), f32), pltpu.VMEM((S, 2, 3 * L, C), f32),
        pltpu.VMEM((S, R, C), f32), pltpu.VMEM((S, 2, R, C), f32),
        pltpu.VMEM((S, R, C), f32), pltpu.VMEM((S, 2, R, C), f32),
        pltpu.SemaphoreType.DMA((n_copies,)), pltpu.SemaphoreType.DMA((n_copies,)),
        pltpu.VMEM((L, R, C), f32), pltpu.VMEM(hx.shape, hx.dtype),
        pltpu.VMEM(hy.shape, hy.dtype), pltpu.SemaphoreType.DMA((3,)),
    ]
    if wide:
        thin = (S, nby, L, R // nby, C)
        scratch += [pltpu.VMEM(thin, f32), pltpu.VMEM(thin, f32)]
    else:
        scratch += [
            pltpu.VMEM((S, L, R, C), f32), pltpu.VMEM((2 * S, nby - 1, L, R, C), f32),
            pltpu.VMEM((S, L, R, C), f32), pltpu.VMEM((S, L, R, C), f32),
        ]
    out = jax.ShapeDtypeStruct(polarization.shape, f32)
    return pl.pallas_call(
        functools.partial(kernel, sizes),
        out_shape=(out, out),
        in_specs=[vmem, hbm, smem, smem, smem, smem, vmem, hbm, hbm],
        out_specs=(vmem, vmem),
        scratch_shapes=scratch,
        compiler_params=pltpu.CompilerParams(
            collective_id=0, has_side_effects=True, vmem_limit_bytes=65 * 1000 * 1000),
    )(polarization, alpha_field, landau, stiffness, permittivity, interfaces, lam, hx, hy)


def fits(L, R, C, nbx, nby):
    slab = R // nby
    return (L == nbx and slab == 8 and slab * nby == R and nby > 1 and C % (8 * L) == 0
            and nbx > 2 and nbx & (nbx - 1) == 0 and nby & (nby - 1) == 0)


def partner(index, mask, size):
    other = 0
    bit = 1
    while bit < size:
        here = index // bit % 2
        other = other + bit * (1 - here if mask // bit % 2 else here)
        bit *= 2
    return other


def join(parts, axis):
    return jnp.concatenate(parts, axis=axis)


def fused(sizes, p_h, alpha_h, landau, stiff, perm, inter, wx_h, wy_h, hx_h, hy_h,
          base_o, down_o, *scratch):
    L, R, C, nbx, nby = sizes
    (p_mid, base, coef, ratio, a_s, a_r, b_s, b_r, c_s, c_r, d_s, d_r,
     row_s, row_r, col_s, col_r, ssem, rsem, known, p_in, alpha, wx, wy, hx, hy, local_sem) = scratch
    slab = R // nby
    per = C // L
    NX, NY = nbx * R, nby * C
    bx = lax.axis_index("bx")
    by = lax.axis_index("by")
    scale = 1.0 / (NX * NY)
    f32 = jnp.float32
    dot = functools.partial(jnp.dot, preferred_element_type=f32)
    slots = [0]
    sends = []

    barrier = pltpu.get_barrier_semaphore()
    at_x = [partner(bx, a, nbx) for a in range(nbx)]
    at_y = [partner(by, b, nby) for b in range(nby)]
    others = [(a, b) for b in range(nby) for a in range(nbx) if a or b]
    others.sort(key=lambda ab: -(ab[0] // 2 + ab[0] % 2 + ab[1] // 2))
    reach = [1 << i for i in range(1, nbx.bit_length() - 1)]
    greeted = [(a, b) for a, b in others if a < 2] + [(a, 0) for a in reach]
    for a, b in greeted:
        pl.semaphore_signal(
            barrier, inc=1, device_id={"bx": at_x[a], "by": at_y[b]}, device_id_type=MESH)
    mine = pl.multiple_of((bx * nby + by) * per, per)
    loads = [pltpu.make_async_copy(src, dst, local_sem.at[at]) for at, (src, dst) in enumerate((
        (p_h, p_in), (alpha_h, alpha), (wx_h, wx), (wy_h.at[pl.ds(mine, per)], wy), (hx_h, hx),
        (hy_h, hy)))]
    for load in loads:
        load.start()

    def push(src, dst, device):
        slot = slots[0]
        slots[0] += 1
        copy = pltpu.make_async_remote_copy(
            src_ref=src, dst_ref=dst, send_sem=ssem.at[slot], recv_sem=rsem.at[slot],
            device_id=device, device_id_type=MESH)
        copy.start()
        sends.append(copy.wait_send)
        return copy

    rows = lax.broadcasted_iota(jnp.int32, (R, C), 0)
    lanes = lax.broadcasted_iota(jnp.int32, (R, C), 1)
    rows8 = lax.broadcasted_iota(jnp.int32, (slab, C), 0)
    lanes8 = lax.broadcasted_iota(jnp.int32, (slab, C), 1)
    zero = jnp.zeros((R, C), f32)
    zero8 = jnp.zeros((slab, C), f32)

    def x_next(f, high):
        return jnp.where(rows == R - 1, high, pltpu.roll(f, R - 1, 0))

    def x_prev(f, low):
        return jnp.where(rows == 0, low, pltpu.roll(f, 1, 0))

    def y_next(f, high):
        return jnp.where(lanes == C - 1, high, pltpu.roll(f, C - 1, 1))

    def y_prev(f, low):
        return jnp.where(lanes == 0, low, pltpu.roll(f, 1, 1))

    def charge(n, src, ring):
        sides = (0, nby - 1)
        edge = zero
        for l in range(L):
            along_x, along_y = src[0, l], src[1, l]
            above = src[2, l + 1] if l + 1 < L else zero
            below = src[2, l - 1] if l else zero
            low = high = left = right = 0.0
            if ring:
                lines, column = ring
                low, high = lines[0][0][l:l + 1], lines[1][0][l:l + 1]
                left = column[:, L + l:L + l + 1]
                right = column[:, C // 2 + L + l:C // 2 + L + l + 1]
            value = -0.5 * ((x_next(along_x, high) - x_prev(along_x, low))
                            + (y_next(along_y, right) - y_prev(along_y, left)) + (above - below))
            for j in range(nby):
                a_s[n, j, l] = value[j * slab:(j + 1) * slab]
            edge = jnp.where(lanes == l, -0.5 * along_y[:, 0:1], edge)
            edge = jnp.where(lanes == L + l, 0.5 * along_y[:, C - 1:C], edge)
        near = [-0.5 * join([src[0, l, 0:1] for l in range(L)], 0),
                0.5 * join([src[0, l, R - 1:R] for l in range(L)], 0)]
        corner = [None, None]
        if ring:
            for side, sign in enumerate((-0.5, 0.5)):
                first, second, third = lines[side]
                turned = (jnp.where(lanes8 == C - 1, 0.0, pltpu.roll(second, C - 1, 1))
                          - jnp.where(lanes8 == 0, 0.0, pltpu.roll(second, 1, 1)))
                risen = (jnp.where(rows8 == L - 1, 0.0, pltpu.roll(third, L - 1, 0))
                         - jnp.where(rows8 == 0, 0.0, pltpu.roll(third, 1, 0)))
                near[side] = near[side] - 0.5 * (turned + risen)
                a_s[n, sides[side], L + 2] = sign * first
                corner[side] = jnp.where(
                    lanes8 == 4 * L, sign * first[:, 0:1] - 0.5 * second[:, 0:1],
                    jnp.where(lanes8 == 4 * L + 1,
                              sign * first[:, C - 1:C] + 0.5 * second[:, C - 1:C], 0.0))
            layer = lanes % L
            turned = -0.5 * (x_next(column, 0.0) - x_prev(column, 0.0))
            risen = -0.5 * (jnp.where(layer == L - 1, 0.0, pltpu.roll(column, C - 1, 1))
                            - jnp.where(layer == 0, 0.0, pltpu.roll(column, 1, 1)))
            both = turned + pltpu.roll(risen, C - 2 * L, 1)
            low = edge + both
            high = edge + pltpu.roll(both, C // 2 + L, 1)
            far_low = -0.5 * pltpu.roll(column, L, 1)
            far_high = 0.5 * pltpu.roll(column, C // 2 + 2 * L, 1)
            group = lanes // L
            edge = jnp.where(group == 0, low, jnp.where(group == 1, high, jnp.where(
                group == 2, far_low, jnp.where(group == 3, far_high, 0.0))))
        for side in range(2):
            a_s[n, sides[side], L + 1] = near[side]
        for j in range(nby):
            piece = edge[j * slab:(j + 1) * slab]
            if ring and j in sides:
                piece = piece + corner[sides.index(j)]
            a_s[n, j, L] = piece
            if j not in sides:
                a_s[n, j, L + 1:L + 3] = jnp.zeros((2, slab, C), f32)

    def ring_of(n):
        weight8 = zero8
        weight = zero
        layer = lanes % L
        for l in range(L):
            weight8 = jnp.where(rows8 == l, step_size * stiff[l], weight8)
            weight = jnp.where(layer == l, step_size * stiff[l], weight)
        lines = [[weight8 * row_s[n, side, c * L:(c + 1) * L] for c in range(3)]
                 for side in range(2)]
        return lines, weight * col_s[n]

    rim_slab = (by == 0) | (by == nby - 1)

    def has_rim(b, here):
        return nby != 4 or (b in (0, nby - 1)) == here

    def either(action):
        if nby != 4:
            action(True)
        else:
            pl.when(rim_slab)(functools.partial(action, True))
            pl.when(jnp.logical_not(rim_slab))(functools.partial(action, False))

    def exchange(targets, build, by_target):
        first = slots[0]
        slots[0] += len(targets)

        def make(at, whole):
            a, b = targets[at]
            src, dst = build(a, b, whole)
            return pltpu.make_async_remote_copy(
                src_ref=src, dst_ref=dst, send_sem=ssem.at[first + at],
                recv_sem=rsem.at[first + at], device_id={"bx": at_x[a], "by": at_y[b]},
                device_id_type=MESH)

        def outgoing(here):
            return [make(at, has_rim(b, here) if by_target else here)
                    for at, (a, b) in enumerate(targets)]

        def start(here):
            for copy in outgoing(here):
                copy.start()

        def sent(here):
            for copy in outgoing(here):
                copy.wait_send()

        def came(here):
            for at, (a, b) in enumerate(targets):
                make(at, here if by_target else has_rim(b, here)).wait_recv()

        either(start)
        sends.append(functools.partial(either, sent))
        return functools.partial(either, came)

    def among_y(source, landing, n, count, by_target):
        def build(a, b, whole):
            part = pl.ds(0, count if whole else L + 1)
            return source.at[n, at_y[b], part], landing.at[n, by, part]

        arrive = exchange([(0, b) for b in range(nby - 1, 0, -1)], build, by_target)
        landing[n, by, 0:count] = source[n, by, 0:count]
        return arrive

    def wait(copies):
        if callable(copies):
            copies()
        else:
            for copy in copies:
                copy.wait_recv()

    def spread(source, landing, n, flip, thick):
        def build(a, b, whole):
            part = pl.ds(0, thick if whole else slab)
            to_x, to_y = at_x[a], at_y[b]
            if flip:
                return source.at[n, to_x, to_y, part], landing.at[n, by, bx, part]
            return source.at[n, to_y, to_x, part], landing.at[n, bx, by, part]

        arrive = exchange(others, build, flip)
        if flip:
            landing[n, by, bx, 0:thick] = source[n, bx, by, 0:thick]
        else:
            landing[n, bx, by, 0:thick] = source[n, by, bx, 0:thick]
        return arrive

    def clear_rims():
        for n in range(2):
            for j in range(nby):
                a_r[n, j, L + 1:L + 3] = jnp.zeros((2, slab, C), f32)
                for e in range(nbx):
                    c_r[n, j, e, slab:2 * slab] = zero8

    def swap_groups(tiles):
        height = tiles[0].shape[0]
        group = lax.broadcasted_iota(jnp.int32, (height, C), 1) // per
        tiles = list(tiles)
        s = 1
        while s < L:
            upper = group % (2 * s) >= s
            for at in range(L):
                if at % (2 * s) < s:
                    low, high = tiles[at], tiles[at + s]
                    tiles[at] = jnp.where(upper, pltpu.roll(high, s * per, 1), low)
                    tiles[at + s] = jnp.where(upper, high, pltpu.roll(low, C - s * per, 1))
            s *= 2
        return tiles

    def swap_rows(tile):
        group = lanes8 // per
        s = 1
        while s < L:
            upper = group % (2 * s) >= s
            later = rows8 % (2 * s) >= s
            ahead = pltpu.roll(pltpu.roll(tile, L - s, 0), s * per, 1)
            behind = pltpu.roll(pltpu.roll(tile, s, 0), C - s * per, 1)
            tile = jnp.where(later, jnp.where(upper, tile, behind), jnp.where(upper, ahead, tile))
            s *= 2
        return tile

    def y_table(full):
        height = full.shape[0]
        high = full.astype(jnp.bfloat16)
        wide = high.astype(f32)
        both = join([wide, full - wide], 0).astype(jnp.bfloat16)
        first = dot(both, hy[0])
        return first[:height] + first[height:] + dot(high, hy[1])

    def y_forward(n):
        columns = []
        for j in range(nby):
            from_left = a_r[n, (j + nby - 1) % nby, L]
            from_right = a_r[n, (j + 1) % nby, L]
            tiles = []
            for l in range(L):
                extra = jnp.where(
                    lanes8 == 0, from_left[:, L + l:L + l + 1],
                    jnp.where(lanes8 == C - 1, from_right[:, l:l + 1], 0.0))
                if n:
                    extra = jnp.where(
                        lanes8 == 1, from_left[:, 3 * L + l:3 * L + l + 1],
                        jnp.where(lanes8 == C - 2, from_right[:, 2 * L + l:2 * L + l + 1], extra))
                tiles.append(a_r[n, j, l] + extra)
            near, far = a_r[n, j, L + 1], zero8
            if n:
                near = near + jnp.where(
                    lanes8 == 0, from_left[:, 4 * L + 1:4 * L + 2],
                    jnp.where(lanes8 == C - 1, from_right[:, 4 * L:4 * L + 1], 0.0))
                far = a_r[n, j, L + 2]
            columns.append(join(tiles + [near, far], 0))
        out = y_table(join(columns, 1))
        tiles = [join([out[l * slab:(l + 1) * slab, t * C:(t + 1) * C] for t in range(nby)], 0)
                 for l in range(L)]
        tiles = swap_groups(tiles)
        for t in range(nby):
            halos = [swap_rows(out[(L + k) * slab:(L + k) * slab + L, t * C:(t + 1) * C])
                     for k in range(1 + n)]
            for e in range(L):
                b_s[n, t, e, 0:slab] = tiles[e][t * slab:(t + 1) * slab]
                for k, halo in enumerate(halos):
                    b_s[n, t, e, slab + k:slab + k + 1] = halo[e:e + 1]

    def y_backward(n):
        tiles = swap_groups([join([c_r[n, t, e, 0:slab] for t in range(nby)], 0)
                             for e in range(L)])
        rims = [join([swap_rows(join([c_r[n, t, e, slab + k:slab + k + 1] for e in range(L)], 0))
                      for t in range(nby)], 1) for k in range(2 - n)]
        if n:
            rims.append(jnp.zeros((slab, NY), f32))
        lines = [join([tiles[l][t * slab:(t + 1) * slab] for t in range(nby)], 1)
                 for l in range(L)]
        out = y_table(join(lines + rims, 0))
        near = out[L * slab:L * slab + L]
        for j in range(nby):
            edge = zero8
            left, right = (j + nby - 1) % nby * C, (j + 1) % nby * C
            wanted = [left + C - 1, right]
            if n == 0:
                wanted += [left + C - 2, right + 1, None, j * C, j * C + C - 1]
                edge = jnp.where(lanes8 == 4 * L, near[:, left + C - 1:left + C],
                                 jnp.where(lanes8 == 4 * L + 1, near[:, right:right + 1], edge))
            for l in range(L):
                line = out[l * slab:(l + 1) * slab]
                d_s[n, j, l] = line[:, j * C:(j + 1) * C]
                for at, column in enumerate(wanted):
                    if column is not None:
                        edge = jnp.where(
                            lanes8 == at * L + l, line[:, column:column + 1], edge)
            d_s[n, j, L] = edge
            for k in range(2 - n):
                d_s[n, j, L + 1 + k] = out[(L + k) * slab:(L + k) * slab + L,
                                           j * C:(j + 1) * C]

    def spectrum(n):
        tiles = []
        for i in range(nbx):
            for j in range(nby):
                tile = b_r[n, i, j, 0:slab]
                for k in range(1 + n):
                    line = slice(slab + k, slab + k + 1)
                    if j == 0:
                        tile = tile + jnp.where(
                            rows8 == k, b_r[n, (i + nbx - 1) % nbx, nby - 1, line], 0.0)
                    if j == nby - 1:
                        tile = tile + jnp.where(
                            rows8 == slab - 1 - k, b_r[n, (i + 1) % nbx, 0, line], 0.0)
                tiles.append(tile)
        full = join(tiles, 0).T
        high = full.astype(jnp.bfloat16)
        wide = high.astype(f32)
        both = join([wide, full - wide], 0).astype(jnp.bfloat16)
        first = dot(both, hx[0])
        out = (first[:C] + first[C:] + dot(high, hx[1])) * scale
        return [out[l * per:(l + 1) * per] for l in range(L)]

    def solve(sources):
        primes = []
        for l in range(L):
            source = sources[l]
            if l:
                source = source + inter[l] * primes[-1]
            primes.append(source * coef[l])
        values = [primes[-1]]
        for l in range(L - 2, -1, -1):
            values.insert(0, primes[l] + ratio[l] * values[0])
        return values

    def x_backward(n, values):
        high, low = halves(join(values, 0))
        turn = functools.partial(
            lax.dot_general, dimension_numbers=(((1,), (1,)), ((), ())),
            preferred_element_type=f32)
        first = turn(hx[...].reshape(2 * NX, NX), high)
        out = first[:NX] + first[NX:] + turn(hx[0], low)
        for i in range(nbx):
            for j in range(nby):
                at = i * R + j * slab
                c_s[n, i, j, 0:slab] = out[at:at + slab]
                for k in range(2 - n):
                    line = (at - 1 - k if j == 0 else at + slab + k) % NX
                    c_s[n, i, j, slab + k:slab + k + 1] = out[line:line + 1]

    def flank_start(n, src):
        tile = zero
        for c in range(3):
            for l in range(L):
                at = c * L + l
                cell = src[c, l]
                row_s[n, 0, at:at + 1] = cell[0:1]
                row_s[n, 1, at:at + 1] = cell[R - 1:R]
                tile = jnp.where(lanes == at, cell[:, 0:1], tile)
                tile = jnp.where(lanes == C // 2 + at, cell[:, C - 1:C], tile)
        col_s[n] = tile

    def flank_send(n):
        return [
            push(row_s.at[n, 1], row_r.at[n, 0], {"bx": (bx + 1) % nbx}),
            push(row_s.at[n, 0], row_r.at[n, 1], {"bx": (bx + nbx - 1) % nbx}),
            push(col_s.at[n], col_r.at[n, 0], {"by": (by + 1) % nby}),
            push(col_s.at[n], col_r.at[n, 1], {"by": (by + nby - 1) % nby})]

    def relax_inside(src):
        for l in range(L):
            cells = [src[c, l] for c in range(3)]
            squares = [cell * cell for cell in cells]
            whole = squares[0] + squares[1] + squares[2]
            for c in range(3):
                cell, square = cells[c], squares[c]
                above = src[c, l + 1] if l + 1 < L else zero
                below = src[c, l - 1] if l else zero
                smooth = stiff[l] * (
                    (x_next(cell, 0.0) + x_prev(cell, 0.0) + y_next(cell, 0.0)
                     + y_prev(cell, 0.0) - 4.0 * cell) + (above + below - 2.0 * cell))
                drive = cell * (
                    2.0 * alpha[l] + 4.0 * landau[0, l] * square
                    + 2.0 * landau[1, l] * (whole - square)
                    + 6.0 * landau[2, l] * (square * square))
                base[c, l] = cell - step_size * (drive - smooth)

    def flank_lines(n):
        return [[row_r[n, side, c * L:(c + 1) * L] for c in range(3)] for side in range(2)]

    def relax_edges(lines, low_col, high_col, target):
        for l in range(L):
            weight = step_size * stiff[l]
            for c in range(3):
                at = c * L + l
                add = jnp.where(lanes == 0, low_col[:, C // 2 + at:C // 2 + at + 1], 0.0)
                add = add + jnp.where(lanes == C - 1, high_col[:, at:at + 1], 0.0)
                add = add + jnp.where(rows == 0, lines[0][c][l:l + 1], 0.0)
                add = add + jnp.where(rows == R - 1, lines[1][c][l:l + 1], 0.0)
                target[c, l] = base[c, l] + weight * add

    def moved_rim():
        lines = flank_lines(1)
        corners = []
        for side, owner in enumerate((0, nby - 1)):
            inner = join([d_r[0, owner, l, side * (slab - 1):side * (slab - 1) + 1]
                          for l in range(L)], 0)
            near, far = d_r[0, owner, L + 1], d_r[0, owner, L + 2]
            edge = d_r[0, owner, L]
            low, high = edge[:, 4 * L:4 * L + 1], edge[:, 4 * L + 1:4 * L + 2]
            down = [inner - far if side == 0 else far - inner,
                    jnp.where(lanes8 == C - 1, high, pltpu.roll(near, C - 1, 1))
                    - jnp.where(lanes8 == 0, low, pltpu.roll(near, 1, 1)),
                    jnp.where(rows8 == L - 1, 0.0, pltpu.roll(near, L - 1, 0))
                    - jnp.where(rows8 == 0, 0.0, pltpu.roll(near, 1, 0))]
            lines[side] = [line - (0.5 * step_size) * part
                           for line, part in zip(lines[side], down)]
            spot = jnp.where(lanes8 == rows8, low, jnp.where(lanes8 == rows8 + L, high, 0.0))
            corners.append(jnp.sum(spot, axis=0, keepdims=True))
        edge = join([d_r[0, j, L] for j in range(nby)], 0)
        layer = lanes % L
        group = lanes // L
        across = pltpu.roll(edge, C - 5 * L, 1) - pltpu.roll(edge, C - 2 * L, 1)
        down = [x_next(edge, corners[1]) - x_prev(edge, corners[0]),
                jnp.where(group == 0, across, -across),
                jnp.where(layer == L - 1, 0.0, pltpu.roll(edge, C - 1, 1))
                - jnp.where(layer == 0, 0.0, pltpu.roll(edge, 1, 1))]
        low_col, high_col = col_r[1, 0], col_r[1, 1]
        for c in range(3):
            part = (0.5 * step_size) * down[c]
            low_col = low_col - jnp.where(
                group == C // (2 * L) + c, pltpu.roll(part, C // 2 + c * L, 1), 0.0)
            high_col = high_col - jnp.where(
                group == c, pltpu.roll(part, (C + c * L - L) % C, 1), 0.0)
        return lines, low_col, high_col

    def field(n):
        edge = join([d_r[n, j, L] for j in range(nby)], 0)
        phis = [join([d_r[n, j, l] for j in range(nby)], 0) for l in range(L)]
        for l in range(L):
            phi = phis[l]
            low = d_r[n, 0, L + 1, l:l + 1]
            high = d_r[n, nby - 1, L + 1, l:l + 1]
            along_x = 0.5 * (x_next(phi, high) - x_prev(phi, low))
            along_y = 0.5 * (y_next(phi, edge[:, L + l:L + l + 1])
                             - y_prev(phi, edge[:, l:l + 1]))
            above = phis[l + 1] if l + 1 < L else zero
            below = phis[l - 1] if l else zero
            yield l, (along_x, along_y, 0.5 * (above - below))

    loads[0].wait()
    charge(0, p_in, None)
    pl.semaphore_wait(barrier, len(greeted))

    def tell(at):
        pl.semaphore_signal(
            known.at[at], inc=1, device_id={"bx": at_x[reach[at]]}, device_id_type=MESH)

    tell(0)
    if nby == 4:
        pl.when(jnp.logical_not(rim_slab))(clear_rims)
    first_a = among_y(a_s, a_r, 0, L + 2, True)
    flank_start(0, p_in)
    loads[1].wait()
    relax_inside(p_in)
    charge(1, base, ring_of(0))
    second_a = among_y(a_s, a_r, 1, L + 3, True)
    for at in range(1, len(reach)):
        pl.semaphore_wait(known.at[at - 1], 1)
        tell(at)
    loads[2].wait()
    loads[3].wait()
    wave_x = wx[0:1]
    wave_y = join([wy[...]] * (NX // C), 1)
    lateral = wave_x + wave_y
    previous = None
    for l in range(L):
        pivot = perm[l] * lateral + inter[l] + inter[l + 1]
        if l:
            pivot = pivot - inter[l] * previous
        inverse = 1.0 / pivot
        coef[l] = inverse
        previous = inter[l + 1] * inverse
        ratio[l] = previous
    loads[4].wait()
    loads[5].wait()
    wait(first_a)
    y_forward(0)
    pl.semaphore_wait(known.at[len(reach) - 1], 1)
    first_b = spread(b_s, b_r, 0, False, slab + 1)
    wait(second_a)
    y_forward(1)
    second_b = spread(b_s, b_r, 1, False, slab + 2)
    flanks = flank_send(0)
    wait(first_b)
    values = solve(spectrum(0))
    x_backward(0, values)
    first_c = spread(c_s, c_r, 0, True, slab + 2)
    bend = -(wave_x * (1.0 - 0.25 * wave_x) + wave_y * (1.0 - 0.25 * wave_y))
    slopes = []
    none = jnp.zeros_like(values[0])
    for l in range(L):
        above = values[l + 1] if l + 1 < L else none
        below = values[l - 1] if l else none
        slopes.append(0.5 * (above - below))
    moved = []
    for l in range(L):
        above = slopes[l + 1] if l + 1 < L else none
        below = slopes[l - 1] if l else none
        moved.append(step_size * (bend * values[l] + 0.5 * (above - below)))
    wait(second_b)
    x_backward(1, solve([here + more for here, more in zip(spectrum(1), moved)]))
    second_c = spread(c_s, c_r, 1, True, slab + 1)
    wait(flanks)
    relax_edges(flank_lines(0), col_r[0, 0], col_r[0, 1], base)
    flank_start(1, base)
    flanks = flank_send(1)
    wait(first_c)
    y_backward(0)
    first_d = among_y(d_s, d_r, 0, L + 3, False)
    wait(second_c)
    y_backward(1)
    second_d = among_y(d_s, d_r, 1, L + 2, False)
    wait(first_d)
    for l, parts in field(0):
        for c in range(3):
            p_mid[c, l] = base[c, l] - step_size * parts[c]
    wait(flanks)
    rim = moved_rim()
    relax_inside(p_mid)
    relax_edges(*rim, base_o)
    wait(second_d)
    for l, parts in field(1):
        for c in range(3):
            down_o[c, l] = parts[c]
    for send in sends:
        send()


def fused_shards(polarization, alpha_field, landau, stiffness, permittivity, interfaces):
    _, L, R, C = polarization.shape
    nbx = lax.axis_size("bx")
    nby = lax.axis_size("by")
    grid_x, grid_y = nbx * R, nby * C
    per = C // L
    line = np.arange(grid_x)
    hx = fixed_table(line[:, None], line[None, :], grid_x)
    line = np.arange(grid_y)
    hy = fixed_table(line[:, None], line[None, :], grid_y)
    wave_x = 4.0 * np.sin(np.pi * np.arange(grid_x) / grid_x) ** 2
    wave_x = jnp.asarray(np.tile(wave_x[None, :], (8, 1)).astype(np.float32))
    at = np.arange(nbx * nby)
    first = (at % nby) * C + (at // nby) * per
    mode = (first[:, None] + np.arange(per)[None, :]).reshape(-1)
    wave_y = 4.0 * np.sin(np.pi * mode / grid_y) ** 2
    wave_y = jnp.asarray(np.tile(wave_y[:, None], (1, C)).astype(np.float32))
    f32 = jnp.float32
    hbm = pl.BlockSpec(memory_space=pltpu.HBM)
    smem = pl.BlockSpec(memory_space=pltpu.SMEM)
    S = 2
    n_copies = S * (4 + 2 * (nby - 1) + 2 * (nbx * nby - 1))
    by_y = pltpu.VMEM((S, nby, L + 3, 8, C), f32)
    by_mode = pltpu.VMEM((S, nby, nbx, 16, C), f32)
    by_place = pltpu.VMEM((S, nbx, nby, 16, C), f32)
    scratch = [
        pltpu.VMEM((3, L, R, C), f32), pltpu.VMEM((3, L, R, C), f32),
        pltpu.VMEM((L, per, grid_x), f32), pltpu.VMEM((L, per, grid_x), f32),
        by_y, by_y, by_mode, by_place, by_place, by_mode, by_y, by_y,
        pltpu.VMEM((S, 2, 3 * L, C), f32), pltpu.VMEM((S, 2, 3 * L, C), f32),
        pltpu.VMEM((S, R, C), f32), pltpu.VMEM((S, 2, R, C), f32),
        pltpu.SemaphoreType.DMA((n_copies,)), pltpu.SemaphoreType.DMA((n_copies,)),
        pltpu.SemaphoreType.REGULAR((nbx.bit_length(),)), pltpu.VMEM((3, L, R, C), f32),
        pltpu.VMEM((L, R, C), f32), pltpu.VMEM(wave_x.shape, f32), pltpu.VMEM((per, C), f32),
        pltpu.VMEM(hx.shape, hx.dtype), pltpu.VMEM(hy.shape, hy.dtype),
        pltpu.SemaphoreType.DMA((6,)),
    ]
    out = pltpu.VMEM(polarization.shape, f32)
    base, down = pl.pallas_call(
        functools.partial(fused, (L, R, C, nbx, nby)),
        out_shape=(out, out),
        in_specs=[hbm, hbm, smem, smem, smem, smem, hbm, hbm, hbm, hbm],
        out_specs=(pl.BlockSpec(memory_space=pltpu.VMEM), pl.BlockSpec(memory_space=pltpu.VMEM)),
        scratch_shapes=scratch,
        compiler_params=pltpu.CompilerParams(
            collective_id=0, has_side_effects=True, vmem_limit_bytes=66 * 1000 * 1000),
    )(polarization, alpha_field, landau, stiffness, permittivity, interfaces,
      wave_x, wave_y, hx, hy)
    return base - step_size * down, -down


def solution(mesh):
    def run(polarization, *rest):
        _, L, R, C = polarization.shape
        body = fused_shards if fits(L, R, C, lax.axis_size("bx"), lax.axis_size("by")) else shards
        return body(polarization, *rest)

    return jax.shard_map(
        run,
        mesh=mesh,
        in_specs=(P(None, None, "bx", "by"), P(None, "bx", "by"), P(), P(), P(), P()),
        out_specs=(P(None, None, "bx", "by"), P(None, None, "bx", "by")),
        check_vma=False,
    )
```

```python
import functools

import jax
import jax.numpy as jnp
import numpy as np
from jax import lax
from jax.experimental import pallas as pl
from jax.experimental.pallas import tpu as pltpu
from jax.sharding import PartitionSpec as P

STEPS = 2
step_size = 0.05
MESH = pl.DeviceIdType.MESH
PAD = 8


def cas_table(left, right, length):
    turns = left * right % length
    angle = 2.0 * jnp.pi / length * turns.astype(jnp.float32)
    table = jnp.cos(angle) + jnp.sin(angle)
    high = lax.reduce_precision(table, 8, 7)
    return jnp.stack([high.astype(jnp.bfloat16), (table - high).astype(jnp.bfloat16)])


def fixed_table(left, right, length):
    angle = 2.0 * np.pi / length * (left * right % length)
    table = (np.cos(angle) + np.sin(angle)).astype(np.float32)
    high = table.astype(jnp.bfloat16)
    low = (table - high.astype(np.float32)).astype(jnp.bfloat16)
    return jnp.asarray(np.stack([high, low]))


def is_wide(rows, nbx, nby, layers):
    return layers % nbx == 0 and rows % (8 * nby) == 0


def halves(value):
    high = value.astype(jnp.bfloat16)
    low = (value - high.astype(jnp.float32)).astype(jnp.bfloat16)
    return high, low


def product(left, right):
    dot = functools.partial(jnp.dot, preferred_element_type=jnp.float32)
    return dot(left[0], right[0]) + (dot(left[0], right[1]) + dot(left[1], right[0]))


def kernel(sizes, p_in, alpha_h, landau, stiff, perm, inter, lam, hx_h, hy_h, p_out, f_out, *scratch):
    L, R, C, nbx, nby, rep, lp, own = sizes
    (p_mid, base, coef, ratio, q, inb, outs, rec_i,
     row_s, row_r, col_s, col_r, pc_s, pc_r, ssem, rsem,
     alpha, hx, hy, local_sem) = scratch[:20]
    wide = is_wide(R, nbx, nby, L)
    if wide:
        z_in, w_out = scratch[20:]
    else:
        rec_f, ybuf, phat, u = scratch[20:]
    thin = R // nby
    R2 = R + PAD
    bx = lax.axis_index("bx")
    by = lax.axis_index("by")
    group = bx // rep
    part = bx % rep
    scale = 1.0 / (R * nbx * C * nby)
    loads = [pltpu.make_async_copy(src, dst, local_sem.at[at]) for at, (src, dst) in
             enumerate(((alpha_h, alpha), (hx_h, hx), (hy_h, hy)))]
    for load in loads:
        load.start()
    slots = [0]
    sends = []

    barrier = pltpu.get_barrier_semaphore()
    others = [(a, b) for b in range(nby) for a in range(nbx) if a or b]
    greeted = [(a, b) for a, b in others if wide or not a or not b]
    for a, b in greeted:
        pl.semaphore_signal(
            barrier, inc=1, device_id={"bx": (bx + a) % nbx, "by": (by + b) % nby},
            device_id_type=MESH)

    def remote(src, dst, device, slot):
        return pltpu.make_async_remote_copy(
            src_ref=src, dst_ref=dst, send_sem=ssem.at[slot], recv_sem=rsem.at[slot],
            device_id=device, device_id_type=MESH)

    def fresh():
        slots[0] += 1
        return slots[0] - 1

    def push(src, dst, device):
        copy = remote(src, dst, device, fresh())
        copy.start()
        sends.append(copy.wait_send)
        return copy

    rows = lax.broadcasted_iota(jnp.int32, (R, C), 0)
    lanes = lax.broadcasted_iota(jnp.int32, (R, C), 1)

    def x_next(f, high):
        return jnp.where(rows == R - 1, high, pltpu.roll(f, R - 1, 0))

    def x_prev(f, low):
        return jnp.where(rows == 0, low, pltpu.roll(f, 1, 0))

    def y_next(f, high):
        return jnp.where(lanes == C - 1, high, pltpu.roll(f, C - 1, 1))

    def y_prev(f, low):
        return jnp.where(lanes == 0, low, pltpu.roll(f, 1, 1))

    def column_tile(blocks):
        tile = jnp.zeros((R, C), jnp.float32)
        for at, block in enumerate(blocks):
            tile = jnp.where(lanes == at, block[:, 0:1], tile)
            tile = jnp.where(lanes == C // 2 + at, block[:, C - 1:C], tile)
        return tile

    def x_start(src, n):
        mine = inb.at[n, :, pl.ds(pl.multiple_of(bx * R, R), R)]
        copies = []
        for k in range(1, nbx):
            to = (bx + k) % nbx
            copies.append(push(src.at[pl.ds(to // rep * lp, lp)], mine, {"bx": to}))
        for layer in range(lp):
            inb[n, layer, pl.ds(pl.multiple_of(bx * R, R), R)] = src[group * lp + layer]
        return copies

    def x_mix(copies, n):
        for copy in copies:
            copy.wait_recv()
        table = (hx[0], hx[1])
        for layer in range(lp):
            outs[n, :, layer] = product(table, halves(inb[n, layer])).reshape(own, R2, C)

    def spread(n, step):
        copies = []
        for a, b in others:
            to_x, to_y = (bx + a) % nbx, (by + b) % nby
            copies.append(push(
                outs.at[n, to_x, :, pl.ds(pl.multiple_of(to_y * thin, thin), thin)],
                z_in.at[step, by, pl.ds(bx * lp, lp)], {"bx": to_x, "by": to_y}))
        for layer in range(lp):
            z_in[step, by, bx * lp + layer] = outs[
                n, bx, layer, pl.ds(pl.multiple_of(by * thin, thin), thin)]
        for copy in copies:
            copy.wait_recv()

    def collect(n, step):
        at = pl.ds(pl.multiple_of(bx * R + by * thin, thin), thin)
        copies = []
        for a, b in others:
            to_x, to_y = (bx + a) % nbx, (by + b) % nby
            copies.append(push(
                w_out.at[step, to_y, pl.ds(to_x * lp, lp)], inb.at[n, :, at],
                {"bx": to_x, "by": to_y}))
        for layer in range(lp):
            inb[n, layer, at] = w_out[step, by, bx * lp + layer]
        return copies

    def solve(spectrum, height):
        primes = []
        for l in range(L):
            source = spectrum[l * height:(l + 1) * height] * scale
            if l:
                source = source + inter[l] * primes[-1]
            primes.append(source * coef[l])
        values = [primes[-1]]
        for l in range(L - 2, -1, -1):
            values.insert(0, primes[l] + ratio[l] * values[0])
        return values

    def x_finish(n, dst, height):
        waits = []
        landing = dst.at[pl.ds(group * lp, lp)]
        for t in range(own):
            local = (group + t) % own
            to = part * own + local
            src = outs.at[n, local, :, pl.ds(0, height)]
            if rep == 1:
                if t == 0:
                    continue
                waits.append(push(src, landing, {"bx": to}).wait_recv)
                continue
            slot = fresh()

            def go(src=src, to=to, slot=slot):
                remote(src, landing, {"bx": to}, slot).start()

            def gone(src=src, to=to, slot=slot):
                @pl.when(to != bx)
                def _():
                    remote(src, landing, {"bx": to}, slot).wait_send()

            def came(src=src, to=to, slot=slot, t=t):
                origin = (bx % own + own - t) % own * rep + bx // own

                @pl.when(origin != bx)
                def _():
                    remote(src, landing, {"bx": to}, slot).wait_recv()

            pl.when(to != bx)(go)
            sends.append(gone)
            waits.append(came)

        def keep():
            for layer in range(lp):
                dst[group * lp + layer] = outs[n, bx % own, layer, 0:height]

        if rep == 1:
            keep()
        else:
            pl.when(bx // own == part)(keep)
        for wait in waits:
            wait()

    def y_pass(src, n):
        copies = [push(src, ybuf.at[n, k - 1], {"by": (by + k) % nby}) for k in range(1, nby)]
        total = product(halves(src[...].reshape(L * R, C)), (hy[0, by], hy[1, by]))
        for k in range(1, nby):
            copies[k - 1].wait_recv()
            origin = (by + nby - k) % nby
            total += product(halves(ybuf[n, k - 1].reshape(L * R, C)), (hy[0, origin], hy[1, origin]))
        return total

    def flank_start(rows_too, step, src):
        copies = []
        if rows_too:
            for c in range(3):
                for l in range(L):
                    at = c * L + l
                    row_s[step, 0, at:at + 1] = src[c, l, 0:1]
                    row_s[step, 1, at:at + 1] = src[c, l, R - 1:R]
            col_s[step] = column_tile([src[c, l] for c in range(3) for l in range(L)])
            if step == 0:
                pl.semaphore_wait(barrier, len(greeted))
            copies.append(push(row_s.at[step, 1], row_r.at[step, 0], {"bx": (bx + 1) % nbx}))
            copies.append(push(row_s.at[step, 0], row_r.at[step, 1], {"bx": (bx + nbx - 1) % nbx}))
            tile, land = col_s.at[step], col_r
        else:
            pc_s[step] = column_tile([src[l, 0:R] for l in range(L)])
            tile, land = pc_s.at[step], pc_r
        copies.append(push(tile, land.at[step, 0], {"by": (by + 1) % nby}))
        copies.append(push(tile, land.at[step, 1], {"by": (by + nby - 1) % nby}))
        return copies

    for step in range(STEPS):
        src = p_in if step == 0 else p_mid
        flanks = flank_start(True, step, src)
        if step == 0:
            lateral = lam[...]
            previous = None
            for l in range(L):
                pivot = perm[l] * lateral + inter[l] + inter[l + 1]
                if l:
                    pivot = pivot - inter[l] * previous
                inverse = 1.0 / pivot
                coef[l] = inverse
                previous = inter[l + 1] * inverse
                ratio[l] = previous
        for copy in flanks:
            copy.wait_recv()
        low_col = col_r[step, 0]
        high_col = col_r[step, 1]

        def edges(c, l):
            at = c * L + l
            return (row_r[step, 0, at:at + 1], row_r[step, 1, at:at + 1],
                    low_col[:, C // 2 + at:C // 2 + at + 1], high_col[:, at:at + 1])

        zero = jnp.zeros((R, C), jnp.float32)
        for l in range(L):
            low, high, _, _ = edges(0, l)
            _, _, left, right = edges(1, l)
            along_x, along_y = src[0, l], src[1, l]
            above = src[2, l + 1] if l + 1 < L else zero
            below = src[2, l - 1] if l else zero
            q[step, l] = -0.5 * (
                (x_next(along_x, high) - x_prev(along_x, low))
                + (y_next(along_y, right) - y_prev(along_y, left)) + (above - below))
        copies = x_start(q.at[step], 2 * step)
        if step == 0:
            for load in loads:
                load.wait()
        for l in range(L):
            cells = [src[c, l] for c in range(3)]
            squares = [cell * cell for cell in cells]
            whole = squares[0] + squares[1] + squares[2]
            for c in range(3):
                cell, square = cells[c], squares[c]
                low, high, left, right = edges(c, l)
                above = src[c, l + 1] if l + 1 < L else zero
                below = src[c, l - 1] if l else zero
                smooth = stiff[l] * (
                    (x_next(cell, high) + x_prev(cell, low) + y_next(cell, right)
                     + y_prev(cell, left) - 4.0 * cell) + (above + below - 2.0 * cell))
                drive = cell * (
                    2.0 * alpha[l] + 4.0 * landau[0, l] * square
                    + 2.0 * landau[1, l] * (whole - square)
                    + 6.0 * landau[2, l] * (square * square))
                base[c, l] = cell - step_size * (drive - smooth)
        n = 2 * step
        x_mix(copies, n)
        if wide:
            spread(n, step)
            table = (hy[0], hy[1])
            full = jnp.concatenate(
                [z_in[step, j].reshape(L * thin, C) for j in range(nby)], axis=1)
            values = solve(product(halves(full), table), thin)
            full = product(halves(jnp.concatenate(values, axis=0)), table)
            for j in range(nby):
                w_out[step, j] = full[:, j * C:(j + 1) * C].reshape(L, thin, C)
            copies = collect(n + 1, step)
        else:
            x_finish(n, rec_f.at[step], R)
            for l, value in enumerate(solve(y_pass(rec_f.at[step], n), R)):
                phat[step, l] = value
            u[step] = y_pass(phat.at[step], n + 1).reshape(L, R, C)
            copies = x_start(u.at[step], n + 1)
        x_mix(copies, n + 1)
        x_finish(n + 1, rec_i.at[step], R2)
        flanks = flank_start(False, step, rec_i.at[step])
        last = step == STEPS - 1
        target = p_out if last else p_mid
        for l in range(L):
            phi = rec_i[step, l, 0:R]
            low = rec_i[step, l, R:R + 1]
            high = rec_i[step, l, R + 1:R + 2]
            along_x = -0.5 * (x_next(phi, high) - x_prev(phi, low))
            above = rec_i[step, l + 1, 0:R] if l + 1 < L else zero
            below = rec_i[step, l - 1, 0:R] if l else zero
            along_z = -0.5 * (above - below)
            target[0, l] = base[0, l] + step_size * along_x
            target[2, l] = base[2, l] + step_size * along_z
            if last:
                f_out[0, l] = along_x
                f_out[2, l] = along_z
        for copy in flanks:
            copy.wait_recv()
        low_phi = pc_r[step, 0]
        high_phi = pc_r[step, 1]
        for l in range(L):
            phi = rec_i[step, l, 0:R]
            along_y = -0.5 * (y_next(phi, high_phi[:, l:l + 1])
                              - y_prev(phi, low_phi[:, C // 2 + l:C // 2 + l + 1]))
            target[1, l] = base[1, l] + step_size * along_y
            if last:
                f_out[1, l] = along_y
    for wait in sends:
        wait()


def shards(polarization, alpha_field, landau, stiffness, permittivity, interfaces):
    _, L, R, C = polarization.shape
    nbx = lax.axis_size("bx")
    nby = lax.axis_size("by")
    bx = lax.axis_index("bx")
    by = lax.axis_index("by")
    rep = max(1, nbx // L)
    lp = max(1, L // nbx)
    own = nbx // rep
    grid_x, grid_y = nbx * R, nby * C
    R2 = R + PAD
    wide = is_wide(R, nbx, nby, L)
    pool = np if wide else jnp
    make = fixed_table if wide else cas_table
    line = pool.arange(R2, dtype=jnp.int32)
    line = pool.where(line < R, line, pool.where(line == R, -1, R))
    owners = pool.arange(own, dtype=jnp.int32)
    if not wide:
        owners = owners + bx % rep * own
    wanted = ((owners[:, None] * R + line[None, :] + grid_x) % grid_x).reshape(own * R2, 1)
    hx = make(wanted, pool.arange(grid_x, dtype=jnp.int32)[None, :], grid_x)
    every_col = pool.arange(grid_y, dtype=jnp.int32)
    my_rows = bx * R + jnp.arange(R, dtype=jnp.int32)
    my_cols = by * C + jnp.arange(C, dtype=jnp.int32)
    if wide:
        hy = make(every_col[:, None], every_col[None, :], grid_y)
        my_rows = bx * R + by * (R // nby) + jnp.arange(R // nby, dtype=jnp.int32)
        my_cols = jnp.arange(grid_y, dtype=jnp.int32)
    else:
        hy = make(every_col[:, None], my_cols[None, :], grid_y).reshape(2, nby, C, C)
    wave_x = jnp.sin(jnp.pi * my_rows.astype(jnp.float32) / grid_x)
    wave_y = jnp.sin(jnp.pi * my_cols.astype(jnp.float32) / grid_y)
    lam = 4.0 * wave_x[:, None] ** 2 + 4.0 * wave_y[None, :] ** 2
    sizes = (L, R, C, nbx, nby, rep, lp, own)
    n_copies = STEPS * (6 + 2 * (nbx * nby + own if wide else nbx + own + nby))
    f32 = jnp.float32
    vmem = pl.BlockSpec(memory_space=pltpu.VMEM)
    hbm = pl.BlockSpec(memory_space=pltpu.HBM)
    smem = pl.BlockSpec(memory_space=pltpu.SMEM)
    S = STEPS
    scratch = [
        pltpu.VMEM((3, L, R, C), f32), pltpu.VMEM((3, L, R, C), f32),
        pltpu.VMEM((L,) + lam.shape, f32), pltpu.VMEM((L,) + lam.shape, f32),
        pltpu.VMEM((S, L, R, C), f32), pltpu.VMEM((2 * S, lp, grid_x, C), f32),
        pltpu.VMEM((2 * S, own, lp, R2, C), f32), pltpu.VMEM((S, L, R2, C), f32),
        pltpu.VMEM((S, 2, 3 * L, C), f32), pltpu.VMEM((S, 2, 3 * L, C), f32),
        pltpu.VMEM((S, R, C), f32), pltpu.VMEM((S, 2, R, C), f32),
        pltpu.VMEM((S, R, C), f32), pltpu.VMEM((S, 2, R, C), f32),
        pltpu.SemaphoreType.DMA((n_copies,)), pltpu.SemaphoreType.DMA((n_copies,)),
        pltpu.VMEM((L, R, C), f32), pltpu.VMEM(hx.shape, hx.dtype),
        pltpu.VMEM(hy.shape, hy.dtype), pltpu.SemaphoreType.DMA((3,)),
    ]
    if wide:
        thin = (S, nby, L, R // nby, C)
        scratch += [pltpu.VMEM(thin, f32), pltpu.VMEM(thin, f32)]
    else:
        scratch += [
            pltpu.VMEM((S, L, R, C), f32), pltpu.VMEM((2 * S, nby - 1, L, R, C), f32),
            pltpu.VMEM((S, L, R, C), f32), pltpu.VMEM((S, L, R, C), f32),
        ]
    out = jax.ShapeDtypeStruct(polarization.shape, f32)
    return pl.pallas_call(
        functools.partial(kernel, sizes),
        out_shape=(out, out),
        in_specs=[vmem, hbm, smem, smem, smem, smem, vmem, hbm, hbm],
        out_specs=(vmem, vmem),
        scratch_shapes=scratch,
        compiler_params=pltpu.CompilerParams(
            collective_id=0, has_side_effects=True, vmem_limit_bytes=65 * 1000 * 1000),
    )(polarization, alpha_field, landau, stiffness, permittivity, interfaces, lam, hx, hy)


def fits(L, R, C, nbx, nby):
    slab = R // nby
    return (L == nbx and slab == 8 and slab * nby == R and nby > 1 and C % (8 * L) == 0
            and nbx > 2 and nbx & (nbx - 1) == 0 and nby & (nby - 1) == 0)


def partner(index, mask, size):
    other = 0
    bit = 1
    while bit < size:
        here = index // bit % 2
        other = other + bit * (1 - here if mask // bit % 2 else here)
        bit *= 2
    return other


def join(parts, axis):
    return jnp.concatenate(parts, axis=axis)


def fused(sizes, p_h, alpha_h, landau, stiff, perm, inter, wx_h, wy_h, hx_h, hy_h,
          base_o, down_o, *scratch):
    L, R, C, nbx, nby = sizes
    (p_mid, base, coef, ratio, a_s, a_r, b_s, b_r, c_s, c_r, d_s, d_r,
     row_s, row_r, col_s, col_r, ssem, rsem, known, p_in, alpha, wx, wy, hx, hy, local_sem) = scratch
    slab = R // nby
    per = C // L
    NX, NY = nbx * R, nby * C
    bx = lax.axis_index("bx")
    by = lax.axis_index("by")
    scale = 1.0 / (NX * NY)
    f32 = jnp.float32
    dot = functools.partial(jnp.dot, preferred_element_type=f32)
    slots = [0]
    sends = []

    barrier = pltpu.get_barrier_semaphore()
    at_x = [partner(bx, a, nbx) for a in range(nbx)]
    at_y = [partner(by, b, nby) for b in range(nby)]
    others = [(a, b) for b in range(nby) for a in range(nbx) if a or b]
    others.sort(key=lambda ab: -(ab[0] // 2 + ab[0] % 2 + ab[1] // 2))
    reach = [1 << i for i in range(1, nbx.bit_length() - 1)]
    greeted = [(a, b) for a, b in others if a < 2] + [(a, 0) for a in reach]
    for a, b in greeted:
        pl.semaphore_signal(
            barrier, inc=1, device_id={"bx": at_x[a], "by": at_y[b]}, device_id_type=MESH)
    mine = pl.multiple_of((bx * nby + by) * per, per)
    loads = [pltpu.make_async_copy(src, dst, local_sem.at[at]) for at, (src, dst) in enumerate((
        (p_h, p_in), (alpha_h, alpha), (wx_h, wx), (wy_h.at[pl.ds(mine, per)], wy), (hx_h, hx),
        (hy_h, hy)))]
    for load in loads:
        load.start()

    def push(src, dst, device):
        slot = slots[0]
        slots[0] += 1
        copy = pltpu.make_async_remote_copy(
            src_ref=src, dst_ref=dst, send_sem=ssem.at[slot], recv_sem=rsem.at[slot],
            device_id=device, device_id_type=MESH)
        copy.start()
        sends.append(copy.wait_send)
        return copy

    rows = lax.broadcasted_iota(jnp.int32, (R, C), 0)
    lanes = lax.broadcasted_iota(jnp.int32, (R, C), 1)
    rows8 = lax.broadcasted_iota(jnp.int32, (slab, C), 0)
    lanes8 = lax.broadcasted_iota(jnp.int32, (slab, C), 1)
    zero = jnp.zeros((R, C), f32)
    zero8 = jnp.zeros((slab, C), f32)

    def x_next(f, high):
        return jnp.where(rows == R - 1, high, pltpu.roll(f, R - 1, 0))

    def x_prev(f, low):
        return jnp.where(rows == 0, low, pltpu.roll(f, 1, 0))

    def y_next(f, high):
        return jnp.where(lanes == C - 1, high, pltpu.roll(f, C - 1, 1))

    def y_prev(f, low):
        return jnp.where(lanes == 0, low, pltpu.roll(f, 1, 1))

    def flush(keep):
        while len(sends) > keep:
            sends.pop(0)()

    def charge(n, src, ring):
        sides = (0, nby - 1)
        edge = zero
        for l in range(L):
            along_x, along_y = src[0, l], src[1, l]
            above = src[2, l + 1] if l + 1 < L else zero
            below = src[2, l - 1] if l else zero
            low = high = left = right = 0.0
            if ring:
                lines, column = ring
                low, high = lines[0][0][l:l + 1], lines[1][0][l:l + 1]
                left = column[:, L + l:L + l + 1]
                right = column[:, C // 2 + L + l:C // 2 + L + l + 1]
            value = -0.5 * ((x_next(along_x, high) - x_prev(along_x, low))
                            + (y_next(along_y, right) - y_prev(along_y, left)) + (above - below))
            for j in range(nby):
                a_s[n, j, l] = value[j * slab:(j + 1) * slab]
            edge = jnp.where(lanes == l, -0.5 * along_y[:, 0:1], edge)
            edge = jnp.where(lanes == L + l, 0.5 * along_y[:, C - 1:C], edge)
        near = [-0.5 * join([src[0, l, 0:1] for l in range(L)], 0),
                0.5 * join([src[0, l, R - 1:R] for l in range(L)], 0)]
        corner = [None, None]
        if ring:
            for side, sign in enumerate((-0.5, 0.5)):
                first, second, third = lines[side]
                turned = (jnp.where(lanes8 == C - 1, 0.0, pltpu.roll(second, C - 1, 1))
                          - jnp.where(lanes8 == 0, 0.0, pltpu.roll(second, 1, 1)))
                risen = (jnp.where(rows8 == L - 1, 0.0, pltpu.roll(third, L - 1, 0))
                         - jnp.where(rows8 == 0, 0.0, pltpu.roll(third, 1, 0)))
                near[side] = near[side] - 0.5 * (turned + risen)
                a_s[n, sides[side], L + 2] = sign * first
                corner[side] = jnp.where(
                    lanes8 == 4 * L, sign * first[:, 0:1] - 0.5 * second[:, 0:1],
                    jnp.where(lanes8 == 4 * L + 1,
                              sign * first[:, C - 1:C] + 0.5 * second[:, C - 1:C], 0.0))
            layer = lanes % L
            turned = -0.5 * (x_next(column, 0.0) - x_prev(column, 0.0))
            risen = -0.5 * (jnp.where(layer == L - 1, 0.0, pltpu.roll(column, C - 1, 1))
                            - jnp.where(layer == 0, 0.0, pltpu.roll(column, 1, 1)))
            both = turned + pltpu.roll(risen, C - 2 * L, 1)
            low = edge + both
            high = edge + pltpu.roll(both, C // 2 + L, 1)
            far_low = -0.5 * pltpu.roll(column, L, 1)
            far_high = 0.5 * pltpu.roll(column, C // 2 + 2 * L, 1)
            group = lanes // L
            edge = jnp.where(group == 0, low, jnp.where(group == 1, high, jnp.where(
                group == 2, far_low, jnp.where(group == 3, far_high, 0.0))))
        for side in range(2):
            a_s[n, sides[side], L + 1] = near[side]
        for j in range(nby):
            piece = edge[j * slab:(j + 1) * slab]
            if ring and j in sides:
                piece = piece + corner[sides.index(j)]
            a_s[n, j, L] = piece
            if j not in sides:
                a_s[n, j, L + 1:L + 3] = jnp.zeros((2, slab, C), f32)

    def ring_of(n):
        weight8 = zero8
        weight = zero
        layer = lanes % L
        for l in range(L):
            weight8 = jnp.where(rows8 == l, step_size * stiff[l], weight8)
            weight = jnp.where(layer == l, step_size * stiff[l], weight)
        lines = [[weight8 * row_s[n, side, c * L:(c + 1) * L] for c in range(3)]
                 for side in range(2)]
        return lines, weight * col_s[n]

    rim_slab = (by == 0) | (by == nby - 1)

    def has_rim(b, here):
        return nby != 4 or (b in (0, nby - 1)) == here

    def either(action):
        if nby != 4:
            action(True)
        else:
            pl.when(rim_slab)(functools.partial(action, True))
            pl.when(jnp.logical_not(rim_slab))(functools.partial(action, False))

    def exchange(targets, build, by_target):
        first = slots[0]
        slots[0] += len(targets)

        def make(at, whole):
            a, b = targets[at]
            src, dst = build(a, b, whole)
            return pltpu.make_async_remote_copy(
                src_ref=src, dst_ref=dst, send_sem=ssem.at[first + at],
                recv_sem=rsem.at[first + at], device_id={"bx": at_x[a], "by": at_y[b]},
                device_id_type=MESH)

        def outgoing(here):
            return [make(at, has_rim(b, here) if by_target else here)
                    for at, (a, b) in enumerate(targets)]

        def start(here):
            for copy in outgoing(here):
                copy.start()

        def sent(here):
            for copy in outgoing(here):
                copy.wait_send()

        def came(here):
            for at, (a, b) in enumerate(targets):
                make(at, here if by_target else has_rim(b, here)).wait_recv()

        either(start)
        sends.append(functools.partial(either, sent))
        return functools.partial(either, came)

    def among_y(source, landing, n, count, by_target):
        def build(a, b, whole):
            part = pl.ds(0, count if whole else L + 1)
            return source.at[n, at_y[b], part], landing.at[n, by, part]

        arrive = exchange([(0, b) for b in range(nby - 1, 0, -1)], build, by_target)
        landing[n, by, 0:count] = source[n, by, 0:count]
        return arrive

    def wait(copies):
        if callable(copies):
            copies()
        else:
            for copy in copies:
                copy.wait_recv()

    def spread(source, landing, n, flip, thick):
        def build(a, b, whole):
            part = pl.ds(0, thick if whole else slab)
            to_x, to_y = at_x[a], at_y[b]
            if flip:
                return source.at[n, to_x, to_y, part], landing.at[n, by, bx, part]
            return source.at[n, to_y, to_x, part], landing.at[n, bx, by, part]

        arrive = exchange(others, build, flip)
        if flip:
            landing[n, by, bx, 0:thick] = source[n, bx, by, 0:thick]
        else:
            landing[n, bx, by, 0:thick] = source[n, by, bx, 0:thick]
        return arrive

    def clear_rims():
        for n in range(2):
            for j in range(nby):
                a_r[n, j, L + 1:L + 3] = jnp.zeros((2, slab, C), f32)
                for e in range(nbx):
                    c_r[n, j, e, slab:2 * slab] = zero8

    def swap_groups(tiles):
        height = tiles[0].shape[0]
        group = lax.broadcasted_iota(jnp.int32, (height, C), 1) // per
        tiles = list(tiles)
        s = 1
        while s < L:
            upper = group % (2 * s) >= s
            for at in range(L):
                if at % (2 * s) < s:
                    low, high = tiles[at], tiles[at + s]
                    tiles[at] = jnp.where(upper, pltpu.roll(high, s * per, 1), low)
                    tiles[at + s] = jnp.where(upper, high, pltpu.roll(low, C - s * per, 1))
            s *= 2
        return tiles

    def swap_rows(tile):
        group = lanes8 // per
        s = 1
        while s < L:
            upper = group % (2 * s) >= s
            later = rows8 % (2 * s) >= s
            ahead = pltpu.roll(pltpu.roll(tile, L - s, 0), s * per, 1)
            behind = pltpu.roll(pltpu.roll(tile, s, 0), C - s * per, 1)
            tile = jnp.where(later, jnp.where(upper, tile, behind), jnp.where(upper, ahead, tile))
            s *= 2
        return tile

    def times(full, table):
        height = full.shape[0]
        high = full.astype(jnp.bfloat16)
        wide = high.astype(f32)
        both = join([wide, full - wide], 0).astype(jnp.bfloat16)
        first = dot(both, hy[table, 0])
        return first[:height] + first[height:] + dot(high, hy[table, 1])

    def y_forward(n):
        columns = []
        for j in range(nby):
            from_left = a_r[n, (j + nby - 1) % nby, L]
            from_right = a_r[n, (j + 1) % nby, L]
            tiles = []
            for l in range(L):
                extra = jnp.where(
                    lanes8 == 0, from_left[:, L + l:L + l + 1],
                    jnp.where(lanes8 == C - 1, from_right[:, l:l + 1], 0.0))
                if n:
                    extra = jnp.where(
                        lanes8 == 1, from_left[:, 3 * L + l:3 * L + l + 1],
                        jnp.where(lanes8 == C - 2, from_right[:, 2 * L + l:2 * L + l + 1], extra))
                tiles.append(a_r[n, j, l] + extra)
            near, far = a_r[n, j, L + 1], zero8
            if n:
                near = near + jnp.where(
                    lanes8 == 0, from_left[:, 4 * L + 1:4 * L + 2],
                    jnp.where(lanes8 == C - 1, from_right[:, 4 * L:4 * L + 1], 0.0))
                far = a_r[n, j, L + 2]
            columns.append(join(tiles + [near, far], 0))
        low, high = join(columns[:nby // 2], 1), join(columns[nby // 2:], 1)
        out = join([times(low + high, 0), times(low - high, 1)], 1)
        tiles = [join([out[l * slab:(l + 1) * slab, t * C:(t + 1) * C] for t in range(nby)], 0)
                 for l in range(L)]
        tiles = swap_groups(tiles)
        for t in range(nby):
            halos = [swap_rows(out[(L + k) * slab:(L + k) * slab + L, t * C:(t + 1) * C])
                     for k in range(1 + n)]
            for e in range(L):
                b_s[n, t, e, 0:slab] = tiles[e][t * slab:(t + 1) * slab]
                for k, halo in enumerate(halos):
                    b_s[n, t, e, slab + k:slab + k + 1] = halo[e:e + 1]

    def y_backward(n):
        tiles = swap_groups([join([c_r[n, t, e, 0:slab] for t in range(nby)], 0)
                             for e in range(L)])
        rims = [join([swap_rows(join([c_r[n, t, e, slab + k:slab + k + 1] for e in range(L)], 0))
                      for t in range(nby)], 1) for k in range(2 - n)]
        if n:
            rims.append(jnp.zeros((slab, NY), f32))
        lines = [join([tiles[l][t * slab:(t + 1) * slab] for t in range(nby)], 1)
                 for l in range(L)]
        full = join(lines + rims, 0)
        even, odd = times(full[:, :NY // 2], 0), times(full[:, NY // 2:], 2)
        out = join([even + odd, even - odd], 1)
        near = out[L * slab:L * slab + L]
        for j in range(nby):
            edge = zero8
            left, right = (j + nby - 1) % nby * C, (j + 1) % nby * C
            wanted = [left + C - 1, right]
            if n == 0:
                wanted += [left + C - 2, right + 1, None, j * C, j * C + C - 1]
                edge = jnp.where(lanes8 == 4 * L, near[:, left + C - 1:left + C],
                                 jnp.where(lanes8 == 4 * L + 1, near[:, right:right + 1], edge))
            for l in range(L):
                line = out[l * slab:(l + 1) * slab]
                d_s[n, j, l] = line[:, j * C:(j + 1) * C]
                for at, column in enumerate(wanted):
                    if column is not None:
                        edge = jnp.where(
                            lanes8 == at * L + l, line[:, column:column + 1], edge)
            d_s[n, j, L] = edge
            for k in range(2 - n):
                d_s[n, j, L + 1 + k] = out[(L + k) * slab:(L + k) * slab + L,
                                           j * C:(j + 1) * C]

    def spectrum(n):
        tiles = []
        for i in range(nbx):
            for j in range(nby):
                tile = b_r[n, i, j, 0:slab]
                for k in range(1 + n):
                    line = slice(slab + k, slab + k + 1)
                    if j == 0:
                        tile = tile + jnp.where(
                            rows8 == k, b_r[n, (i + nbx - 1) % nbx, nby - 1, line], 0.0)
                    if j == nby - 1:
                        tile = tile + jnp.where(
                            rows8 == slab - 1 - k, b_r[n, (i + 1) % nbx, 0, line], 0.0)
                tiles.append(tile)
        full = join(tiles, 0).T
        high = full.astype(jnp.bfloat16)
        wide = high.astype(f32)
        both = join([wide, full - wide], 0).astype(jnp.bfloat16)
        first = dot(both, hx[0])
        out = (first[:C] + first[C:] + dot(high, hx[1])) * scale
        return [out[l * per:(l + 1) * per] for l in range(L)]

    def solve(sources):
        primes = []
        for l in range(L):
            source = sources[l]
            if l:
                source = source + inter[l] * primes[-1]
            primes.append(source * coef[l])
        values = [primes[-1]]
        for l in range(L - 2, -1, -1):
            values.insert(0, primes[l] + ratio[l] * values[0])
        return values

    def x_backward(n, values):
        high, low = halves(join(values, 0))
        turn = functools.partial(
            lax.dot_general, dimension_numbers=(((1,), (1,)), ((), ())),
            preferred_element_type=f32)
        first = turn(hx[...].reshape(2 * NX, NX), high)
        out = first[:NX] + first[NX:] + turn(hx[0], low)
        for i in range(nbx):
            for j in range(nby):
                at = i * R + j * slab
                c_s[n, i, j, 0:slab] = out[at:at + slab]
                for k in range(2 - n):
                    line = (at - 1 - k if j == 0 else at + slab + k) % NX
                    c_s[n, i, j, slab + k:slab + k + 1] = out[line:line + 1]

    def flank_start(n, src):
        tile = zero
        for c in range(3):
            for l in range(L):
                at = c * L + l
                cell = src[c, l]
                row_s[n, 0, at:at + 1] = cell[0:1]
                row_s[n, 1, at:at + 1] = cell[R - 1:R]
                tile = jnp.where(lanes == at, cell[:, 0:1], tile)
                tile = jnp.where(lanes == C // 2 + at, cell[:, C - 1:C], tile)
        col_s[n] = tile

    def flank_send(n):
        return [
            push(row_s.at[n, 1], row_r.at[n, 0], {"bx": (bx + 1) % nbx}),
            push(row_s.at[n, 0], row_r.at[n, 1], {"bx": (bx + nbx - 1) % nbx}),
            push(col_s.at[n], col_r.at[n, 0], {"by": (by + 1) % nby}),
            push(col_s.at[n], col_r.at[n, 1], {"by": (by + nby - 1) % nby})]

    def relax_inside(src):
        for l in range(L):
            cells = [src[c, l] for c in range(3)]
            squares = [cell * cell for cell in cells]
            whole = squares[0] + squares[1] + squares[2]
            for c in range(3):
                cell, square = cells[c], squares[c]
                above = src[c, l + 1] if l + 1 < L else zero
                below = src[c, l - 1] if l else zero
                smooth = stiff[l] * (
                    (x_next(cell, 0.0) + x_prev(cell, 0.0) + y_next(cell, 0.0)
                     + y_prev(cell, 0.0) - 4.0 * cell) + (above + below - 2.0 * cell))
                drive = cell * (
                    2.0 * alpha[l] + 4.0 * landau[0, l] * square
                    + 2.0 * landau[1, l] * (whole - square)
                    + 6.0 * landau[2, l] * (square * square))
                base[c, l] = cell - step_size * (drive - smooth)

    def flank_lines(n):
        return [[row_r[n, side, c * L:(c + 1) * L] for c in range(3)] for side in range(2)]

    def relax_edges(lines, low_col, high_col, target):
        for l in range(L):
            weight = step_size * stiff[l]
            for c in range(3):
                at = c * L + l
                add = jnp.where(lanes == 0, low_col[:, C // 2 + at:C // 2 + at + 1], 0.0)
                add = add + jnp.where(lanes == C - 1, high_col[:, at:at + 1], 0.0)
                add = add + jnp.where(rows == 0, lines[0][c][l:l + 1], 0.0)
                add = add + jnp.where(rows == R - 1, lines[1][c][l:l + 1], 0.0)
                target[c, l] = base[c, l] + weight * add

    def moved_rim():
        lines = flank_lines(1)
        corners = []
        for side, owner in enumerate((0, nby - 1)):
            inner = join([d_r[0, owner, l, side * (slab - 1):side * (slab - 1) + 1]
                          for l in range(L)], 0)
            near, far = d_r[0, owner, L + 1], d_r[0, owner, L + 2]
            edge = d_r[0, owner, L]
            low, high = edge[:, 4 * L:4 * L + 1], edge[:, 4 * L + 1:4 * L + 2]
            down = [inner - far if side == 0 else far - inner,
                    jnp.where(lanes8 == C - 1, high, pltpu.roll(near, C - 1, 1))
                    - jnp.where(lanes8 == 0, low, pltpu.roll(near, 1, 1)),
                    jnp.where(rows8 == L - 1, 0.0, pltpu.roll(near, L - 1, 0))
                    - jnp.where(rows8 == 0, 0.0, pltpu.roll(near, 1, 0))]
            lines[side] = [line - (0.5 * step_size) * part
                           for line, part in zip(lines[side], down)]
            spot = jnp.where(lanes8 == rows8, low, jnp.where(lanes8 == rows8 + L, high, 0.0))
            corners.append(jnp.sum(spot, axis=0, keepdims=True))
        edge = join([d_r[0, j, L] for j in range(nby)], 0)
        layer = lanes % L
        group = lanes // L
        across = pltpu.roll(edge, C - 5 * L, 1) - pltpu.roll(edge, C - 2 * L, 1)
        down = [x_next(edge, corners[1]) - x_prev(edge, corners[0]),
                jnp.where(group == 0, across, -across),
                jnp.where(layer == L - 1, 0.0, pltpu.roll(edge, C - 1, 1))
                - jnp.where(layer == 0, 0.0, pltpu.roll(edge, 1, 1))]
        low_col, high_col = col_r[1, 0], col_r[1, 1]
        for c in range(3):
            part = (0.5 * step_size) * down[c]
            low_col = low_col - jnp.where(
                group == C // (2 * L) + c, pltpu.roll(part, C // 2 + c * L, 1), 0.0)
            high_col = high_col - jnp.where(
                group == c, pltpu.roll(part, (C + c * L - L) % C, 1), 0.0)
        return lines, low_col, high_col

    def field(n):
        edge = join([d_r[n, j, L] for j in range(nby)], 0)
        phis = [join([d_r[n, j, l] for j in range(nby)], 0) for l in range(L)]
        for l in range(L):
            phi = phis[l]
            low = d_r[n, 0, L + 1, l:l + 1]
            high = d_r[n, nby - 1, L + 1, l:l + 1]
            along_x = 0.5 * (x_next(phi, high) - x_prev(phi, low))
            along_y = 0.5 * (y_next(phi, edge[:, L + l:L + l + 1])
                             - y_prev(phi, edge[:, l:l + 1]))
            above = phis[l + 1] if l + 1 < L else zero
            below = phis[l - 1] if l else zero
            yield l, (along_x, along_y, 0.5 * (above - below))

    loads[0].wait()
    charge(0, p_in, None)
    pl.semaphore_wait(barrier, len(greeted))

    def tell(at):
        pl.semaphore_signal(
            known.at[at], inc=1, device_id={"bx": at_x[reach[at]]}, device_id_type=MESH)

    tell(0)
    if nby == 4:
        pl.when(jnp.logical_not(rim_slab))(clear_rims)
    first_a = among_y(a_s, a_r, 0, L + 2, True)
    flank_start(0, p_in)
    loads[1].wait()
    relax_inside(p_in)
    charge(1, base, ring_of(0))
    second_a = among_y(a_s, a_r, 1, L + 3, True)
    for at in range(1, len(reach)):
        pl.semaphore_wait(known.at[at - 1], 1)
        tell(at)
    loads[2].wait()
    loads[3].wait()
    wave_x = wx[0:1]
    wave_y = join([wy[...]] * (NX // C), 1)
    lateral = wave_x + wave_y
    previous = None
    for l in range(L):
        pivot = perm[l] * lateral + inter[l] + inter[l + 1]
        if l:
            pivot = pivot - inter[l] * previous
        inverse = 1.0 / pivot
        coef[l] = inverse
        previous = inter[l + 1] * inverse
        ratio[l] = previous
    loads[4].wait()
    loads[5].wait()
    wait(first_a)
    y_forward(0)
    pl.semaphore_wait(known.at[len(reach) - 1], 1)
    first_b = spread(b_s, b_r, 0, False, slab + 1)
    wait(second_a)
    y_forward(1)
    second_b = spread(b_s, b_r, 1, False, slab + 2)
    flanks = flank_send(0)
    wait(first_b)
    values = solve(spectrum(0))
    x_backward(0, values)
    first_c = spread(c_s, c_r, 0, True, slab + 2)
    bend = -(wave_x * (1.0 - 0.25 * wave_x) + wave_y * (1.0 - 0.25 * wave_y))
    slopes = []
    none = jnp.zeros_like(values[0])
    for l in range(L):
        above = values[l + 1] if l + 1 < L else none
        below = values[l - 1] if l else none
        slopes.append(0.5 * (above - below))
    moved = []
    for l in range(L):
        above = slopes[l + 1] if l + 1 < L else none
        below = slopes[l - 1] if l else none
        moved.append(step_size * (bend * values[l] + 0.5 * (above - below)))
    wait(second_b)
    x_backward(1, solve([here + more for here, more in zip(spectrum(1), moved)]))
    second_c = spread(c_s, c_r, 1, True, slab + 1)
    wait(flanks)
    relax_edges(flank_lines(0), col_r[0, 0], col_r[0, 1], base)
    flank_start(1, base)
    flanks = flank_send(1)
    flush(len(flanks) + 2)
    wait(first_c)
    y_backward(0)
    first_d = among_y(d_s, d_r, 0, L + 3, False)
    wait(second_c)
    y_backward(1)
    second_d = among_y(d_s, d_r, 1, L + 2, False)
    wait(first_d)
    for l, parts in field(0):
        for c in range(3):
            p_mid[c, l] = base[c, l] - step_size * parts[c]
    wait(flanks)
    rim = moved_rim()
    relax_inside(p_mid)
    relax_edges(*rim, base_o)
    flush(1)
    wait(second_d)
    for l, parts in field(1):
        for c in range(3):
            down_o[c, l] = parts[c]
    flush(0)


def fused_shards(polarization, alpha_field, landau, stiffness, permittivity, interfaces):
    _, L, R, C = polarization.shape
    nbx = lax.axis_size("bx")
    nby = lax.axis_size("by")
    grid_x, grid_y = nbx * R, nby * C
    per = C // L
    line = np.arange(grid_x)
    hx = fixed_table(line[:, None], line[None, :], grid_x)
    line = np.arange(grid_y // 2)
    modes = np.concatenate([2 * line, 2 * line + 1])
    hy = jnp.stack([fixed_table(left, right, grid_y) for left, right in (
        (line[:, None], 2 * line[None, :]), (line[:, None], 2 * line[None, :] + 1),
        (2 * line[:, None] + 1, line[None, :]))])
    wave_x = 4.0 * np.sin(np.pi * np.arange(grid_x) / grid_x) ** 2
    wave_x = jnp.asarray(np.tile(wave_x[None, :], (8, 1)).astype(np.float32))
    at = np.arange(nbx * nby)
    first = (at % nby) * C + (at // nby) * per
    mode = modes[(first[:, None] + np.arange(per)[None, :]).reshape(-1)]
    wave_y = 4.0 * np.sin(np.pi * mode / grid_y) ** 2
    wave_y = jnp.asarray(np.tile(wave_y[:, None], (1, C)).astype(np.float32))
    f32 = jnp.float32
    hbm = pl.BlockSpec(memory_space=pltpu.HBM)
    smem = pl.BlockSpec(memory_space=pltpu.SMEM)
    S = 2
    n_copies = S * (4 + 2 * (nby - 1) + 2 * (nbx * nby - 1))
    by_y = pltpu.VMEM((S, nby, L + 3, 8, C), f32)
    by_mode = pltpu.VMEM((S, nby, nbx, 16, C), f32)
    by_place = pltpu.VMEM((S, nbx, nby, 16, C), f32)
    scratch = [
        pltpu.VMEM((3, L, R, C), f32), pltpu.VMEM((3, L, R, C), f32),
        pltpu.VMEM((L, per, grid_x), f32), pltpu.VMEM((L, per, grid_x), f32),
        by_y, by_y, by_mode, by_place, by_place, by_mode, by_y, by_y,
        pltpu.VMEM((S, 2, 3 * L, C), f32), pltpu.VMEM((S, 2, 3 * L, C), f32),
        pltpu.VMEM((S, R, C), f32), pltpu.VMEM((S, 2, R, C), f32),
        pltpu.SemaphoreType.DMA((n_copies,)), pltpu.SemaphoreType.DMA((n_copies,)),
        pltpu.SemaphoreType.REGULAR((nbx.bit_length(),)), pltpu.VMEM((3, L, R, C), f32),
        pltpu.VMEM((L, R, C), f32), pltpu.VMEM(wave_x.shape, f32), pltpu.VMEM((per, C), f32),
        pltpu.VMEM(hx.shape, hx.dtype), pltpu.VMEM(hy.shape, hy.dtype),
        pltpu.SemaphoreType.DMA((6,)),
    ]
    out = pltpu.VMEM(polarization.shape, f32)
    base, down = pl.pallas_call(
        functools.partial(fused, (L, R, C, nbx, nby)),
        out_shape=(out, out),
        in_specs=[hbm, hbm, smem, smem, smem, smem, hbm, hbm, hbm, hbm],
        out_specs=(pl.BlockSpec(memory_space=pltpu.VMEM), pl.BlockSpec(memory_space=pltpu.VMEM)),
        scratch_shapes=scratch,
        compiler_params=pltpu.CompilerParams(
            collective_id=0, has_side_effects=True, vmem_limit_bytes=66 * 1000 * 1000),
    )(polarization, alpha_field, landau, stiffness, permittivity, interfaces,
      wave_x, wave_y, hx, hy)
    return base - step_size * down, -down


def solution(mesh):
    def run(polarization, *rest):
        _, L, R, C = polarization.shape
        body = fused_shards if fits(L, R, C, lax.axis_size("bx"), lax.axis_size("by")) else shards
        return body(polarization, *rest)

    return jax.shard_map(
        run,
        mesh=mesh,
        in_specs=(P(None, None, "bx", "by"), P(None, "bx", "by"), P(), P(), P(), P()),
        out_specs=(P(None, None, "bx", "by"), P(None, None, "bx", "by")),
        check_vma=False,
    )
```

```python
import functools

import jax
import jax.numpy as jnp
import numpy as np
from jax import lax
from jax.experimental import pallas as pl
from jax.experimental.pallas import tpu as pltpu
from jax.sharding import PartitionSpec as P

STEPS = 2
step_size = 0.05
MESH = pl.DeviceIdType.MESH
PAD = 8


def cas_table(left, right, length):
    turns = left * right % length
    angle = 2.0 * jnp.pi / length * turns.astype(jnp.float32)
    table = jnp.cos(angle) + jnp.sin(angle)
    high = lax.reduce_precision(table, 8, 7)
    return jnp.stack([high.astype(jnp.bfloat16), (table - high).astype(jnp.bfloat16)])


def fixed_table(left, right, length):
    angle = 2.0 * np.pi / length * (left * right % length)
    table = (np.cos(angle) + np.sin(angle)).astype(np.float32)
    high = table.astype(jnp.bfloat16)
    low = (table - high.astype(np.float32)).astype(jnp.bfloat16)
    return jnp.asarray(np.stack([high, low]))


def is_wide(rows, nbx, nby, layers):
    return layers % nbx == 0 and rows % (8 * nby) == 0


def halves(value):
    high = value.astype(jnp.bfloat16)
    low = (value - high.astype(jnp.float32)).astype(jnp.bfloat16)
    return high, low


def product(left, right):
    dot = functools.partial(jnp.dot, preferred_element_type=jnp.float32)
    return dot(left[0], right[0]) + (dot(left[0], right[1]) + dot(left[1], right[0]))


def kernel(sizes, p_in, alpha_h, landau, stiff, perm, inter, lam, hx_h, hy_h, p_out, f_out, *scratch):
    L, R, C, nbx, nby, rep, lp, own = sizes
    (p_mid, base, coef, ratio, q, inb, outs, rec_i,
     row_s, row_r, col_s, col_r, pc_s, pc_r, ssem, rsem,
     alpha, hx, hy, local_sem) = scratch[:20]
    wide = is_wide(R, nbx, nby, L)
    if wide:
        z_in, w_out = scratch[20:]
    else:
        rec_f, ybuf, phat, u = scratch[20:]
    thin = R // nby
    R2 = R + PAD
    bx = lax.axis_index("bx")
    by = lax.axis_index("by")
    group = bx // rep
    part = bx % rep
    scale = 1.0 / (R * nbx * C * nby)
    loads = [pltpu.make_async_copy(src, dst, local_sem.at[at]) for at, (src, dst) in
             enumerate(((alpha_h, alpha), (hx_h, hx), (hy_h, hy)))]
    for load in loads:
        load.start()
    slots = [0]
    sends = []

    barrier = pltpu.get_barrier_semaphore()
    others = [(a, b) for b in range(nby) for a in range(nbx) if a or b]
    greeted = [(a, b) for a, b in others if wide or not a or not b]
    for a, b in greeted:
        pl.semaphore_signal(
            barrier, inc=1, device_id={"bx": (bx + a) % nbx, "by": (by + b) % nby},
            device_id_type=MESH)

    def remote(src, dst, device, slot):
        return pltpu.make_async_remote_copy(
            src_ref=src, dst_ref=dst, send_sem=ssem.at[slot], recv_sem=rsem.at[slot],
            device_id=device, device_id_type=MESH)

    def fresh():
        slots[0] += 1
        return slots[0] - 1

    def push(src, dst, device):
        copy = remote(src, dst, device, fresh())
        copy.start()
        sends.append(copy.wait_send)
        return copy

    rows = lax.broadcasted_iota(jnp.int32, (R, C), 0)
    lanes = lax.broadcasted_iota(jnp.int32, (R, C), 1)

    def x_next(f, high):
        return jnp.where(rows == R - 1, high, pltpu.roll(f, R - 1, 0))

    def x_prev(f, low):
        return jnp.where(rows == 0, low, pltpu.roll(f, 1, 0))

    def y_next(f, high):
        return jnp.where(lanes == C - 1, high, pltpu.roll(f, C - 1, 1))

    def y_prev(f, low):
        return jnp.where(lanes == 0, low, pltpu.roll(f, 1, 1))

    def column_tile(blocks):
        tile = jnp.zeros((R, C), jnp.float32)
        for at, block in enumerate(blocks):
            tile = jnp.where(lanes == at, block[:, 0:1], tile)
            tile = jnp.where(lanes == C // 2 + at, block[:, C - 1:C], tile)
        return tile

    def x_start(src, n):
        mine = inb.at[n, :, pl.ds(pl.multiple_of(bx * R, R), R)]
        copies = []
        for k in range(1, nbx):
            to = (bx + k) % nbx
            copies.append(push(src.at[pl.ds(to // rep * lp, lp)], mine, {"bx": to}))
        for layer in range(lp):
            inb[n, layer, pl.ds(pl.multiple_of(bx * R, R), R)] = src[group * lp + layer]
        return copies

    def x_mix(copies, n):
        for copy in copies:
            copy.wait_recv()
        table = (hx[0], hx[1])
        for layer in range(lp):
            outs[n, :, layer] = product(table, halves(inb[n, layer])).reshape(own, R2, C)

    def spread(n, step):
        copies = []
        for a, b in others:
            to_x, to_y = (bx + a) % nbx, (by + b) % nby
            copies.append(push(
                outs.at[n, to_x, :, pl.ds(pl.multiple_of(to_y * thin, thin), thin)],
                z_in.at[step, by, pl.ds(bx * lp, lp)], {"bx": to_x, "by": to_y}))
        for layer in range(lp):
            z_in[step, by, bx * lp + layer] = outs[
                n, bx, layer, pl.ds(pl.multiple_of(by * thin, thin), thin)]
        for copy in copies:
            copy.wait_recv()

    def collect(n, step):
        at = pl.ds(pl.multiple_of(bx * R + by * thin, thin), thin)
        copies = []
        for a, b in others:
            to_x, to_y = (bx + a) % nbx, (by + b) % nby
            copies.append(push(
                w_out.at[step, to_y, pl.ds(to_x * lp, lp)], inb.at[n, :, at],
                {"bx": to_x, "by": to_y}))
        for layer in range(lp):
            inb[n, layer, at] = w_out[step, by, bx * lp + layer]
        return copies

    def solve(spectrum, height):
        primes = []
        for l in range(L):
            source = spectrum[l * height:(l + 1) * height] * scale
            if l:
                source = source + inter[l] * primes[-1]
            primes.append(source * coef[l])
        values = [primes[-1]]
        for l in range(L - 2, -1, -1):
            values.insert(0, primes[l] + ratio[l] * values[0])
        return values

    def x_finish(n, dst, height):
        waits = []
        landing = dst.at[pl.ds(group * lp, lp)]
        for t in range(own):
            local = (group + t) % own
            to = part * own + local
            src = outs.at[n, local, :, pl.ds(0, height)]
            if rep == 1:
                if t == 0:
                    continue
                waits.append(push(src, landing, {"bx": to}).wait_recv)
                continue
            slot = fresh()

            def go(src=src, to=to, slot=slot):
                remote(src, landing, {"bx": to}, slot).start()

            def gone(src=src, to=to, slot=slot):
                @pl.when(to != bx)
                def _():
                    remote(src, landing, {"bx": to}, slot).wait_send()

            def came(src=src, to=to, slot=slot, t=t):
                origin = (bx % own + own - t) % own * rep + bx // own

                @pl.when(origin != bx)
                def _():
                    remote(src, landing, {"bx": to}, slot).wait_recv()

            pl.when(to != bx)(go)
            sends.append(gone)
            waits.append(came)

        def keep():
            for layer in range(lp):
                dst[group * lp + layer] = outs[n, bx % own, layer, 0:height]

        if rep == 1:
            keep()
        else:
            pl.when(bx // own == part)(keep)
        for wait in waits:
            wait()

    def y_pass(src, n):
        copies = [push(src, ybuf.at[n, k - 1], {"by": (by + k) % nby}) for k in range(1, nby)]
        total = product(halves(src[...].reshape(L * R, C)), (hy[0, by], hy[1, by]))
        for k in range(1, nby):
            copies[k - 1].wait_recv()
            origin = (by + nby - k) % nby
            total += product(halves(ybuf[n, k - 1].reshape(L * R, C)), (hy[0, origin], hy[1, origin]))
        return total

    def flank_start(rows_too, step, src):
        copies = []
        if rows_too:
            for c in range(3):
                for l in range(L):
                    at = c * L + l
                    row_s[step, 0, at:at + 1] = src[c, l, 0:1]
                    row_s[step, 1, at:at + 1] = src[c, l, R - 1:R]
            col_s[step] = column_tile([src[c, l] for c in range(3) for l in range(L)])
            if step == 0:
                pl.semaphore_wait(barrier, len(greeted))
            copies.append(push(row_s.at[step, 1], row_r.at[step, 0], {"bx": (bx + 1) % nbx}))
            copies.append(push(row_s.at[step, 0], row_r.at[step, 1], {"bx": (bx + nbx - 1) % nbx}))
            tile, land = col_s.at[step], col_r
        else:
            pc_s[step] = column_tile([src[l, 0:R] for l in range(L)])
            tile, land = pc_s.at[step], pc_r
        copies.append(push(tile, land.at[step, 0], {"by": (by + 1) % nby}))
        copies.append(push(tile, land.at[step, 1], {"by": (by + nby - 1) % nby}))
        return copies

    for step in range(STEPS):
        src = p_in if step == 0 else p_mid
        flanks = flank_start(True, step, src)
        if step == 0:
            lateral = lam[...]
            previous = None
            for l in range(L):
                pivot = perm[l] * lateral + inter[l] + inter[l + 1]
                if l:
                    pivot = pivot - inter[l] * previous
                inverse = 1.0 / pivot
                coef[l] = inverse
                previous = inter[l + 1] * inverse
                ratio[l] = previous
        for copy in flanks:
            copy.wait_recv()
        low_col = col_r[step, 0]
        high_col = col_r[step, 1]

        def edges(c, l):
            at = c * L + l
            return (row_r[step, 0, at:at + 1], row_r[step, 1, at:at + 1],
                    low_col[:, C // 2 + at:C // 2 + at + 1], high_col[:, at:at + 1])

        zero = jnp.zeros((R, C), jnp.float32)
        for l in range(L):
            low, high, _, _ = edges(0, l)
            _, _, left, right = edges(1, l)
            along_x, along_y = src[0, l], src[1, l]
            above = src[2, l + 1] if l + 1 < L else zero
            below = src[2, l - 1] if l else zero
            q[step, l] = -0.5 * (
                (x_next(along_x, high) - x_prev(along_x, low))
                + (y_next(along_y, right) - y_prev(along_y, left)) + (above - below))
        copies = x_start(q.at[step], 2 * step)
        if step == 0:
            for load in loads:
                load.wait()
        for l in range(L):
            cells = [src[c, l] for c in range(3)]
            squares = [cell * cell for cell in cells]
            whole = squares[0] + squares[1] + squares[2]
            for c in range(3):
                cell, square = cells[c], squares[c]
                low, high, left, right = edges(c, l)
                above = src[c, l + 1] if l + 1 < L else zero
                below = src[c, l - 1] if l else zero
                smooth = stiff[l] * (
                    (x_next(cell, high) + x_prev(cell, low) + y_next(cell, right)
                     + y_prev(cell, left) - 4.0 * cell) + (above + below - 2.0 * cell))
                drive = cell * (
                    2.0 * alpha[l] + 4.0 * landau[0, l] * square
                    + 2.0 * landau[1, l] * (whole - square)
                    + 6.0 * landau[2, l] * (square * square))
                base[c, l] = cell - step_size * (drive - smooth)
        n = 2 * step
        x_mix(copies, n)
        if wide:
            spread(n, step)
            table = (hy[0], hy[1])
            full = jnp.concatenate(
                [z_in[step, j].reshape(L * thin, C) for j in range(nby)], axis=1)
            values = solve(product(halves(full), table), thin)
            full = product(halves(jnp.concatenate(values, axis=0)), table)
            for j in range(nby):
                w_out[step, j] = full[:, j * C:(j + 1) * C].reshape(L, thin, C)
            copies = collect(n + 1, step)
        else:
            x_finish(n, rec_f.at[step], R)
            for l, value in enumerate(solve(y_pass(rec_f.at[step], n), R)):
                phat[step, l] = value
            u[step] = y_pass(phat.at[step], n + 1).reshape(L, R, C)
            copies = x_start(u.at[step], n + 1)
        x_mix(copies, n + 1)
        x_finish(n + 1, rec_i.at[step], R2)
        flanks = flank_start(False, step, rec_i.at[step])
        last = step == STEPS - 1
        target = p_out if last else p_mid
        for l in range(L):
            phi = rec_i[step, l, 0:R]
            low = rec_i[step, l, R:R + 1]
            high = rec_i[step, l, R + 1:R + 2]
            along_x = -0.5 * (x_next(phi, high) - x_prev(phi, low))
            above = rec_i[step, l + 1, 0:R] if l + 1 < L else zero
            below = rec_i[step, l - 1, 0:R] if l else zero
            along_z = -0.5 * (above - below)
            target[0, l] = base[0, l] + step_size * along_x
            target[2, l] = base[2, l] + step_size * along_z
            if last:
                f_out[0, l] = along_x
                f_out[2, l] = along_z
        for copy in flanks:
            copy.wait_recv()
        low_phi = pc_r[step, 0]
        high_phi = pc_r[step, 1]
        for l in range(L):
            phi = rec_i[step, l, 0:R]
            along_y = -0.5 * (y_next(phi, high_phi[:, l:l + 1])
                              - y_prev(phi, low_phi[:, C // 2 + l:C // 2 + l + 1]))
            target[1, l] = base[1, l] + step_size * along_y
            if last:
                f_out[1, l] = along_y
    for wait in sends:
        wait()


def shards(polarization, alpha_field, landau, stiffness, permittivity, interfaces):
    _, L, R, C = polarization.shape
    nbx = lax.axis_size("bx")
    nby = lax.axis_size("by")
    bx = lax.axis_index("bx")
    by = lax.axis_index("by")
    rep = max(1, nbx // L)
    lp = max(1, L // nbx)
    own = nbx // rep
    grid_x, grid_y = nbx * R, nby * C
    R2 = R + PAD
    wide = is_wide(R, nbx, nby, L)
    pool = np if wide else jnp
    make = fixed_table if wide else cas_table
    line = pool.arange(R2, dtype=jnp.int32)
    line = pool.where(line < R, line, pool.where(line == R, -1, R))
    owners = pool.arange(own, dtype=jnp.int32)
    if not wide:
        owners = owners + bx % rep * own
    wanted = ((owners[:, None] * R + line[None, :] + grid_x) % grid_x).reshape(own * R2, 1)
    hx = make(wanted, pool.arange(grid_x, dtype=jnp.int32)[None, :], grid_x)
    every_col = pool.arange(grid_y, dtype=jnp.int32)
    my_rows = bx * R + jnp.arange(R, dtype=jnp.int32)
    my_cols = by * C + jnp.arange(C, dtype=jnp.int32)
    if wide:
        hy = make(every_col[:, None], every_col[None, :], grid_y)
        my_rows = bx * R + by * (R // nby) + jnp.arange(R // nby, dtype=jnp.int32)
        my_cols = jnp.arange(grid_y, dtype=jnp.int32)
    else:
        hy = make(every_col[:, None], my_cols[None, :], grid_y).reshape(2, nby, C, C)
    wave_x = jnp.sin(jnp.pi * my_rows.astype(jnp.float32) / grid_x)
    wave_y = jnp.sin(jnp.pi * my_cols.astype(jnp.float32) / grid_y)
    lam = 4.0 * wave_x[:, None] ** 2 + 4.0 * wave_y[None, :] ** 2
    sizes = (L, R, C, nbx, nby, rep, lp, own)
    n_copies = STEPS * (6 + 2 * (nbx * nby + own if wide else nbx + own + nby))
    f32 = jnp.float32
    vmem = pl.BlockSpec(memory_space=pltpu.VMEM)
    hbm = pl.BlockSpec(memory_space=pltpu.HBM)
    smem = pl.BlockSpec(memory_space=pltpu.SMEM)
    S = STEPS
    scratch = [
        pltpu.VMEM((3, L, R, C), f32), pltpu.VMEM((3, L, R, C), f32),
        pltpu.VMEM((L,) + lam.shape, f32), pltpu.VMEM((L,) + lam.shape, f32),
        pltpu.VMEM((S, L, R, C), f32), pltpu.VMEM((2 * S, lp, grid_x, C), f32),
        pltpu.VMEM((2 * S, own, lp, R2, C), f32), pltpu.VMEM((S, L, R2, C), f32),
        pltpu.VMEM((S, 2, 3 * L, C), f32), pltpu.VMEM((S, 2, 3 * L, C), f32),
        pltpu.VMEM((S, R, C), f32), pltpu.VMEM((S, 2, R, C), f32),
        pltpu.VMEM((S, R, C), f32), pltpu.VMEM((S, 2, R, C), f32),
        pltpu.SemaphoreType.DMA((n_copies,)), pltpu.SemaphoreType.DMA((n_copies,)),
        pltpu.VMEM((L, R, C), f32), pltpu.VMEM(hx.shape, hx.dtype),
        pltpu.VMEM(hy.shape, hy.dtype), pltpu.SemaphoreType.DMA((3,)),
    ]
    if wide:
        thin = (S, nby, L, R // nby, C)
        scratch += [pltpu.VMEM(thin, f32), pltpu.VMEM(thin, f32)]
    else:
        scratch += [
            pltpu.VMEM((S, L, R, C), f32), pltpu.VMEM((2 * S, nby - 1, L, R, C), f32),
            pltpu.VMEM((S, L, R, C), f32), pltpu.VMEM((S, L, R, C), f32),
        ]
    out = jax.ShapeDtypeStruct(polarization.shape, f32)
    return pl.pallas_call(
        functools.partial(kernel, sizes),
        out_shape=(out, out),
        in_specs=[vmem, hbm, smem, smem, smem, smem, vmem, hbm, hbm],
        out_specs=(vmem, vmem),
        scratch_shapes=scratch,
        compiler_params=pltpu.CompilerParams(
            collective_id=0, has_side_effects=True, vmem_limit_bytes=65 * 1000 * 1000),
    )(polarization, alpha_field, landau, stiffness, permittivity, interfaces, lam, hx, hy)


def fits(L, R, C, nbx, nby):
    slab = R // nby
    return (L == nbx and slab == 8 and slab * nby == R and nby > 1 and C % (8 * L) == 0
            and nbx > 2 and nbx & (nbx - 1) == 0 and nby & (nby - 1) == 0)


def partner(index, mask, size):
    other = 0
    bit = 1
    while bit < size:
        here = index // bit % 2
        other = other + bit * (1 - here if mask // bit % 2 else here)
        bit *= 2
    return other


def join(parts, axis):
    return jnp.concatenate(parts, axis=axis)


def fused(sizes, p_h, alpha_h, landau_h, stiff_h, perm_h, inter_h, wx_h, wy_h, hx_h, hy_h,
          base_o, down_o, *scratch):
    L, R, C, nbx, nby = sizes
    (p_mid, base, coef, ratio, a_s, a_r, b_s, b_r, c_s, c_r, d_s, d_r,
     row_s, row_r, col_s, col_r, ssem, rsem, known, p_in, alpha, wx, wy, hx, hy,
     landau, stiff, perm, inter, local_sem) = scratch
    slab = R // nby
    per = C // L
    NX, NY = nbx * R, nby * C
    bx = lax.axis_index("bx")
    by = lax.axis_index("by")
    scale = 1.0 / (NX * NY)
    f32 = jnp.float32
    dot = functools.partial(jnp.dot, preferred_element_type=f32)
    slots = [0]
    sends = []

    barrier = pltpu.get_barrier_semaphore()
    at_x = [partner(bx, a, nbx) for a in range(nbx)]
    at_y = [partner(by, b, nby) for b in range(nby)]
    others = [(a, b) for b in range(nby) for a in range(nbx) if a or b]
    others.sort(key=lambda ab: -(ab[0] // 2 + ab[0] % 2 + ab[1] // 2))
    reach = [1 << i for i in range(1, nbx.bit_length() - 1)]
    greeted = [(a, b) for a, b in others if a < 2] + [(a, 0) for a in reach]
    for a, b in greeted:
        pl.semaphore_signal(
            barrier, inc=1, device_id={"bx": at_x[a], "by": at_y[b]}, device_id_type=MESH)
    mine = pl.multiple_of((bx * nby + by) * per, per)
    loads = [pltpu.make_async_copy(src, dst, local_sem.at[at]) for at, (src, dst) in enumerate((
        (p_h, p_in), (alpha_h, alpha), (wx_h, wx), (wy_h.at[pl.ds(mine, per)], wy), (hx_h, hx),
        (hy_h, hy), (landau_h, landau), (stiff_h, stiff), (perm_h, perm), (inter_h, inter)))]
    for load in loads:
        load.start()

    def push(src, dst, device):
        slot = slots[0]
        slots[0] += 1
        copy = pltpu.make_async_remote_copy(
            src_ref=src, dst_ref=dst, send_sem=ssem.at[slot], recv_sem=rsem.at[slot],
            device_id=device, device_id_type=MESH)
        copy.start()
        sends.append(copy.wait_send)
        return copy

    rows = lax.broadcasted_iota(jnp.int32, (R, C), 0)
    lanes = lax.broadcasted_iota(jnp.int32, (R, C), 1)
    rows8 = lax.broadcasted_iota(jnp.int32, (slab, C), 0)
    lanes8 = lax.broadcasted_iota(jnp.int32, (slab, C), 1)
    zero = jnp.zeros((R, C), f32)
    zero8 = jnp.zeros((slab, C), f32)

    def x_next(f, high):
        return jnp.where(rows == R - 1, high, pltpu.roll(f, R - 1, 0))

    def x_prev(f, low):
        return jnp.where(rows == 0, low, pltpu.roll(f, 1, 0))

    def y_next(f, high):
        return jnp.where(lanes == C - 1, high, pltpu.roll(f, C - 1, 1))

    def y_prev(f, low):
        return jnp.where(lanes == 0, low, pltpu.roll(f, 1, 1))

    def flush(keep):
        while len(sends) > keep:
            sends.pop(0)()

    def charge(n, src, ring):
        sides = (0, nby - 1)
        edge = zero
        for l in range(L):
            along_x, along_y = src[0, l], src[1, l]
            above = src[2, l + 1] if l + 1 < L else zero
            below = src[2, l - 1] if l else zero
            low = high = left = right = 0.0
            if ring:
                lines, column = ring
                low, high = lines[0][0][l:l + 1], lines[1][0][l:l + 1]
                left = column[:, L + l:L + l + 1]
                right = column[:, C // 2 + L + l:C // 2 + L + l + 1]
            value = -0.5 * ((x_next(along_x, high) - x_prev(along_x, low))
                            + (y_next(along_y, right) - y_prev(along_y, left)) + (above - below))
            for j in range(nby):
                a_s[n, j, l] = value[j * slab:(j + 1) * slab]
            edge = jnp.where(lanes == l, -0.5 * along_y[:, 0:1], edge)
            edge = jnp.where(lanes == L + l, 0.5 * along_y[:, C - 1:C], edge)
        near = [-0.5 * join([src[0, l, 0:1] for l in range(L)], 0),
                0.5 * join([src[0, l, R - 1:R] for l in range(L)], 0)]
        corner = [None, None]
        if ring:
            for side, sign in enumerate((-0.5, 0.5)):
                first, second, third = lines[side]
                turned = (jnp.where(lanes8 == C - 1, 0.0, pltpu.roll(second, C - 1, 1))
                          - jnp.where(lanes8 == 0, 0.0, pltpu.roll(second, 1, 1)))
                risen = (jnp.where(rows8 == L - 1, 0.0, pltpu.roll(third, L - 1, 0))
                         - jnp.where(rows8 == 0, 0.0, pltpu.roll(third, 1, 0)))
                near[side] = near[side] - 0.5 * (turned + risen)
                a_s[n, sides[side], L + 2] = sign * first
                corner[side] = jnp.where(
                    lanes8 == 4 * L, sign * first[:, 0:1] - 0.5 * second[:, 0:1],
                    jnp.where(lanes8 == 4 * L + 1,
                              sign * first[:, C - 1:C] + 0.5 * second[:, C - 1:C], 0.0))
            layer = lanes % L
            turned = -0.5 * (x_next(column, 0.0) - x_prev(column, 0.0))
            risen = -0.5 * (jnp.where(layer == L - 1, 0.0, pltpu.roll(column, C - 1, 1))
                            - jnp.where(layer == 0, 0.0, pltpu.roll(column, 1, 1)))
            both = turned + pltpu.roll(risen, C - 2 * L, 1)
            low = edge + both
            high = edge + pltpu.roll(both, C // 2 + L, 1)
            far_low = -0.5 * pltpu.roll(column, L, 1)
            far_high = 0.5 * pltpu.roll(column, C // 2 + 2 * L, 1)
            group = lanes // L
            edge = jnp.where(group == 0, low, jnp.where(group == 1, high, jnp.where(
                group == 2, far_low, jnp.where(group == 3, far_high, 0.0))))
        for side in range(2):
            a_s[n, sides[side], L + 1] = near[side]
        for j in range(nby):
            piece = edge[j * slab:(j + 1) * slab]
            if ring and j in sides:
                piece = piece + corner[sides.index(j)]
            a_s[n, j, L] = piece
            if j not in sides:
                a_s[n, j, L + 1:L + 3] = jnp.zeros((2, slab, C), f32)

    def ring_of(n):
        weight8 = zero8
        weight = zero
        layer = lanes % L
        for l in range(L):
            weight8 = jnp.where(rows8 == l, step_size * stiff[l], weight8)
            weight = jnp.where(layer == l, step_size * stiff[l], weight)
        lines = [[weight8 * row_s[n, side, c * L:(c + 1) * L] for c in range(3)]
                 for side in range(2)]
        return lines, weight * col_s[n]

    rim_slab = (by == 0) | (by == nby - 1)

    def has_rim(b, here):
        return nby != 4 or (b in (0, nby - 1)) == here

    def either(action):
        if nby != 4:
            action(True)
        else:
            pl.when(rim_slab)(functools.partial(action, True))
            pl.when(jnp.logical_not(rim_slab))(functools.partial(action, False))

    def exchange(targets, build, by_target):
        first = slots[0]
        slots[0] += len(targets)

        def make(at, whole):
            a, b = targets[at]
            src, dst = build(a, b, whole)
            return pltpu.make_async_remote_copy(
                src_ref=src, dst_ref=dst, send_sem=ssem.at[first + at],
                recv_sem=rsem.at[first + at], device_id={"bx": at_x[a], "by": at_y[b]},
                device_id_type=MESH)

        def outgoing(here):
            return [make(at, has_rim(b, here) if by_target else here)
                    for at, (a, b) in enumerate(targets)]

        def start(here):
            for copy in outgoing(here):
                copy.start()

        def sent(here):
            for copy in outgoing(here):
                copy.wait_send()

        def came(here):
            for at, (a, b) in enumerate(targets):
                make(at, here if by_target else has_rim(b, here)).wait_recv()

        either(start)
        sends.append(functools.partial(either, sent))
        return functools.partial(either, came)

    def among_y(source, landing, n, count, by_target):
        def build(a, b, whole):
            part = pl.ds(0, count if whole else L + 1)
            return source.at[n, at_y[b], part], landing.at[n, by, part]

        arrive = exchange([(0, b) for b in range(nby - 1, 0, -1)], build, by_target)
        landing[n, by, 0:count] = source[n, by, 0:count]
        return arrive

    def wait(copies):
        if callable(copies):
            copies()
        else:
            for copy in copies:
                copy.wait_recv()

    def spread(source, landing, n, flip, thick):
        def build(a, b, whole):
            part = pl.ds(0, thick if whole else slab)
            to_x, to_y = at_x[a], at_y[b]
            if flip:
                return source.at[n, to_x, to_y, part], landing.at[n, by, bx, part]
            return source.at[n, to_y, to_x, part], landing.at[n, bx, by, part]

        arrive = exchange(others, build, flip)
        if flip:
            landing[n, by, bx, 0:thick] = source[n, bx, by, 0:thick]
        else:
            landing[n, bx, by, 0:thick] = source[n, by, bx, 0:thick]
        return arrive

    def clear_rims():
        for n in range(2):
            for j in range(nby):
                a_r[n, j, L + 1:L + 3] = jnp.zeros((2, slab, C), f32)
                for e in range(nbx):
                    c_r[n, j, e, slab:2 * slab] = zero8

    def swap_groups(tiles):
        height = tiles[0].shape[0]
        group = lax.broadcasted_iota(jnp.int32, (height, C), 1) // per
        tiles = list(tiles)
        s = 1
        while s < L:
            upper = group % (2 * s) >= s
            for at in range(L):
                if at % (2 * s) < s:
                    low, high = tiles[at], tiles[at + s]
                    tiles[at] = jnp.where(upper, pltpu.roll(high, s * per, 1), low)
                    tiles[at + s] = jnp.where(upper, high, pltpu.roll(low, C - s * per, 1))
            s *= 2
        return tiles

    def swap_rows(tile):
        group = lanes8 // per
        s = 1
        while s < L:
            upper = group % (2 * s) >= s
            later = rows8 % (2 * s) >= s
            ahead = pltpu.roll(pltpu.roll(tile, L - s, 0), s * per, 1)
            behind = pltpu.roll(pltpu.roll(tile, s, 0), C - s * per, 1)
            tile = jnp.where(later, jnp.where(upper, tile, behind), jnp.where(upper, ahead, tile))
            s *= 2
        return tile

    def times(full, table):
        height = full.shape[0]
        high = full.astype(jnp.bfloat16)
        wide = high.astype(f32)
        both = join([wide, full - wide], 0).astype(jnp.bfloat16)
        first = dot(both, hy[table, 0])
        return first[:height] + first[height:] + dot(high, hy[table, 1])

    def y_forward(n):
        columns = []
        for j in range(nby):
            from_left = a_r[n, (j + nby - 1) % nby, L]
            from_right = a_r[n, (j + 1) % nby, L]
            tiles = []
            for l in range(L):
                extra = jnp.where(
                    lanes8 == 0, from_left[:, L + l:L + l + 1],
                    jnp.where(lanes8 == C - 1, from_right[:, l:l + 1], 0.0))
                if n:
                    extra = jnp.where(
                        lanes8 == 1, from_left[:, 3 * L + l:3 * L + l + 1],
                        jnp.where(lanes8 == C - 2, from_right[:, 2 * L + l:2 * L + l + 1], extra))
                tiles.append(a_r[n, j, l] + extra)
            near, far = a_r[n, j, L + 1], zero8
            if n:
                near = near + jnp.where(
                    lanes8 == 0, from_left[:, 4 * L + 1:4 * L + 2],
                    jnp.where(lanes8 == C - 1, from_right[:, 4 * L:4 * L + 1], 0.0))
                far = a_r[n, j, L + 2]
            columns.append(join(tiles + [near, far], 0))
        low, high = join(columns[:nby // 2], 1), join(columns[nby // 2:], 1)
        out = join([times(low + high, 0), times(low - high, 1)], 1)
        tiles = [join([out[l * slab:(l + 1) * slab, t * C:(t + 1) * C] for t in range(nby)], 0)
                 for l in range(L)]
        tiles = swap_groups(tiles)
        for t in range(nby):
            halos = [swap_rows(out[(L + k) * slab:(L + k) * slab + L, t * C:(t + 1) * C])
                     for k in range(1 + n)]
            for e in range(L):
                b_s[n, t, e, 0:slab] = tiles[e][t * slab:(t + 1) * slab]
                for k, halo in enumerate(halos):
                    b_s[n, t, e, slab + k:slab + k + 1] = halo[e:e + 1]

    def y_backward(n):
        tiles = swap_groups([join([c_r[n, t, e, 0:slab] for t in range(nby)], 0)
                             for e in range(L)])
        rims = [join([swap_rows(join([c_r[n, t, e, slab + k:slab + k + 1] for e in range(L)], 0))
                      for t in range(nby)], 1) for k in range(2 - n)]
        if n:
            rims.append(jnp.zeros((slab, NY), f32))
        lines = [join([tiles[l][t * slab:(t + 1) * slab] for t in range(nby)], 1)
                 for l in range(L)]
        full = join(lines + rims, 0)
        even, odd = times(full[:, :NY // 2], 0), times(full[:, NY // 2:], 2)
        out = join([even + odd, even - odd], 1)
        near = out[L * slab:L * slab + L]
        for j in range(nby):
            edge = zero8
            left, right = (j + nby - 1) % nby * C, (j + 1) % nby * C
            wanted = [left + C - 1, right]
            if n == 0:
                wanted += [left + C - 2, right + 1, None, j * C, j * C + C - 1]
                edge = jnp.where(lanes8 == 4 * L, near[:, left + C - 1:left + C],
                                 jnp.where(lanes8 == 4 * L + 1, near[:, right:right + 1], edge))
            for l in range(L):
                line = out[l * slab:(l + 1) * slab]
                d_s[n, j, l] = line[:, j * C:(j + 1) * C]
                for at, column in enumerate(wanted):
                    if column is not None:
                        edge = jnp.where(
                            lanes8 == at * L + l, line[:, column:column + 1], edge)
            d_s[n, j, L] = edge
            for k in range(2 - n):
                d_s[n, j, L + 1 + k] = out[(L + k) * slab:(L + k) * slab + L,
                                           j * C:(j + 1) * C]

    def spectrum(n):
        tiles = []
        for i in range(nbx):
            for j in range(nby):
                tile = b_r[n, i, j, 0:slab]
                for k in range(1 + n):
                    line = slice(slab + k, slab + k + 1)
                    if j == 0:
                        tile = tile + jnp.where(
                            rows8 == k, b_r[n, (i + nbx - 1) % nbx, nby - 1, line], 0.0)
                    if j == nby - 1:
                        tile = tile + jnp.where(
                            rows8 == slab - 1 - k, b_r[n, (i + 1) % nbx, 0, line], 0.0)
                tiles.append(tile)
        full = join(tiles, 0).T
        high = full.astype(jnp.bfloat16)
        wide = high.astype(f32)
        both = join([wide, full - wide], 0).astype(jnp.bfloat16)
        first = dot(both, hx[0])
        out = (first[:C] + first[C:] + dot(high, hx[1])) * scale
        return [out[l * per:(l + 1) * per] for l in range(L)]

    def solve(sources):
        primes = []
        for l in range(L):
            source = sources[l]
            if l:
                source = source + inter[l] * primes[-1]
            primes.append(source * coef[l])
        values = [primes[-1]]
        for l in range(L - 2, -1, -1):
            values.insert(0, primes[l] + ratio[l] * values[0])
        return values

    def x_backward(n, values):
        high, low = halves(join(values, 0))
        turn = functools.partial(
            lax.dot_general, dimension_numbers=(((1,), (1,)), ((), ())),
            preferred_element_type=f32)
        first = turn(hx[...].reshape(2 * NX, NX), high)
        out = first[:NX] + first[NX:] + turn(hx[0], low)
        for i in range(nbx):
            for j in range(nby):
                at = i * R + j * slab
                c_s[n, i, j, 0:slab] = out[at:at + slab]
                for k in range(2 - n):
                    line = (at - 1 - k if j == 0 else at + slab + k) % NX
                    c_s[n, i, j, slab + k:slab + k + 1] = out[line:line + 1]

    def flank_start(n, src):
        tile = zero
        for c in range(3):
            for l in range(L):
                at = c * L + l
                cell = src[c, l]
                row_s[n, 0, at:at + 1] = cell[0:1]
                row_s[n, 1, at:at + 1] = cell[R - 1:R]
                tile = jnp.where(lanes == at, cell[:, 0:1], tile)
                tile = jnp.where(lanes == C // 2 + at, cell[:, C - 1:C], tile)
        col_s[n] = tile

    def flank_send(n):
        return [
            push(row_s.at[n, 1], row_r.at[n, 0], {"bx": (bx + 1) % nbx}),
            push(row_s.at[n, 0], row_r.at[n, 1], {"bx": (bx + nbx - 1) % nbx}),
            push(col_s.at[n], col_r.at[n, 0], {"by": (by + 1) % nby}),
            push(col_s.at[n], col_r.at[n, 1], {"by": (by + nby - 1) % nby})]

    def relax_inside(src):
        for l in range(L):
            cells = [src[c, l] for c in range(3)]
            squares = [cell * cell for cell in cells]
            whole = squares[0] + squares[1] + squares[2]
            for c in range(3):
                cell, square = cells[c], squares[c]
                above = src[c, l + 1] if l + 1 < L else zero
                below = src[c, l - 1] if l else zero
                smooth = stiff[l] * (
                    (x_next(cell, 0.0) + x_prev(cell, 0.0) + y_next(cell, 0.0)
                     + y_prev(cell, 0.0) - 4.0 * cell) + (above + below - 2.0 * cell))
                drive = cell * (
                    2.0 * alpha[l] + 4.0 * landau[0, l] * square
                    + 2.0 * landau[1, l] * (whole - square)
                    + 6.0 * landau[2, l] * (square * square))
                base[c, l] = cell - step_size * (drive - smooth)

    def flank_lines(n):
        return [[row_r[n, side, c * L:(c + 1) * L] for c in range(3)] for side in range(2)]

    def relax_edges(lines, low_col, high_col, target):
        for l in range(L):
            weight = step_size * stiff[l]
            for c in range(3):
                at = c * L + l
                add = jnp.where(lanes == 0, low_col[:, C // 2 + at:C // 2 + at + 1], 0.0)
                add = add + jnp.where(lanes == C - 1, high_col[:, at:at + 1], 0.0)
                add = add + jnp.where(rows == 0, lines[0][c][l:l + 1], 0.0)
                add = add + jnp.where(rows == R - 1, lines[1][c][l:l + 1], 0.0)
                target[c, l] = base[c, l] + weight * add

    def moved_rim():
        lines = flank_lines(1)
        corners = []
        for side, owner in enumerate((0, nby - 1)):
            inner = join([d_r[0, owner, l, side * (slab - 1):side * (slab - 1) + 1]
                          for l in range(L)], 0)
            near, far = d_r[0, owner, L + 1], d_r[0, owner, L + 2]
            edge = d_r[0, owner, L]
            low, high = edge[:, 4 * L:4 * L + 1], edge[:, 4 * L + 1:4 * L + 2]
            down = [inner - far if side == 0 else far - inner,
                    jnp.where(lanes8 == C - 1, high, pltpu.roll(near, C - 1, 1))
                    - jnp.where(lanes8 == 0, low, pltpu.roll(near, 1, 1)),
                    jnp.where(rows8 == L - 1, 0.0, pltpu.roll(near, L - 1, 0))
                    - jnp.where(rows8 == 0, 0.0, pltpu.roll(near, 1, 0))]
            lines[side] = [line - (0.5 * step_size) * part
                           for line, part in zip(lines[side], down)]
            spot = jnp.where(lanes8 == rows8, low, jnp.where(lanes8 == rows8 + L, high, 0.0))
            corners.append(jnp.sum(spot, axis=0, keepdims=True))
        edge = join([d_r[0, j, L] for j in range(nby)], 0)
        layer = lanes % L
        group = lanes // L
        across = pltpu.roll(edge, C - 5 * L, 1) - pltpu.roll(edge, C - 2 * L, 1)
        down = [x_next(edge, corners[1]) - x_prev(edge, corners[0]),
                jnp.where(group == 0, across, -across),
                jnp.where(layer == L - 1, 0.0, pltpu.roll(edge, C - 1, 1))
                - jnp.where(layer == 0, 0.0, pltpu.roll(edge, 1, 1))]
        low_col, high_col = col_r[1, 0], col_r[1, 1]
        for c in range(3):
            part = (0.5 * step_size) * down[c]
            low_col = low_col - jnp.where(
                group == C // (2 * L) + c, pltpu.roll(part, C // 2 + c * L, 1), 0.0)
            high_col = high_col - jnp.where(
                group == c, pltpu.roll(part, (C + c * L - L) % C, 1), 0.0)
        return lines, low_col, high_col

    def field(n):
        edge = join([d_r[n, j, L] for j in range(nby)], 0)
        phis = [join([d_r[n, j, l] for j in range(nby)], 0) for l in range(L)]
        for l in range(L):
            phi = phis[l]
            low = d_r[n, 0, L + 1, l:l + 1]
            high = d_r[n, nby - 1, L + 1, l:l + 1]
            along_x = 0.5 * (x_next(phi, high) - x_prev(phi, low))
            along_y = 0.5 * (y_next(phi, edge[:, L + l:L + l + 1])
                             - y_prev(phi, edge[:, l:l + 1]))
            above = phis[l + 1] if l + 1 < L else zero
            below = phis[l - 1] if l else zero
            yield l, (along_x, along_y, 0.5 * (above - below))

    loads[0].wait()
    charge(0, p_in, None)
    pl.semaphore_wait(barrier, len(greeted))

    def tell(at):
        pl.semaphore_signal(
            known.at[at], inc=1, device_id={"bx": at_x[reach[at]]}, device_id_type=MESH)

    tell(0)
    first_a = among_y(a_s, a_r, 0, L + 2, True)
    if nby == 4:
        pl.when(jnp.logical_not(rim_slab))(clear_rims)
    flank_start(0, p_in)
    loads[1].wait()
    for load in loads[6:]:
        load.wait()
    relax_inside(p_in)
    charge(1, base, ring_of(0))
    second_a = among_y(a_s, a_r, 1, L + 3, True)
    for at in range(1, len(reach)):
        pl.semaphore_wait(known.at[at - 1], 1)
        tell(at)
    loads[2].wait()
    loads[3].wait()
    wave_x = wx[0:1]
    wave_y = join([wy[...]] * (NX // C), 1)
    lateral = wave_x + wave_y
    previous = None
    for l in range(L):
        pivot = perm[l] * lateral + inter[l] + inter[l + 1]
        if l:
            pivot = pivot - inter[l] * previous
        inverse = 1.0 / pivot
        coef[l] = inverse
        previous = inter[l + 1] * inverse
        ratio[l] = previous
    loads[4].wait()
    loads[5].wait()
    wait(first_a)
    y_forward(0)
    pl.semaphore_wait(known.at[len(reach) - 1], 1)
    first_b = spread(b_s, b_r, 0, False, slab + 1)
    wait(second_a)
    y_forward(1)
    second_b = spread(b_s, b_r, 1, False, slab + 2)
    flanks = flank_send(0)
    wait(first_b)
    values = solve(spectrum(0))
    x_backward(0, values)
    first_c = spread(c_s, c_r, 0, True, slab + 2)
    bend = -(wave_x * (1.0 - 0.25 * wave_x) + wave_y * (1.0 - 0.25 * wave_y))
    slopes = []
    none = jnp.zeros_like(values[0])
    for l in range(L):
        above = values[l + 1] if l + 1 < L else none
        below = values[l - 1] if l else none
        slopes.append(0.5 * (above - below))
    moved = []
    for l in range(L):
        above = slopes[l + 1] if l + 1 < L else none
        below = slopes[l - 1] if l else none
        moved.append(step_size * (bend * values[l] + 0.5 * (above - below)))
    wait(second_b)
    x_backward(1, solve([here + more for here, more in zip(spectrum(1), moved)]))
    second_c = spread(c_s, c_r, 1, True, slab + 1)
    wait(flanks)
    relax_edges(flank_lines(0), col_r[0, 0], col_r[0, 1], base)
    flank_start(1, base)
    flanks = flank_send(1)
    flush(len(flanks) + 2)
    wait(first_c)
    y_backward(0)
    first_d = among_y(d_s, d_r, 0, L + 3, False)
    wait(second_c)
    y_backward(1)
    second_d = among_y(d_s, d_r, 1, L + 2, False)
    wait(first_d)
    for l, parts in field(0):
        for c in range(3):
            p_mid[c, l] = base[c, l] - step_size * parts[c]
    wait(flanks)
    rim = moved_rim()
    relax_inside(p_mid)
    relax_edges(*rim, base_o)
    flush(1)
    wait(second_d)
    for l, parts in field(1):
        for c in range(3):
            down_o[c, l] = parts[c]
    flush(0)


def fused_shards(polarization, alpha_field, landau, stiffness, permittivity, interfaces):
    _, L, R, C = polarization.shape
    nbx = lax.axis_size("bx")
    nby = lax.axis_size("by")
    grid_x, grid_y = nbx * R, nby * C
    per = C // L
    line = np.arange(grid_x)
    hx = fixed_table(line[:, None], line[None, :], grid_x)
    line = np.arange(grid_y // 2)
    modes = np.concatenate([2 * line, 2 * line + 1])
    hy = jnp.stack([fixed_table(left, right, grid_y) for left, right in (
        (line[:, None], 2 * line[None, :]), (line[:, None], 2 * line[None, :] + 1),
        (2 * line[:, None] + 1, line[None, :]))])
    wave_x = 4.0 * np.sin(np.pi * np.arange(grid_x) / grid_x) ** 2
    wave_x = jnp.asarray(np.tile(wave_x[None, :], (8, 1)).astype(np.float32))
    at = np.arange(nbx * nby)
    first = (at % nby) * C + (at // nby) * per
    mode = modes[(first[:, None] + np.arange(per)[None, :]).reshape(-1)]
    wave_y = 4.0 * np.sin(np.pi * mode / grid_y) ** 2
    wave_y = jnp.asarray(np.tile(wave_y[:, None], (1, C)).astype(np.float32))
    f32 = jnp.float32
    hbm = pl.BlockSpec(memory_space=pltpu.HBM)
    S = 2
    n_copies = S * (4 + 2 * (nby - 1) + 2 * (nbx * nby - 1))
    by_y = pltpu.VMEM((S, nby, L + 3, 8, C), f32)
    by_mode = pltpu.VMEM((S, nby, nbx, 16, C), f32)
    by_place = pltpu.VMEM((S, nbx, nby, 16, C), f32)
    scratch = [
        pltpu.VMEM((3, L, R, C), f32), pltpu.VMEM((3, L, R, C), f32),
        pltpu.VMEM((L, per, grid_x), f32), pltpu.VMEM((L, per, grid_x), f32),
        by_y, by_y, by_mode, by_place, by_place, by_mode, by_y, by_y,
        pltpu.VMEM((S, 2, 3 * L, C), f32), pltpu.VMEM((S, 2, 3 * L, C), f32),
        pltpu.VMEM((S, R, C), f32), pltpu.VMEM((S, 2, R, C), f32),
        pltpu.SemaphoreType.DMA((n_copies,)), pltpu.SemaphoreType.DMA((n_copies,)),
        pltpu.SemaphoreType.REGULAR((nbx.bit_length(),)), pltpu.VMEM((3, L, R, C), f32),
        pltpu.VMEM((L, R, C), f32), pltpu.VMEM(wave_x.shape, f32), pltpu.VMEM((per, C), f32),
        pltpu.VMEM(hx.shape, hx.dtype), pltpu.VMEM(hy.shape, hy.dtype),
        pltpu.SMEM(landau.shape, f32), pltpu.SMEM(stiffness.shape, f32),
        pltpu.SMEM(permittivity.shape, f32), pltpu.SMEM(interfaces.shape, f32),
        pltpu.SemaphoreType.DMA((10,)),
    ]
    out = pltpu.VMEM(polarization.shape, f32)
    base, down = pl.pallas_call(
        functools.partial(fused, (L, R, C, nbx, nby)),
        out_shape=(out, out),
        in_specs=[hbm] * 10,
        out_specs=(pl.BlockSpec(memory_space=pltpu.VMEM), pl.BlockSpec(memory_space=pltpu.VMEM)),
        scratch_shapes=scratch,
        compiler_params=pltpu.CompilerParams(
            collective_id=0, has_side_effects=True, vmem_limit_bytes=66 * 1000 * 1000),
    )(polarization, alpha_field, landau, stiffness, permittivity, interfaces,
      wave_x, wave_y, hx, hy)
    return base - step_size * down, -down


def solution(mesh):
    def run(polarization, *rest):
        _, L, R, C = polarization.shape
        body = fused_shards if fits(L, R, C, lax.axis_size("bx"), lax.axis_size("by")) else shards
        return body(polarization, *rest)

    return jax.shard_map(
        run,
        mesh=mesh,
        in_specs=(P(None, None, "bx", "by"), P(None, "bx", "by"), P(), P(), P(), P()),
        out_specs=(P(None, None, "bx", "by"), P(None, None, "bx", "by")),
        check_vma=False,
    )
```

```python
import functools

import jax
import jax.numpy as jnp
import numpy as np
from jax import lax
from jax.experimental import pallas as pl
from jax.experimental.pallas import tpu as pltpu
from jax.sharding import PartitionSpec as P

STEPS = 2
step_size = 0.05
MESH = pl.DeviceIdType.MESH
PAD = 8


def cas_table(left, right, length):
    turns = left * right % length
    angle = 2.0 * jnp.pi / length * turns.astype(jnp.float32)
    table = jnp.cos(angle) + jnp.sin(angle)
    high = lax.reduce_precision(table, 8, 7)
    return jnp.stack([high.astype(jnp.bfloat16), (table - high).astype(jnp.bfloat16)])


def fixed_table(left, right, length):
    angle = 2.0 * np.pi / length * (left * right % length)
    table = (np.cos(angle) + np.sin(angle)).astype(np.float32)
    high = table.astype(jnp.bfloat16)
    low = (table - high.astype(np.float32)).astype(jnp.bfloat16)
    return jnp.asarray(np.stack([high, low]))


def is_wide(rows, nbx, nby, layers):
    return layers % nbx == 0 and rows % (8 * nby) == 0


def halves(value):
    high = value.astype(jnp.bfloat16)
    low = (value - high.astype(jnp.float32)).astype(jnp.bfloat16)
    return high, low


def product(left, right):
    dot = functools.partial(jnp.dot, preferred_element_type=jnp.float32)
    return dot(left[0], right[0]) + (dot(left[0], right[1]) + dot(left[1], right[0]))


def kernel(sizes, p_in, alpha_h, landau, stiff, perm, inter, lam, hx_h, hy_h, p_out, f_out, *scratch):
    L, R, C, nbx, nby, rep, lp, own = sizes
    (p_mid, base, coef, ratio, q, inb, outs, rec_i,
     row_s, row_r, col_s, col_r, pc_s, pc_r, ssem, rsem,
     alpha, hx, hy, local_sem) = scratch[:20]
    wide = is_wide(R, nbx, nby, L)
    if wide:
        z_in, w_out = scratch[20:]
    else:
        rec_f, ybuf, phat, u = scratch[20:]
    thin = R // nby
    R2 = R + PAD
    bx = lax.axis_index("bx")
    by = lax.axis_index("by")
    group = bx // rep
    part = bx % rep
    scale = 1.0 / (R * nbx * C * nby)
    loads = [pltpu.make_async_copy(src, dst, local_sem.at[at]) for at, (src, dst) in
             enumerate(((alpha_h, alpha), (hx_h, hx), (hy_h, hy)))]
    for load in loads:
        load.start()
    slots = [0]
    sends = []

    barrier = pltpu.get_barrier_semaphore()
    others = [(a, b) for b in range(nby) for a in range(nbx) if a or b]
    greeted = [(a, b) for a, b in others if wide or not a or not b]
    for a, b in greeted:
        pl.semaphore_signal(
            barrier, inc=1, device_id={"bx": (bx + a) % nbx, "by": (by + b) % nby},
            device_id_type=MESH)

    def remote(src, dst, device, slot):
        return pltpu.make_async_remote_copy(
            src_ref=src, dst_ref=dst, send_sem=ssem.at[slot], recv_sem=rsem.at[slot],
            device_id=device, device_id_type=MESH)

    def fresh():
        slots[0] += 1
        return slots[0] - 1

    def push(src, dst, device):
        copy = remote(src, dst, device, fresh())
        copy.start()
        sends.append(copy.wait_send)
        return copy

    rows = lax.broadcasted_iota(jnp.int32, (R, C), 0)
    lanes = lax.broadcasted_iota(jnp.int32, (R, C), 1)

    def x_next(f, high):
        return jnp.where(rows == R - 1, high, pltpu.roll(f, R - 1, 0))

    def x_prev(f, low):
        return jnp.where(rows == 0, low, pltpu.roll(f, 1, 0))

    def y_next(f, high):
        return jnp.where(lanes == C - 1, high, pltpu.roll(f, C - 1, 1))

    def y_prev(f, low):
        return jnp.where(lanes == 0, low, pltpu.roll(f, 1, 1))

    def column_tile(blocks):
        tile = jnp.zeros((R, C), jnp.float32)
        for at, block in enumerate(blocks):
            tile = jnp.where(lanes == at, block[:, 0:1], tile)
            tile = jnp.where(lanes == C // 2 + at, block[:, C - 1:C], tile)
        return tile

    def x_start(src, n):
        mine = inb.at[n, :, pl.ds(pl.multiple_of(bx * R, R), R)]
        copies = []
        for k in range(1, nbx):
            to = (bx + k) % nbx
            copies.append(push(src.at[pl.ds(to // rep * lp, lp)], mine, {"bx": to}))
        for layer in range(lp):
            inb[n, layer, pl.ds(pl.multiple_of(bx * R, R), R)] = src[group * lp + layer]
        return copies

    def x_mix(copies, n):
        for copy in copies:
            copy.wait_recv()
        table = (hx[0], hx[1])
        for layer in range(lp):
            outs[n, :, layer] = product(table, halves(inb[n, layer])).reshape(own, R2, C)

    def spread(n, step):
        copies = []
        for a, b in others:
            to_x, to_y = (bx + a) % nbx, (by + b) % nby
            copies.append(push(
                outs.at[n, to_x, :, pl.ds(pl.multiple_of(to_y * thin, thin), thin)],
                z_in.at[step, by, pl.ds(bx * lp, lp)], {"bx": to_x, "by": to_y}))
        for layer in range(lp):
            z_in[step, by, bx * lp + layer] = outs[
                n, bx, layer, pl.ds(pl.multiple_of(by * thin, thin), thin)]
        for copy in copies:
            copy.wait_recv()

    def collect(n, step):
        at = pl.ds(pl.multiple_of(bx * R + by * thin, thin), thin)
        copies = []
        for a, b in others:
            to_x, to_y = (bx + a) % nbx, (by + b) % nby
            copies.append(push(
                w_out.at[step, to_y, pl.ds(to_x * lp, lp)], inb.at[n, :, at],
                {"bx": to_x, "by": to_y}))
        for layer in range(lp):
            inb[n, layer, at] = w_out[step, by, bx * lp + layer]
        return copies

    def solve(spectrum, height):
        primes = []
        for l in range(L):
            source = spectrum[l * height:(l + 1) * height] * scale
            if l:
                source = source + inter[l] * primes[-1]
            primes.append(source * coef[l])
        values = [primes[-1]]
        for l in range(L - 2, -1, -1):
            values.insert(0, primes[l] + ratio[l] * values[0])
        return values

    def x_finish(n, dst, height):
        waits = []
        landing = dst.at[pl.ds(group * lp, lp)]
        for t in range(own):
            local = (group + t) % own
            to = part * own + local
            src = outs.at[n, local, :, pl.ds(0, height)]
            if rep == 1:
                if t == 0:
                    continue
                waits.append(push(src, landing, {"bx": to}).wait_recv)
                continue
            slot = fresh()

            def go(src=src, to=to, slot=slot):
                remote(src, landing, {"bx": to}, slot).start()

            def gone(src=src, to=to, slot=slot):
                @pl.when(to != bx)
                def _():
                    remote(src, landing, {"bx": to}, slot).wait_send()

            def came(src=src, to=to, slot=slot, t=t):
                origin = (bx % own + own - t) % own * rep + bx // own

                @pl.when(origin != bx)
                def _():
                    remote(src, landing, {"bx": to}, slot).wait_recv()

            pl.when(to != bx)(go)
            sends.append(gone)
            waits.append(came)

        def keep():
            for layer in range(lp):
                dst[group * lp + layer] = outs[n, bx % own, layer, 0:height]

        if rep == 1:
            keep()
        else:
            pl.when(bx // own == part)(keep)
        for wait in waits:
            wait()

    def y_pass(src, n):
        copies = [push(src, ybuf.at[n, k - 1], {"by": (by + k) % nby}) for k in range(1, nby)]
        total = product(halves(src[...].reshape(L * R, C)), (hy[0, by], hy[1, by]))
        for k in range(1, nby):
            copies[k - 1].wait_recv()
            origin = (by + nby - k) % nby
            total += product(halves(ybuf[n, k - 1].reshape(L * R, C)), (hy[0, origin], hy[1, origin]))
        return total

    def flank_start(rows_too, step, src):
        copies = []
        if rows_too:
            for c in range(3):
                for l in range(L):
                    at = c * L + l
                    row_s[step, 0, at:at + 1] = src[c, l, 0:1]
                    row_s[step, 1, at:at + 1] = src[c, l, R - 1:R]
            col_s[step] = column_tile([src[c, l] for c in range(3) for l in range(L)])
            if step == 0:
                pl.semaphore_wait(barrier, len(greeted))
            copies.append(push(row_s.at[step, 1], row_r.at[step, 0], {"bx": (bx + 1) % nbx}))
            copies.append(push(row_s.at[step, 0], row_r.at[step, 1], {"bx": (bx + nbx - 1) % nbx}))
            tile, land = col_s.at[step], col_r
        else:
            pc_s[step] = column_tile([src[l, 0:R] for l in range(L)])
            tile, land = pc_s.at[step], pc_r
        copies.append(push(tile, land.at[step, 0], {"by": (by + 1) % nby}))
        copies.append(push(tile, land.at[step, 1], {"by": (by + nby - 1) % nby}))
        return copies

    for step in range(STEPS):
        src = p_in if step == 0 else p_mid
        flanks = flank_start(True, step, src)
        if step == 0:
            lateral = lam[...]
            previous = None
            for l in range(L):
                pivot = perm[l] * lateral + inter[l] + inter[l + 1]
                if l:
                    pivot = pivot - inter[l] * previous
                inverse = 1.0 / pivot
                coef[l] = inverse
                previous = inter[l + 1] * inverse
                ratio[l] = previous
        for copy in flanks:
            copy.wait_recv()
        low_col = col_r[step, 0]
        high_col = col_r[step, 1]

        def edges(c, l):
            at = c * L + l
            return (row_r[step, 0, at:at + 1], row_r[step, 1, at:at + 1],
                    low_col[:, C // 2 + at:C // 2 + at + 1], high_col[:, at:at + 1])

        zero = jnp.zeros((R, C), jnp.float32)
        for l in range(L):
            low, high, _, _ = edges(0, l)
            _, _, left, right = edges(1, l)
            along_x, along_y = src[0, l], src[1, l]
            above = src[2, l + 1] if l + 1 < L else zero
            below = src[2, l - 1] if l else zero
            q[step, l] = -0.5 * (
                (x_next(along_x, high) - x_prev(along_x, low))
                + (y_next(along_y, right) - y_prev(along_y, left)) + (above - below))
        copies = x_start(q.at[step], 2 * step)
        if step == 0:
            for load in loads:
                load.wait()
        for l in range(L):
            cells = [src[c, l] for c in range(3)]
            squares = [cell * cell for cell in cells]
            whole = squares[0] + squares[1] + squares[2]
            for c in range(3):
                cell, square = cells[c], squares[c]
                low, high, left, right = edges(c, l)
                above = src[c, l + 1] if l + 1 < L else zero
                below = src[c, l - 1] if l else zero
                smooth = stiff[l] * (
                    (x_next(cell, high) + x_prev(cell, low) + y_next(cell, right)
                     + y_prev(cell, left) - 4.0 * cell) + (above + below - 2.0 * cell))
                drive = cell * (
                    2.0 * alpha[l] + 4.0 * landau[0, l] * square
                    + 2.0 * landau[1, l] * (whole - square)
                    + 6.0 * landau[2, l] * (square * square))
                base[c, l] = cell - step_size * (drive - smooth)
        n = 2 * step
        x_mix(copies, n)
        if wide:
            spread(n, step)
            table = (hy[0], hy[1])
            full = jnp.concatenate(
                [z_in[step, j].reshape(L * thin, C) for j in range(nby)], axis=1)
            values = solve(product(halves(full), table), thin)
            full = product(halves(jnp.concatenate(values, axis=0)), table)
            for j in range(nby):
                w_out[step, j] = full[:, j * C:(j + 1) * C].reshape(L, thin, C)
            copies = collect(n + 1, step)
        else:
            x_finish(n, rec_f.at[step], R)
            for l, value in enumerate(solve(y_pass(rec_f.at[step], n), R)):
                phat[step, l] = value
            u[step] = y_pass(phat.at[step], n + 1).reshape(L, R, C)
            copies = x_start(u.at[step], n + 1)
        x_mix(copies, n + 1)
        x_finish(n + 1, rec_i.at[step], R2)
        flanks = flank_start(False, step, rec_i.at[step])
        last = step == STEPS - 1
        target = p_out if last else p_mid
        for l in range(L):
            phi = rec_i[step, l, 0:R]
            low = rec_i[step, l, R:R + 1]
            high = rec_i[step, l, R + 1:R + 2]
            along_x = -0.5 * (x_next(phi, high) - x_prev(phi, low))
            above = rec_i[step, l + 1, 0:R] if l + 1 < L else zero
            below = rec_i[step, l - 1, 0:R] if l else zero
            along_z = -0.5 * (above - below)
            target[0, l] = base[0, l] + step_size * along_x
            target[2, l] = base[2, l] + step_size * along_z
            if last:
                f_out[0, l] = along_x
                f_out[2, l] = along_z
        for copy in flanks:
            copy.wait_recv()
        low_phi = pc_r[step, 0]
        high_phi = pc_r[step, 1]
        for l in range(L):
            phi = rec_i[step, l, 0:R]
            along_y = -0.5 * (y_next(phi, high_phi[:, l:l + 1])
                              - y_prev(phi, low_phi[:, C // 2 + l:C // 2 + l + 1]))
            target[1, l] = base[1, l] + step_size * along_y
            if last:
                f_out[1, l] = along_y
    for wait in sends:
        wait()


def shards(polarization, alpha_field, landau, stiffness, permittivity, interfaces):
    _, L, R, C = polarization.shape
    nbx = lax.axis_size("bx")
    nby = lax.axis_size("by")
    bx = lax.axis_index("bx")
    by = lax.axis_index("by")
    rep = max(1, nbx // L)
    lp = max(1, L // nbx)
    own = nbx // rep
    grid_x, grid_y = nbx * R, nby * C
    R2 = R + PAD
    wide = is_wide(R, nbx, nby, L)
    pool = np if wide else jnp
    make = fixed_table if wide else cas_table
    line = pool.arange(R2, dtype=jnp.int32)
    line = pool.where(line < R, line, pool.where(line == R, -1, R))
    owners = pool.arange(own, dtype=jnp.int32)
    if not wide:
        owners = owners + bx % rep * own
    wanted = ((owners[:, None] * R + line[None, :] + grid_x) % grid_x).reshape(own * R2, 1)
    hx = make(wanted, pool.arange(grid_x, dtype=jnp.int32)[None, :], grid_x)
    every_col = pool.arange(grid_y, dtype=jnp.int32)
    my_rows = bx * R + jnp.arange(R, dtype=jnp.int32)
    my_cols = by * C + jnp.arange(C, dtype=jnp.int32)
    if wide:
        hy = make(every_col[:, None], every_col[None, :], grid_y)
        my_rows = bx * R + by * (R // nby) + jnp.arange(R // nby, dtype=jnp.int32)
        my_cols = jnp.arange(grid_y, dtype=jnp.int32)
    else:
        hy = make(every_col[:, None], my_cols[None, :], grid_y).reshape(2, nby, C, C)
    wave_x = jnp.sin(jnp.pi * my_rows.astype(jnp.float32) / grid_x)
    wave_y = jnp.sin(jnp.pi * my_cols.astype(jnp.float32) / grid_y)
    lam = 4.0 * wave_x[:, None] ** 2 + 4.0 * wave_y[None, :] ** 2
    sizes = (L, R, C, nbx, nby, rep, lp, own)
    n_copies = STEPS * (6 + 2 * (nbx * nby + own if wide else nbx + own + nby))
    f32 = jnp.float32
    vmem = pl.BlockSpec(memory_space=pltpu.VMEM)
    hbm = pl.BlockSpec(memory_space=pltpu.HBM)
    smem = pl.BlockSpec(memory_space=pltpu.SMEM)
    S = STEPS
    scratch = [
        pltpu.VMEM((3, L, R, C), f32), pltpu.VMEM((3, L, R, C), f32),
        pltpu.VMEM((L,) + lam.shape, f32), pltpu.VMEM((L,) + lam.shape, f32),
        pltpu.VMEM((S, L, R, C), f32), pltpu.VMEM((2 * S, lp, grid_x, C), f32),
        pltpu.VMEM((2 * S, own, lp, R2, C), f32), pltpu.VMEM((S, L, R2, C), f32),
        pltpu.VMEM((S, 2, 3 * L, C), f32), pltpu.VMEM((S, 2, 3 * L, C), f32),
        pltpu.VMEM((S, R, C), f32), pltpu.VMEM((S, 2, R, C), f32),
        pltpu.VMEM((S, R, C), f32), pltpu.VMEM((S, 2, R, C), f32),
        pltpu.SemaphoreType.DMA((n_copies,)), pltpu.SemaphoreType.DMA((n_copies,)),
        pltpu.VMEM((L, R, C), f32), pltpu.VMEM(hx.shape, hx.dtype),
        pltpu.VMEM(hy.shape, hy.dtype), pltpu.SemaphoreType.DMA((3,)),
    ]
    if wide:
        thin = (S, nby, L, R // nby, C)
        scratch += [pltpu.VMEM(thin, f32), pltpu.VMEM(thin, f32)]
    else:
        scratch += [
            pltpu.VMEM((S, L, R, C), f32), pltpu.VMEM((2 * S, nby - 1, L, R, C), f32),
            pltpu.VMEM((S, L, R, C), f32), pltpu.VMEM((S, L, R, C), f32),
        ]
    out = jax.ShapeDtypeStruct(polarization.shape, f32)
    return pl.pallas_call(
        functools.partial(kernel, sizes),
        out_shape=(out, out),
        in_specs=[vmem, hbm, smem, smem, smem, smem, vmem, hbm, hbm],
        out_specs=(vmem, vmem),
        scratch_shapes=scratch,
        compiler_params=pltpu.CompilerParams(
            collective_id=0, has_side_effects=True, vmem_limit_bytes=65 * 1000 * 1000),
    )(polarization, alpha_field, landau, stiffness, permittivity, interfaces, lam, hx, hy)


def fits(L, R, C, nbx, nby):
    slab = R // nby
    return (L == nbx and slab == 8 and slab * nby == R and nby > 1 and C % (8 * L) == 0
            and nbx > 2 and nbx & (nbx - 1) == 0 and nby & (nby - 1) == 0)


def partner(index, mask, size):
    other = 0
    bit = 1
    while bit < size:
        here = index // bit % 2
        other = other + bit * (1 - here if mask // bit % 2 else here)
        bit *= 2
    return other


def join(parts, axis):
    return jnp.concatenate(parts, axis=axis)


def fused(sizes, p_h, alpha_h, landau_h, stiff_h, perm_h, inter_h, wx_h, wy_h, hx_h, hy_h,
          base_o, down_o, *scratch):
    L, R, C, nbx, nby = sizes
    (p_mid, base, coef, ratio, a_s, a_r, b_s, b_r, c_s, c_r, d_s, d_r,
     row_s, row_r, col_s, col_r, ssem, rsem, known, p_in, alpha, wx, wy, hx, hy,
     landau, stiff, perm, inter, local_sem) = scratch
    slab = R // nby
    per = C // L
    NX, NY = nbx * R, nby * C
    bx = lax.axis_index("bx")
    by = lax.axis_index("by")
    scale = 1.0 / (NX * NY)
    f32 = jnp.float32
    dot = functools.partial(jnp.dot, preferred_element_type=f32)
    slots = [0]
    sends = []

    barrier = pltpu.get_barrier_semaphore()
    at_x = [partner(bx, a, nbx) for a in range(nbx)]
    at_y = [partner(by, b, nby) for b in range(nby)]
    others = [(a, b) for b in range(nby) for a in range(nbx) if a or b]
    others.sort(key=lambda ab: -(2 * (ab[0] // 4) + ab[0] // 2 % 2 + ab[0] % 2 + ab[1] // 2))
    reach = [1 << i for i in range(1, nbx.bit_length() - 1)]
    greeted = [(a, b) for a, b in others if a < 2] + [(a, 0) for a in reach]
    for a, b in greeted:
        pl.semaphore_signal(
            barrier, inc=1, device_id={"bx": at_x[a], "by": at_y[b]}, device_id_type=MESH)
    mine = pl.multiple_of((bx * nby + by) * per, per)
    loads = [pltpu.make_async_copy(src, dst, local_sem.at[at]) for at, (src, dst) in enumerate((
        (p_h, p_in), (alpha_h, alpha), (wx_h, wx), (wy_h.at[pl.ds(mine, per)], wy), (hx_h, hx),
        (hy_h, hy), (landau_h, landau), (stiff_h, stiff), (perm_h, perm), (inter_h, inter)))]
    for load in loads:
        load.start()

    def push(src, dst, device):
        slot = slots[0]
        slots[0] += 1
        copy = pltpu.make_async_remote_copy(
            src_ref=src, dst_ref=dst, send_sem=ssem.at[slot], recv_sem=rsem.at[slot],
            device_id=device, device_id_type=MESH)
        copy.start()
        sends.append(copy.wait_send)
        return copy

    rows = lax.broadcasted_iota(jnp.int32, (R, C), 0)
    lanes = lax.broadcasted_iota(jnp.int32, (R, C), 1)
    rows8 = lax.broadcasted_iota(jnp.int32, (slab, C), 0)
    lanes8 = lax.broadcasted_iota(jnp.int32, (slab, C), 1)
    zero = jnp.zeros((R, C), f32)
    zero8 = jnp.zeros((slab, C), f32)

    def x_next(f, high):
        return jnp.where(rows == R - 1, high, pltpu.roll(f, R - 1, 0))

    def x_prev(f, low):
        return jnp.where(rows == 0, low, pltpu.roll(f, 1, 0))

    def y_next(f, high):
        return jnp.where(lanes == C - 1, high, pltpu.roll(f, C - 1, 1))

    def y_prev(f, low):
        return jnp.where(lanes == 0, low, pltpu.roll(f, 1, 1))

    def flush(keep):
        while len(sends) > keep:
            sends.pop(0)()

    def charge(n, src, ring):
        sides = (0, nby - 1)
        edge = zero
        for l in range(L):
            along_x, along_y = src[0, l], src[1, l]
            above = src[2, l + 1] if l + 1 < L else zero
            below = src[2, l - 1] if l else zero
            low = high = left = right = 0.0
            if ring:
                lines, column = ring
                low, high = lines[0][0][l:l + 1], lines[1][0][l:l + 1]
                left = column[:, L + l:L + l + 1]
                right = column[:, C // 2 + L + l:C // 2 + L + l + 1]
            value = -0.5 * ((x_next(along_x, high) - x_prev(along_x, low))
                            + (y_next(along_y, right) - y_prev(along_y, left)) + (above - below))
            for j in range(nby):
                a_s[n, j, l] = value[j * slab:(j + 1) * slab]
            edge = jnp.where(lanes == l, -0.5 * along_y[:, 0:1], edge)
            edge = jnp.where(lanes == L + l, 0.5 * along_y[:, C - 1:C], edge)
        near = [-0.5 * join([src[0, l, 0:1] for l in range(L)], 0),
                0.5 * join([src[0, l, R - 1:R] for l in range(L)], 0)]
        corner = [None, None]
        if ring:
            for side, sign in enumerate((-0.5, 0.5)):
                first, second, third = lines[side]
                turned = (jnp.where(lanes8 == C - 1, 0.0, pltpu.roll(second, C - 1, 1))
                          - jnp.where(lanes8 == 0, 0.0, pltpu.roll(second, 1, 1)))
                risen = (jnp.where(rows8 == L - 1, 0.0, pltpu.roll(third, L - 1, 0))
                         - jnp.where(rows8 == 0, 0.0, pltpu.roll(third, 1, 0)))
                near[side] = near[side] - 0.5 * (turned + risen)
                a_s[n, sides[side], L + 2] = sign * first
                corner[side] = jnp.where(
                    lanes8 == 4 * L, sign * first[:, 0:1] - 0.5 * second[:, 0:1],
                    jnp.where(lanes8 == 4 * L + 1,
                              sign * first[:, C - 1:C] + 0.5 * second[:, C - 1:C], 0.0))
            layer = lanes % L
            turned = -0.5 * (x_next(column, 0.0) - x_prev(column, 0.0))
            risen = -0.5 * (jnp.where(layer == L - 1, 0.0, pltpu.roll(column, C - 1, 1))
                            - jnp.where(layer == 0, 0.0, pltpu.roll(column, 1, 1)))
            both = turned + pltpu.roll(risen, C - 2 * L, 1)
            low = edge + both
            high = edge + pltpu.roll(both, C // 2 + L, 1)
            far_low = -0.5 * pltpu.roll(column, L, 1)
            far_high = 0.5 * pltpu.roll(column, C // 2 + 2 * L, 1)
            group = lanes // L
            edge = jnp.where(group == 0, low, jnp.where(group == 1, high, jnp.where(
                group == 2, far_low, jnp.where(group == 3, far_high, 0.0))))
        for side in range(2):
            a_s[n, sides[side], L + 1] = near[side]
        for j in range(nby):
            piece = edge[j * slab:(j + 1) * slab]
            if ring and j in sides:
                piece = piece + corner[sides.index(j)]
            a_s[n, j, L] = piece
            if j not in sides:
                a_s[n, j, L + 1:L + 3] = jnp.zeros((2, slab, C), f32)

    def ring_of(n):
        weight8 = zero8
        weight = zero
        layer = lanes % L
        for l in range(L):
            weight8 = jnp.where(rows8 == l, step_size * stiff[l], weight8)
            weight = jnp.where(layer == l, step_size * stiff[l], weight)
        lines = [[weight8 * row_s[n, side, c * L:(c + 1) * L] for c in range(3)]
                 for side in range(2)]
        return lines, weight * col_s[n]

    rim_slab = (by == 0) | (by == nby - 1)

    def has_rim(b, here):
        return nby != 4 or (b in (0, nby - 1)) == here

    def either(action):
        if nby != 4:
            action(True)
        else:
            pl.when(rim_slab)(functools.partial(action, True))
            pl.when(jnp.logical_not(rim_slab))(functools.partial(action, False))

    def exchange(targets, build, by_target):
        first = slots[0]
        slots[0] += len(targets)

        def make(at, whole):
            a, b = targets[at]
            src, dst = build(a, b, whole)
            return pltpu.make_async_remote_copy(
                src_ref=src, dst_ref=dst, send_sem=ssem.at[first + at],
                recv_sem=rsem.at[first + at], device_id={"bx": at_x[a], "by": at_y[b]},
                device_id_type=MESH)

        def outgoing(here):
            return [make(at, has_rim(b, here) if by_target else here)
                    for at, (a, b) in enumerate(targets)]

        def start(here):
            for copy in outgoing(here):
                copy.start()

        def sent(here):
            for copy in outgoing(here):
                copy.wait_send()

        def came(here):
            for at, (a, b) in enumerate(targets):
                make(at, here if by_target else has_rim(b, here)).wait_recv()

        either(start)
        sends.append(functools.partial(either, sent))
        return functools.partial(either, came)

    def among_y(source, landing, n, count, by_target):
        def build(a, b, whole):
            part = pl.ds(0, count if whole else L + 1)
            return source.at[n, at_y[b], part], landing.at[n, by, part]

        arrive = exchange([(0, b) for b in range(nby - 1, 0, -1)], build, by_target)
        landing[n, by, 0:count] = source[n, by, 0:count]
        return arrive

    def wait(copies):
        if callable(copies):
            copies()
        else:
            for copy in copies:
                copy.wait_recv()

    def spread(source, landing, n, flip, thick):
        def build(a, b, whole):
            part = pl.ds(0, thick if whole else slab)
            to_x, to_y = at_x[a], at_y[b]
            if flip:
                return source.at[n, to_x, to_y, part], landing.at[n, by, bx, part]
            return source.at[n, to_y, to_x, part], landing.at[n, bx, by, part]

        arrive = exchange(others, build, flip)
        if flip:
            landing[n, by, bx, 0:thick] = source[n, bx, by, 0:thick]
        else:
            landing[n, bx, by, 0:thick] = source[n, by, bx, 0:thick]
        return arrive

    def clear_rims():
        for n in range(2):
            for j in range(nby):
                a_r[n, j, L + 1:L + 3] = jnp.zeros((2, slab, C), f32)
                for e in range(nbx):
                    c_r[n, j, e, slab:2 * slab] = zero8

    def swap_groups(tiles):
        height = tiles[0].shape[0]
        group = lax.broadcasted_iota(jnp.int32, (height, C), 1) // per
        tiles = list(tiles)
        s = 1
        while s < L:
            upper = group % (2 * s) >= s
            for at in range(L):
                if at % (2 * s) < s:
                    low, high = tiles[at], tiles[at + s]
                    tiles[at] = jnp.where(upper, pltpu.roll(high, s * per, 1), low)
                    tiles[at + s] = jnp.where(upper, high, pltpu.roll(low, C - s * per, 1))
            s *= 2
        return tiles

    def swap_rows(tile):
        group = lanes8 // per
        s = 1
        while s < L:
            upper = group % (2 * s) >= s
            later = rows8 % (2 * s) >= s
            ahead = pltpu.roll(pltpu.roll(tile, L - s, 0), s * per, 1)
            behind = pltpu.roll(pltpu.roll(tile, s, 0), C - s * per, 1)
            tile = jnp.where(later, jnp.where(upper, tile, behind), jnp.where(upper, ahead, tile))
            s *= 2
        return tile

    def times(full, table):
        height = full.shape[0]
        high = full.astype(jnp.bfloat16)
        wide = high.astype(f32)
        both = join([wide, full - wide], 0).astype(jnp.bfloat16)
        first = dot(both, hy[table, 0])
        return first[:height] + first[height:] + dot(high, hy[table, 1])

    def y_forward(n):
        columns = []
        for j in range(nby):
            from_left = a_r[n, (j + nby - 1) % nby, L]
            from_right = a_r[n, (j + 1) % nby, L]
            tiles = []
            for l in range(L):
                extra = jnp.where(
                    lanes8 == 0, from_left[:, L + l:L + l + 1],
                    jnp.where(lanes8 == C - 1, from_right[:, l:l + 1], 0.0))
                if n:
                    extra = jnp.where(
                        lanes8 == 1, from_left[:, 3 * L + l:3 * L + l + 1],
                        jnp.where(lanes8 == C - 2, from_right[:, 2 * L + l:2 * L + l + 1], extra))
                tiles.append(a_r[n, j, l] + extra)
            near, far = a_r[n, j, L + 1], zero8
            if n:
                near = near + jnp.where(
                    lanes8 == 0, from_left[:, 4 * L + 1:4 * L + 2],
                    jnp.where(lanes8 == C - 1, from_right[:, 4 * L:4 * L + 1], 0.0))
                far = a_r[n, j, L + 2]
            columns.append(join(tiles + [near, far], 0))
        low, high = join(columns[:nby // 2], 1), join(columns[nby // 2:], 1)
        out = join([times(low + high, 0), times(low - high, 1)], 1)
        tiles = [join([out[l * slab:(l + 1) * slab, t * C:(t + 1) * C] for t in range(nby)], 0)
                 for l in range(L)]
        tiles = swap_groups(tiles)
        for t in range(nby):
            halos = [swap_rows(out[(L + k) * slab:(L + k) * slab + L, t * C:(t + 1) * C])
                     for k in range(1 + n)]
            for e in range(L):
                b_s[n, t, e, 0:slab] = tiles[e][t * slab:(t + 1) * slab]
                for k, halo in enumerate(halos):
                    b_s[n, t, e, slab + k:slab + k + 1] = halo[e:e + 1]

    def y_backward(n):
        tiles = swap_groups([join([c_r[n, t, e, 0:slab] for t in range(nby)], 0)
                             for e in range(L)])
        rims = [join([swap_rows(join([c_r[n, t, e, slab + k:slab + k + 1] for e in range(L)], 0))
                      for t in range(nby)], 1) for k in range(2 - n)]
        if n:
            rims.append(jnp.zeros((slab, NY), f32))
        lines = [join([tiles[l][t * slab:(t + 1) * slab] for t in range(nby)], 1)
                 for l in range(L)]
        full = join(lines + rims, 0)
        even, odd = times(full[:, :NY // 2], 0), times(full[:, NY // 2:], 2)
        out = join([even + odd, even - odd], 1)
        near = out[L * slab:L * slab + L]
        for j in range(nby):
            edge = zero8
            left, right = (j + nby - 1) % nby * C, (j + 1) % nby * C
            wanted = [left + C - 1, right]
            if n == 0:
                wanted += [left + C - 2, right + 1, None, j * C, j * C + C - 1]
                edge = jnp.where(lanes8 == 4 * L, near[:, left + C - 1:left + C],
                                 jnp.where(lanes8 == 4 * L + 1, near[:, right:right + 1], edge))
            for l in range(L):
                line = out[l * slab:(l + 1) * slab]
                d_s[n, j, l] = line[:, j * C:(j + 1) * C]
                for at, column in enumerate(wanted):
                    if column is not None:
                        edge = jnp.where(
                            lanes8 == at * L + l, line[:, column:column + 1], edge)
            d_s[n, j, L] = edge
            for k in range(2 - n):
                d_s[n, j, L + 1 + k] = out[(L + k) * slab:(L + k) * slab + L,
                                           j * C:(j + 1) * C]

    def spectrum(n):
        tiles = []
        for i in range(nbx):
            for j in range(nby):
                tile = b_r[n, i, j, 0:slab]
                for k in range(1 + n):
                    line = slice(slab + k, slab + k + 1)
                    if j == 0:
                        tile = tile + jnp.where(
                            rows8 == k, b_r[n, (i + nbx - 1) % nbx, nby - 1, line], 0.0)
                    if j == nby - 1:
                        tile = tile + jnp.where(
                            rows8 == slab - 1 - k, b_r[n, (i + 1) % nbx, 0, line], 0.0)
                tiles.append(tile)
        full = join(tiles, 0).T
        high = full.astype(jnp.bfloat16)
        wide = high.astype(f32)
        both = join([wide, full - wide], 0).astype(jnp.bfloat16)
        first = dot(both, hx[0])
        out = (first[:C] + first[C:] + dot(high, hx[1])) * scale
        return [out[l * per:(l + 1) * per] for l in range(L)]

    def solve(sources):
        primes = []
        for l in range(L):
            source = sources[l]
            if l:
                source = source + inter[l] * primes[-1]
            primes.append(source * coef[l])
        values = [primes[-1]]
        for l in range(L - 2, -1, -1):
            values.insert(0, primes[l] + ratio[l] * values[0])
        return values

    def x_backward(n, values):
        high, low = halves(join(values, 0))
        turn = functools.partial(
            lax.dot_general, dimension_numbers=(((1,), (1,)), ((), ())),
            preferred_element_type=f32)
        first = turn(hx[...].reshape(2 * NX, NX), high)
        out = first[:NX] + first[NX:] + turn(hx[0], low)
        for i in range(nbx):
            for j in range(nby):
                at = i * R + j * slab
                c_s[n, i, j, 0:slab] = out[at:at + slab]
                for k in range(2 - n):
                    line = (at - 1 - k if j == 0 else at + slab + k) % NX
                    c_s[n, i, j, slab + k:slab + k + 1] = out[line:line + 1]

    def flank_start(n, src):
        tile = zero
        for c in range(3):
            for l in range(L):
                at = c * L + l
                cell = src[c, l]
                row_s[n, 0, at:at + 1] = cell[0:1]
                row_s[n, 1, at:at + 1] = cell[R - 1:R]
                tile = jnp.where(lanes == at, cell[:, 0:1], tile)
                tile = jnp.where(lanes == C // 2 + at, cell[:, C - 1:C], tile)
        col_s[n] = tile

    def flank_send(n):
        return [
            push(row_s.at[n, 1], row_r.at[n, 0], {"bx": (bx + 1) % nbx}),
            push(row_s.at[n, 0], row_r.at[n, 1], {"bx": (bx + nbx - 1) % nbx}),
            push(col_s.at[n], col_r.at[n, 0], {"by": (by + 1) % nby}),
            push(col_s.at[n], col_r.at[n, 1], {"by": (by + nby - 1) % nby})]

    def relax_inside(src):
        for l in range(L):
            cells = [src[c, l] for c in range(3)]
            squares = [cell * cell for cell in cells]
            whole = squares[0] + squares[1] + squares[2]
            for c in range(3):
                cell, square = cells[c], squares[c]
                above = src[c, l + 1] if l + 1 < L else zero
                below = src[c, l - 1] if l else zero
                smooth = stiff[l] * (
                    (x_next(cell, 0.0) + x_prev(cell, 0.0) + y_next(cell, 0.0)
                     + y_prev(cell, 0.0) - 4.0 * cell) + (above + below - 2.0 * cell))
                drive = cell * (
                    2.0 * alpha[l] + 4.0 * landau[0, l] * square
                    + 2.0 * landau[1, l] * (whole - square)
                    + 6.0 * landau[2, l] * (square * square))
                base[c, l] = cell - step_size * (drive - smooth)

    def flank_lines(n):
        return [[row_r[n, side, c * L:(c + 1) * L] for c in range(3)] for side in range(2)]

    def relax_edges(lines, low_col, high_col, target):
        for l in range(L):
            weight = step_size * stiff[l]
            for c in range(3):
                at = c * L + l
                add = jnp.where(lanes == 0, low_col[:, C // 2 + at:C // 2 + at + 1], 0.0)
                add = add + jnp.where(lanes == C - 1, high_col[:, at:at + 1], 0.0)
                add = add + jnp.where(rows == 0, lines[0][c][l:l + 1], 0.0)
                add = add + jnp.where(rows == R - 1, lines[1][c][l:l + 1], 0.0)
                target[c, l] = base[c, l] + weight * add

    def moved_rim():
        lines = flank_lines(1)
        corners = []
        for side, owner in enumerate((0, nby - 1)):
            inner = join([d_r[0, owner, l, side * (slab - 1):side * (slab - 1) + 1]
                          for l in range(L)], 0)
            near, far = d_r[0, owner, L + 1], d_r[0, owner, L + 2]
            edge = d_r[0, owner, L]
            low, high = edge[:, 4 * L:4 * L + 1], edge[:, 4 * L + 1:4 * L + 2]
            down = [inner - far if side == 0 else far - inner,
                    jnp.where(lanes8 == C - 1, high, pltpu.roll(near, C - 1, 1))
                    - jnp.where(lanes8 == 0, low, pltpu.roll(near, 1, 1)),
                    jnp.where(rows8 == L - 1, 0.0, pltpu.roll(near, L - 1, 0))
                    - jnp.where(rows8 == 0, 0.0, pltpu.roll(near, 1, 0))]
            lines[side] = [line - (0.5 * step_size) * part
                           for line, part in zip(lines[side], down)]
            spot = jnp.where(lanes8 == rows8, low, jnp.where(lanes8 == rows8 + L, high, 0.0))
            corners.append(jnp.sum(spot, axis=0, keepdims=True))
        edge = join([d_r[0, j, L] for j in range(nby)], 0)
        layer = lanes % L
        group = lanes // L
        across = pltpu.roll(edge, C - 5 * L, 1) - pltpu.roll(edge, C - 2 * L, 1)
        down = [x_next(edge, corners[1]) - x_prev(edge, corners[0]),
                jnp.where(group == 0, across, -across),
                jnp.where(layer == L - 1, 0.0, pltpu.roll(edge, C - 1, 1))
                - jnp.where(layer == 0, 0.0, pltpu.roll(edge, 1, 1))]
        low_col, high_col = col_r[1, 0], col_r[1, 1]
        for c in range(3):
            part = (0.5 * step_size) * down[c]
            low_col = low_col - jnp.where(
                group == C // (2 * L) + c, pltpu.roll(part, C // 2 + c * L, 1), 0.0)
            high_col = high_col - jnp.where(
                group == c, pltpu.roll(part, (C + c * L - L) % C, 1), 0.0)
        return lines, low_col, high_col

    def field(n):
        edge = join([d_r[n, j, L] for j in range(nby)], 0)
        phis = [join([d_r[n, j, l] for j in range(nby)], 0) for l in range(L)]
        for l in range(L):
            phi = phis[l]
            low = d_r[n, 0, L + 1, l:l + 1]
            high = d_r[n, nby - 1, L + 1, l:l + 1]
            along_x = 0.5 * (x_next(phi, high) - x_prev(phi, low))
            along_y = 0.5 * (y_next(phi, edge[:, L + l:L + l + 1])
                             - y_prev(phi, edge[:, l:l + 1]))
            above = phis[l + 1] if l + 1 < L else zero
            below = phis[l - 1] if l else zero
            yield l, (along_x, along_y, 0.5 * (above - below))

    loads[0].wait()
    charge(0, p_in, None)
    pl.semaphore_wait(barrier, len(greeted))

    def tell(at):
        pl.semaphore_signal(
            known.at[at], inc=1, device_id={"bx": at_x[reach[at]]}, device_id_type=MESH)

    tell(0)
    first_a = among_y(a_s, a_r, 0, L + 2, True)
    if nby == 4:
        pl.when(jnp.logical_not(rim_slab))(clear_rims)
    flank_start(0, p_in)
    loads[1].wait()
    for load in loads[6:]:
        load.wait()
    relax_inside(p_in)
    charge(1, base, ring_of(0))
    second_a = among_y(a_s, a_r, 1, L + 3, True)
    for at in range(1, len(reach)):
        pl.semaphore_wait(known.at[at - 1], 1)
        tell(at)
    loads[2].wait()
    loads[3].wait()
    wave_x = wx[0:1]
    wave_y = join([wy[...]] * (NX // C), 1)
    lateral = wave_x + wave_y
    previous = None
    for l in range(L):
        pivot = perm[l] * lateral + inter[l] + inter[l + 1]
        if l:
            pivot = pivot - inter[l] * previous
        inverse = 1.0 / pivot
        coef[l] = inverse
        previous = inter[l + 1] * inverse
        ratio[l] = previous
    loads[4].wait()
    loads[5].wait()
    wait(first_a)
    y_forward(0)
    pl.semaphore_wait(known.at[len(reach) - 1], 1)
    first_b = spread(b_s, b_r, 0, False, slab + 1)
    wait(second_a)
    y_forward(1)
    second_b = spread(b_s, b_r, 1, False, slab + 2)
    flanks = flank_send(0)
    wait(first_b)
    values = solve(spectrum(0))
    x_backward(0, values)
    first_c = spread(c_s, c_r, 0, True, slab + 2)
    bend = -(wave_x * (1.0 - 0.25 * wave_x) + wave_y * (1.0 - 0.25 * wave_y))
    slopes = []
    none = jnp.zeros_like(values[0])
    for l in range(L):
        above = values[l + 1] if l + 1 < L else none
        below = values[l - 1] if l else none
        slopes.append(0.5 * (above - below))
    moved = []
    for l in range(L):
        above = slopes[l + 1] if l + 1 < L else none
        below = slopes[l - 1] if l else none
        moved.append(step_size * (bend * values[l] + 0.5 * (above - below)))
    wait(second_b)
    x_backward(1, solve([here + more for here, more in zip(spectrum(1), moved)]))
    second_c = spread(c_s, c_r, 1, True, slab + 1)
    wait(flanks)
    relax_edges(flank_lines(0), col_r[0, 0], col_r[0, 1], base)
    flank_start(1, base)
    flanks = flank_send(1)
    flush(len(flanks) + 2)
    wait(first_c)
    y_backward(0)
    first_d = among_y(d_s, d_r, 0, L + 3, False)
    wait(second_c)
    y_backward(1)
    second_d = among_y(d_s, d_r, 1, L + 2, False)
    wait(first_d)
    for l, parts in field(0):
        for c in range(3):
            p_mid[c, l] = base[c, l] - step_size * parts[c]
    wait(flanks)
    rim = moved_rim()
    relax_inside(p_mid)
    relax_edges(*rim, base_o)
    flush(1)
    wait(second_d)
    for l, parts in field(1):
        for c in range(3):
            down_o[c, l] = parts[c]
    flush(0)


def fused_shards(polarization, alpha_field, landau, stiffness, permittivity, interfaces):
    _, L, R, C = polarization.shape
    nbx = lax.axis_size("bx")
    nby = lax.axis_size("by")
    grid_x, grid_y = nbx * R, nby * C
    per = C // L
    line = np.arange(grid_x)
    hx = fixed_table(line[:, None], line[None, :], grid_x)
    line = np.arange(grid_y // 2)
    modes = np.concatenate([2 * line, 2 * line + 1])
    hy = jnp.stack([fixed_table(left, right, grid_y) for left, right in (
        (line[:, None], 2 * line[None, :]), (line[:, None], 2 * line[None, :] + 1),
        (2 * line[:, None] + 1, line[None, :]))])
    wave_x = 4.0 * np.sin(np.pi * np.arange(grid_x) / grid_x) ** 2
    wave_x = jnp.asarray(np.tile(wave_x[None, :], (8, 1)).astype(np.float32))
    at = np.arange(nbx * nby)
    first = (at % nby) * C + (at // nby) * per
    mode = modes[(first[:, None] + np.arange(per)[None, :]).reshape(-1)]
    wave_y = 4.0 * np.sin(np.pi * mode / grid_y) ** 2
    wave_y = jnp.asarray(np.tile(wave_y[:, None], (1, C)).astype(np.float32))
    f32 = jnp.float32
    hbm = pl.BlockSpec(memory_space=pltpu.HBM)
    S = 2
    n_copies = S * (4 + 2 * (nby - 1) + 2 * (nbx * nby - 1))
    by_y = pltpu.VMEM((S, nby, L + 3, 8, C), f32)
    by_mode = pltpu.VMEM((S, nby, nbx, 16, C), f32)
    by_place = pltpu.VMEM((S, nbx, nby, 16, C), f32)
    scratch = [
        pltpu.VMEM((3, L, R, C), f32), pltpu.VMEM((3, L, R, C), f32),
        pltpu.VMEM((L, per, grid_x), f32), pltpu.VMEM((L, per, grid_x), f32),
        by_y, by_y, by_mode, by_place, by_place, by_mode, by_y, by_y,
        pltpu.VMEM((S, 2, 3 * L, C), f32), pltpu.VMEM((S, 2, 3 * L, C), f32),
        pltpu.VMEM((S, R, C), f32), pltpu.VMEM((S, 2, R, C), f32),
        pltpu.SemaphoreType.DMA((n_copies,)), pltpu.SemaphoreType.DMA((n_copies,)),
        pltpu.SemaphoreType.REGULAR((nbx.bit_length(),)), pltpu.VMEM((3, L, R, C), f32),
        pltpu.VMEM((L, R, C), f32), pltpu.VMEM(wave_x.shape, f32), pltpu.VMEM((per, C), f32),
        pltpu.VMEM(hx.shape, hx.dtype), pltpu.VMEM(hy.shape, hy.dtype),
        pltpu.SMEM(landau.shape, f32), pltpu.SMEM(stiffness.shape, f32),
        pltpu.SMEM(permittivity.shape, f32), pltpu.SMEM(interfaces.shape, f32),
        pltpu.SemaphoreType.DMA((10,)),
    ]
    out = pltpu.VMEM(polarization.shape, f32)
    base, down = pl.pallas_call(
        functools.partial(fused, (L, R, C, nbx, nby)),
        out_shape=(out, out),
        in_specs=[hbm] * 10,
        out_specs=(pl.BlockSpec(memory_space=pltpu.VMEM), pl.BlockSpec(memory_space=pltpu.VMEM)),
        scratch_shapes=scratch,
        compiler_params=pltpu.CompilerParams(
            collective_id=0, has_side_effects=True, vmem_limit_bytes=66 * 1000 * 1000),
    )(polarization, alpha_field, landau, stiffness, permittivity, interfaces,
      wave_x, wave_y, hx, hy)
    return base - step_size * down, -down


def solution(mesh):
    def run(polarization, *rest):
        _, L, R, C = polarization.shape
        body = fused_shards if fits(L, R, C, lax.axis_size("bx"), lax.axis_size("by")) else shards
        return body(polarization, *rest)

    return jax.shard_map(
        run,
        mesh=mesh,
        in_specs=(P(None, None, "bx", "by"), P(None, "bx", "by"), P(), P(), P(), P()),
        out_specs=(P(None, None, "bx", "by"), P(None, None, "bx", "by")),
        check_vma=False,
    )
```

```python
import functools

import jax
import jax.numpy as jnp
import numpy as np
from jax import lax
from jax.experimental import pallas as pl
from jax.experimental.pallas import tpu as pltpu
from jax.sharding import PartitionSpec as P

STEPS = 2
step_size = 0.05
MESH = pl.DeviceIdType.MESH
PAD = 8


def cas_table(left, right, length):
    turns = left * right % length
    angle = 2.0 * jnp.pi / length * turns.astype(jnp.float32)
    table = jnp.cos(angle) + jnp.sin(angle)
    high = lax.reduce_precision(table, 8, 7)
    return jnp.stack([high.astype(jnp.bfloat16), (table - high).astype(jnp.bfloat16)])


def fixed_table(left, right, length):
    angle = 2.0 * np.pi / length * (left * right % length)
    table = (np.cos(angle) + np.sin(angle)).astype(np.float32)
    high = table.astype(jnp.bfloat16)
    low = (table - high.astype(np.float32)).astype(jnp.bfloat16)
    return jnp.asarray(np.stack([high, low]))


def is_wide(rows, nbx, nby, layers):
    return layers % nbx == 0 and rows % (8 * nby) == 0


def halves(value):
    high = value.astype(jnp.bfloat16)
    low = (value - high.astype(jnp.float32)).astype(jnp.bfloat16)
    return high, low


def product(left, right):
    dot = functools.partial(jnp.dot, preferred_element_type=jnp.float32)
    return dot(left[0], right[0]) + (dot(left[0], right[1]) + dot(left[1], right[0]))


def kernel(sizes, p_in, alpha_h, landau, stiff, perm, inter, lam, hx_h, hy_h, p_out, f_out, *scratch):
    L, R, C, nbx, nby, rep, lp, own = sizes
    (p_mid, base, coef, ratio, q, inb, outs, rec_i,
     row_s, row_r, col_s, col_r, pc_s, pc_r, ssem, rsem,
     alpha, hx, hy, local_sem) = scratch[:20]
    wide = is_wide(R, nbx, nby, L)
    if wide:
        z_in, w_out = scratch[20:]
    else:
        rec_f, ybuf, phat, u = scratch[20:]
    thin = R // nby
    R2 = R + PAD
    bx = lax.axis_index("bx")
    by = lax.axis_index("by")
    group = bx // rep
    part = bx % rep
    scale = 1.0 / (R * nbx * C * nby)
    loads = [pltpu.make_async_copy(src, dst, local_sem.at[at]) for at, (src, dst) in
             enumerate(((alpha_h, alpha), (hx_h, hx), (hy_h, hy)))]
    for load in loads:
        load.start()
    slots = [0]
    sends = []

    barrier = pltpu.get_barrier_semaphore()
    others = [(a, b) for b in range(nby) for a in range(nbx) if a or b]
    greeted = [(a, b) for a, b in others if wide or not a or not b]
    for a, b in greeted:
        pl.semaphore_signal(
            barrier, inc=1, device_id={"bx": (bx + a) % nbx, "by": (by + b) % nby},
            device_id_type=MESH)

    def remote(src, dst, device, slot):
        return pltpu.make_async_remote_copy(
            src_ref=src, dst_ref=dst, send_sem=ssem.at[slot], recv_sem=rsem.at[slot],
            device_id=device, device_id_type=MESH)

    def fresh():
        slots[0] += 1
        return slots[0] - 1

    def push(src, dst, device):
        copy = remote(src, dst, device, fresh())
        copy.start()
        sends.append(copy.wait_send)
        return copy

    rows = lax.broadcasted_iota(jnp.int32, (R, C), 0)
    lanes = lax.broadcasted_iota(jnp.int32, (R, C), 1)

    def x_next(f, high):
        return jnp.where(rows == R - 1, high, pltpu.roll(f, R - 1, 0))

    def x_prev(f, low):
        return jnp.where(rows == 0, low, pltpu.roll(f, 1, 0))

    def y_next(f, high):
        return jnp.where(lanes == C - 1, high, pltpu.roll(f, C - 1, 1))

    def y_prev(f, low):
        return jnp.where(lanes == 0, low, pltpu.roll(f, 1, 1))

    def column_tile(blocks):
        tile = jnp.zeros((R, C), jnp.float32)
        for at, block in enumerate(blocks):
            tile = jnp.where(lanes == at, block[:, 0:1], tile)
            tile = jnp.where(lanes == C // 2 + at, block[:, C - 1:C], tile)
        return tile

    def x_start(src, n):
        mine = inb.at[n, :, pl.ds(pl.multiple_of(bx * R, R), R)]
        copies = []
        for k in range(1, nbx):
            to = (bx + k) % nbx
            copies.append(push(src.at[pl.ds(to // rep * lp, lp)], mine, {"bx": to}))
        for layer in range(lp):
            inb[n, layer, pl.ds(pl.multiple_of(bx * R, R), R)] = src[group * lp + layer]
        return copies

    def x_mix(copies, n):
        for copy in copies:
            copy.wait_recv()
        table = (hx[0], hx[1])
        for layer in range(lp):
            outs[n, :, layer] = product(table, halves(inb[n, layer])).reshape(own, R2, C)

    def spread(n, step):
        copies = []
        for a, b in others:
            to_x, to_y = (bx + a) % nbx, (by + b) % nby
            copies.append(push(
                outs.at[n, to_x, :, pl.ds(pl.multiple_of(to_y * thin, thin), thin)],
                z_in.at[step, by, pl.ds(bx * lp, lp)], {"bx": to_x, "by": to_y}))
        for layer in range(lp):
            z_in[step, by, bx * lp + layer] = outs[
                n, bx, layer, pl.ds(pl.multiple_of(by * thin, thin), thin)]
        for copy in copies:
            copy.wait_recv()

    def collect(n, step):
        at = pl.ds(pl.multiple_of(bx * R + by * thin, thin), thin)
        copies = []
        for a, b in others:
            to_x, to_y = (bx + a) % nbx, (by + b) % nby
            copies.append(push(
                w_out.at[step, to_y, pl.ds(to_x * lp, lp)], inb.at[n, :, at],
                {"bx": to_x, "by": to_y}))
        for layer in range(lp):
            inb[n, layer, at] = w_out[step, by, bx * lp + layer]
        return copies

    def solve(spectrum, height):
        primes = []
        for l in range(L):
            source = spectrum[l * height:(l + 1) * height] * scale
            if l:
                source = source + inter[l] * primes[-1]
            primes.append(source * coef[l])
        values = [primes[-1]]
        for l in range(L - 2, -1, -1):
            values.insert(0, primes[l] + ratio[l] * values[0])
        return values

    def x_finish(n, dst, height):
        waits = []
        landing = dst.at[pl.ds(group * lp, lp)]
        for t in range(own):
            local = (group + t) % own
            to = part * own + local
            src = outs.at[n, local, :, pl.ds(0, height)]
            if rep == 1:
                if t == 0:
                    continue
                waits.append(push(src, landing, {"bx": to}).wait_recv)
                continue
            slot = fresh()

            def go(src=src, to=to, slot=slot):
                remote(src, landing, {"bx": to}, slot).start()

            def gone(src=src, to=to, slot=slot):
                @pl.when(to != bx)
                def _():
                    remote(src, landing, {"bx": to}, slot).wait_send()

            def came(src=src, to=to, slot=slot, t=t):
                origin = (bx % own + own - t) % own * rep + bx // own

                @pl.when(origin != bx)
                def _():
                    remote(src, landing, {"bx": to}, slot).wait_recv()

            pl.when(to != bx)(go)
            sends.append(gone)
            waits.append(came)

        def keep():
            for layer in range(lp):
                dst[group * lp + layer] = outs[n, bx % own, layer, 0:height]

        if rep == 1:
            keep()
        else:
            pl.when(bx // own == part)(keep)
        for wait in waits:
            wait()

    def y_pass(src, n):
        copies = [push(src, ybuf.at[n, k - 1], {"by": (by + k) % nby}) for k in range(1, nby)]
        total = product(halves(src[...].reshape(L * R, C)), (hy[0, by], hy[1, by]))
        for k in range(1, nby):
            copies[k - 1].wait_recv()
            origin = (by + nby - k) % nby
            total += product(halves(ybuf[n, k - 1].reshape(L * R, C)), (hy[0, origin], hy[1, origin]))
        return total

    def flank_start(rows_too, step, src):
        copies = []
        if rows_too:
            for c in range(3):
                for l in range(L):
                    at = c * L + l
                    row_s[step, 0, at:at + 1] = src[c, l, 0:1]
                    row_s[step, 1, at:at + 1] = src[c, l, R - 1:R]
            col_s[step] = column_tile([src[c, l] for c in range(3) for l in range(L)])
            if step == 0:
                pl.semaphore_wait(barrier, len(greeted))
            copies.append(push(row_s.at[step, 1], row_r.at[step, 0], {"bx": (bx + 1) % nbx}))
            copies.append(push(row_s.at[step, 0], row_r.at[step, 1], {"bx": (bx + nbx - 1) % nbx}))
            tile, land = col_s.at[step], col_r
        else:
            pc_s[step] = column_tile([src[l, 0:R] for l in range(L)])
            tile, land = pc_s.at[step], pc_r
        copies.append(push(tile, land.at[step, 0], {"by": (by + 1) % nby}))
        copies.append(push(tile, land.at[step, 1], {"by": (by + nby - 1) % nby}))
        return copies

    for step in range(STEPS):
        src = p_in if step == 0 else p_mid
        flanks = flank_start(True, step, src)
        if step == 0:
            lateral = lam[...]
            previous = None
            for l in range(L):
                pivot = perm[l] * lateral + inter[l] + inter[l + 1]
                if l:
                    pivot = pivot - inter[l] * previous
                inverse = 1.0 / pivot
                coef[l] = inverse
                previous = inter[l + 1] * inverse
                ratio[l] = previous
        for copy in flanks:
            copy.wait_recv()
        low_col = col_r[step, 0]
        high_col = col_r[step, 1]

        def edges(c, l):
            at = c * L + l
            return (row_r[step, 0, at:at + 1], row_r[step, 1, at:at + 1],
                    low_col[:, C // 2 + at:C // 2 + at + 1], high_col[:, at:at + 1])

        zero = jnp.zeros((R, C), jnp.float32)
        for l in range(L):
            low, high, _, _ = edges(0, l)
            _, _, left, right = edges(1, l)
            along_x, along_y = src[0, l], src[1, l]
            above = src[2, l + 1] if l + 1 < L else zero
            below = src[2, l - 1] if l else zero
            q[step, l] = -0.5 * (
                (x_next(along_x, high) - x_prev(along_x, low))
                + (y_next(along_y, right) - y_prev(along_y, left)) + (above - below))
        copies = x_start(q.at[step], 2 * step)
        if step == 0:
            for load in loads:
                load.wait()
        for l in range(L):
            cells = [src[c, l] for c in range(3)]
            squares = [cell * cell for cell in cells]
            whole = squares[0] + squares[1] + squares[2]
            for c in range(3):
                cell, square = cells[c], squares[c]
                low, high, left, right = edges(c, l)
                above = src[c, l + 1] if l + 1 < L else zero
                below = src[c, l - 1] if l else zero
                smooth = stiff[l] * (
                    (x_next(cell, high) + x_prev(cell, low) + y_next(cell, right)
                     + y_prev(cell, left) - 4.0 * cell) + (above + below - 2.0 * cell))
                drive = cell * (
                    2.0 * alpha[l] + 4.0 * landau[0, l] * square
                    + 2.0 * landau[1, l] * (whole - square)
                    + 6.0 * landau[2, l] * (square * square))
                base[c, l] = cell - step_size * (drive - smooth)
        n = 2 * step
        x_mix(copies, n)
        if wide:
            spread(n, step)
            table = (hy[0], hy[1])
            full = jnp.concatenate(
                [z_in[step, j].reshape(L * thin, C) for j in range(nby)], axis=1)
            values = solve(product(halves(full), table), thin)
            full = product(halves(jnp.concatenate(values, axis=0)), table)
            for j in range(nby):
                w_out[step, j] = full[:, j * C:(j + 1) * C].reshape(L, thin, C)
            copies = collect(n + 1, step)
        else:
            x_finish(n, rec_f.at[step], R)
            for l, value in enumerate(solve(y_pass(rec_f.at[step], n), R)):
                phat[step, l] = value
            u[step] = y_pass(phat.at[step], n + 1).reshape(L, R, C)
            copies = x_start(u.at[step], n + 1)
        x_mix(copies, n + 1)
        x_finish(n + 1, rec_i.at[step], R2)
        flanks = flank_start(False, step, rec_i.at[step])
        last = step == STEPS - 1
        target = p_out if last else p_mid
        for l in range(L):
            phi = rec_i[step, l, 0:R]
            low = rec_i[step, l, R:R + 1]
            high = rec_i[step, l, R + 1:R + 2]
            along_x = -0.5 * (x_next(phi, high) - x_prev(phi, low))
            above = rec_i[step, l + 1, 0:R] if l + 1 < L else zero
            below = rec_i[step, l - 1, 0:R] if l else zero
            along_z = -0.5 * (above - below)
            target[0, l] = base[0, l] + step_size * along_x
            target[2, l] = base[2, l] + step_size * along_z
            if last:
                f_out[0, l] = along_x
                f_out[2, l] = along_z
        for copy in flanks:
            copy.wait_recv()
        low_phi = pc_r[step, 0]
        high_phi = pc_r[step, 1]
        for l in range(L):
            phi = rec_i[step, l, 0:R]
            along_y = -0.5 * (y_next(phi, high_phi[:, l:l + 1])
                              - y_prev(phi, low_phi[:, C // 2 + l:C // 2 + l + 1]))
            target[1, l] = base[1, l] + step_size * along_y
            if last:
                f_out[1, l] = along_y
    for wait in sends:
        wait()


def shards(polarization, alpha_field, landau, stiffness, permittivity, interfaces):
    _, L, R, C = polarization.shape
    nbx = lax.axis_size("bx")
    nby = lax.axis_size("by")
    bx = lax.axis_index("bx")
    by = lax.axis_index("by")
    rep = max(1, nbx // L)
    lp = max(1, L // nbx)
    own = nbx // rep
    grid_x, grid_y = nbx * R, nby * C
    R2 = R + PAD
    wide = is_wide(R, nbx, nby, L)
    pool = np if wide else jnp
    make = fixed_table if wide else cas_table
    line = pool.arange(R2, dtype=jnp.int32)
    line = pool.where(line < R, line, pool.where(line == R, -1, R))
    owners = pool.arange(own, dtype=jnp.int32)
    if not wide:
        owners = owners + bx % rep * own
    wanted = ((owners[:, None] * R + line[None, :] + grid_x) % grid_x).reshape(own * R2, 1)
    hx = make(wanted, pool.arange(grid_x, dtype=jnp.int32)[None, :], grid_x)
    every_col = pool.arange(grid_y, dtype=jnp.int32)
    my_rows = bx * R + jnp.arange(R, dtype=jnp.int32)
    my_cols = by * C + jnp.arange(C, dtype=jnp.int32)
    if wide:
        hy = make(every_col[:, None], every_col[None, :], grid_y)
        my_rows = bx * R + by * (R // nby) + jnp.arange(R // nby, dtype=jnp.int32)
        my_cols = jnp.arange(grid_y, dtype=jnp.int32)
    else:
        hy = make(every_col[:, None], my_cols[None, :], grid_y).reshape(2, nby, C, C)
    wave_x = jnp.sin(jnp.pi * my_rows.astype(jnp.float32) / grid_x)
    wave_y = jnp.sin(jnp.pi * my_cols.astype(jnp.float32) / grid_y)
    lam = 4.0 * wave_x[:, None] ** 2 + 4.0 * wave_y[None, :] ** 2
    sizes = (L, R, C, nbx, nby, rep, lp, own)
    n_copies = STEPS * (6 + 2 * (nbx * nby + own if wide else nbx + own + nby))
    f32 = jnp.float32
    vmem = pl.BlockSpec(memory_space=pltpu.VMEM)
    hbm = pl.BlockSpec(memory_space=pltpu.HBM)
    smem = pl.BlockSpec(memory_space=pltpu.SMEM)
    S = STEPS
    scratch = [
        pltpu.VMEM((3, L, R, C), f32), pltpu.VMEM((3, L, R, C), f32),
        pltpu.VMEM((L,) + lam.shape, f32), pltpu.VMEM((L,) + lam.shape, f32),
        pltpu.VMEM((S, L, R, C), f32), pltpu.VMEM((2 * S, lp, grid_x, C), f32),
        pltpu.VMEM((2 * S, own, lp, R2, C), f32), pltpu.VMEM((S, L, R2, C), f32),
        pltpu.VMEM((S, 2, 3 * L, C), f32), pltpu.VMEM((S, 2, 3 * L, C), f32),
        pltpu.VMEM((S, R, C), f32), pltpu.VMEM((S, 2, R, C), f32),
        pltpu.VMEM((S, R, C), f32), pltpu.VMEM((S, 2, R, C), f32),
        pltpu.SemaphoreType.DMA((n_copies,)), pltpu.SemaphoreType.DMA((n_copies,)),
        pltpu.VMEM((L, R, C), f32), pltpu.VMEM(hx.shape, hx.dtype),
        pltpu.VMEM(hy.shape, hy.dtype), pltpu.SemaphoreType.DMA((3,)),
    ]
    if wide:
        thin = (S, nby, L, R // nby, C)
        scratch += [pltpu.VMEM(thin, f32), pltpu.VMEM(thin, f32)]
    else:
        scratch += [
            pltpu.VMEM((S, L, R, C), f32), pltpu.VMEM((2 * S, nby - 1, L, R, C), f32),
            pltpu.VMEM((S, L, R, C), f32), pltpu.VMEM((S, L, R, C), f32),
        ]
    out = jax.ShapeDtypeStruct(polarization.shape, f32)
    return pl.pallas_call(
        functools.partial(kernel, sizes),
        out_shape=(out, out),
        in_specs=[vmem, hbm, smem, smem, smem, smem, vmem, hbm, hbm],
        out_specs=(vmem, vmem),
        scratch_shapes=scratch,
        compiler_params=pltpu.CompilerParams(
            collective_id=0, has_side_effects=True, vmem_limit_bytes=65 * 1000 * 1000),
    )(polarization, alpha_field, landau, stiffness, permittivity, interfaces, lam, hx, hy)


def fits(L, R, C, nbx, nby):
    slab = R // nby
    return (L == nbx and slab == 8 and slab * nby == R and nby > 1 and C % (8 * L) == 0
            and nbx > 2 and nbx & (nbx - 1) == 0 and nby & (nby - 1) == 0)


def partner(index, mask, size):
    other = 0
    bit = 1
    while bit < size:
        here = index // bit % 2
        other = other + bit * (1 - here if mask // bit % 2 else here)
        bit *= 2
    return other


def join(parts, axis):
    return jnp.concatenate(parts, axis=axis)


def fused(sizes, p_h, alpha_h, landau_h, stiff_h, perm_h, inter_h, wx_h, wy_h, hx_h, hy_h,
          base_o, down_o, *scratch):
    L, R, C, nbx, nby = sizes
    (p_mid, base, coef, ratio, a_s, a_r, b_s, b_r, c_s, c_r, d_s, d_r,
     row_s, row_r, col_s, col_r, ssem, rsem, known, p_in, alpha, wx, wy, hx, hy,
     landau, stiff, perm, inter, local_sem) = scratch
    slab = R // nby
    per = C // L
    NX, NY = nbx * R, nby * C
    bx = lax.axis_index("bx")
    by = lax.axis_index("by")
    scale = 1.0 / (NX * NY)
    f32 = jnp.float32
    dot = functools.partial(jnp.dot, preferred_element_type=f32)
    slots = [0]
    sends = []

    barrier = pltpu.get_barrier_semaphore()
    at_x = [partner(bx, a, nbx) for a in range(nbx)]
    at_y = [partner(by, b, nby) for b in range(nby)]
    others = [(a, b) for b in range(nby) for a in range(nbx) if a or b]
    others.sort(key=lambda ab: -(2 * (ab[0] // 4) + ab[0] // 2 % 2 + ab[0] % 2 + ab[1] // 2))
    reach = [1 << i for i in range(1, nbx.bit_length() - 1)]
    greeted = [(a, b) for a, b in others if a < 2] + [(a, 0) for a in reach]
    for a, b in greeted:
        pl.semaphore_signal(
            barrier, inc=1, device_id={"bx": at_x[a], "by": at_y[b]}, device_id_type=MESH)
    mine = pl.multiple_of((bx * nby + by) * per, per)
    loads = [pltpu.make_async_copy(src, dst, local_sem.at[at]) for at, (src, dst) in enumerate((
        (p_h, p_in), (alpha_h, alpha), (wx_h, wx), (wy_h.at[pl.ds(mine, per)], wy), (hx_h, hx),
        (hy_h, hy), (landau_h, landau), (stiff_h, stiff), (perm_h, perm), (inter_h, inter)))]
    for load in loads:
        load.start()

    def push(src, dst, device):
        slot = slots[0]
        slots[0] += 1
        copy = pltpu.make_async_remote_copy(
            src_ref=src, dst_ref=dst, send_sem=ssem.at[slot], recv_sem=rsem.at[slot],
            device_id=device, device_id_type=MESH)
        copy.start()
        sends.append(copy.wait_send)
        return copy

    rows = lax.broadcasted_iota(jnp.int32, (R, C), 0)
    lanes = lax.broadcasted_iota(jnp.int32, (R, C), 1)
    rows8 = lax.broadcasted_iota(jnp.int32, (slab, C), 0)
    lanes8 = lax.broadcasted_iota(jnp.int32, (slab, C), 1)
    zero = jnp.zeros((R, C), f32)
    zero8 = jnp.zeros((slab, C), f32)

    def x_next(f, high):
        return jnp.where(rows == R - 1, high, pltpu.roll(f, R - 1, 0))

    def x_prev(f, low):
        return jnp.where(rows == 0, low, pltpu.roll(f, 1, 0))

    def y_next(f, high):
        return jnp.where(lanes == C - 1, high, pltpu.roll(f, C - 1, 1))

    def y_prev(f, low):
        return jnp.where(lanes == 0, low, pltpu.roll(f, 1, 1))

    def flush(keep):
        while len(sends) > keep:
            sends.pop(0)()

    def charge(n, src, ring):
        sides = (0, nby - 1)
        edge = zero
        for l in range(L):
            along_x, along_y = src[0, l], src[1, l]
            above = src[2, l + 1] if l + 1 < L else zero
            below = src[2, l - 1] if l else zero
            low = high = left = right = 0.0
            if ring:
                lines, column = ring
                low, high = lines[0][0][l:l + 1], lines[1][0][l:l + 1]
                left = column[:, L + l:L + l + 1]
                right = column[:, C // 2 + L + l:C // 2 + L + l + 1]
            value = -0.5 * ((x_next(along_x, high) - x_prev(along_x, low))
                            + (y_next(along_y, right) - y_prev(along_y, left)) + (above - below))
            for j in range(nby):
                a_s[n, j, l] = value[j * slab:(j + 1) * slab]
            edge = jnp.where(lanes == l, -0.5 * along_y[:, 0:1], edge)
            edge = jnp.where(lanes == L + l, 0.5 * along_y[:, C - 1:C], edge)
        near = [-0.5 * join([src[0, l, 0:1] for l in range(L)], 0),
                0.5 * join([src[0, l, R - 1:R] for l in range(L)], 0)]
        corner = [None, None]
        if ring:
            for side, sign in enumerate((-0.5, 0.5)):
                first, second, third = lines[side]
                turned = (jnp.where(lanes8 == C - 1, 0.0, pltpu.roll(second, C - 1, 1))
                          - jnp.where(lanes8 == 0, 0.0, pltpu.roll(second, 1, 1)))
                risen = (jnp.where(rows8 == L - 1, 0.0, pltpu.roll(third, L - 1, 0))
                         - jnp.where(rows8 == 0, 0.0, pltpu.roll(third, 1, 0)))
                near[side] = near[side] - 0.5 * (turned + risen)
                a_s[n, sides[side], L + 2] = sign * first
                corner[side] = jnp.where(
                    lanes8 == 4 * L, sign * first[:, 0:1] - 0.5 * second[:, 0:1],
                    jnp.where(lanes8 == 4 * L + 1,
                              sign * first[:, C - 1:C] + 0.5 * second[:, C - 1:C], 0.0))
            layer = lanes % L
            turned = -0.5 * (x_next(column, 0.0) - x_prev(column, 0.0))
            risen = -0.5 * (jnp.where(layer == L - 1, 0.0, pltpu.roll(column, C - 1, 1))
                            - jnp.where(layer == 0, 0.0, pltpu.roll(column, 1, 1)))
            both = turned + pltpu.roll(risen, C - 2 * L, 1)
            low = edge + both
            high = edge + pltpu.roll(both, C // 2 + L, 1)
            far_low = -0.5 * pltpu.roll(column, L, 1)
            far_high = 0.5 * pltpu.roll(column, C // 2 + 2 * L, 1)
            group = lanes // L
            edge = jnp.where(group == 0, low, jnp.where(group == 1, high, jnp.where(
                group == 2, far_low, jnp.where(group == 3, far_high, 0.0))))
        for side in range(2):
            a_s[n, sides[side], L + 1] = near[side]
        for j in range(nby):
            piece = edge[j * slab:(j + 1) * slab]
            if ring and j in sides:
                piece = piece + corner[sides.index(j)]
            a_s[n, j, L] = piece
            if j not in sides:
                a_s[n, j, L + 1:L + 3] = jnp.zeros((2, slab, C), f32)

    def ring_of(n):
        weight8 = zero8
        weight = zero
        layer = lanes % L
        for l in range(L):
            weight8 = jnp.where(rows8 == l, step_size * stiff[l], weight8)
            weight = jnp.where(layer == l, step_size * stiff[l], weight)
        lines = [[weight8 * row_s[n, side, c * L:(c + 1) * L] for c in range(3)]
                 for side in range(2)]
        return lines, weight * col_s[n]

    rim_slab = (by == 0) | (by == nby - 1)

    def has_rim(b, here):
        return nby != 4 or (b in (0, nby - 1)) == here

    def either(action):
        if nby != 4:
            action(True)
        else:
            pl.when(rim_slab)(functools.partial(action, True))
            pl.when(jnp.logical_not(rim_slab))(functools.partial(action, False))

    def exchange(targets, build, by_target):
        first = slots[0]
        slots[0] += len(targets)

        def make(at, whole):
            a, b = targets[at]
            src, dst = build(a, b, whole)
            return pltpu.make_async_remote_copy(
                src_ref=src, dst_ref=dst, send_sem=ssem.at[first + at],
                recv_sem=rsem.at[first + at], device_id={"bx": at_x[a], "by": at_y[b]},
                device_id_type=MESH)

        def outgoing(here):
            return [make(at, has_rim(b, here) if by_target else here)
                    for at, (a, b) in enumerate(targets)]

        def start(here):
            for copy in outgoing(here):
                copy.start()

        def sent(here):
            for copy in outgoing(here):
                copy.wait_send()

        def came(here):
            for at, (a, b) in enumerate(targets):
                make(at, here if by_target else has_rim(b, here)).wait_recv()

        either(start)
        sends.append(functools.partial(either, sent))
        return functools.partial(either, came)

    def among_y(source, landing, n, count, by_target):
        def build(a, b, whole):
            part = pl.ds(0, count if whole else L + 1)
            return source.at[n, at_y[b], part], landing.at[n, by, part]

        arrive = exchange([(0, b) for b in range(nby - 1, 0, -1)], build, by_target)
        landing[n, by, 0:count] = source[n, by, 0:count]
        return arrive

    def wait(copies):
        if callable(copies):
            copies()
        else:
            for copy in copies:
                copy.wait_recv()

    def spread(source, landing, n, flip, thick):
        def build(a, b, whole):
            part = pl.ds(0, thick if whole else slab)
            to_x, to_y = at_x[a], at_y[b]
            if flip:
                return source.at[n, to_x, to_y, part], landing.at[n, by, bx, part]
            return source.at[n, to_y, to_x, part], landing.at[n, bx, by, part]

        arrive = exchange(others, build, flip)
        if flip:
            landing[n, by, bx, 0:thick] = source[n, bx, by, 0:thick]
        else:
            landing[n, bx, by, 0:thick] = source[n, by, bx, 0:thick]
        return arrive

    def clear_rims():
        for n in range(2):
            for j in range(nby):
                a_r[n, j, L + 1:L + 3] = jnp.zeros((2, slab, C), f32)
                for e in range(nbx):
                    c_r[n, j, e, slab:2 * slab] = zero8

    def swap_groups(tiles):
        height = tiles[0].shape[0]
        group = lax.broadcasted_iota(jnp.int32, (height, C), 1) // per
        tiles = list(tiles)
        s = 1
        while s < L:
            upper = group % (2 * s) >= s
            for at in range(L):
                if at % (2 * s) < s:
                    low, high = tiles[at], tiles[at + s]
                    tiles[at] = jnp.where(upper, pltpu.roll(high, s * per, 1), low)
                    tiles[at + s] = jnp.where(upper, high, pltpu.roll(low, C - s * per, 1))
            s *= 2
        return tiles

    def swap_rows(tile):
        group = lanes8 // per
        s = 1
        while s < L:
            upper = group % (2 * s) >= s
            later = rows8 % (2 * s) >= s
            ahead = pltpu.roll(pltpu.roll(tile, L - s, 0), s * per, 1)
            behind = pltpu.roll(pltpu.roll(tile, s, 0), C - s * per, 1)
            tile = jnp.where(later, jnp.where(upper, tile, behind), jnp.where(upper, ahead, tile))
            s *= 2
        return tile

    def times(full, table):
        height = full.shape[0]
        high = full.astype(jnp.bfloat16)
        wide = high.astype(f32)
        both = join([wide, full - wide], 0).astype(jnp.bfloat16)
        first = dot(both, hy[table, 0])
        return first[:height] + first[height:] + dot(high, hy[table, 1])

    def y_forward(n):
        columns = []
        for j in range(nby):
            from_left = a_r[n, (j + nby - 1) % nby, L]
            from_right = a_r[n, (j + 1) % nby, L]
            tiles = []
            for l in range(L):
                extra = jnp.where(
                    lanes8 == 0, from_left[:, L + l:L + l + 1],
                    jnp.where(lanes8 == C - 1, from_right[:, l:l + 1], 0.0))
                if n:
                    extra = jnp.where(
                        lanes8 == 1, from_left[:, 3 * L + l:3 * L + l + 1],
                        jnp.where(lanes8 == C - 2, from_right[:, 2 * L + l:2 * L + l + 1], extra))
                tiles.append(a_r[n, j, l] + extra)
            near, far = a_r[n, j, L + 1], zero8
            if n:
                near = near + jnp.where(
                    lanes8 == 0, from_left[:, 4 * L + 1:4 * L + 2],
                    jnp.where(lanes8 == C - 1, from_right[:, 4 * L:4 * L + 1], 0.0))
                far = a_r[n, j, L + 2]
            columns.append(join(tiles + [near, far], 0))
        low, high = join(columns[:nby // 2], 1), join(columns[nby // 2:], 1)
        out = join([times(low + high, 0), times(low - high, 1)], 1)
        tiles = [join([out[l * slab:(l + 1) * slab, t * C:(t + 1) * C] for t in range(nby)], 0)
                 for l in range(L)]
        tiles = swap_groups(tiles)
        for t in range(nby):
            halos = [swap_rows(out[(L + k) * slab:(L + k) * slab + L, t * C:(t + 1) * C])
                     for k in range(1 + n)]
            for e in range(L):
                b_s[n, t, e, 0:slab] = tiles[e][t * slab:(t + 1) * slab]
                for k, halo in enumerate(halos):
                    b_s[n, t, e, slab + k:slab + k + 1] = halo[e:e + 1]

    def y_backward(n):
        tiles = swap_groups([join([c_r[n, t, e, 0:slab] for t in range(nby)], 0)
                             for e in range(L)])
        rims = [join([swap_rows(join([c_r[n, t, e, slab + k:slab + k + 1] for e in range(L)], 0))
                      for t in range(nby)], 1) for k in range(2 - n)]
        if n:
            rims.append(jnp.zeros((slab, NY), f32))
        lines = [join([tiles[l][t * slab:(t + 1) * slab] for t in range(nby)], 1)
                 for l in range(L)]
        full = join(lines + rims, 0)
        even, odd = times(full[:, :NY // 2], 0), times(full[:, NY // 2:], 2)
        out = join([even + odd, even - odd], 1)
        near = out[L * slab:L * slab + L]
        for j in range(nby):
            edge = zero8
            left, right = (j + nby - 1) % nby * C, (j + 1) % nby * C
            wanted = [left + C - 1, right]
            if n == 0:
                wanted += [left + C - 2, right + 1, None, j * C, j * C + C - 1]
                edge = jnp.where(lanes8 == 4 * L, near[:, left + C - 1:left + C],
                                 jnp.where(lanes8 == 4 * L + 1, near[:, right:right + 1], edge))
            for l in range(L):
                line = out[l * slab:(l + 1) * slab]
                d_s[n, j, l] = line[:, j * C:(j + 1) * C]
                for at, column in enumerate(wanted):
                    if column is not None:
                        edge = jnp.where(
                            lanes8 == at * L + l, line[:, column:column + 1], edge)
            d_s[n, j, L] = edge
            for k in range(2 - n):
                d_s[n, j, L + 1 + k] = out[(L + k) * slab:(L + k) * slab + L,
                                           j * C:(j + 1) * C]

    def spectrum(n):
        tiles = []
        for i in range(nbx):
            for j in range(nby):
                tile = b_r[n, i, j, 0:slab]
                for k in range(1 + n):
                    line = slice(slab + k, slab + k + 1)
                    if j == 0:
                        tile = tile + jnp.where(
                            rows8 == k, b_r[n, (i + nbx - 1) % nbx, nby - 1, line], 0.0)
                    if j == nby - 1:
                        tile = tile + jnp.where(
                            rows8 == slab - 1 - k, b_r[n, (i + 1) % nbx, 0, line], 0.0)
                tiles.append(tile)
        full = join(tiles, 0).T
        high = full.astype(jnp.bfloat16)
        wide = high.astype(f32)
        both = join([wide, full - wide], 0).astype(jnp.bfloat16)
        first = dot(both, hx[0])
        out = (first[:C] + first[C:] + dot(high, hx[1])) * scale
        return [out[l * per:(l + 1) * per] for l in range(L)]

    def solve(sources):
        primes = []
        for l in range(L):
            source = sources[l]
            if l:
                source = source + inter[l] * primes[-1]
            primes.append(source * coef[l])
        values = [primes[-1]]
        for l in range(L - 2, -1, -1):
            values.insert(0, primes[l] + ratio[l] * values[0])
        return values

    def x_backward(n, values):
        high, low = halves(join(values, 0))
        turn = functools.partial(
            lax.dot_general, dimension_numbers=(((1,), (1,)), ((), ())),
            preferred_element_type=f32)
        first = turn(hx[...].reshape(2 * NX, NX), high)
        out = first[:NX] + first[NX:] + turn(hx[0], low)
        for i in range(nbx):
            for j in range(nby):
                at = i * R + j * slab
                c_s[n, i, j, 0:slab] = out[at:at + slab]
                for k in range(2 - n):
                    line = (at - 1 - k if j == 0 else at + slab + k) % NX
                    c_s[n, i, j, slab + k:slab + k + 1] = out[line:line + 1]

    def flank_start(n, src):
        tile = zero
        for c in range(3):
            for l in range(L):
                at = c * L + l
                cell = src[c, l]
                row_s[n, 0, at:at + 1] = cell[0:1]
                row_s[n, 1, at:at + 1] = cell[R - 1:R]
                tile = jnp.where(lanes == at, cell[:, 0:1], tile)
                tile = jnp.where(lanes == C // 2 + at, cell[:, C - 1:C], tile)
        col_s[n] = tile

    def flank_send(n):
        return [
            push(row_s.at[n, 1], row_r.at[n, 0], {"bx": (bx + 1) % nbx}),
            push(row_s.at[n, 0], row_r.at[n, 1], {"bx": (bx + nbx - 1) % nbx}),
            push(col_s.at[n], col_r.at[n, 0], {"by": (by + 1) % nby}),
            push(col_s.at[n], col_r.at[n, 1], {"by": (by + nby - 1) % nby})]

    def relax_inside(src):
        for l in range(L):
            cells = [src[c, l] for c in range(3)]
            squares = [cell * cell for cell in cells]
            whole = squares[0] + squares[1] + squares[2]
            for c in range(3):
                cell, square = cells[c], squares[c]
                above = src[c, l + 1] if l + 1 < L else zero
                below = src[c, l - 1] if l else zero
                smooth = stiff[l] * (
                    (x_next(cell, 0.0) + x_prev(cell, 0.0) + y_next(cell, 0.0)
                     + y_prev(cell, 0.0) - 4.0 * cell) + (above + below - 2.0 * cell))
                drive = cell * (
                    2.0 * alpha[l] + 4.0 * landau[0, l] * square
                    + 2.0 * landau[1, l] * (whole - square)
                    + 6.0 * landau[2, l] * (square * square))
                base[c, l] = cell - step_size * (drive - smooth)

    def flank_lines(n):
        return [[row_r[n, side, c * L:(c + 1) * L] for c in range(3)] for side in range(2)]

    def relax_edges(lines, low_col, high_col, target):
        for l in range(L):
            weight = step_size * stiff[l]
            for c in range(3):
                at = c * L + l
                add = jnp.where(lanes == 0, low_col[:, C // 2 + at:C // 2 + at + 1], 0.0)
                add = add + jnp.where(lanes == C - 1, high_col[:, at:at + 1], 0.0)
                add = add + jnp.where(rows == 0, lines[0][c][l:l + 1], 0.0)
                add = add + jnp.where(rows == R - 1, lines[1][c][l:l + 1], 0.0)
                target[c, l] = base[c, l] + weight * add

    def moved_rim():
        lines = flank_lines(1)
        corners = []
        for side, owner in enumerate((0, nby - 1)):
            inner = join([d_r[0, owner, l, side * (slab - 1):side * (slab - 1) + 1]
                          for l in range(L)], 0)
            near, far = d_r[0, owner, L + 1], d_r[0, owner, L + 2]
            edge = d_r[0, owner, L]
            low, high = edge[:, 4 * L:4 * L + 1], edge[:, 4 * L + 1:4 * L + 2]
            down = [inner - far if side == 0 else far - inner,
                    jnp.where(lanes8 == C - 1, high, pltpu.roll(near, C - 1, 1))
                    - jnp.where(lanes8 == 0, low, pltpu.roll(near, 1, 1)),
                    jnp.where(rows8 == L - 1, 0.0, pltpu.roll(near, L - 1, 0))
                    - jnp.where(rows8 == 0, 0.0, pltpu.roll(near, 1, 0))]
            lines[side] = [line - (0.5 * step_size) * part
                           for line, part in zip(lines[side], down)]
            spot = jnp.where(lanes8 == rows8, low, jnp.where(lanes8 == rows8 + L, high, 0.0))
            corners.append(jnp.sum(spot, axis=0, keepdims=True))
        edge = join([d_r[0, j, L] for j in range(nby)], 0)
        layer = lanes % L
        group = lanes // L
        across = pltpu.roll(edge, C - 5 * L, 1) - pltpu.roll(edge, C - 2 * L, 1)
        down = [x_next(edge, corners[1]) - x_prev(edge, corners[0]),
                jnp.where(group == 0, across, -across),
                jnp.where(layer == L - 1, 0.0, pltpu.roll(edge, C - 1, 1))
                - jnp.where(layer == 0, 0.0, pltpu.roll(edge, 1, 1))]
        low_col, high_col = col_r[1, 0], col_r[1, 1]
        for c in range(3):
            part = (0.5 * step_size) * down[c]
            low_col = low_col - jnp.where(
                group == C // (2 * L) + c, pltpu.roll(part, C // 2 + c * L, 1), 0.0)
            high_col = high_col - jnp.where(
                group == c, pltpu.roll(part, (C + c * L - L) % C, 1), 0.0)
        return lines, low_col, high_col

    def field(n):
        edge = join([d_r[n, j, L] for j in range(nby)], 0)
        phis = [join([d_r[n, j, l] for j in range(nby)], 0) for l in range(L)]
        for l in range(L):
            phi = phis[l]
            low = d_r[n, 0, L + 1, l:l + 1]
            high = d_r[n, nby - 1, L + 1, l:l + 1]
            along_x = 0.5 * (x_next(phi, high) - x_prev(phi, low))
            along_y = 0.5 * (y_next(phi, edge[:, L + l:L + l + 1])
                             - y_prev(phi, edge[:, l:l + 1]))
            above = phis[l + 1] if l + 1 < L else zero
            below = phis[l - 1] if l else zero
            yield l, (along_x, along_y, 0.5 * (above - below))

    loads[0].wait()
    charge(0, p_in, None)
    pl.semaphore_wait(barrier, len(greeted))

    def tell(at):
        pl.semaphore_signal(
            known.at[at], inc=1, device_id={"bx": at_x[reach[at]]}, device_id_type=MESH)

    tell(0)
    first_a = among_y(a_s, a_r, 0, L + 2, True)
    if nby == 4:
        pl.when(jnp.logical_not(rim_slab))(clear_rims)
    flank_start(0, p_in)
    loads[1].wait()
    for load in loads[6:]:
        load.wait()
    relax_inside(p_in)
    charge(1, base, ring_of(0))
    second_a = among_y(a_s, a_r, 1, L + 3, True)
    for at in range(1, len(reach)):
        pl.semaphore_wait(known.at[at - 1], 1)
        tell(at)
    loads[2].wait()
    loads[3].wait()
    wave_x = wx[0:1]
    wave_y = join([wy[...]] * (NX // C), 1)
    lateral = wave_x + wave_y
    previous = None
    for l in range(L):
        pivot = perm[l] * lateral + inter[l] + inter[l + 1]
        if l:
            pivot = pivot - inter[l] * previous
        inverse = 1.0 / pivot
        coef[l] = inverse
        previous = inter[l + 1] * inverse
        ratio[l] = previous
    loads[4].wait()
    loads[5].wait()
    wait(first_a)
    y_forward(0)
    pl.semaphore_wait(known.at[len(reach) - 1], 1)
    first_b = spread(b_s, b_r, 0, False, slab + 1)
    wait(second_a)
    y_forward(1)
    second_b = spread(b_s, b_r, 1, False, slab + 2)
    flanks = flank_send(0)
    wait(first_b)
    values = solve(spectrum(0))
    x_backward(0, values)
    first_c = spread(c_s, c_r, 0, True, slab + 2)
    bend = -(wave_x * (1.0 - 0.25 * wave_x) + wave_y * (1.0 - 0.25 * wave_y))
    slopes = []
    none = jnp.zeros_like(values[0])
    for l in range(L):
        above = values[l + 1] if l + 1 < L else none
        below = values[l - 1] if l else none
        slopes.append(0.5 * (above - below))
    moved = []
    for l in range(L):
        above = slopes[l + 1] if l + 1 < L else none
        below = slopes[l - 1] if l else none
        moved.append(step_size * (bend * values[l] + 0.5 * (above - below)))
    wait(second_b)
    x_backward(1, solve([here + more for here, more in zip(spectrum(1), moved)]))
    second_c = spread(c_s, c_r, 1, True, slab + 1)
    wait(flanks)
    relax_edges(flank_lines(0), col_r[0, 0], col_r[0, 1], base)
    flank_start(1, base)
    flanks = flank_send(1)
    flush(len(flanks) + 2)
    wait(first_c)
    y_backward(0)
    first_d = among_y(d_s, d_r, 0, L + 3, False)
    wait(second_c)
    y_backward(1)
    second_d = among_y(d_s, d_r, 1, L + 2, False)
    wait(first_d)
    for l, parts in field(0):
        for c in range(3):
            p_mid[c, l] = base[c, l] - step_size * parts[c]
    wait(flanks)
    rim = moved_rim()
    relax_inside(p_mid)
    relax_edges(*rim, base_o)
    flush(1)
    wait(second_d)
    for l, parts in field(1):
        for c in range(3):
            down_o[c, l] = -parts[c]
            base_o[c, l] -= step_size * parts[c]
    flush(0)


def hand_over(first, second, first_h, second_h, sem):
    copies = [pltpu.make_async_copy(first, first_h, sem.at[0]),
              pltpu.make_async_copy(second, second_h, sem.at[1])]
    for copy in copies:
        copy.start()
    for copy in copies:
        copy.wait()


def fused_shards(polarization, alpha_field, landau, stiffness, permittivity, interfaces):
    _, L, R, C = polarization.shape
    nbx = lax.axis_size("bx")
    nby = lax.axis_size("by")
    grid_x, grid_y = nbx * R, nby * C
    per = C // L
    line = np.arange(grid_x)
    hx = fixed_table(line[:, None], line[None, :], grid_x)
    line = np.arange(grid_y // 2)
    modes = np.concatenate([2 * line, 2 * line + 1])
    hy = jnp.stack([fixed_table(left, right, grid_y) for left, right in (
        (line[:, None], 2 * line[None, :]), (line[:, None], 2 * line[None, :] + 1),
        (2 * line[:, None] + 1, line[None, :]))])
    wave_x = 4.0 * np.sin(np.pi * np.arange(grid_x) / grid_x) ** 2
    wave_x = jnp.asarray(np.tile(wave_x[None, :], (8, 1)).astype(np.float32))
    at = np.arange(nbx * nby)
    first = (at % nby) * C + (at // nby) * per
    mode = modes[(first[:, None] + np.arange(per)[None, :]).reshape(-1)]
    wave_y = 4.0 * np.sin(np.pi * mode / grid_y) ** 2
    wave_y = jnp.asarray(np.tile(wave_y[:, None], (1, C)).astype(np.float32))
    f32 = jnp.float32
    hbm = pl.BlockSpec(memory_space=pltpu.HBM)
    S = 2
    n_copies = S * (4 + 2 * (nby - 1) + 2 * (nbx * nby - 1))
    by_y = pltpu.VMEM((S, nby, L + 3, 8, C), f32)
    by_mode = pltpu.VMEM((S, nby, nbx, 16, C), f32)
    by_place = pltpu.VMEM((S, nbx, nby, 16, C), f32)
    scratch = [
        pltpu.VMEM((3, L, R, C), f32), pltpu.VMEM((3, L, R, C), f32),
        pltpu.VMEM((L, per, grid_x), f32), pltpu.VMEM((L, per, grid_x), f32),
        by_y, by_y, by_mode, by_place, by_place, by_mode, by_y, by_y,
        pltpu.VMEM((S, 2, 3 * L, C), f32), pltpu.VMEM((S, 2, 3 * L, C), f32),
        pltpu.VMEM((S, R, C), f32), pltpu.VMEM((S, 2, R, C), f32),
        pltpu.SemaphoreType.DMA((n_copies,)), pltpu.SemaphoreType.DMA((n_copies,)),
        pltpu.SemaphoreType.REGULAR((nbx.bit_length(),)), pltpu.VMEM((3, L, R, C), f32),
        pltpu.VMEM((L, R, C), f32), pltpu.VMEM(wave_x.shape, f32), pltpu.VMEM((per, C), f32),
        pltpu.VMEM(hx.shape, hx.dtype), pltpu.VMEM(hy.shape, hy.dtype),
        pltpu.SMEM(landau.shape, f32), pltpu.SMEM(stiffness.shape, f32),
        pltpu.SMEM(permittivity.shape, f32), pltpu.SMEM(interfaces.shape, f32),
        pltpu.SemaphoreType.DMA((10,)),
    ]
    out = pltpu.VMEM(polarization.shape, f32)
    base, down = pl.pallas_call(
        functools.partial(fused, (L, R, C, nbx, nby)),
        out_shape=(out, out),
        in_specs=[hbm] * 10,
        out_specs=(pl.BlockSpec(memory_space=pltpu.VMEM), pl.BlockSpec(memory_space=pltpu.VMEM)),
        scratch_shapes=scratch,
        compiler_params=pltpu.CompilerParams(
            collective_id=0, has_side_effects=True, vmem_limit_bytes=66 * 1000 * 1000),
    )(polarization, alpha_field, landau, stiffness, permittivity, interfaces,
      wave_x, wave_y, hx, hy)
    out = jax.ShapeDtypeStruct(polarization.shape, f32)
    chip = pl.BlockSpec(memory_space=pltpu.VMEM)
    return pl.pallas_call(
        hand_over, out_shape=(out, out), in_specs=[chip, chip], out_specs=(hbm, hbm),
        scratch_shapes=[pltpu.SemaphoreType.DMA((2,))],
    )(base, down)


def solution(mesh):
    def run(polarization, *rest):
        _, L, R, C = polarization.shape
        body = fused_shards if fits(L, R, C, lax.axis_size("bx"), lax.axis_size("by")) else shards
        return body(polarization, *rest)

    return jax.shard_map(
        run,
        mesh=mesh,
        in_specs=(P(None, None, "bx", "by"), P(None, "bx", "by"), P(), P(), P(), P()),
        out_specs=(P(None, None, "bx", "by"), P(None, None, "bx", "by")),
        check_vma=False,
    )
```
